32 devices in a mesh: dp: 8 (over z, x), mp: 4 (over y, core).
Axes of the slice: x: 2, y: 2, z: 4, core: 2. Of those that a mesh axis runs over, the one named last changes fastest.
Arguments:
- tokens: bfloat16 [24576, 768], P('dp', 'mp'), may hold values from -80 to 80
- image_ids: int32 [24, 1024], P('dp'), may hold values from 0 to 5, never falling along the last dimension, each value on 1 to 512 neighbouring positions
- norm_gain: bfloat16 [768], P('mp'), may hold values from 0.25 to 1.75
- qkv_weight: bfloat16 [768, 3, 768], P(None, None, 'mp'), may hold values from -0.21875 to 0.21875
- qk_gain: bfloat16 [2, 768], P(None, 'mp'), may hold values from 0.25 to 1.75
- attn_weight: bfloat16 [768, 768], P('mp'), may hold values from -1.5 to 1.5
- up_weight: bfloat16 [768, 3072], P(None, 'mp'), may hold values from -1 to 1
- up_bias: bfloat16 [3072], P('mp'), may hold values from -3 to 3
- down_weight: bfloat16 [3072, 768], P('mp'), may hold values from -0.109375 to 0.109375
- down_bias: bfloat16 [768], P('mp'), may hold values from -3 to 3
- cotangent: bfloat16 [24576, 768], P('dp'), may hold values from -6 to 6
Outputs:
- block_out: bfloat16 [24576, 768], P('dp', 'mp')
- token_grad: float32 [24576, 768], P('dp', 'mp')
- gain_grad: float32 [768], P('mp')
- qkv_grad: float32 [768, 3, 768], P(None, None, 'mp')
- qkgain_grad: float32 [2, 768], P(None, 'mp')
- attn_grad: float32 [768, 768], P('mp')
- up_grad: float32 [768, 3072], P(None, 'mp')
- upbias_grad: float32 [3072], P('mp')
- down_grad: float32 [3072, 768], P('mp')
- downbias_grad: float32 [768], P('mp')
The draws below stay inside these ranges and needn't reach their ends.
Inputs may be any that keep to these rules, and one draw needn't show every extreme that they name: `image_ids`: in each sequence the image ids start at 0 and never fall; each of the 6 images has 1 to 512 tokens, and one has exactly 512.
All inputs are finite; a program needn't handle non-finite values.
Results may differ from the reference program's by a relative error of at most 0.012.
Values may be sent and summed in bfloat16 or wider, within the bound.
No kernel may reach another device: no remote copies, remote signals or barrier semaphores. Data moves between devices by JAX's collectives and lax.ppermute only.
A program may use at most 192 MiB of HBM per device.

```python
import math
import jax
import jax.numpy as jnp
import numpy as np
from jax import lax

D = 768
H = 12
DH = 64
FF = 3072
LEN = 1024
SEQ_DEV = 3
IMAGES = 6
MOST = 512
SEQS = 24
TOKENS = 24576


def draw_tokens(key, part):
    sub_keys = jax.random.split(key, 3)
    row_scale = jnp.exp(jax.random.uniform(sub_keys[0], (TOKENS, 1), jnp.float32, jnp.log(0.3), jnp.log(3.0)))
    column_place = jnp.arange(D, dtype=jnp.float32)[None, :] / D
    column_scale = 3.0 ** (column_place - 0.5) * jnp.exp(jax.random.uniform(sub_keys[1], (1, D), jnp.float32, -0.3, 0.3))
    base_values = jnp.clip(jax.random.normal(sub_keys[2], (TOKENS, D), jnp.float32), -6.0, 6.0)
    return (base_values * row_scale * column_scale).astype(jnp.bfloat16)


def draw_up_weight(key, part):
    sub_keys = jax.random.split(key, 2)
    base_values = jnp.clip(jax.random.normal(sub_keys[0], (D, FF), jnp.float32), -6.0, 6.0)
    column_offset = 0.5 * jnp.clip(jax.random.normal(sub_keys[1], (1, FF), jnp.float32), -3.0, 3.0)
    return ((base_values + column_offset) * (1.0 / jnp.sqrt(jnp.float32(D)))).astype(jnp.bfloat16)


def levels(stream_key, dims, cuts, least, top_value):
    def one(position, shards_of):
        steps = jax.random.uniform(jax.random.fold_in(jax.random.fold_in(stream_key, 6), position), (shards_of,), jnp.float32, least / len(cuts), top_value / len(cuts))
        return jnp.repeat(jnp.exp(steps), dims[position] // shards_of).reshape((-1,) + (1,) * (len(dims) - position - 1))

    level = one(*cuts[0])
    for cut in cuts[1:]:
        level = level * one(*cut)
    return level


def profile(number_of, total, limit, skew):
    portions = [(1 << 20) // math.isqrt(rank ** skew) + 1 for rank in range(2, number_of + 1)]
    surplus, holding = total - limit - (number_of - 1), [1] * (number_of - 1)
    while surplus > 0:
        free = [i for i in range(number_of - 1) if holding[i] < limit]
        mass, left = sum([portions[i] for i in free]), surplus
        for i in free:
            more = min(limit - holding[i], max(1, left * portions[i] // mass), surplus)
            holding[i] = holding[i] + more
            surplus = surplus - more
    return np.array([limit] + holding)


def uneven(key, number_of, total, limit, lean):
    if number_of == 2:
        one = jax.random.randint(key, (), max(1, total - limit), min(limit, total - 1) + 1)
        return jnp.stack([one, total - one])
    tallies = jnp.asarray(profile(number_of, total, limit, lean), jnp.int32)
    pairs = (number_of - 1) // 2
    donor, sink = tallies[1:1 + 2 * pairs:2], tallies[2:2 + 2 * pairs:2]
    slack = jnp.minimum(donor - 1, limit - sink)
    moved = jax.random.randint(jax.random.fold_in(key, 1), (pairs,), 0, 1 << 20) % (slack + 1)
    tallies = tallies.at[1:1 + 2 * pairs:2].set(donor - moved).at[2:2 + 2 * pairs:2].set(sink + moved)
    return tallies[jax.random.permutation(jax.random.fold_in(key, 2), number_of)]


def normal_values(key, shape, scale, reach, cuts=(), kind=jnp.bfloat16):
    level = levels(key, shape, cuts, -0.22, 0.18) if cuts else 1.0
    entries = jax.random.normal(key, shape, jnp.float32) * scale * level
    return jnp.minimum(jnp.maximum(entries, -reach), reach).astype(kind)


def setup_inputs(seed: int = 0) -> dict:
    key_of = jax.random.split(jax.random.key(seed), 12)
    return {
        "tokens": draw_tokens(jax.random.fold_in(key_of[11], 71), 0),
        "image_ids": jax.vmap(lambda own: jnp.searchsorted(jnp.cumsum(uneven(own, IMAGES, LEN, MOST, 1)), jnp.arange(LEN), side="right"))(jax.random.split(key_of[1], SEQS)).reshape((SEQS, LEN)).astype(jnp.int32),
        "norm_gain": jnp.clip(1.0 + 0.15 * jax.random.normal(key_of[2], (D,), jnp.float32), 0.25, 1.75).astype(jnp.bfloat16),
        "qkv_weight": normal_values(key_of[3], (D, 3, D), D ** -0.5, 0.21875, ((2, 4),)),
        "qk_gain": jnp.clip(1.0 + 0.15 * jax.random.normal(key_of[4], (2, D), jnp.float32), 0.25, 1.75).astype(jnp.bfloat16),
        "attn_weight": normal_values(key_of[5], (D, D), (max(D // 48, 1)) ** -0.5, 1.5, ((0, 4),)),
        "up_weight": draw_up_weight(jax.random.fold_in(key_of[11], 71), 0),
        "up_bias": normal_values(key_of[7], (FF,), 0.5, 3.0, ((0, 4),)),
        "down_weight": normal_values(key_of[8], (FF, D), FF ** -0.5, 0.109375, ((0, 4),)),
        "down_bias": normal_values(key_of[9], (D,), 0.5, 3.0, ((0, 4),)),
        "cotangent": normal_values(key_of[10], (TOKENS, D), 1.0, 6.0, ((0, 8),)),
    }


EPSILON = 1e-06
MASKED = -1e+30
PRECISE = lax.Precision.HIGHEST

@jax.custom_vjp
def low(v):
    return lax.optimization_barrier(v.astype(jnp.bfloat16)).astype(jnp.float32)

@jax.custom_vjp
def low_back(v):
    return v

def low_keep(v):
    return (low(v), None)

def low_pass(kept, grad):
    return (grad,)

def back_keep(v):
    return (v, None)

def back_low(kept, grad):
    return (low(grad),)
low.defvjp(low_keep, low_pass)
low_back.defvjp(back_keep, back_low)

def matmul(left, right):
    return jnp.dot(left, right, precision=PRECISE, preferred_element_type=jnp.float32)

def layer_norm(rows, gain):
    centre = lax.optimization_barrier(jnp.mean(rows, axis=-1, keepdims=True))
    spread = lax.optimization_barrier(jnp.mean(rows * rows, axis=-1, keepdims=True)) - centre * centre
    return (rows - centre) * lax.rsqrt(spread + EPSILON) * gain

def head_norm(raw_rows, head_gain):
    centre = lax.optimization_barrier(jnp.mean(raw_rows, axis=-1, keepdims=True))
    shifted = raw_rows - centre
    spread = lax.optimization_barrier(jnp.mean(shifted * shifted, axis=-1, keepdims=True))
    return shifted * lax.rsqrt(spread + EPSILON) * head_gain

def attend(block_item):
    queries, key_rows, value_rows, id_seq = block_item
    scores = jnp.einsum('qhd,khd->hqk', queries, key_rows, precision=PRECISE)
    scores = low_back(scores)
    same_image = (id_seq[:, None] == id_seq[None, :])[None]
    scores = jnp.where(same_image, scores, MASKED)
    weights = low(jax.nn.softmax(scores, axis=-1))
    return jnp.einsum('hqk,khd->qhd', weights, value_rows, precision=PRECISE)

def forward(rows_in, norm_gain, qkv_weight, qk_gain, attn_weight, up_weight, up_bias, down_weight, down_bias, id_group):
    rows_flat = rows_in.reshape(-1, D)
    token_count = rows_flat.shape[0]
    normed = low(layer_norm(rows_flat, norm_gain))
    qkv_raw = low_back(matmul(normed, qkv_weight.reshape(D, 3 * D)))
    head_gains = qk_gain.reshape(2, H, DH)
    queries = head_norm(qkv_raw[:, :D].reshape(token_count, H, DH), head_gains[0]) * DH ** (-0.5)
    key_rows = head_norm(qkv_raw[:, D:2 * D].reshape(token_count, H, DH), head_gains[1])
    value_rows = qkv_raw[:, 2 * D:].reshape(token_count, H, DH)
    queries = low(queries).reshape(-1, LEN, H, DH)
    key_rows = low(key_rows).reshape(-1, LEN, H, DH)
    value_rows = low(value_rows).reshape(-1, LEN, H, DH)
    attended = lax.map(jax.checkpoint(attend), (queries, key_rows, value_rows, id_group))
    attended = low(low_back(attended.reshape(token_count, D)))
    hidden_pre = low_back(matmul(normed, up_weight) + up_bias)
    active = low(jax.nn.gelu(hidden_pre))
    branch = matmul(attended, attn_weight) + matmul(active, down_weight)
    return rows_flat + branch + down_bias

def reference(tokens, image_ids, norm_gain, qkv_weight, qk_gain, attn_weight, up_weight, up_bias, down_weight, down_bias, cotangent):
    params = tuple((p.astype(jnp.float32) for p in (norm_gain, qkv_weight, qk_gain, attn_weight, up_weight, up_bias, down_weight, down_bias)))
    groups = SEQS // SEQ_DEV
    token_groups = tokens.astype(jnp.float32).reshape(groups, SEQ_DEV, LEN, D)
    cot_groups = cotangent.astype(jnp.float32).reshape(groups, SEQ_DEV * LEN, D)
    id_groups = image_ids.reshape(groups, SEQ_DEV, LEN)

    def group_step(totals, block_item):
        rows_in, cot_rows, id_group = block_item

        def run_block(rows_arg, *param_args):
            return forward(rows_arg, *param_args, id_group)
        result, pullback = jax.vjp(run_block, rows_in, *params)
        grads = pullback(cot_rows)
        totals = tuple((t + g for t, g in zip(totals, grads[1:])))
        return (totals, (result.astype(jnp.bfloat16), grads[0]))
    zeros = tuple((jnp.zeros(p.shape, jnp.float32) for p in params))
    totals, (outputs, input_grads) = lax.scan(group_step, zeros, (token_groups, cot_groups, id_groups))
    block_out = outputs.reshape(TOKENS, D)
    token_grad = input_grads.reshape(TOKENS, D)
    return (block_out, token_grad, totals[0], totals[1], totals[2], totals[3], totals[4], totals[5], totals[6], totals[7])
```

```python
import functools

import jax
import jax.numpy as jnp
from jax import lax
from jax.experimental import pallas as pl
from jax.experimental.pallas import tpu as pltpu
from jax.sharding import PartitionSpec as P

DH = 64
LEN = 1024
EPSILON = 1e-06
IMAGE_SLOTS = 16
PENALTY = 1024.0
BI = 256
BJ = 256
F32 = jnp.float32
BF16 = jnp.bfloat16

NN = (((1,), (0,)), ((), ()))
NT = (((1,), (1,)), ((), ()))


def dot(left, right, dims=NN):
    return lax.dot_general(left, right, dims, preferred_element_type=F32)


def fold_lanes(rows):
    total = rows[:, :128]
    for start in range(128, rows.shape[1], 128):
        total = total + rows[:, start : start + 128]
    return total


def hidden_kernel(
    own, flip_y, flip_c, flip_cy, gain, up_t, up_bias, d_act, normed, active, d_pre, stats, bias_sum
):
    pieces = (own, flip_y, flip_c, flip_cy)
    part = own.shape[0]
    width = part * 4
    total = 0.0
    squares = 0.0
    for piece in pieces:
        rows = piece[...].astype(F32)
        total = total + jnp.sum(rows, axis=0, keepdims=True)
        squares = squares + jnp.sum(rows * rows, axis=0, keepdims=True)
    mean = total * (1.0 / width)
    scale = lax.rsqrt(squares * (1.0 / width) - mean * mean + EPSILON)
    stats[0:1, :] = mean
    stats[1:2, :] = scale
    stats[2:8, :] = jnp.zeros((6, stats.shape[1]), F32)
    for slot, piece in enumerate(pieces):
        rows = piece[...].astype(F32)
        here = slice(slot * part, (slot + 1) * part)
        normed[here, :] = ((rows - mean) * scale * gain[here, :]).astype(BF16)

    @pl.when(pl.program_id(0) == 0)
    def _():
        bias_sum[...] = jnp.zeros_like(bias_sum)

    c0 = 0.7978845608028654
    c1 = 0.044715 * c0
    for start in range(0, up_t.shape[0], 256):
        here = slice(start, start + 256)
        pre = dot(up_t[here, :], normed[...]) + up_bias[here, :]
        square = pre * pre
        half = 0.5 * jnp.tanh(pre * (c0 + c1 * square)) + 0.5
        active[here, :] = (pre * half).astype(BF16)
        slope = half + pre * (half - half * half) * (2.0 * c0 + 6.0 * c1 * square)
        grad = (d_act[here, :].astype(F32) * slope).astype(BF16)
        d_pre[here, :] = grad
        bias_sum[here, :] += fold_lanes(grad.astype(F32))


def hidden_call(pieces, gain, up_t, up_bias, d_act, seq, block=512):
    part = pieces[0].shape[0]
    width = 4 * part
    hidden = up_t.shape[0]
    steps = LEN // block
    lanes = lambda i: (0, i)
    fixed = lambda i: (0, 0)
    return pl.pallas_call(
        hidden_kernel,
        grid=(steps,),
        in_specs=[pl.BlockSpec((part, block), lanes)] * 4
        + [
            pl.BlockSpec((width, 1), fixed),
            pl.BlockSpec((hidden, width), fixed),
            pl.BlockSpec((hidden, 1), fixed),
            pl.BlockSpec((hidden, block), lambda i: (0, seq * steps + i)),
        ],
        out_specs=[
            pl.BlockSpec((width, block), lanes),
            pl.BlockSpec((hidden, block), lanes),
            pl.BlockSpec((hidden, block), lanes),
            pl.BlockSpec((8, block), lanes),
            pl.BlockSpec((hidden, 128), fixed),
        ],
        out_shape=[
            jax.ShapeDtypeStruct((width, LEN), BF16),
            jax.ShapeDtypeStruct((hidden, LEN), BF16),
            jax.ShapeDtypeStruct((hidden, LEN), BF16),
            jax.ShapeDtypeStruct((8, LEN), F32),
            jax.ShapeDtypeStruct((hidden, 128), F32),
        ],
        cost_estimate=pl.CostEstimate(
            flops=3 * 2 * LEN * width * hidden, bytes_accessed=12_000_000, transcendentals=LEN * hidden
        ),
        name="hidden",
    )(*pieces, gain, up_t, up_bias, d_act)


def attention_kernel(
    first, count, qkv, d_att, mask_q, mask_k, gains, attended, d_mixed, gain_sum,
    qx, kx, vn, kt, vt, es, ps, oa, dqa, dka, dva,
):
    part = attended.shape[0]
    heads = part // DH
    inv_dh = 1.0 / DH

    def unit(start):
        raw = qkv[start : start + DH, :]
        shifted = raw - jnp.sum(raw, axis=0, keepdims=True) * inv_dh
        scale = lax.rsqrt(jnp.sum(shifted * shifted, axis=0, keepdims=True) * inv_dh + EPSILON)
        return shifted * scale, scale

    zeros = jnp.zeros((128 - DH - IMAGE_SLOTS, LEN), BF16)
    for head in range(heads):
        rows = slice(head * DH, (head + 1) * DH)
        query, _ = unit(head * DH)
        query = (query * (gains[rows, :] * 0.125)).astype(BF16)
        qx[head] = jnp.concatenate([query, mask_q[...], zeros], axis=0)
        key, _ = unit(part + head * DH)
        key = (key * gains[part + head * DH : part + (head + 1) * DH, :]).astype(BF16)
        kt[rows, :] = key
        kx[head] = jnp.concatenate([key, mask_k[...], zeros], axis=0).T
        value = qkv[2 * part + head * DH : 2 * part + (head + 1) * DH, :].astype(BF16)
        vt[rows, :] = value
        vn[head] = value.T
    dka[...] = jnp.zeros_like(dka)
    dva[...] = jnp.zeros_like(dva)

    def query_block(ib, _):
        i0 = pl.multiple_of(ib * BI, BI)
        icols = pl.ds(i0, BI)
        base = first[ib]
        trips = count[ib]

        def scores(j, carry):
            j0 = pl.multiple_of((base + j) * BJ, BJ)
            slot = pl.multiple_of(j * BJ, BJ)
            out = []
            for head in range(heads):
                rows = slice(head * DH, (head + 1) * DH)
                e = jnp.exp(dot(kx[head, pl.ds(j0, BJ), :], qx[head, :, icols]))
                p = dot(vn[head, pl.ds(j0, BJ), :], d_att[rows, icols])
                es[head, pl.ds(slot, BJ), :] = e
                ps[head, pl.ds(slot, BJ), :] = p
                out.append(carry[2 * head] + jnp.sum(e.reshape(BJ // 8, 8, BI), axis=0))
                out.append(carry[2 * head + 1] + jnp.sum((e * p).reshape(BJ // 8, 8, BI), axis=0))
            return tuple(out)

        sums = lax.fori_loop(0, trips, scores, tuple(jnp.zeros((8, BI), F32) for _ in range(2 * heads)))
        inverse = []
        inner = []
        for head in range(heads):
            inv = 1.0 / jnp.sum(sums[2 * head], axis=0, keepdims=True)
            inverse.append(inv)
            inner.append(jnp.sum(sums[2 * head + 1], axis=0, keepdims=True) * inv)
        oa[...] = jnp.zeros_like(oa)
        dqa[:, icols] = jnp.zeros((part, BI), F32)

        def grads(j, _):
            j0 = pl.multiple_of((base + j) * BJ, BJ)
            slot = pl.multiple_of(j * BJ, BJ)
            jcols = pl.ds(j0, BJ)
            for head in range(heads):
                rows = slice(head * DH, (head + 1) * DH)
                w = es[head, pl.ds(slot, BJ), :] * inverse[head]
                d = (w * (ps[head, pl.ds(slot, BJ), :] - inner[head])).astype(BF16)
                w = w.astype(BF16)
                oa[rows, :] += dot(vt[rows, jcols], w)
                dqa[rows, icols] += dot(kt[rows, jcols], d)
                dva[rows, jcols] += dot(d_att[rows, icols], w, NT)
                dka[rows, jcols] += dot(qx[head, :DH, icols], d, NT)
            return 0

        lax.fori_loop(0, trips, grads, 0)
        attended[:, icols] = oa[...].astype(BF16)
        return 0

    lax.fori_loop(0, LEN // BI, query_block, 0)

    for source, offset, factor in ((dqa, 0, 0.125), (dka, part, 1.0)):
        for head in range(heads):
            start = offset + head * DH
            u, scale = unit(start)
            e = source[head * DH : (head + 1) * DH, :] * factor
            gain_sum[start : start + DH, :] = fold_lanes(e * u)
            f = e * gains[start : start + DH, :]
            mean_f = jnp.sum(f, axis=0, keepdims=True) * inv_dh
            mean_fu = jnp.sum(f * u, axis=0, keepdims=True) * inv_dh
            d_mixed[start : start + DH, :] = ((f - mean_f - u * mean_fu) * scale).astype(BF16)
    d_mixed[2 * part :, :] = dva[...].astype(BF16)


def attention_call(first, count, qkv, d_att, mask_q, mask_k, gains, seq):
    part = d_att.shape[0]
    heads = part // DH
    once = lambda i, *_: (0, 0)
    grid_spec = pltpu.PrefetchScalarGridSpec(
        num_scalar_prefetch=2,
        grid=(1,),
        in_specs=[
            pl.BlockSpec((3 * part, LEN), once),
            pl.BlockSpec((part, LEN), lambda i, *_: (0, seq)),
            pl.BlockSpec((None, IMAGE_SLOTS, LEN), lambda i, *_: (seq, 0, 0)),
            pl.BlockSpec((None, IMAGE_SLOTS, LEN), lambda i, *_: (seq, 0, 0)),
            pl.BlockSpec((2 * part, 1), once),
        ],
        out_specs=[
            pl.BlockSpec((part, LEN), once),
            pl.BlockSpec((3 * part, LEN), once),
            pl.BlockSpec((2 * part, 128), once),
        ],
        scratch_shapes=[
            pltpu.VMEM((heads, 128, LEN), BF16),
            pltpu.VMEM((heads, LEN, 128), BF16),
            pltpu.VMEM((heads, LEN, DH), BF16),
            pltpu.VMEM((part, LEN), BF16),
            pltpu.VMEM((part, LEN), BF16),
            pltpu.VMEM((heads, LEN, BI), F32),
            pltpu.VMEM((heads, LEN, BI), F32),
            pltpu.VMEM((part, BI), F32),
            pltpu.VMEM((part, LEN), F32),
            pltpu.VMEM((part, LEN), F32),
            pltpu.VMEM((part, LEN), F32),
        ],
    )
    return pl.pallas_call(
        attention_kernel,
        grid_spec=grid_spec,
        out_shape=[
            jax.ShapeDtypeStruct((part, LEN), BF16),
            jax.ShapeDtypeStruct((3 * part, LEN), BF16),
            jax.ShapeDtypeStruct((2 * part, 128), F32),
        ],
        cost_estimate=pl.CostEstimate(
            flops=heads * 6 * 2 * LEN * LEN * 128, bytes_accessed=6_000_000, transcendentals=heads * LEN * LEN
        ),
        name="attention",
    )(first, count, qkv, d_att, mask_q, mask_k, gains)


def project_kernel(
    active, attended, d_pre, d_mixed, normed, down_t, attn_t, up, mixed, gain, keep, send, sums, gain_sum
):
    half = keep.shape[1]
    out = dot(down_t[...], active[...]) + dot(attn_t[...], attended[...])
    keep[0] = out[:half].astype(BF16)
    send[0] = out[half:].astype(BF16)
    grad = dot(up[...], d_pre[...]) + dot(mixed[...], d_mixed[...])
    keep[1] = grad[:half].astype(BF16)
    send[1] = grad[half:].astype(BF16)
    product = grad * normed[...].astype(F32)
    sums[0:1, :] = jnp.sum(grad * gain[...], axis=0, keepdims=True)
    sums[1:2, :] = jnp.sum(product, axis=0, keepdims=True)
    sums[2:8, :] = jnp.zeros((6, sums.shape[1]), F32)

    @pl.when(pl.program_id(0) == 0)
    def _():
        gain_sum[...] = jnp.zeros_like(gain_sum)

    gain_sum[...] += fold_lanes(product)


def project_call(active, attended, d_pre, d_mixed, normed, down_t, attn_t, up, mixed, gain, block=256):
    width, hidden = down_t.shape
    part = attended.shape[0]
    half = width // 2
    lanes = lambda i: (0, i)
    fixed = lambda i: (0, 0)
    return pl.pallas_call(
        project_kernel,
        grid=(LEN // block,),
        in_specs=[
            pl.BlockSpec((hidden, block), lanes),
            pl.BlockSpec((part, block), lanes),
            pl.BlockSpec((hidden, block), lanes),
            pl.BlockSpec((3 * part, block), lanes),
            pl.BlockSpec((width, block), lanes),
            pl.BlockSpec((width, hidden), fixed),
            pl.BlockSpec((width, part), fixed),
            pl.BlockSpec((width, hidden), fixed),
            pl.BlockSpec((width, 3 * part), fixed),
            pl.BlockSpec((width, 1), fixed),
        ],
        out_specs=[
            pl.BlockSpec((2, half, block), lambda i: (0, 0, i)),
            pl.BlockSpec((2, half, block), lambda i: (0, 0, i)),
            pl.BlockSpec((8, block), lanes),
            pl.BlockSpec((width, 128), fixed),
        ],
        out_shape=[
            jax.ShapeDtypeStruct((2, half, LEN), BF16),
            jax.ShapeDtypeStruct((2, half, LEN), BF16),
            jax.ShapeDtypeStruct((8, LEN), F32),
            jax.ShapeDtypeStruct((width, 128), F32),
        ],
        cost_estimate=pl.CostEstimate(
            flops=2 * LEN * width * (2 * hidden + 4 * part), bytes_accessed=16_000_000, transcendentals=0
        ),
        name="project",
    )(active, attended, d_pre, d_mixed, normed, down_t, attn_t, up, mixed, gain)


def finish_kernel(
    keep, from_core, from_y, own_t, tokens, cot, stats, sums, gain, bias, block_out, token_grad
):
    width = 4 * own_t.shape[0]
    branch = keep[0].astype(F32) + from_core[0].astype(F32) + from_y[0].astype(F32)
    block_out[...] = (tokens[...].astype(F32) + branch.T + bias[...]).astype(BF16)
    grad = keep[1].astype(F32) + from_core[1].astype(F32) + from_y[1].astype(F32)
    mean = stats[0:1, :]
    scale = stats[1:2, :]
    hat = (own_t[...].astype(F32) - mean) * scale
    inner = grad * gain[...] - sums[0:1, :] * (1.0 / width) - hat * (sums[1:2, :] * (1.0 / width))
    token_grad[...] = cot[...].astype(F32) + (inner * scale).T


def finish_call(keep, from_core, from_y, own_t, tokens, cot, stats, sums, gain, bias, seq, block=512):
    part = own_t.shape[0]
    steps = LEN // block
    lanes = lambda i: (0, i)
    fixed = lambda i: (0, 0)
    packed = pl.BlockSpec((2, part, block), lambda i: (0, 0, i))
    here = pl.BlockSpec((block, part), lambda i: (seq * steps + i, 0))
    return pl.pallas_call(
        finish_kernel,
        grid=(steps,),
        in_specs=[
            packed, packed, packed,
            pl.BlockSpec((part, block), lanes),
            here, here,
            pl.BlockSpec((8, block), lanes),
            pl.BlockSpec((8, block), lanes),
            pl.BlockSpec((part, 1), fixed),
            pl.BlockSpec((1, part), fixed),
        ],
        out_specs=[pl.BlockSpec((block, part), lambda i: (i, 0))] * 2,
        out_shape=[
            jax.ShapeDtypeStruct((LEN, part), BF16),
            jax.ShapeDtypeStruct((LEN, part), F32),
        ],
        cost_estimate=pl.CostEstimate(flops=20 * LEN * part, bytes_accessed=5_000_000, transcendentals=0),
        name="finish",
    )(keep, from_core, from_y, own_t, tokens, cot, stats, sums, gain, bias)


def flip(value, axis, size, bit):
    return lax.ppermute(value, axis, [(i, i ^ bit) for i in range(size)])


def scatter_sum(value, size, index):
    bit = 1
    while bit < size:
        half = value.shape[0] // 2
        side = (index // bit) % 2
        send = lax.dynamic_slice_in_dim(value, (1 - side) * half, half, 0)
        held = lax.dynamic_slice_in_dim(value, side * half, half, 0)
        arrived = flip(send, "dp", size, bit)
        value = (held.astype(F32) + arrived.astype(F32)).astype(BF16)
        bit *= 2
    return value


def gather_back(value, size, index):
    bit = size // 2
    while bit >= 1:
        side = (index // bit) % 2
        arrived = flip(value, "dp", size, bit)
        value = jnp.where(
            side == 1,
            jnp.concatenate([arrived, value], axis=0),
            jnp.concatenate([value, arrived], axis=0),
        )
        bit //= 2
    return value


def sum_over_dp(value, size, index):
    return gather_back(scatter_sum(value, size, index), size, index)


def body(
    dp_size,
    tokens,
    image_ids,
    norm_gain,
    qkv_weight,
    qk_gain,
    attn_weight,
    up_weight,
    up_bias,
    down_weight,
    down_bias,
    cotangent,
):
    part = tokens.shape[1]
    width = cotangent.shape[1]
    seqs = image_ids.shape[0]
    me = lax.axis_index("mp")
    dp = lax.axis_index("dp")
    order = (0, 2, 1, 3)

    def relative(rows):
        return jnp.concatenate(
            [lax.dynamic_slice_in_dim(rows, jnp.bitwise_xor(me, m) * part, part, 0) for m in order], axis=0
        )

    gain_own = jnp.broadcast_to(norm_gain[:, None], (part, 128))
    gain_y = flip(gain_own, "mp", 4, 2)
    gain_pieces = (gain_own, gain_y, flip(gain_own, "mp", 4, 1), flip(gain_y, "mp", 4, 1))
    gain_all = jnp.concatenate([g[:, :1] for g in gain_pieces], axis=0).astype(F32)
    pieces = []
    for seq in range(seqs):
        own = tokens[seq * LEN : (seq + 1) * LEN].T
        from_y = flip(own, "mp", 4, 2)
        pieces.append((own, from_y, flip(own, "mp", 4, 1), flip(from_y, "mp", 4, 1)))

    mixed_rel = relative(qkv_weight.reshape(width, 3 * part))
    mixed_t = mixed_rel.T
    up_rel = relative(up_weight)
    up_t = up_rel.T
    down_t = relative(down_weight.T)
    attn_t = relative(attn_weight.T)
    up_bias_col = up_bias.astype(F32)[:, None]
    head_gains = qk_gain.astype(F32).reshape(2 * part, 1)

    slots = jnp.arange(IMAGE_SLOTS, dtype=jnp.int32)[None, :, None]
    same = image_ids[:, None, :] == slots
    mask_q = same.astype(BF16)
    mask_k = jnp.where(same | (slots >= 8), 0.0, -PENALTY).astype(BF16)
    block_first = image_ids[:, ::BI]
    block_last = image_ids[:, BI - 1 :: BI]
    starts = jnp.sum(image_ids[:, None, :] < block_first[:, :, None], axis=2, dtype=jnp.int32)
    ends = jnp.sum(image_ids[:, None, :] <= block_last[:, :, None], axis=2, dtype=jnp.int32)
    first = starts // BJ
    count = (ends + BJ - 1) // BJ - first

    d_att = dot(attn_weight, cotangent, NT).astype(BF16)
    d_act = dot(down_weight, cotangent, NT).astype(BF16)
    cot_own = lax.dynamic_slice_in_dim(cotangent, me * part, part, 1)
    downbias_part = jnp.sum(cot_own.astype(F32), axis=0)

    hidden = [hidden_call(pieces[s], gain_all, up_t, up_bias_col, d_act, s) for s in range(seqs)]
    normed_t = jnp.concatenate([h[0] for h in hidden], axis=1)
    active_t = jnp.concatenate([h[1] for h in hidden], axis=1)
    d_pre_t = jnp.concatenate([h[2] for h in hidden], axis=1)
    upbias_part = jnp.sum(sum(h[4] for h in hidden), axis=1)

    down_grad = sum_over_dp(dot(active_t, cotangent).astype(BF16), dp_size, dp).astype(F32)
    up_grad = sum_over_dp(dot(normed_t, d_pre_t, NT).astype(BF16), dp_size, dp)

    qkv_t = [dot(mixed_t, h[0]) for h in hidden]
    gain_bias = down_bias.astype(F32)[None, :]
    gain_col = norm_gain.astype(F32)[:, None]
    outs = []
    grads = []
    gain_parts = []
    attended = []
    d_mixed = []
    qk_parts = []
    for seq in range(seqs):
        att, dm, gs = attention_call(first[seq], count[seq], qkv_t[seq], d_att, mask_q, mask_k, head_gains, seq)
        attended.append(att)
        d_mixed.append(dm)
        qk_parts.append(gs)
        normed, active, d_pre, stats, _ = hidden[seq]
        keep, send, sums, gp = project_call(
            active, att, d_pre, dm, normed, down_t, attn_t, up_rel, mixed_rel, gain_all
        )
        gain_parts.append(gp)
        sums = sums[:2] + flip(sums[:2], "mp", 4, 1)
        sums = sums + flip(sums, "mp", 4, 2)
        sums = jnp.concatenate([sums, jnp.zeros((6, LEN), F32)], axis=0)
        from_core = flip(send, "mp", 4, 1)
        onward = (keep[:, part:].astype(F32) + from_core[:, part:].astype(F32)).astype(BF16)
        from_y = flip(onward, "mp", 4, 2)
        out, grad = finish_call(
            keep, from_core, from_y, pieces[seq][0], tokens, cot_own, stats, sums, gain_col, gain_bias, seq
        )
        outs.append(out)
        grads.append(grad)
    block_out = jnp.concatenate(outs, axis=0)
    token_grad = jnp.concatenate(grads, axis=0)

    attended_t = jnp.concatenate(attended, axis=1)
    d_mixed_t = jnp.concatenate(d_mixed, axis=1)
    attn_grad = sum_over_dp(dot(attended_t, cotangent).astype(BF16), dp_size, dp).astype(F32)
    qkv_grad = sum_over_dp(dot(normed_t, d_mixed_t, NT).astype(BF16), dp_size, dp)

    def natural(rows):
        pieces = []
        for shard in range(4):
            m = jnp.bitwise_xor(me, shard)
            slot = jnp.where(m == 1, 2, jnp.where(m == 2, 1, m))
            pieces.append(lax.dynamic_slice_in_dim(rows, slot * part, part, 0))
        return jnp.concatenate(pieces, axis=0).astype(F32)

    gain_vec = jnp.sum(sum(gain_parts), axis=1)
    gain_shares = gain_vec.reshape(2, 2 * part)
    gain_half = gain_shares[0] + flip(gain_shares[1], "mp", 4, 1)
    gain_own_sum = gain_half[:part] + flip(gain_half[part:], "mp", 4, 2)
    short = jnp.concatenate(
        [gain_own_sum / norm_gain.astype(F32), jnp.sum(sum(qk_parts), axis=1), upbias_part, downbias_part]
    )
    bit = 1
    while bit < dp_size:
        short = short + flip(short, "dp", dp_size, bit)
        bit *= 2
    gain_grad = short[:part]
    qkgain_grad = short[part : 3 * part].reshape(2, part)
    upbias_grad = short[3 * part : 3 * part + upbias_part.shape[0]]
    downbias_grad = short[3 * part + upbias_part.shape[0] :]
    return (
        block_out,
        token_grad,
        gain_grad,
        natural(qkv_grad).reshape(width, 3, part),
        qkgain_grad,
        attn_grad,
        natural(up_grad),
        upbias_grad,
        down_grad,
        downbias_grad,
    )


def solution(mesh):
    in_specs = (
        P("dp", "mp"),
        P("dp", None),
        P("mp"),
        P(None, None, "mp"),
        P(None, "mp"),
        P("mp", None),
        P(None, "mp"),
        P("mp"),
        P("mp", None),
        P("mp"),
        P("dp", None),
    )
    out_specs = (
        P("dp", "mp"),
        P("dp", "mp"),
        P("mp"),
        P(None, None, "mp"),
        P(None, "mp"),
        P("mp", None),
        P(None, "mp"),
        P("mp"),
        P("mp", None),
        P("mp"),
    )
    run = functools.partial(body, mesh.shape["dp"])
    return jax.shard_map(run, mesh=mesh, in_specs=in_specs, out_specs=out_specs, check_vma=False)
```

```python
import functools

import jax
import jax.numpy as jnp
from jax import lax
from jax.experimental import pallas as pl
from jax.experimental.pallas import tpu as pltpu
from jax.sharding import PartitionSpec as P

DH = 64
LEN = 1024
EPSILON = 1e-06
IMAGE_SLOTS = 16
PENALTY = 1024.0
BI = 256
BJ = 256
SUM_ROWS = 16
F32 = jnp.float32
BF16 = jnp.bfloat16

NN = (((1,), (0,)), ((), ()))
NT = (((1,), (1,)), ((), ()))
ANY = pl.BlockSpec(memory_space=pl.ANY)


def dot(left, right, dims=NN):
    return lax.dot_general(left, right, dims, preferred_element_type=F32)


def fold_lanes(rows):
    total = rows[:, :128]
    for start in range(128, rows.shape[1], 128):
        total = total + rows[:, start : start + 128]
    return total


def cost(microseconds, nbytes):
    return pl.CostEstimate(flops=int(microseconds * 1e9), bytes_accessed=nbytes, transcendentals=0)


def early_kernel(cot, down, attn, d_act, d_att, bias_sum):
    rows = cot[...]
    d_act[...] = dot(down[...], rows, NT).astype(BF16)
    d_att[...] = dot(attn[...], rows, NT).astype(BF16)

    @pl.when(pl.program_id(0) == 0)
    def _():
        bias_sum[...] = jnp.zeros_like(bias_sum)

    wide = rows.astype(F32)
    bias_sum[...] += jnp.sum(wide.reshape(wide.shape[0] // 8, 8, wide.shape[1]), axis=0)


def early_call(cot, down, attn, block=512):
    tokens, width = cot.shape
    hidden, part = down.shape[0], attn.shape[0]
    fixed = lambda i: (0, 0)
    lanes = lambda i: (0, i)
    return pl.pallas_call(
        early_kernel,
        grid=(tokens // block,),
        in_specs=[
            pl.BlockSpec((block, width), lambda i: (i, 0)),
            pl.BlockSpec((hidden, width), fixed),
            pl.BlockSpec((part, width), fixed),
        ],
        out_specs=[
            pl.BlockSpec((hidden, block), lanes),
            pl.BlockSpec((part, block), lanes),
            pl.BlockSpec((8, width), fixed),
        ],
        out_shape=[
            jax.ShapeDtypeStruct((hidden, tokens), BF16),
            jax.ShapeDtypeStruct((part, tokens), BF16),
            jax.ShapeDtypeStruct((8, width), F32),
        ],
        cost_estimate=cost(7, 12_000_000),
        name="early",
    )(cot, down, attn)


def hidden_kernel(
    place, own, flip_y, flip_c, flip_cy, gain, up_t, up_bias, d_act, *rest
):
    normed, active, d_pre, stats, bias_sum = rest[-5:]
    pieces = (own, flip_y, flip_c, flip_cy)
    part = own.shape[0]
    width = part * 4
    total = 0.0
    squares = 0.0
    for piece in pieces:
        rows = piece[...].astype(F32)
        total = total + jnp.sum(rows, axis=0, keepdims=True)
        squares = squares + jnp.sum(rows * rows, axis=0, keepdims=True)
    mean = total * (1.0 / width)
    scale = lax.rsqrt(squares * (1.0 / width) - mean * mean + EPSILON)
    stats[0:1, :] = mean
    stats[1:2, :] = scale
    stats[2:8, :] = jnp.zeros((6, stats.shape[1]), F32)
    for slot, piece in enumerate(pieces):
        rows = piece[...].astype(F32)
        here = pl.ds(pl.multiple_of(place[slot], part), part)
        normed[here, :] = ((rows - mean) * scale * gain[here, :]).astype(BF16)

    @pl.when(pl.program_id(0) == 0)
    def _():
        bias_sum[...] = jnp.zeros_like(bias_sum)

    c0 = 0.7978845608028654
    c1 = 0.044715 * c0
    for start in range(0, up_t.shape[0], 256):
        here = slice(start, start + 256)
        pre = dot(up_t[here, :], normed[...]) + up_bias[here, :]
        square = pre * pre
        half = 0.5 * jnp.tanh(pre * (c0 + c1 * square)) + 0.5
        active[here, :] = (pre * half).astype(BF16)
        slope = half + pre * (half - half * half) * (2.0 * c0 + 6.0 * c1 * square)
        grad = (d_act[here, :].astype(F32) * slope).astype(BF16)
        d_pre[here, :] = grad
        bias_sum[here, :] += fold_lanes(grad.astype(F32))


def hidden_call(place, pieces, gain, up_t, up_bias, d_act, before, seq, block=512):
    part = pieces[0].shape[0]
    width = 4 * part
    hidden, tokens = d_act.shape
    steps = LEN // block
    lanes = lambda i, *_: (0, i)
    ours = lambda i, *_: (0, seq * steps + i)
    fixed = lambda i, *_: (0, 0)
    grid_spec = pltpu.PrefetchScalarGridSpec(
        num_scalar_prefetch=1,
        grid=(steps,),
        in_specs=[pl.BlockSpec((part, block), lanes)] * 4
        + [
            pl.BlockSpec((width, 1), fixed),
            pl.BlockSpec((hidden, width), fixed),
            pl.BlockSpec((hidden, 1), fixed),
            pl.BlockSpec((hidden, block), ours),
        ]
        + [ANY] * len(before),
        out_specs=[
            pl.BlockSpec((width, block), ours),
            pl.BlockSpec((hidden, block), ours),
            pl.BlockSpec((hidden, block), ours),
            pl.BlockSpec((8, block), lanes),
            pl.BlockSpec((hidden, 128), fixed),
        ],
    )
    return pl.pallas_call(
        hidden_kernel,
        grid_spec=grid_spec,
        out_shape=[
            jax.ShapeDtypeStruct((width, tokens), BF16),
            jax.ShapeDtypeStruct((hidden, tokens), BF16),
            jax.ShapeDtypeStruct((hidden, tokens), BF16),
            jax.ShapeDtypeStruct((8, LEN), F32),
            jax.ShapeDtypeStruct((hidden, 128), F32),
        ],
        input_output_aliases={9 + i: i for i in range(len(before))},
        cost_estimate=cost(7, 8_000_000),
        name="hidden",
    )(place, *pieces, gain, up_t, up_bias, d_act, *before)


def split_store(side, low, high, keep, send):
    @pl.when(side == 0)
    def _():
        keep[...] = low[...].astype(BF16)
        send[...] = high[...].astype(BF16)

    @pl.when(side != 0)
    def _():
        keep[...] = high[...].astype(BF16)
        send[...] = low[...].astype(BF16)


def mlp_grad_kernel(side, active, cot, normed, d_pre, keep, send, low, high):
    down = dot(active[...], cot[...])
    up = dot(normed[...], d_pre[...], NT)

    @pl.when(pl.program_id(0) == 0)
    def _():
        low[...] = down
        high[...] = up

    @pl.when(pl.program_id(0) > 0)
    def _():
        low[...] += down
        high[...] += up

    @pl.when(pl.program_id(0) == pl.num_programs(0) - 1)
    def _():
        split_store(side[0], low, high, keep, send)


def mlp_grad_call(side, active, cot, normed, d_pre, block=1024):
    hidden, tokens = active.shape
    width = normed.shape[0]
    lanes = lambda i, *_: (0, i)
    fixed = lambda i, *_: (0, 0)
    grid_spec = pltpu.PrefetchScalarGridSpec(
        num_scalar_prefetch=1,
        grid=(tokens // block,),
        in_specs=[
            pl.BlockSpec((hidden, block), lanes),
            pl.BlockSpec((block, width), lambda i, *_: (i, 0)),
            pl.BlockSpec((width, block), lanes),
            pl.BlockSpec((hidden, block), lanes),
        ],
        out_specs=[pl.BlockSpec((hidden, width), fixed)] * 2,
        scratch_shapes=[pltpu.VMEM((hidden, width), F32)] * 2,
    )
    return pl.pallas_call(
        mlp_grad_kernel,
        grid_spec=grid_spec,
        out_shape=[jax.ShapeDtypeStruct((hidden, width), BF16)] * 2,
        cost_estimate=cost(10, 20_000_000),
        name="mlp_grad",
    )(side, active, cot, normed, d_pre)


def mix_grad_kernel(side, d_mixed, normed, attended, cot, keep, send, total):
    split = d_mixed.shape[0]
    mixed = dot(d_mixed[...], normed[...], NT)
    attn = dot(attended[...], cot[...])

    @pl.when(pl.program_id(0) == 0)
    def _():
        total[:split, :] = mixed
        total[split:, :] = attn

    @pl.when(pl.program_id(0) > 0)
    def _():
        total[:split, :] += mixed
        total[split:, :] += attn

    @pl.when(pl.program_id(0) == pl.num_programs(0) - 1)
    def _():
        half = keep.shape[0]
        split_store(side[0], total.at[:half], total.at[half:], keep, send)


def mix_grad_call(side, d_mixed, normed, attended, cot, block=1024):
    mixed, tokens = d_mixed.shape
    width = normed.shape[0]
    part = attended.shape[0]
    lanes = lambda i, *_: (0, i)
    fixed = lambda i, *_: (0, 0)
    half = (mixed + part) // 2
    grid_spec = pltpu.PrefetchScalarGridSpec(
        num_scalar_prefetch=1,
        grid=(tokens // block,),
        in_specs=[
            pl.BlockSpec((mixed, block), lanes),
            pl.BlockSpec((width, block), lanes),
            pl.BlockSpec((part, block), lanes),
            pl.BlockSpec((block, width), lambda i, *_: (i, 0)),
        ],
        out_specs=[pl.BlockSpec((half, width), fixed)] * 2,
        scratch_shapes=[pltpu.VMEM((2 * half, width), F32)],
    )
    return pl.pallas_call(
        mix_grad_kernel,
        grid_spec=grid_spec,
        out_shape=[jax.ShapeDtypeStruct((half, width), BF16)] * 2,
        cost_estimate=cost(6, 15_000_000),
        name="mix_grad",
    )(side, d_mixed, normed, attended, cot)


def attention_kernel(first, count, normed, mixed_t, d_att, mask_q, mask_k, gains, *rest):
    (attended, d_mixed, gain_sum, qkv, qx, kx, vn, kt, vt, es, ps, oa, dqa, dka, dva) = rest[-15:]
    part = attended.shape[0]
    heads = part // DH
    inv_dh = 1.0 / DH

    qkv[...] = dot(mixed_t[...], normed[...])

    def unit(start):
        raw = qkv[start : start + DH, :]
        shifted = raw - jnp.sum(raw, axis=0, keepdims=True) * inv_dh
        scale = lax.rsqrt(jnp.sum(shifted * shifted, axis=0, keepdims=True) * inv_dh + EPSILON)
        return shifted * scale, scale

    zeros = jnp.zeros((128 - DH - IMAGE_SLOTS, LEN), BF16)
    for head in range(heads):
        rows = slice(head * DH, (head + 1) * DH)
        query, _ = unit(head * DH)
        query = (query * (gains[rows, :] * 0.125)).astype(BF16)
        qx[head] = jnp.concatenate([query, mask_q[...], zeros], axis=0)
        key, _ = unit(part + head * DH)
        key = (key * gains[part + head * DH : part + (head + 1) * DH, :]).astype(BF16)
        kt[rows, :] = key
        kx[head] = jnp.concatenate([key, mask_k[...], zeros], axis=0).T
        value = qkv[2 * part + head * DH : 2 * part + (head + 1) * DH, :].astype(BF16)
        vt[rows, :] = value
        vn[head] = value.T
    dka[...] = jnp.zeros_like(dka)
    dva[...] = jnp.zeros_like(dva)

    def query_block(ib, _):
        i0 = pl.multiple_of(ib * BI, BI)
        icols = pl.ds(i0, BI)
        base = first[ib]
        trips = count[ib]

        def scores(j, carry):
            j0 = pl.multiple_of((base + j) * BJ, BJ)
            slot = pl.multiple_of(j * BJ, BJ)
            out = []
            for head in range(heads):
                rows = slice(head * DH, (head + 1) * DH)
                e = jnp.exp(dot(kx[head, pl.ds(j0, BJ), :], qx[head, :, icols]))
                p = dot(vn[head, pl.ds(j0, BJ), :], d_att[rows, icols])
                es[head, pl.ds(slot, BJ), :] = e
                ps[head, pl.ds(slot, BJ), :] = p
                out.append(carry[2 * head] + jnp.sum(e.reshape(BJ // 8, 8, BI), axis=0))
                out.append(carry[2 * head + 1] + jnp.sum((e * p).reshape(BJ // 8, 8, BI), axis=0))
            return tuple(out)

        sums = lax.fori_loop(0, trips, scores, tuple(jnp.zeros((8, BI), F32) for _ in range(2 * heads)))
        inverse = []
        inner = []
        for head in range(heads):
            inv = 1.0 / jnp.sum(sums[2 * head], axis=0, keepdims=True)
            inverse.append(inv)
            inner.append(jnp.sum(sums[2 * head + 1], axis=0, keepdims=True) * inv)
        oa[...] = jnp.zeros_like(oa)
        dqa[:, icols] = jnp.zeros((part, BI), F32)

        def grads(j, _):
            j0 = pl.multiple_of((base + j) * BJ, BJ)
            slot = pl.multiple_of(j * BJ, BJ)
            jcols = pl.ds(j0, BJ)
            for head in range(heads):
                rows = slice(head * DH, (head + 1) * DH)
                w = es[head, pl.ds(slot, BJ), :] * inverse[head]
                d = (w * (ps[head, pl.ds(slot, BJ), :] - inner[head])).astype(BF16)
                w = w.astype(BF16)
                oa[rows, :] += dot(vt[rows, jcols], w)
                dqa[rows, icols] += dot(kt[rows, jcols], d)
                dva[rows, jcols] += dot(d_att[rows, icols], w, NT)
                dka[rows, jcols] += dot(qx[head, :DH, icols], d, NT)
            return 0

        lax.fori_loop(0, trips, grads, 0)
        attended[:, icols] = oa[...].astype(BF16)
        return 0

    lax.fori_loop(0, LEN // BI, query_block, 0)

    for source, offset, factor in ((dqa, 0, 0.125), (dka, part, 1.0)):
        for head in range(heads):
            start = offset + head * DH
            u, scale = unit(start)
            e = source[head * DH : (head + 1) * DH, :] * factor
            gain_sum[start : start + DH, :] = fold_lanes(e * u)
            f = e * gains[start : start + DH, :]
            mean_f = jnp.sum(f, axis=0, keepdims=True) * inv_dh
            mean_fu = jnp.sum(f * u, axis=0, keepdims=True) * inv_dh
            d_mixed[start : start + DH, :] = ((f - mean_f - u * mean_fu) * scale).astype(BF16)
    d_mixed[2 * part :, :] = dva[...].astype(BF16)


def attention_call(first, count, normed, mixed_t, d_att, mask_q, mask_k, gains, before, seq):
    part, tokens = d_att.shape
    width = normed.shape[0]
    heads = part // DH
    once = lambda i, *_: (0, 0)
    ours = lambda i, *_: (0, seq)
    grid_spec = pltpu.PrefetchScalarGridSpec(
        num_scalar_prefetch=2,
        grid=(1,),
        in_specs=[
            pl.BlockSpec((width, LEN), ours),
            pl.BlockSpec((3 * part, width), once),
            pl.BlockSpec((part, LEN), ours),
            pl.BlockSpec((None, IMAGE_SLOTS, LEN), lambda i, *_: (seq, 0, 0)),
            pl.BlockSpec((None, IMAGE_SLOTS, LEN), lambda i, *_: (seq, 0, 0)),
            pl.BlockSpec((2 * part, 1), once),
        ]
        + [ANY] * len(before),
        out_specs=[
            pl.BlockSpec((part, LEN), ours),
            pl.BlockSpec((3 * part, LEN), ours),
            pl.BlockSpec((2 * part, 128), once),
        ],
        scratch_shapes=[
            pltpu.VMEM((3 * part, LEN), F32),
            pltpu.VMEM((heads, 128, LEN), BF16),
            pltpu.VMEM((heads, LEN, 128), BF16),
            pltpu.VMEM((heads, LEN, DH), BF16),
            pltpu.VMEM((part, LEN), BF16),
            pltpu.VMEM((part, LEN), BF16),
            pltpu.VMEM((heads, LEN, BI), F32),
            pltpu.VMEM((heads, LEN, BI), F32),
            pltpu.VMEM((part, BI), F32),
            pltpu.VMEM((part, LEN), F32),
            pltpu.VMEM((part, LEN), F32),
            pltpu.VMEM((part, LEN), F32),
        ],
    )
    return pl.pallas_call(
        attention_kernel,
        grid_spec=grid_spec,
        out_shape=[
            jax.ShapeDtypeStruct((part, tokens), BF16),
            jax.ShapeDtypeStruct((3 * part, tokens), BF16),
            jax.ShapeDtypeStruct((2 * part, 128), F32),
        ],
        input_output_aliases={8 + i: i for i in range(len(before))},
        cost_estimate=cost(15, 5_000_000),
        name="attention",
    )(first, count, normed, mixed_t, d_att, mask_q, mask_k, gains, *before)


def project_kernel(
    shard, active, attended, d_pre, d_mixed, normed, down_t, attn_t, up, mixed, gain, keep, send, gain_sum
):
    me = shard[0]
    part = attended.shape[0]
    out = dot(down_t[...], active[...]) + dot(attn_t[...], attended[...])
    grad = dot(up[...], d_pre[...]) + dot(mixed[...], d_mixed[...])
    product = grad * normed[...].astype(F32)
    sums = []
    for row in (jnp.sum(grad * gain[...], axis=0, keepdims=True), jnp.sum(product, axis=0, keepdims=True)):
        high = row.astype(BF16)
        sums += [high, (row - high.astype(F32)).astype(BF16)]
    sums = jnp.concatenate(sums + [jnp.zeros((SUM_ROWS - 4, sums[0].shape[1]), BF16)], axis=0)
    for target in (keep, send):
        for slot in range(2):
            target[slot, 2 * part :, :] = sums
    for index in range(4):
        rows = slice(index * part, (index + 1) * part)
        away = jnp.bitwise_xor(me, index)
        slot = away // 2

        @pl.when(away % 2 == 0)
        def _():
            keep[slot, :part, :] = out[rows].astype(BF16)
            keep[slot, part : 2 * part, :] = grad[rows].astype(BF16)

        @pl.when(away % 2 == 1)
        def _():
            send[slot, :part, :] = out[rows].astype(BF16)
            send[slot, part : 2 * part, :] = grad[rows].astype(BF16)

    @pl.when(pl.program_id(0) == 0)
    def _():
        gain_sum[...] = jnp.zeros_like(gain_sum)

    gain_sum[...] += fold_lanes(product)


def project_call(shard, active, attended, d_pre, d_mixed, normed, down_t, attn_t, up, mixed, gain, seq, block=256):
    width, hidden = down_t.shape
    part = attended.shape[0]
    steps = LEN // block
    ours = lambda i, *_: (0, seq * steps + i)
    fixed = lambda i, *_: (0, 0)
    rows = 2 * part + SUM_ROWS
    grid_spec = pltpu.PrefetchScalarGridSpec(
        num_scalar_prefetch=1,
        grid=(steps,),
        in_specs=[
            pl.BlockSpec((hidden, block), ours),
            pl.BlockSpec((part, block), ours),
            pl.BlockSpec((hidden, block), ours),
            pl.BlockSpec((3 * part, block), ours),
            pl.BlockSpec((width, block), ours),
            pl.BlockSpec((width, hidden), fixed),
            pl.BlockSpec((width, part), fixed),
            pl.BlockSpec((width, hidden), fixed),
            pl.BlockSpec((width, 3 * part), fixed),
            pl.BlockSpec((width, 1), fixed),
        ],
        out_specs=[
            pl.BlockSpec((2, rows, block), lambda i, *_: (0, 0, i)),
            pl.BlockSpec((2, rows, block), lambda i, *_: (0, 0, i)),
            pl.BlockSpec((width, 128), fixed),
        ],
    )
    return pl.pallas_call(
        project_kernel,
        grid_spec=grid_spec,
        out_shape=[
            jax.ShapeDtypeStruct((2, rows, LEN), BF16),
            jax.ShapeDtypeStruct((2, rows, LEN), BF16),
            jax.ShapeDtypeStruct((width, 128), F32),
        ],
        cost_estimate=cost(8, 16_000_000),
        name="project",
    )(shard, active, attended, d_pre, d_mixed, normed, down_t, attn_t, up, mixed, gain)


def finish_kernel(keep, from_core, from_y, own_t, tokens, cot, stats, gain, bias, *rest):
    block_out, token_grad = rest[-2:]
    part = own_t.shape[0]
    inv_width = 0.25 / part
    total = keep[...].astype(F32) + from_core[...].astype(F32) + from_y[...].astype(F32)
    block_out[...] = (tokens[...].astype(F32) + total[:part].T + bias[...]).astype(BF16)
    grad = total[part : 2 * part]
    sums = total[2 * part :]
    mean = stats[0:1, :]
    scale = stats[1:2, :]
    hat = (own_t[...].astype(F32) - mean) * scale
    inner = grad * gain[...] - (sums[0:1] + sums[1:2]) * inv_width - hat * ((sums[2:3] + sums[3:4]) * inv_width)
    token_grad[...] = cot[...].astype(F32) + (inner * scale).T


def finish_call(keep, from_core, from_y, own_t, tokens, cot, stats, gain, bias, before, seq, block=512):
    part = own_t.shape[0]
    steps = LEN // block
    lanes = lambda i: (0, i)
    fixed = lambda i: (0, 0)
    packed = pl.BlockSpec((None, 2 * part + SUM_ROWS, block), lambda i: (0, 0, i))
    here = pl.BlockSpec((block, part), lambda i: (seq * steps + i, 0))
    return pl.pallas_call(
        finish_kernel,
        grid=(steps,),
        in_specs=[
            packed, packed, packed,
            pl.BlockSpec((part, block), lanes),
            here, here,
            pl.BlockSpec((8, block), lanes),
            pl.BlockSpec((part, 1), fixed),
            pl.BlockSpec((1, part), fixed),
        ]
        + [ANY] * len(before),
        out_specs=[here, here],
        out_shape=[
            jax.ShapeDtypeStruct(tokens.shape, BF16),
            jax.ShapeDtypeStruct(tokens.shape, F32),
        ],
        input_output_aliases={9 + i: i for i in range(len(before))},
        cost_estimate=cost(3, 5_000_000),
        name="finish",
    )(keep, from_core, from_y, own_t, tokens, cot, stats, gain, bias, *before)


def flip(value, axis, size, bit):
    return lax.ppermute(value, axis, [(i, i ^ bit) for i in range(size)])


def tie(*trees):
    return lax.optimization_barrier(trees)


class SumOverDp:
    def __init__(self, keep, send, size, index):
        self.size, self.index = size, index
        self.keep, self.send = keep, send
        self.bits = []
        bit = 1
        while bit < size:
            self.bits.append(("sum", bit))
            bit *= 2
        self.bits += [("join", bit) for _, bit in reversed(self.bits)]
        if not self.bits:
            self.other = send

    def side(self, bit):
        return (self.index // bit) % 2

    def more(self):
        return bool(self.bits)

    def move(self, send):
        return flip(send, "dp", self.size, self.bits[0][1])

    def take(self, arrived):
        kind, bit = self.bits.pop(0)
        if kind == "sum":
            following = self.bits[0]
            if following[0] == "sum":
                half = self.keep.shape[0] // 2
                side = self.side(following[1])

                def add(which):
                    held = lax.dynamic_slice_in_dim(self.keep, which * half, half, 0)
                    came = lax.dynamic_slice_in_dim(arrived, which * half, half, 0)
                    return (held.astype(F32) + came.astype(F32)).astype(BF16)

                self.send, self.keep = add(1 - side), add(side)
            else:
                self.keep = (self.keep.astype(F32) + arrived.astype(F32)).astype(BF16)
                self.send = self.keep
        elif self.bits:
            side = self.side(bit)
            self.keep = jnp.where(
                side == 1,
                jnp.concatenate([arrived, self.keep], axis=0),
                jnp.concatenate([self.keep, arrived], axis=0),
            )
            self.send = self.keep
        else:
            self.other = arrived

    def halves(self):
        side = self.side(1)
        low = jnp.where(side == 1, self.other, self.keep)
        high = jnp.where(side == 1, self.keep, self.other)
        return low, high


class ScatterOverMp:
    def __init__(self, keep, send):
        self.keep, self.send = keep, send
        self.bits = [1, 2]

    def more(self):
        return bool(self.bits)

    def move(self, send):
        return flip(send, "mp", 4, self.bits[0])

    def take(self, arrived):
        bit = self.bits.pop(0)
        if bit == 1:
            self.from_core = arrived
            self.send = (self.keep[1].astype(F32) + arrived[1].astype(F32)).astype(BF16)[None]
        else:
            self.from_y = arrived


def beside(movers, inputs, work):
    movers = [m for m in movers if m.more()]
    inputs, sends = tie(inputs, [m.send for m in movers])
    arrivals = [m.move(s) for m, s in zip(movers, sends)]
    outputs = work(inputs)
    outputs, arrivals = tie(outputs, arrivals)
    for mover, arrived in zip(movers, arrivals):
        mover.take(arrived)
    return outputs


def body(
    dp_size,
    tokens,
    image_ids,
    norm_gain,
    qkv_weight,
    qk_gain,
    attn_weight,
    up_weight,
    up_bias,
    down_weight,
    down_bias,
    cotangent,
):
    part = tokens.shape[1]
    width = cotangent.shape[1]
    seqs = image_ids.shape[0]
    me = lax.axis_index("mp")
    dp = lax.axis_index("dp")
    shard = me.astype(jnp.int32)[None]
    side = (dp % 2).astype(jnp.int32)[None]
    away = jnp.array([0, 2, 1, 3], jnp.int32)
    place = jnp.bitwise_xor(shard, away) * part

    pieces = []
    for seq in range(seqs):
        own = tokens[seq * LEN : (seq + 1) * LEN].T
        from_y = flip(own, "mp", 4, 2)
        pieces.append((own, from_y, flip(own, "mp", 4, 1), flip(from_y, "mp", 4, 1)))
    gain_own = jnp.broadcast_to(norm_gain[:, None], (part, 128))
    gain_y = flip(gain_own, "mp", 4, 2)
    gain_pieces = jnp.stack([g[:, :1] for g in (gain_own, flip(gain_own, "mp", 4, 1), gain_y, flip(gain_y, "mp", 4, 1))])
    gain_all = jnp.concatenate(
        [lax.dynamic_index_in_dim(gain_pieces, jnp.bitwise_xor(me, i), 0, False) for i in range(4)], axis=0
    ).astype(F32)

    mixed_t = jnp.transpose(qkv_weight, (1, 2, 0)).reshape(3 * part, width)
    mixed = mixed_t.T
    up_t = up_weight.T
    down_t = down_weight.T
    attn_t = attn_weight.T
    up_bias_col = up_bias.astype(F32)[:, None]
    head_gains = qk_gain.astype(F32).reshape(2 * part, 1)

    slots = jnp.arange(IMAGE_SLOTS, dtype=jnp.int32)[None, :, None]
    same = image_ids[:, None, :] == slots
    mask_q = same.astype(BF16)
    mask_k = jnp.where(same | (slots >= 8), 0.0, -PENALTY).astype(BF16)
    block_first = image_ids[:, ::BI]
    block_last = image_ids[:, BI - 1 :: BI]
    starts = jnp.sum(image_ids[:, None, :] < block_first[:, :, None], axis=2, dtype=jnp.int32)
    ends = jnp.sum(image_ids[:, None, :] <= block_last[:, :, None], axis=2, dtype=jnp.int32)
    first = starts // BJ
    count = (ends + BJ - 1) // BJ - first

    d_act, d_att, cot_sum = early_call(cotangent, down_weight, attn_weight)
    cot_own = lax.dynamic_slice_in_dim(cotangent, me * part, part, 1)
    downbias_part = lax.dynamic_slice_in_dim(jnp.sum(cot_sum, axis=0), me * part, part, 0)

    wide = ()
    stats = []
    upbias_part = 0.0
    for seq in range(seqs):
        *wide, stat, ub = hidden_call(place, pieces[seq], gain_all, up_t, up_bias_col, d_act, wide, seq)
        stats.append(stat)
        upbias_part = upbias_part + ub
    normed, active, d_pre = wide
    upbias_part = jnp.sum(upbias_part, axis=1)

    mlp = SumOverDp(*mlp_grad_call(side, active, cotangent, normed, d_pre), dp_size, dp)

    heads_out = ()
    qk_part = 0.0
    for seq in range(seqs):

        def attend(tied, seq=seq):
            normed, before = tied
            return attention_call(
                first[seq], count[seq], normed, mixed_t, d_att, mask_q, mask_k, head_gains, before, seq
            )

        *heads_out, qk = beside([mlp], (normed, heads_out), attend)
        qk_part = qk_part + qk
    attended, d_mixed = heads_out

    mix = SumOverDp(
        *beside([mlp], (d_mixed,), lambda t: mix_grad_call(side, t[0], normed, attended, cotangent)), dp_size, dp
    )

    scatters = []
    gain_part = 0.0
    for seq in range(seqs):

        def project(tied, seq=seq):
            return project_call(
                shard, active, attended, d_pre, tied[0], normed, down_t, attn_t, up_weight, mixed, gain_all, seq
            )

        keep, send, gp = beside([mlp, mix] + scatters[-2:], (d_mixed,), project)
        gain_part = gain_part + gp
        scatters.append(ScatterOverMp(keep, send))

    gain_vec = jnp.sum(gain_part, axis=1).reshape(4, part)
    gain_half = [lax.dynamic_index_in_dim(gain_vec, jnp.bitwise_xor(me, m), 0, False) for m in range(4)]
    gain_kept = jnp.stack([gain_half[0], gain_half[2]]) + flip(jnp.stack([gain_half[1], gain_half[3]]), "mp", 4, 1)
    gain_mine = gain_kept[0] + flip(gain_kept[1], "mp", 4, 2)
    short = jnp.concatenate(
        [gain_mine / norm_gain.astype(F32), jnp.sum(qk_part, axis=1), upbias_part, downbias_part]
    )
    bit = 1
    while bit < dp_size:
        short = short + flip(short, "dp", dp_size, bit)
        bit *= 2

    gain_bias = down_bias.astype(F32)[None, :]
    gain_col = norm_gain.astype(F32)[:, None]
    finished = ()
    for seq, scatter in enumerate(scatters):
        while scatter.more():
            scatter.take(scatter.move(scatter.send))
        finished = finish_call(
            scatter.keep, scatter.from_core, scatter.from_y, pieces[seq][0], tokens, cot_own, stats[seq],
            gain_col, gain_bias, finished, seq,
        )
    block_out, token_grad = finished

    for mover in (mlp, mix):
        while mover.more():
            mover.take(mover.move(mover.send))
    down_grad, up_grad = mlp.halves()
    mixed_grad = jnp.concatenate(mix.halves(), axis=0).astype(F32)
    qkv_grad = jnp.transpose(mixed_grad[: 3 * part].reshape(3, part, width), (2, 0, 1))

    gain_grad = short[:part]
    qkgain_grad = short[part : 3 * part].reshape(2, part)
    upbias_grad = short[3 * part : 3 * part + upbias_part.shape[0]]
    downbias_grad = short[3 * part + upbias_part.shape[0] :]
    return (
        block_out,
        token_grad,
        gain_grad,
        qkv_grad,
        qkgain_grad,
        mixed_grad[3 * part :],
        up_grad.astype(F32),
        upbias_grad,
        down_grad.astype(F32),
        downbias_grad,
    )


def solution(mesh):
    in_specs = (
        P("dp", "mp"),
        P("dp", None),
        P("mp"),
        P(None, None, "mp"),
        P(None, "mp"),
        P("mp", None),
        P(None, "mp"),
        P("mp"),
        P("mp", None),
        P("mp"),
        P("dp", None),
    )
    out_specs = (
        P("dp", "mp"),
        P("dp", "mp"),
        P("mp"),
        P(None, None, "mp"),
        P(None, "mp"),
        P("mp", None),
        P(None, "mp"),
        P("mp"),
        P("mp", None),
        P("mp"),
    )
    run = functools.partial(body, mesh.shape["dp"])
    return jax.shard_map(run, mesh=mesh, in_specs=in_specs, out_specs=out_specs, check_vma=False)
```

```python
import functools

import jax
import jax.numpy as jnp
from jax import lax
from jax.experimental import pallas as pl
from jax.experimental.pallas import tpu as pltpu
from jax.sharding import PartitionSpec as P

DH = 64
LEN = 1024
EPSILON = 1e-06
IMAGE_SLOTS = 16
PENALTY = 1024.0
BI = 256
BJ = 256
SUM_ROWS = 16
MIB = 1 << 20
F32 = jnp.float32
BF16 = jnp.bfloat16

NN = (((1,), (0,)), ((), ()))
NT = (((1,), (1,)), ((), ()))
ANY = pl.BlockSpec(memory_space=pl.ANY)


def dot(left, right, dims=NN):
    return lax.dot_general(left, right, dims, preferred_element_type=F32)


def fold_lanes(rows):
    total = rows[:, :128]
    for start in range(128, rows.shape[1], 128):
        total = total + rows[:, start : start + 128]
    return total


def cost(microseconds, nbytes):
    return pl.CostEstimate(flops=int(microseconds * 1e9), bytes_accessed=nbytes, transcendentals=0)


def early_kernel(cot, down, attn, d_act, d_att, bias_sum):
    rows = cot[...]
    d_act[...] = dot(down[...], rows, NT).astype(BF16)
    d_att[...] = dot(attn[...], rows, NT).astype(BF16)

    @pl.when(pl.program_id(0) == 0)
    def _():
        bias_sum[...] = jnp.zeros_like(bias_sum)

    wide = rows.astype(F32)
    bias_sum[...] += jnp.sum(wide.reshape(wide.shape[0] // 8, 8, wide.shape[1]), axis=0)


def early_call(cot, down, attn, block=512):
    tokens, width = cot.shape
    hidden, part = down.shape[0], attn.shape[0]
    fixed = lambda i: (0, 0)
    lanes = lambda i: (0, i)
    return pl.pallas_call(
        early_kernel,
        grid=(tokens // block,),
        in_specs=[
            pl.BlockSpec((block, width), lambda i: (i, 0)),
            pl.BlockSpec((hidden, width), fixed),
            pl.BlockSpec((part, width), fixed),
        ],
        out_specs=[
            pl.BlockSpec((hidden, block), lanes),
            pl.BlockSpec((part, block), lanes),
            pl.BlockSpec((8, width), fixed),
        ],
        out_shape=[
            jax.ShapeDtypeStruct((hidden, tokens), BF16),
            jax.ShapeDtypeStruct((part, tokens), BF16),
            jax.ShapeDtypeStruct((8, width), F32),
        ],
        cost_estimate=cost(7, 12_000_000),
        name="early",
        compiler_params=pltpu.CompilerParams(vmem_limit_bytes=14 * MIB),
    )(cot, down, attn)


def hidden_kernel(
    place, own, flip_y, flip_c, flip_cy, gain, up_t, up_bias, d_act, *rest
):
    normed, active, d_pre, stats, bias_sum = rest[-5:]
    pieces = (own, flip_y, flip_c, flip_cy)
    part = own.shape[0]
    width = part * 4
    total = 0.0
    squares = 0.0
    for piece in pieces:
        rows = piece[...].astype(F32)
        total = total + jnp.sum(rows, axis=0, keepdims=True)
        squares = squares + jnp.sum(rows * rows, axis=0, keepdims=True)
    mean = total * (1.0 / width)
    scale = lax.rsqrt(squares * (1.0 / width) - mean * mean + EPSILON)
    stats[0:1, :] = mean
    stats[1:2, :] = scale
    stats[2:8, :] = jnp.zeros((6, stats.shape[1]), F32)
    for slot, piece in enumerate(pieces):
        rows = piece[...].astype(F32)
        here = pl.ds(pl.multiple_of(place[slot], part), part)
        normed[here, :] = ((rows - mean) * scale * gain[here, :]).astype(BF16)

    @pl.when(pl.program_id(0) == 0)
    def _():
        bias_sum[...] = jnp.zeros_like(bias_sum)

    c0 = 0.7978845608028654
    c1 = 0.044715 * c0
    for start in range(0, up_t.shape[0], 256):
        here = slice(start, start + 256)
        pre = dot(up_t[here, :], normed[...]) + up_bias[here, :]
        square = pre * pre
        half = 0.5 * jnp.tanh(pre * (c0 + c1 * square)) + 0.5
        active[here, :] = (pre * half).astype(BF16)
        slope = half + pre * (half - half * half) * (2.0 * c0 + 6.0 * c1 * square)
        grad = (d_act[here, :].astype(F32) * slope).astype(BF16)
        d_pre[here, :] = grad
        bias_sum[here, :] += fold_lanes(grad.astype(F32))


def hidden_call(place, pieces, gain, up_t, up_bias, d_act, before, seq, block=512):
    part = pieces[0].shape[0]
    width = 4 * part
    hidden, tokens = d_act.shape
    steps = LEN // block
    lanes = lambda i, *_: (0, i)
    ours = lambda i, *_: (0, seq * steps + i)
    fixed = lambda i, *_: (0, 0)
    grid_spec = pltpu.PrefetchScalarGridSpec(
        num_scalar_prefetch=1,
        grid=(steps,),
        in_specs=[pl.BlockSpec((part, block), lanes)] * 4
        + [
            pl.BlockSpec((width, 1), fixed),
            pl.BlockSpec((hidden, width), fixed),
            pl.BlockSpec((hidden, 1), fixed),
            pl.BlockSpec((hidden, block), ours),
        ]
        + [ANY] * len(before),
        out_specs=[
            pl.BlockSpec((width, block), ours),
            pl.BlockSpec((hidden, block), ours),
            pl.BlockSpec((hidden, block), ours),
            pl.BlockSpec((8, block), lanes),
            pl.BlockSpec((hidden, 128), fixed),
        ],
    )
    return pl.pallas_call(
        hidden_kernel,
        grid_spec=grid_spec,
        out_shape=[
            jax.ShapeDtypeStruct((width, tokens), BF16),
            jax.ShapeDtypeStruct((hidden, tokens), BF16),
            jax.ShapeDtypeStruct((hidden, tokens), BF16),
            jax.ShapeDtypeStruct((8, LEN), F32),
            jax.ShapeDtypeStruct((hidden, 128), F32),
        ],
        input_output_aliases={9 + i: i for i in range(len(before))},
        cost_estimate=cost(7, 8_000_000),
        name="hidden",
        compiler_params=pltpu.CompilerParams(vmem_limit_bytes=14 * MIB),
    )(place, *pieces, gain, up_t, up_bias, d_act, *before)


def split_store(side, low, high, keep, send):
    @pl.when(side == 0)
    def _():
        keep[...] = low[...].astype(BF16)
        send[...] = high[...].astype(BF16)

    @pl.when(side != 0)
    def _():
        keep[...] = high[...].astype(BF16)
        send[...] = low[...].astype(BF16)


def mlp_grad_kernel(side, active, cot, normed, d_pre, keep, send, low, high):
    down = dot(active[...], cot[...])
    up = dot(normed[...], d_pre[...], NT)

    @pl.when(pl.program_id(0) == 0)
    def _():
        low[...] = down
        high[...] = up

    @pl.when(pl.program_id(0) > 0)
    def _():
        low[...] += down
        high[...] += up

    @pl.when(pl.program_id(0) == pl.num_programs(0) - 1)
    def _():
        split_store(side[0], low, high, keep, send)


def mlp_grad_call(side, active, cot, normed, d_pre, block=1024):
    hidden, tokens = active.shape
    width = normed.shape[0]
    lanes = lambda i, *_: (0, i)
    fixed = lambda i, *_: (0, 0)
    grid_spec = pltpu.PrefetchScalarGridSpec(
        num_scalar_prefetch=1,
        grid=(tokens // block,),
        in_specs=[
            pl.BlockSpec((hidden, block), lanes),
            pl.BlockSpec((block, width), lambda i, *_: (i, 0)),
            pl.BlockSpec((width, block), lanes),
            pl.BlockSpec((hidden, block), lanes),
        ],
        out_specs=[pl.BlockSpec((hidden, width), fixed)] * 2,
        scratch_shapes=[pltpu.VMEM((hidden, width), F32)] * 2,
    )
    return pl.pallas_call(
        mlp_grad_kernel,
        grid_spec=grid_spec,
        out_shape=[jax.ShapeDtypeStruct((hidden, width), BF16)] * 2,
        cost_estimate=cost(10, 20_000_000),
        name="mlp_grad",
        compiler_params=pltpu.CompilerParams(vmem_limit_bytes=28 * MIB),
    )(side, active, cot, normed, d_pre)


def mix_grad_kernel(side, d_mixed, normed, attended, cot, keep, send, total):
    split = d_mixed.shape[0]
    mixed = dot(d_mixed[...], normed[...], NT)
    attn = dot(attended[...], cot[...])

    @pl.when(pl.program_id(0) == 0)
    def _():
        total[:split, :] = mixed
        total[split:, :] = attn

    @pl.when(pl.program_id(0) > 0)
    def _():
        total[:split, :] += mixed
        total[split:, :] += attn

    @pl.when(pl.program_id(0) == pl.num_programs(0) - 1)
    def _():
        half = keep.shape[0]
        split_store(side[0], total.at[:half], total.at[half:], keep, send)


def mix_grad_call(side, d_mixed, normed, attended, cot, block=1024):
    mixed, tokens = d_mixed.shape
    width = normed.shape[0]
    part = attended.shape[0]
    lanes = lambda i, *_: (0, i)
    fixed = lambda i, *_: (0, 0)
    half = (mixed + part) // 2
    grid_spec = pltpu.PrefetchScalarGridSpec(
        num_scalar_prefetch=1,
        grid=(tokens // block,),
        in_specs=[
            pl.BlockSpec((mixed, block), lanes),
            pl.BlockSpec((width, block), lanes),
            pl.BlockSpec((part, block), lanes),
            pl.BlockSpec((block, width), lambda i, *_: (i, 0)),
        ],
        out_specs=[pl.BlockSpec((half, width), fixed)] * 2,
        scratch_shapes=[pltpu.VMEM((2 * half, width), F32)],
    )
    return pl.pallas_call(
        mix_grad_kernel,
        grid_spec=grid_spec,
        out_shape=[jax.ShapeDtypeStruct((half, width), BF16)] * 2,
        cost_estimate=cost(6, 15_000_000),
        name="mix_grad",
        compiler_params=pltpu.CompilerParams(vmem_limit_bytes=24 * MIB),
    )(side, d_mixed, normed, attended, cot)


def attention_kernel(first, count, normed, mixed_t, d_att, mask_q, mask_k, gains, *rest):
    (attended, d_mixed, gain_sum, qkv, qx, kx, vn, kt, vt, es, ps, oa, dqa, dka, dva) = rest[-15:]
    part = attended.shape[0]
    heads = part // DH
    inv_dh = 1.0 / DH

    qkv[...] = dot(mixed_t[...], normed[...])

    def unit(start):
        raw = qkv[start : start + DH, :]
        shifted = raw - jnp.sum(raw, axis=0, keepdims=True) * inv_dh
        scale = lax.rsqrt(jnp.sum(shifted * shifted, axis=0, keepdims=True) * inv_dh + EPSILON)
        return shifted * scale, scale

    zeros = jnp.zeros((128 - DH - IMAGE_SLOTS, LEN), BF16)
    for head in range(heads):
        rows = slice(head * DH, (head + 1) * DH)
        query, _ = unit(head * DH)
        query = (query * (gains[rows, :] * 0.125)).astype(BF16)
        qx[head] = jnp.concatenate([query, mask_q[...], zeros], axis=0)
        key, _ = unit(part + head * DH)
        key = (key * gains[part + head * DH : part + (head + 1) * DH, :]).astype(BF16)
        kt[rows, :] = key
        kx[head] = jnp.concatenate([key, mask_k[...], zeros], axis=0).T
        value = qkv[2 * part + head * DH : 2 * part + (head + 1) * DH, :].astype(BF16)
        vt[rows, :] = value
        vn[head] = value.T
    dka[...] = jnp.zeros_like(dka)
    dva[...] = jnp.zeros_like(dva)

    def query_block(ib, _):
        i0 = pl.multiple_of(ib * BI, BI)
        icols = pl.ds(i0, BI)
        base = first[ib]
        trips = count[ib]

        def scores(j, carry):
            j0 = pl.multiple_of((base + j) * BJ, BJ)
            slot = pl.multiple_of(j * BJ, BJ)
            out = []
            for head in range(heads):
                rows = slice(head * DH, (head + 1) * DH)
                e = jnp.exp(dot(kx[head, pl.ds(j0, BJ), :], qx[head, :, icols]))
                p = dot(vn[head, pl.ds(j0, BJ), :], d_att[rows, icols])
                es[head, pl.ds(slot, BJ), :] = e
                ps[head, pl.ds(slot, BJ), :] = p
                out.append(carry[2 * head] + jnp.sum(e.reshape(BJ // 8, 8, BI), axis=0))
                out.append(carry[2 * head + 1] + jnp.sum((e * p).reshape(BJ // 8, 8, BI), axis=0))
            return tuple(out)

        sums = lax.fori_loop(0, trips, scores, tuple(jnp.zeros((8, BI), F32) for _ in range(2 * heads)))
        inverse = []
        inner = []
        for head in range(heads):
            inv = 1.0 / jnp.sum(sums[2 * head], axis=0, keepdims=True)
            inverse.append(inv)
            inner.append(jnp.sum(sums[2 * head + 1], axis=0, keepdims=True) * inv)
        oa[...] = jnp.zeros_like(oa)
        dqa[:, icols] = jnp.zeros((part, BI), F32)

        def grads(j, _):
            j0 = pl.multiple_of((base + j) * BJ, BJ)
            slot = pl.multiple_of(j * BJ, BJ)
            jcols = pl.ds(j0, BJ)
            for head in range(heads):
                rows = slice(head * DH, (head + 1) * DH)
                w = es[head, pl.ds(slot, BJ), :] * inverse[head]
                d = (w * (ps[head, pl.ds(slot, BJ), :] - inner[head])).astype(BF16)
                w = w.astype(BF16)
                oa[rows, :] += dot(vt[rows, jcols], w)
                dqa[rows, icols] += dot(kt[rows, jcols], d)
                dva[rows, jcols] += dot(d_att[rows, icols], w, NT)
                dka[rows, jcols] += dot(qx[head, :DH, icols], d, NT)
            return 0

        lax.fori_loop(0, trips, grads, 0)
        attended[:, icols] = oa[...].astype(BF16)
        return 0

    lax.fori_loop(0, LEN // BI, query_block, 0)

    for source, offset, factor in ((dqa, 0, 0.125), (dka, part, 1.0)):
        for head in range(heads):
            start = offset + head * DH
            u, scale = unit(start)
            e = source[head * DH : (head + 1) * DH, :] * factor
            gain_sum[start : start + DH, :] = fold_lanes(e * u)
            f = e * gains[start : start + DH, :]
            mean_f = jnp.sum(f, axis=0, keepdims=True) * inv_dh
            mean_fu = jnp.sum(f * u, axis=0, keepdims=True) * inv_dh
            d_mixed[start : start + DH, :] = ((f - mean_f - u * mean_fu) * scale).astype(BF16)
    d_mixed[2 * part :, :] = dva[...].astype(BF16)


def attention_call(first, count, normed, mixed_t, d_att, mask_q, mask_k, gains, before, seq):
    part, tokens = d_att.shape
    width = normed.shape[0]
    heads = part // DH
    once = lambda i, *_: (0, 0)
    ours = lambda i, *_: (0, seq)
    grid_spec = pltpu.PrefetchScalarGridSpec(
        num_scalar_prefetch=2,
        grid=(1,),
        in_specs=[
            pl.BlockSpec((width, LEN), ours),
            pl.BlockSpec((3 * part, width), once),
            pl.BlockSpec((part, LEN), ours),
            pl.BlockSpec((None, IMAGE_SLOTS, LEN), lambda i, *_: (seq, 0, 0)),
            pl.BlockSpec((None, IMAGE_SLOTS, LEN), lambda i, *_: (seq, 0, 0)),
            pl.BlockSpec((2 * part, 1), once),
        ]
        + [ANY] * len(before),
        out_specs=[
            pl.BlockSpec((part, LEN), ours),
            pl.BlockSpec((3 * part, LEN), ours),
            pl.BlockSpec((2 * part, 128), once),
        ],
        scratch_shapes=[
            pltpu.VMEM((3 * part, LEN), F32),
            pltpu.VMEM((heads, 128, LEN), BF16),
            pltpu.VMEM((heads, LEN, 128), BF16),
            pltpu.VMEM((heads, LEN, DH), BF16),
            pltpu.VMEM((part, LEN), BF16),
            pltpu.VMEM((part, LEN), BF16),
            pltpu.VMEM((heads, LEN, BI), F32),
            pltpu.VMEM((heads, LEN, BI), F32),
            pltpu.VMEM((part, BI), F32),
            pltpu.VMEM((part, LEN), F32),
            pltpu.VMEM((part, LEN), F32),
            pltpu.VMEM((part, LEN), F32),
        ],
    )
    return pl.pallas_call(
        attention_kernel,
        grid_spec=grid_spec,
        out_shape=[
            jax.ShapeDtypeStruct((part, tokens), BF16),
            jax.ShapeDtypeStruct((3 * part, tokens), BF16),
            jax.ShapeDtypeStruct((2 * part, 128), F32),
        ],
        input_output_aliases={8 + i: i for i in range(len(before))},
        cost_estimate=cost(15, 5_000_000),
        name="attention",
        compiler_params=pltpu.CompilerParams(vmem_limit_bytes=26 * MIB),
    )(first, count, normed, mixed_t, d_att, mask_q, mask_k, gains, *before)


def project_kernel(
    shard, active, attended, d_pre, d_mixed, normed, down_t, attn_t, up, mixed, gain, keep, send, gain_sum
):
    me = shard[0]
    part = attended.shape[0]
    out = dot(down_t[...], active[...]) + dot(attn_t[...], attended[...])
    grad = dot(up[...], d_pre[...]) + dot(mixed[...], d_mixed[...])
    product = grad * normed[...].astype(F32)
    sums = []
    for row in (jnp.sum(grad * gain[...], axis=0, keepdims=True), jnp.sum(product, axis=0, keepdims=True)):
        high = row.astype(BF16)
        sums += [high, (row - high.astype(F32)).astype(BF16)]
    sums = jnp.concatenate(sums + [jnp.zeros((SUM_ROWS - 4, sums[0].shape[1]), BF16)], axis=0)
    for target in (keep, send):
        for slot in range(2):
            target[slot, 2 * part :, :] = sums
    for index in range(4):
        rows = slice(index * part, (index + 1) * part)
        away = jnp.bitwise_xor(me, index)
        slot = away // 2

        @pl.when(away % 2 == 0)
        def _():
            keep[slot, :part, :] = out[rows].astype(BF16)
            keep[slot, part : 2 * part, :] = grad[rows].astype(BF16)

        @pl.when(away % 2 == 1)
        def _():
            send[slot, :part, :] = out[rows].astype(BF16)
            send[slot, part : 2 * part, :] = grad[rows].astype(BF16)

    @pl.when(pl.program_id(0) == 0)
    def _():
        gain_sum[...] = jnp.zeros_like(gain_sum)

    gain_sum[...] += fold_lanes(product)


def project_call(shard, active, attended, d_pre, d_mixed, normed, down_t, attn_t, up, mixed, gain, seq, block=256):
    width, hidden = down_t.shape
    part = attended.shape[0]
    steps = LEN // block
    ours = lambda i, *_: (0, seq * steps + i)
    fixed = lambda i, *_: (0, 0)
    rows = 2 * part + SUM_ROWS
    grid_spec = pltpu.PrefetchScalarGridSpec(
        num_scalar_prefetch=1,
        grid=(steps,),
        in_specs=[
            pl.BlockSpec((hidden, block), ours),
            pl.BlockSpec((part, block), ours),
            pl.BlockSpec((hidden, block), ours),
            pl.BlockSpec((3 * part, block), ours),
            pl.BlockSpec((width, block), ours),
            pl.BlockSpec((width, hidden), fixed),
            pl.BlockSpec((width, part), fixed),
            pl.BlockSpec((width, hidden), fixed),
            pl.BlockSpec((width, 3 * part), fixed),
            pl.BlockSpec((width, 1), fixed),
        ],
        out_specs=[
            pl.BlockSpec((2, rows, block), lambda i, *_: (0, 0, i)),
            pl.BlockSpec((2, rows, block), lambda i, *_: (0, 0, i)),
            pl.BlockSpec((width, 128), fixed),
        ],
    )
    return pl.pallas_call(
        project_kernel,
        grid_spec=grid_spec,
        out_shape=[
            jax.ShapeDtypeStruct((2, rows, LEN), BF16),
            jax.ShapeDtypeStruct((2, rows, LEN), BF16),
            jax.ShapeDtypeStruct((width, 128), F32),
        ],
        cost_estimate=cost(8, 16_000_000),
        name="project",
        compiler_params=pltpu.CompilerParams(vmem_limit_bytes=22 * MIB),
    )(shard, active, attended, d_pre, d_mixed, normed, down_t, attn_t, up, mixed, gain)


def finish_kernel(keep, from_core, from_y, own_t, tokens, cot, stats, gain, bias, *rest):
    block_out, token_grad = rest[-2:]
    part = own_t.shape[0]
    inv_width = 0.25 / part
    total = keep[...].astype(F32) + from_core[...].astype(F32) + from_y[...].astype(F32)
    block_out[...] = (tokens[...].astype(F32) + total[:part].T + bias[...]).astype(BF16)
    grad = total[part : 2 * part]
    sums = total[2 * part :]
    mean = stats[0:1, :]
    scale = stats[1:2, :]
    hat = (own_t[...].astype(F32) - mean) * scale
    inner = grad * gain[...] - (sums[0:1] + sums[1:2]) * inv_width - hat * ((sums[2:3] + sums[3:4]) * inv_width)
    token_grad[...] = cot[...].astype(F32) + (inner * scale).T


def finish_call(keep, from_core, from_y, own_t, tokens, cot, stats, gain, bias, before, seq, block=512):
    part = own_t.shape[0]
    steps = LEN // block
    lanes = lambda i: (0, i)
    fixed = lambda i: (0, 0)
    packed = pl.BlockSpec((None, 2 * part + SUM_ROWS, block), lambda i: (0, 0, i))
    here = pl.BlockSpec((block, part), lambda i: (seq * steps + i, 0))
    return pl.pallas_call(
        finish_kernel,
        grid=(steps,),
        in_specs=[
            packed, packed, packed,
            pl.BlockSpec((part, block), lanes),
            here, here,
            pl.BlockSpec((8, block), lanes),
            pl.BlockSpec((part, 1), fixed),
            pl.BlockSpec((1, part), fixed),
        ]
        + [ANY] * len(before),
        out_specs=[here, here],
        out_shape=[
            jax.ShapeDtypeStruct(tokens.shape, BF16),
            jax.ShapeDtypeStruct(tokens.shape, F32),
        ],
        input_output_aliases={9 + i: i for i in range(len(before))},
        cost_estimate=cost(3, 5_000_000),
        name="finish",
        compiler_params=pltpu.CompilerParams(vmem_limit_bytes=10 * MIB),
    )(keep, from_core, from_y, own_t, tokens, cot, stats, gain, bias, *before)


def flip(value, axis, size, bit):
    return lax.ppermute(value, axis, [(i, i ^ bit) for i in range(size)])


def tie(*trees):
    return lax.optimization_barrier(trees)


class SumOverDp:
    def __init__(self, keep, send, size, index):
        self.size, self.index = size, index
        self.keep, self.send = keep, send
        self.bits = []
        bit = 1
        while bit < size:
            self.bits.append(("sum", bit))
            bit *= 2
        self.bits += [("join", bit) for _, bit in reversed(self.bits)]
        if not self.bits:
            self.other = send

    def side(self, bit):
        return (self.index // bit) % 2

    def more(self):
        return bool(self.bits)

    def move(self, send):
        return flip(send, "dp", self.size, self.bits[0][1])

    def take(self, arrived):
        kind, bit = self.bits.pop(0)
        if kind == "sum":
            following = self.bits[0]
            if following[0] == "sum":
                half = self.keep.shape[0] // 2
                side = self.side(following[1])

                def add(which):
                    held = lax.dynamic_slice_in_dim(self.keep, which * half, half, 0)
                    came = lax.dynamic_slice_in_dim(arrived, which * half, half, 0)
                    return (held.astype(F32) + came.astype(F32)).astype(BF16)

                self.send, self.keep = add(1 - side), add(side)
            else:
                self.keep = (self.keep.astype(F32) + arrived.astype(F32)).astype(BF16)
                self.send = self.keep
        elif self.bits:
            side = self.side(bit)
            self.keep = jnp.where(
                side == 1,
                jnp.concatenate([arrived, self.keep], axis=0),
                jnp.concatenate([self.keep, arrived], axis=0),
            )
            self.send = self.keep
        else:
            self.other = arrived

    def halves(self):
        side = self.side(1)
        low = jnp.where(side == 1, self.other, self.keep)
        high = jnp.where(side == 1, self.keep, self.other)
        return low, high


class ScatterOverMp:
    def __init__(self, keep, send):
        self.keep, self.send = keep, send
        self.bits = [1, 2]

    def more(self):
        return bool(self.bits)

    def move(self, send):
        return flip(send, "mp", 4, self.bits[0])

    def take(self, arrived):
        bit = self.bits.pop(0)
        if bit == 1:
            self.from_core = arrived
            self.send = (self.keep[1].astype(F32) + arrived[1].astype(F32)).astype(BF16)[None]
        else:
            self.from_y = arrived


def beside(movers, inputs, work):
    movers = [m for m in movers if m.more()]
    inputs, sends = tie(inputs, [m.send for m in movers])
    arrivals = [m.move(s) for m, s in zip(movers, sends)]
    outputs = work(inputs)
    outputs, arrivals = tie(outputs, arrivals)
    for mover, arrived in zip(movers, arrivals):
        mover.take(arrived)
    return outputs


def body(
    dp_size,
    tokens,
    image_ids,
    norm_gain,
    qkv_weight,
    qk_gain,
    attn_weight,
    up_weight,
    up_bias,
    down_weight,
    down_bias,
    cotangent,
):
    part = tokens.shape[1]
    width = cotangent.shape[1]
    seqs = image_ids.shape[0]
    me = lax.axis_index("mp")
    dp = lax.axis_index("dp")
    shard = me.astype(jnp.int32)[None]
    side = (dp % 2).astype(jnp.int32)[None]
    away = jnp.array([0, 2, 1, 3], jnp.int32)
    place = jnp.bitwise_xor(shard, away) * part

    pieces = []
    for seq in range(seqs):
        own = tokens[seq * LEN : (seq + 1) * LEN].T
        from_y = flip(own, "mp", 4, 2)
        pieces.append((own, from_y, flip(own, "mp", 4, 1), flip(from_y, "mp", 4, 1)))
    gain_own = jnp.broadcast_to(norm_gain[:, None], (part, 128))
    gain_y = flip(gain_own, "mp", 4, 2)
    gain_pieces = jnp.stack([g[:, :1] for g in (gain_own, flip(gain_own, "mp", 4, 1), gain_y, flip(gain_y, "mp", 4, 1))])
    gain_all = jnp.concatenate(
        [lax.dynamic_index_in_dim(gain_pieces, jnp.bitwise_xor(me, i), 0, False) for i in range(4)], axis=0
    ).astype(F32)

    mixed_t = jnp.transpose(qkv_weight, (1, 2, 0)).reshape(3 * part, width)
    mixed = mixed_t.T
    up_t = up_weight.T
    down_t = down_weight.T
    attn_t = attn_weight.T
    up_bias_col = up_bias.astype(F32)[:, None]
    head_gains = qk_gain.astype(F32).reshape(2 * part, 1)

    slots = jnp.arange(IMAGE_SLOTS, dtype=jnp.int32)[None, :, None]
    same = image_ids[:, None, :] == slots
    mask_q = same.astype(BF16)
    mask_k = jnp.where(same | (slots >= 8), 0.0, -PENALTY).astype(BF16)
    block_first = image_ids[:, ::BI]
    block_last = image_ids[:, BI - 1 :: BI]
    starts = jnp.sum(image_ids[:, None, :] < block_first[:, :, None], axis=2, dtype=jnp.int32)
    ends = jnp.sum(image_ids[:, None, :] <= block_last[:, :, None], axis=2, dtype=jnp.int32)
    first = starts // BJ
    count = (ends + BJ - 1) // BJ - first

    d_act, d_att, cot_sum = early_call(cotangent, down_weight, attn_weight)
    cot_own = lax.dynamic_slice_in_dim(cotangent, me * part, part, 1)
    downbias_part = lax.dynamic_slice_in_dim(jnp.sum(cot_sum, axis=0), me * part, part, 0)

    wide = ()
    stats = []
    upbias_part = 0.0
    for seq in range(seqs):
        *wide, stat, ub = hidden_call(place, pieces[seq], gain_all, up_t, up_bias_col, d_act, wide, seq)
        stats.append(stat)
        upbias_part = upbias_part + ub
    normed, active, d_pre = wide
    upbias_part = jnp.sum(upbias_part, axis=1)

    mlp = SumOverDp(*mlp_grad_call(side, active, cotangent, normed, d_pre), dp_size, dp)

    heads_out = ()
    qk_part = 0.0
    for seq in range(seqs):

        def attend(tied, seq=seq):
            normed, before = tied
            return attention_call(
                first[seq], count[seq], normed, mixed_t, d_att, mask_q, mask_k, head_gains, before, seq
            )

        *heads_out, qk = beside([mlp], (normed, heads_out), attend)
        qk_part = qk_part + qk
    attended, d_mixed = heads_out

    mix = SumOverDp(
        *beside([mlp], (d_mixed,), lambda t: mix_grad_call(side, t[0], normed, attended, cotangent)), dp_size, dp
    )

    scatters = []
    gain_part = 0.0
    for seq in range(seqs):

        def project(tied, seq=seq):
            return project_call(
                shard, active, attended, d_pre, tied[0], normed, down_t, attn_t, up_weight, mixed, gain_all, seq
            )

        keep, send, gp = beside([mlp, mix] + scatters[-2:], (d_mixed,), project)
        gain_part = gain_part + gp
        scatters.append(ScatterOverMp(keep, send))

    gain_vec = jnp.sum(gain_part, axis=1).reshape(4, part)
    gain_half = [lax.dynamic_index_in_dim(gain_vec, jnp.bitwise_xor(me, m), 0, False) for m in range(4)]
    gain_kept = jnp.stack([gain_half[0], gain_half[2]]) + flip(jnp.stack([gain_half[1], gain_half[3]]), "mp", 4, 1)
    gain_mine = gain_kept[0] + flip(gain_kept[1], "mp", 4, 2)
    short = jnp.concatenate(
        [gain_mine / norm_gain.astype(F32), jnp.sum(qk_part, axis=1), upbias_part, downbias_part]
    )
    bit = 1
    while bit < dp_size:
        short = short + flip(short, "dp", dp_size, bit)
        bit *= 2

    gain_bias = down_bias.astype(F32)[None, :]
    gain_col = norm_gain.astype(F32)[:, None]
    finished = ()
    for seq, scatter in enumerate(scatters):
        while scatter.more():
            scatter.take(scatter.move(scatter.send))
        finished = finish_call(
            scatter.keep, scatter.from_core, scatter.from_y, pieces[seq][0], tokens, cot_own, stats[seq],
            gain_col, gain_bias, finished, seq,
        )
    block_out, token_grad = finished

    for mover in (mlp, mix):
        while mover.more():
            mover.take(mover.move(mover.send))
    down_grad, up_grad = mlp.halves()
    mixed_grad = jnp.concatenate(mix.halves(), axis=0).astype(F32)
    qkv_grad = jnp.transpose(mixed_grad[: 3 * part].reshape(3, part, width), (2, 0, 1))

    gain_grad = short[:part]
    qkgain_grad = short[part : 3 * part].reshape(2, part)
    upbias_grad = short[3 * part : 3 * part + upbias_part.shape[0]]
    downbias_grad = short[3 * part + upbias_part.shape[0] :]
    return (
        block_out,
        token_grad,
        gain_grad,
        qkv_grad,
        qkgain_grad,
        mixed_grad[3 * part :],
        up_grad.astype(F32),
        upbias_grad,
        down_grad.astype(F32),
        downbias_grad,
    )


def solution(mesh):
    in_specs = (
        P("dp", "mp"),
        P("dp", None),
        P("mp"),
        P(None, None, "mp"),
        P(None, "mp"),
        P("mp", None),
        P(None, "mp"),
        P("mp"),
        P("mp", None),
        P("mp"),
        P("dp", None),
    )
    out_specs = (
        P("dp", "mp"),
        P("dp", "mp"),
        P("mp"),
        P(None, None, "mp"),
        P(None, "mp"),
        P("mp", None),
        P(None, "mp"),
        P("mp"),
        P("mp", None),
        P("mp"),
    )
    run = functools.partial(body, mesh.shape["dp"])
    return jax.shard_map(run, mesh=mesh, in_specs=in_specs, out_specs=out_specs, check_vma=False)
```

```python
import functools

import jax
import jax.numpy as jnp
from jax import lax
from jax.experimental import pallas as pl
from jax.experimental.pallas import tpu as pltpu
from jax.sharding import PartitionSpec as P

DH = 64
LEN = 1024
EPSILON = 1e-06
IMAGE_SLOTS = 16
PENALTY = 1024.0
BI = 256
BJ = 256
SUM_ROWS = 16
F32 = jnp.float32
BF16 = jnp.bfloat16

NN = (((1,), (0,)), ((), ()))
NT = (((1,), (1,)), ((), ()))
ANY = pl.BlockSpec(memory_space=pl.ANY)


def dot(left, right, dims=NN):
    return lax.dot_general(left, right, dims, preferred_element_type=F32)


def fold_lanes(rows):
    total = rows[:, :128]
    for start in range(128, rows.shape[1], 128):
        total = total + rows[:, start : start + 128]
    return total


def cost(microseconds, nbytes):
    return pl.CostEstimate(flops=int(microseconds * 1e9), bytes_accessed=nbytes, transcendentals=0)


def early_kernel(cot, down, attn, d_act, d_att, bias_sum):
    rows = cot[...]
    d_act[...] = dot(down[...], rows, NT).astype(BF16)
    d_att[...] = dot(attn[...], rows, NT).astype(BF16)

    @pl.when(pl.program_id(0) == 0)
    def _():
        bias_sum[...] = jnp.zeros_like(bias_sum)

    wide = rows.astype(F32)
    bias_sum[...] += jnp.sum(wide.reshape(wide.shape[0] // 8, 8, wide.shape[1]), axis=0)


def early_call(cot, down, attn, block=512):
    tokens, width = cot.shape
    seqs = tokens // LEN
    hidden, part = down.shape[0], attn.shape[0]
    steps = LEN // block
    fixed = lambda i: (0, 0)
    by_seq = lambda i: (i // steps, 0, i % steps)
    return pl.pallas_call(
        early_kernel,
        grid=(tokens // block,),
        in_specs=[
            pl.BlockSpec((block, width), lambda i: (i, 0)),
            pl.BlockSpec((hidden, width), fixed),
            pl.BlockSpec((part, width), fixed),
        ],
        out_specs=[
            pl.BlockSpec((None, hidden, block), by_seq),
            pl.BlockSpec((None, part, block), by_seq),
            pl.BlockSpec((8, width), fixed),
        ],
        out_shape=[
            jax.ShapeDtypeStruct((seqs, hidden, LEN), BF16),
            jax.ShapeDtypeStruct((seqs, part, LEN), BF16),
            jax.ShapeDtypeStruct((8, width), F32),
        ],
        cost_estimate=cost(10, 12_000_000),
        name="early",
    )(cot, down, attn)


def split_store(side, low, high, keep, send):
    @pl.when(side == 0)
    def _():
        keep[...] = low[...].astype(BF16)
        send[...] = high[...].astype(BF16)

    @pl.when(side != 0)
    def _():
        keep[...] = high[...].astype(BF16)
        send[...] = low[...].astype(BF16)


def mlp_kernel(
    place, own, flip_y, flip_c, flip_cy, gain_own, gain_y, gain_c, gain_cy, up_t, up_bias, d_act, cot,
    normed, active, d_pre, stats, bias_sum, gain_all, down_grad, up_grad, low, high
):
    pieces = (own, flip_y, flip_c, flip_cy)
    part = own.shape[0]
    width = part * 4
    first = pl.program_id(0) == 0
    last = pl.program_id(0) == pl.num_programs(0) - 1

    @pl.when(first)
    def _():
        bias_sum[...] = jnp.zeros_like(bias_sum)
        low[...] = jnp.zeros_like(low)
        high[...] = jnp.zeros_like(high)
        for slot, piece in enumerate((gain_own, gain_y, gain_c, gain_cy)):
            gain_all[pl.ds(pl.multiple_of(place[slot], part), part), :] = piece[...].astype(F32)

    total = 0.0
    squares = 0.0
    for piece in pieces:
        rows = piece[...].astype(F32)
        total = total + jnp.sum(rows, axis=0, keepdims=True)
        squares = squares + jnp.sum(rows * rows, axis=0, keepdims=True)
    mean = total * (1.0 / width)
    scale = lax.rsqrt(squares * (1.0 / width) - mean * mean + EPSILON)
    stats[0:1, :] = mean
    stats[1:2, :] = scale
    stats[2:8, :] = jnp.zeros((6, stats.shape[1]), F32)
    for slot, piece in enumerate(pieces):
        rows = piece[...].astype(F32)
        here = pl.ds(pl.multiple_of(place[slot], part), part)
        normed[here, :] = ((rows - mean) * scale * gain_all[here, :1]).astype(BF16)

    c0 = 0.7978845608028654
    c1 = 0.044715 * c0
    for start in range(0, up_t.shape[0], 256):
        here = slice(start, start + 256)
        pre = dot(up_t[here, :], normed[...]) + up_bias[here, :]
        square = pre * pre
        half = 0.5 * jnp.tanh(pre * (c0 + c1 * square)) + 0.5
        act = (pre * half).astype(BF16)
        active[here, :] = act
        slope = half + pre * (half - half * half) * (2.0 * c0 + 6.0 * c1 * square)
        grad = (d_act[here, :].astype(F32) * slope).astype(BF16)
        d_pre[here, :] = grad
        bias_sum[here, :] += fold_lanes(grad.astype(F32))
        low[here, :] += dot(act, cot[...])
        high[:, here] += dot(normed[...], grad, NT)

    @pl.when(last)
    def _():
        down_grad[...] = low[...].astype(BF16)
        up_grad[...] = high[...].astype(BF16)


def mlp_call(place, pieces, gains, up_t, up_bias, d_act, cot, block=512):
    part, tokens = pieces[0].shape
    width = 4 * part
    seqs, hidden, _ = d_act.shape
    steps = LEN // block
    lanes = lambda i, *_: (0, i)
    by_seq = lambda i, *_: (i // steps, 0, i % steps)
    fixed = lambda i, *_: (0, 0)
    grid_spec = pltpu.PrefetchScalarGridSpec(
        num_scalar_prefetch=1,
        grid=(tokens // block,),
        in_specs=[pl.BlockSpec((part, block), lanes)] * 4
        + [pl.BlockSpec((part, 128), fixed)] * 4
        + [
            pl.BlockSpec((hidden, width), fixed),
            pl.BlockSpec((hidden, 1), fixed),
            pl.BlockSpec((None, hidden, block), by_seq),
            pl.BlockSpec((block, width), lambda i, *_: (i, 0)),
        ],
        out_specs=[
            pl.BlockSpec((None, width, block), by_seq),
            pl.BlockSpec((None, hidden, block), by_seq),
            pl.BlockSpec((None, hidden, block), by_seq),
            pl.BlockSpec((8, block), lanes),
            pl.BlockSpec((hidden, 128), fixed),
            pl.BlockSpec((width, 128), fixed),
            pl.BlockSpec((hidden, width), fixed),
            pl.BlockSpec((width, hidden), fixed),
        ],
        scratch_shapes=[pltpu.VMEM((hidden, width), F32), pltpu.VMEM((width, hidden), F32)],
    )
    return pl.pallas_call(
        mlp_kernel,
        grid_spec=grid_spec,
        out_shape=[
            jax.ShapeDtypeStruct((seqs, width, LEN), BF16),
            jax.ShapeDtypeStruct((seqs, hidden, LEN), BF16),
            jax.ShapeDtypeStruct((seqs, hidden, LEN), BF16),
            jax.ShapeDtypeStruct((8, tokens), F32),
            jax.ShapeDtypeStruct((hidden, 128), F32),
            jax.ShapeDtypeStruct((width, 128), F32),
            jax.ShapeDtypeStruct((hidden, width), BF16),
            jax.ShapeDtypeStruct((width, hidden), BF16),
        ],
        cost_estimate=cost(20, 30_000_000),
        name="mlp",
    )(place, *pieces, *gains, up_t, up_bias, d_act, cot)


def attention_kernel(last, seq, first, count, normed, mixed_t, d_att, mask_q, mask_k, gains, cot_hbm, *rest):
    if seq:
        before_hbm, rest = rest[0], rest[1:]
    (
        attended, d_mixed, gain_sum, grads, qkv, qx, kx, vn, kt, vt, es, ps, oa, dqa, dka, dva, cot, before, cot_sem,
        before_sem,
    ) = rest
    part = attended.shape[0]
    heads = part // DH
    inv_dh = 1.0 / DH
    copies = [pltpu.make_async_copy(cot_hbm.at[pl.ds(seq * LEN, LEN), :], cot, cot_sem)]
    if seq:
        copies.append(pltpu.make_async_copy(before_hbm, before, before_sem))
    for copy in copies:
        copy.start()

    qkv[...] = dot(mixed_t[...], normed[...])

    def unit(start):
        raw = qkv[start : start + DH, :]
        shifted = raw - jnp.sum(raw, axis=0, keepdims=True) * inv_dh
        scale = lax.rsqrt(jnp.sum(shifted * shifted, axis=0, keepdims=True) * inv_dh + EPSILON)
        return shifted * scale, scale

    zeros = jnp.zeros((128 - DH - IMAGE_SLOTS, LEN), BF16)
    for head in range(heads):
        rows = slice(head * DH, (head + 1) * DH)
        query, _ = unit(head * DH)
        query = (query * (gains[rows, :] * 0.125)).astype(BF16)
        qx[head] = jnp.concatenate([query, mask_q[...], zeros], axis=0)
        key, _ = unit(part + head * DH)
        key = (key * gains[part + head * DH : part + (head + 1) * DH, :]).astype(BF16)
        kt[rows, :] = key
        kx[head] = jnp.concatenate([key, mask_k[...], zeros], axis=0).T
        value = qkv[2 * part + head * DH : 2 * part + (head + 1) * DH, :].astype(BF16)
        vt[rows, :] = value
        vn[head] = value.T
    dka[...] = jnp.zeros_like(dka)
    dva[...] = jnp.zeros_like(dva)

    def query_block(ib, _):
        i0 = pl.multiple_of(ib * BI, BI)
        icols = pl.ds(i0, BI)
        base = first[ib]
        trips = count[ib]

        def scores(j, carry):
            j0 = pl.multiple_of((base + j) * BJ, BJ)
            slot = pl.multiple_of(j * BJ, BJ)
            out = []
            for head in range(heads):
                rows = slice(head * DH, (head + 1) * DH)
                e = jnp.exp(dot(kx[head, pl.ds(j0, BJ), :], qx[head, :, icols]))
                p = dot(vn[head, pl.ds(j0, BJ), :], d_att[rows, icols])
                es[head, pl.ds(slot, BJ), :] = e
                ps[head, pl.ds(slot, BJ), :] = p
                out.append(carry[2 * head] + jnp.sum(e.reshape(BJ // 8, 8, BI), axis=0))
                out.append(carry[2 * head + 1] + jnp.sum((e * p).reshape(BJ // 8, 8, BI), axis=0))
            return tuple(out)

        sums = lax.fori_loop(0, trips, scores, tuple(jnp.zeros((8, BI), F32) for _ in range(2 * heads)))
        inverse = []
        inner = []
        for head in range(heads):
            inv = 1.0 / jnp.sum(sums[2 * head], axis=0, keepdims=True)
            inverse.append(inv)
            inner.append(jnp.sum(sums[2 * head + 1], axis=0, keepdims=True) * inv)
        oa[...] = jnp.zeros_like(oa)
        dqa[:, icols] = jnp.zeros((part, BI), F32)

        def row_grads(j, _):
            j0 = pl.multiple_of((base + j) * BJ, BJ)
            slot = pl.multiple_of(j * BJ, BJ)
            jcols = pl.ds(j0, BJ)
            for head in range(heads):
                rows = slice(head * DH, (head + 1) * DH)
                w = es[head, pl.ds(slot, BJ), :] * inverse[head]
                d = (w * (ps[head, pl.ds(slot, BJ), :] - inner[head])).astype(BF16)
                w = w.astype(BF16)
                oa[rows, :] += dot(vt[rows, jcols], w)
                dqa[rows, icols] += dot(kt[rows, jcols], d)
                dva[rows, jcols] += dot(d_att[rows, icols], w, NT)
                dka[rows, jcols] += dot(qx[head, :DH, icols], d, NT)
            return 0

        lax.fori_loop(0, trips, row_grads, 0)
        attended[:, icols] = oa[...].astype(BF16)
        return 0

    lax.fori_loop(0, LEN // BI, query_block, 0)

    for source, offset, factor in ((dqa, 0, 0.125), (dka, part, 1.0)):
        for head in range(heads):
            start = offset + head * DH
            u, scale = unit(start)
            e = source[head * DH : (head + 1) * DH, :] * factor
            gain_sum[start : start + DH, :] = fold_lanes(e * u)
            f = e * gains[start : start + DH, :]
            mean_f = jnp.sum(f, axis=0, keepdims=True) * inv_dh
            mean_fu = jnp.sum(f * u, axis=0, keepdims=True) * inv_dh
            d_mixed[start : start + DH, :] = ((f - mean_f - u * mean_fu) * scale).astype(BF16)
    d_mixed[2 * part :, :] = dva[...].astype(BF16)

    for copy in copies:
        copy.wait()
    split = 3 * part
    for rows, value in (
        (slice(0, split), dot(d_mixed[...], normed[...], NT)),
        (slice(split, split + part), dot(attended[...], cot[...])),
    ):
        if seq:
            value = value + before[rows, :]
        grads[rows, :] = value.astype(grads.dtype)


def attention_call(first, count, normed, mixed_t, d_att, mask_q, mask_k, gains, cot, before, seq, last):
    seqs, part, _ = d_att.shape
    width = normed.shape[1]
    heads = part // DH
    once = lambda i, *_: (0, 0)
    ours = lambda i, *_: (seq, 0, 0)
    grid_spec = pltpu.PrefetchScalarGridSpec(
        num_scalar_prefetch=2,
        grid=(1,),
        in_specs=[
            pl.BlockSpec((None, width, LEN), ours),
            pl.BlockSpec((3 * part, width), once),
            pl.BlockSpec((None, part, LEN), ours),
            pl.BlockSpec((None, IMAGE_SLOTS, LEN), ours),
            pl.BlockSpec((None, IMAGE_SLOTS, LEN), ours),
            pl.BlockSpec((2 * part, 1), once),
            ANY,
        ]
        + [ANY] * len(before),
        out_specs=[
            pl.BlockSpec((part, LEN), once),
            pl.BlockSpec((3 * part, LEN), once),
            pl.BlockSpec((2 * part, 128), once),
            pl.BlockSpec((4 * part, width), once),
        ],
        scratch_shapes=[
            pltpu.VMEM((3 * part, LEN), F32),
            pltpu.VMEM((heads, 128, LEN), BF16),
            pltpu.VMEM((heads, LEN, 128), BF16),
            pltpu.VMEM((heads, LEN, DH), BF16),
            pltpu.VMEM((part, LEN), BF16),
            pltpu.VMEM((part, LEN), BF16),
            pltpu.VMEM((heads, LEN, BI), F32),
            pltpu.VMEM((heads, LEN, BI), F32),
            pltpu.VMEM((part, BI), F32),
            pltpu.VMEM((part, LEN), F32),
            pltpu.VMEM((part, LEN), F32),
            pltpu.VMEM((part, LEN), F32),
            pltpu.VMEM((LEN, width), BF16),
            pltpu.VMEM((4 * part, width), F32),
            pltpu.SemaphoreType.DMA(()),
            pltpu.SemaphoreType.DMA(()),
        ],
    )
    return pl.pallas_call(
        functools.partial(attention_kernel, last, seq),
        grid_spec=grid_spec,
        out_shape=[
            jax.ShapeDtypeStruct((part, LEN), BF16),
            jax.ShapeDtypeStruct((3 * part, LEN), BF16),
            jax.ShapeDtypeStruct((2 * part, 128), F32),
            jax.ShapeDtypeStruct((4 * part, width), BF16 if last else F32),
        ],
        cost_estimate=cost(18, 5_000_000),
        name="attention",
    )(first, count, normed, mixed_t, d_att, mask_q, mask_k, gains, cot, *before)


def project_kernel(
    shard, active, attended, d_pre, d_mixed, normed, down_t, attn_t, up, mixed, gain, keep, send, gain_sum
):
    me = shard[0]
    part = attended.shape[0]
    out = dot(down_t[...], active[...]) + dot(attn_t[...], attended[...])
    grad = dot(up[...], d_pre[...]) + dot(mixed[...], d_mixed[...])
    product = grad * normed[...].astype(F32)
    sums = []
    for row in (jnp.sum(grad * gain[:, :1], axis=0, keepdims=True), jnp.sum(product, axis=0, keepdims=True)):
        high = row.astype(BF16)
        sums += [high, (row - high.astype(F32)).astype(BF16)]
    sums = jnp.concatenate(sums + [jnp.zeros((SUM_ROWS - 4, sums[0].shape[1]), BF16)], axis=0)
    for target in (keep, send):
        for slot in range(2):
            target[slot, 2 * part :, :] = sums
    for index in range(4):
        rows = slice(index * part, (index + 1) * part)
        away = jnp.bitwise_xor(me, index)
        slot = away // 2

        @pl.when(away % 2 == 0)
        def _():
            keep[slot, :part, :] = out[rows].astype(BF16)
            keep[slot, part : 2 * part, :] = grad[rows].astype(BF16)

        @pl.when(away % 2 == 1)
        def _():
            send[slot, :part, :] = out[rows].astype(BF16)
            send[slot, part : 2 * part, :] = grad[rows].astype(BF16)

    @pl.when(pl.program_id(0) == 0)
    def _():
        gain_sum[...] = jnp.zeros_like(gain_sum)

    gain_sum[...] += fold_lanes(product)


def project_call(shard, active, attended, d_pre, d_mixed, normed, down_t, attn_t, up, mixed, gain, seq, block=256):
    width, hidden = down_t.shape
    part = attended.shape[0]
    steps = LEN // block
    lanes = lambda i, *_: (0, i)
    ours = lambda i, *_: (seq, 0, i)
    fixed = lambda i, *_: (0, 0)
    rows = 2 * part + SUM_ROWS
    grid_spec = pltpu.PrefetchScalarGridSpec(
        num_scalar_prefetch=1,
        grid=(steps,),
        in_specs=[
            pl.BlockSpec((None, hidden, block), ours),
            pl.BlockSpec((part, block), lanes),
            pl.BlockSpec((None, hidden, block), ours),
            pl.BlockSpec((3 * part, block), lanes),
            pl.BlockSpec((None, width, block), ours),
            pl.BlockSpec((width, hidden), fixed),
            pl.BlockSpec((width, part), fixed),
            pl.BlockSpec((width, hidden), fixed),
            pl.BlockSpec((width, 3 * part), fixed),
            pl.BlockSpec((width, 128), fixed),
        ],
        out_specs=[
            pl.BlockSpec((2, rows, block), lambda i, *_: (0, 0, i)),
            pl.BlockSpec((2, rows, block), lambda i, *_: (0, 0, i)),
            pl.BlockSpec((width, 128), fixed),
        ],
    )
    return pl.pallas_call(
        project_kernel,
        grid_spec=grid_spec,
        out_shape=[
            jax.ShapeDtypeStruct((2, rows, LEN), BF16),
            jax.ShapeDtypeStruct((2, rows, LEN), BF16),
            jax.ShapeDtypeStruct((width, 128), F32),
        ],
        cost_estimate=cost(8, 16_000_000),
        name="project",
    )(shard, active, attended, d_pre, d_mixed, normed, down_t, attn_t, up, mixed, gain)


def finish_kernel(keep, from_core, from_y, own_t, tokens, cot, stats, gain, bias, *rest):
    block_out, token_grad = rest[-2:]
    part = own_t.shape[0]
    inv_width = 0.25 / part
    total = keep[...].astype(F32) + from_core[...].astype(F32) + from_y[...].astype(F32)
    block_out[...] = (tokens[...].astype(F32) + total[:part].T + bias[...]).astype(BF16)
    grad = total[part : 2 * part]
    sums = total[2 * part :]
    mean = stats[0:1, :]
    scale = stats[1:2, :]
    hat = (own_t[...].astype(F32) - mean) * scale
    inner = grad * gain[...] - (sums[0:1] + sums[1:2]) * inv_width - hat * ((sums[2:3] + sums[3:4]) * inv_width)
    token_grad[...] = cot[...].astype(F32) + (inner * scale).T


def finish_call(keep, from_core, from_y, own_t, tokens, cot, stats, gain, bias, before, seq, block=512):
    part = own_t.shape[0]
    steps = LEN // block
    fixed = lambda i: (0, 0)
    ours = lambda i: (0, seq * steps + i)
    packed = pl.BlockSpec((None, 2 * part + SUM_ROWS, block), lambda i: (0, 0, i))
    here = pl.BlockSpec((block, part), lambda i: (seq * steps + i, 0))
    return pl.pallas_call(
        finish_kernel,
        grid=(steps,),
        in_specs=[
            packed, packed, packed,
            pl.BlockSpec((part, block), ours),
            here, here,
            pl.BlockSpec((8, block), ours),
            pl.BlockSpec((part, 1), fixed),
            pl.BlockSpec((1, part), fixed),
        ]
        + [ANY] * len(before),
        out_specs=[here, here],
        out_shape=[
            jax.ShapeDtypeStruct(tokens.shape, BF16),
            jax.ShapeDtypeStruct(tokens.shape, F32),
        ],
        input_output_aliases={9 + i: i for i in range(len(before))},
        cost_estimate=cost(3, 5_000_000),
        name="finish",
    )(keep, from_core, from_y, own_t, tokens, cot, stats, gain, bias, *before)


def flip(value, axis, size, bit):
    return lax.ppermute(value, axis, [(i, i ^ bit) for i in range(size)])


def tie(*trees):
    return lax.optimization_barrier(trees)


class SumOverDp:
    def __init__(self, value, size, index, turn):
        self.size, self.index = size, index
        bits = [1 << i for i in range(size.bit_length() - 1)]
        bits = bits[turn:] + bits[:turn]
        self.steps = [("sum", bit) for bit in bits] + [("join", bit) for bit in reversed(bits)]
        self.prepare(value, None)

    def prepare(self, held, arrived):
        def part(which, half):
            rows = lax.dynamic_slice_in_dim(held, which * half, half, 0)
            if arrived is None:
                return rows
            came = lax.dynamic_slice_in_dim(arrived, which * half, half, 0)
            return (rows.astype(F32) + came.astype(F32)).astype(BF16)

        rows = held.shape[0]
        if self.steps and self.steps[0][0] == "sum":
            side = self.side(self.steps[0][1])
            self.send, self.keep = part(1 - side, rows // 2), part(side, rows // 2)
        else:
            self.keep = part(0, rows)
            self.send = self.keep

    def side(self, bit):
        return (self.index & bit) // bit

    def more(self):
        return bool(self.steps)

    def move(self, send):
        return flip(send, "dp", self.size, self.steps[0][1])

    def take(self, arrived):
        kind, bit = self.steps.pop(0)
        if kind == "sum":
            self.prepare(self.keep, arrived)
            return
        self.keep = jnp.where(
            self.side(bit) == 1,
            jnp.concatenate([arrived, self.keep], axis=0),
            jnp.concatenate([self.keep, arrived], axis=0),
        )
        self.send = self.keep


class ScatterOverMp:
    def __init__(self, keep, send):
        self.keep, self.send = keep, send
        self.bits = [1, 2]

    def more(self):
        return bool(self.bits)

    def move(self, send):
        return flip(send, "mp", 4, self.bits[0])

    def take(self, arrived):
        bit = self.bits.pop(0)
        if bit == 1:
            self.from_core = arrived
            self.send = (self.keep[1].astype(F32) + arrived[1].astype(F32)).astype(BF16)[None]
        else:
            self.from_y = arrived


def launch(movers, inputs):
    movers = [m for m in movers if m.more()]
    inputs, sends = tie(inputs, [m.send for m in movers])
    return inputs, [(m, m.move(s)) for m, s in zip(movers, sends)]


def land(flights, outputs):
    outputs, arrivals = tie(outputs, [f[1] for f in flights])
    for (mover, _), arrived in zip(flights, arrivals):
        mover.take(arrived)
    return outputs


def body(
    dp_size,
    tokens,
    image_ids,
    norm_gain,
    qkv_weight,
    qk_gain,
    attn_weight,
    up_weight,
    up_bias,
    down_weight,
    down_bias,
    cotangent,
):
    part = tokens.shape[1]
    width = cotangent.shape[1]
    seqs = image_ids.shape[0]
    me = lax.axis_index("mp")
    dp = lax.axis_index("dp")
    shard = me.astype(jnp.int32)[None]
    place = jnp.bitwise_xor(shard, jnp.array([0, 2, 1, 3], jnp.int32)) * part

    own_t = tokens.T
    from_y = flip(own_t, "mp", 4, 2)
    gain_own = jnp.broadcast_to(norm_gain[:, None], (part, 128))
    gain_y = flip(gain_own, "mp", 4, 2)
    gains = (gain_own, gain_y, flip(gain_own, "mp", 4, 1), flip(gain_y, "mp", 4, 1))

    mixed_t = jnp.transpose(qkv_weight, (1, 2, 0)).reshape(3 * part, width)
    mixed = mixed_t.T
    up_t = up_weight.T
    down_t = down_weight.T
    attn_t = attn_weight.T
    up_bias_col = up_bias.astype(F32)[:, None]
    head_gains = qk_gain.astype(F32).reshape(2 * part, 1)

    slots = jnp.arange(IMAGE_SLOTS, dtype=jnp.int32)[None, :, None]
    same = image_ids[:, None, :] == slots
    mask_q = same.astype(BF16)
    mask_k = jnp.where(same | (slots >= 8), 0.0, -PENALTY).astype(BF16)
    block_first = image_ids[:, ::BI]
    block_last = image_ids[:, BI - 1 :: BI]
    starts = jnp.sum(image_ids[:, None, :] < block_first[:, :, None], axis=2, dtype=jnp.int32)
    ends = jnp.sum(image_ids[:, None, :] <= block_last[:, :, None], axis=2, dtype=jnp.int32)
    first = starts // BJ
    count = (ends + BJ - 1) // BJ - first

    d_act, d_att, cot_sum = early_call(cotangent, down_weight, attn_weight)
    (d_act, d_att), from_y = tie((d_act, d_att), from_y)
    pieces = (own_t, from_y, flip(own_t, "mp", 4, 1), flip(from_y, "mp", 4, 1))
    cot_own = lax.dynamic_slice_in_dim(cotangent, me * part, part, 1)
    downbias_part = lax.dynamic_slice_in_dim(jnp.sum(cot_sum, axis=0), me * part, part, 0)

    normed, active, d_pre, stats, upbias_part, gain_all, down_part, up_part = mlp_call(
        place, pieces, gains, up_t, up_bias_col, d_act, cotangent
    )
    upbias_part = jnp.sum(upbias_part, axis=1)
    down_sum = SumOverDp(down_part, dp_size, dp, 0)
    up_sum = SumOverDp(up_part, dp_size, dp, 1)

    heads_out = []
    before = ()
    qk_part = 0.0
    for seq in range(seqs):
        (states, before), flights = launch([down_sum, up_sum], (normed, before))
        *out, qk, total = attention_call(
            first[seq], count[seq], states, mixed_t, d_att, mask_q, mask_k, head_gains, cotangent, before, seq,
            seq == seqs - 1,
        )
        out, qk, total = land(flights, (out, qk, total))
        heads_out.append(out)
        before = (total,)
        qk_part = qk_part + qk
    mix_sum = SumOverDp(before[0], dp_size, dp, 0)

    scatters = []
    gain_part = 0.0
    waiting = []
    for seq in range(seqs):
        ahead = [[down_sum, up_sum, mix_sum], [down_sum, up_sum], [down_sum, up_sum, mix_sum]][seq % 3]
        (attended, d_mixed), flights = launch(ahead + scatters[-2:], heads_out[seq])
        keep, send, gp = project_call(
            shard, active, attended, d_pre, d_mixed, normed, down_t, attn_t, up_weight, mixed, gain_all, seq
        )
        later = [f for f in flights if f[0] is mix_sum and seq == 0]
        keep, send, gp = land([f for f in flights if f not in later] + waiting, (keep, send, gp))
        waiting = later
        gain_part = gain_part + gp
        scatters.append(ScatterOverMp(keep, send))

    gain_vec = jnp.sum(gain_part, axis=1).reshape(4, part)
    gain_half = [lax.dynamic_index_in_dim(gain_vec, jnp.bitwise_xor(me, m), 0, False) for m in range(4)]
    gain_kept = jnp.stack([gain_half[0], gain_half[2]]) + flip(jnp.stack([gain_half[1], gain_half[3]]), "mp", 4, 1)
    gain_mine = gain_kept[0] + flip(gain_kept[1], "mp", 4, 2)
    short = jnp.concatenate(
        [gain_mine / norm_gain.astype(F32), jnp.sum(qk_part, axis=1), upbias_part, downbias_part]
    )
    bit = 1
    while bit < dp_size:
        short = short + flip(short, "dp", dp_size, bit)
        bit *= 2

    gain_bias = down_bias.astype(F32)[None, :]
    gain_col = norm_gain.astype(F32)[:, None]
    finished = ()
    for seq, scatter in enumerate(scatters):
        while scatter.more():
            scatter.take(scatter.move(scatter.send))
        finished = finish_call(
            scatter.keep, scatter.from_core, scatter.from_y, own_t, tokens, cot_own, stats,
            gain_col, gain_bias, finished, seq,
        )
    block_out, token_grad = finished

    movers = [down_sum, up_sum, mix_sum]
    while any(m.more() for m in movers):
        for mover in movers:
            if mover.more():
                mover.take(mover.move(mover.send))
    mixed_grad = mix_sum.keep.astype(F32)
    qkv_grad = jnp.transpose(mixed_grad[: 3 * part].reshape(3, part, width), (2, 0, 1))

    gain_grad = short[:part]
    qkgain_grad = short[part : 3 * part].reshape(2, part)
    upbias_grad = short[3 * part : 3 * part + upbias_part.shape[0]]
    downbias_grad = short[3 * part + upbias_part.shape[0] :]
    return (
        block_out,
        token_grad,
        gain_grad,
        qkv_grad,
        qkgain_grad,
        mixed_grad[3 * part :],
        up_sum.keep.astype(F32),
        upbias_grad,
        down_sum.keep.astype(F32),
        downbias_grad,
    )


def solution(mesh):
    in_specs = (
        P("dp", "mp"),
        P("dp", None),
        P("mp"),
        P(None, None, "mp"),
        P(None, "mp"),
        P("mp", None),
        P(None, "mp"),
        P("mp"),
        P("mp", None),
        P("mp"),
        P("dp", None),
    )
    out_specs = (
        P("dp", "mp"),
        P("dp", "mp"),
        P("mp"),
        P(None, None, "mp"),
        P(None, "mp"),
        P("mp", None),
        P(None, "mp"),
        P("mp"),
        P("mp", None),
        P("mp"),
    )
    run = functools.partial(body, mesh.shape["dp"])
    return jax.shard_map(run, mesh=mesh, in_specs=in_specs, out_specs=out_specs, check_vma=False)
```

```python
import functools

import jax
import jax.numpy as jnp
from jax import lax
from jax.experimental import pallas as pl
from jax.experimental.pallas import tpu as pltpu
from jax.sharding import PartitionSpec as P

DH = 64
LEN = 1024
EPSILON = 1e-06
IMAGE_SLOTS = 16
PENALTY = 1024.0
BI = 256
BJ = 256
SUM_ROWS = 16
F32 = jnp.float32
BF16 = jnp.bfloat16

NN = (((1,), (0,)), ((), ()))
NT = (((1,), (1,)), ((), ()))
ANY = pl.BlockSpec(memory_space=pl.ANY)


def dot(left, right, dims=NN):
    return lax.dot_general(left, right, dims, preferred_element_type=F32)


def fold_lanes(rows):
    total = rows[:, :128]
    for start in range(128, rows.shape[1], 128):
        total = total + rows[:, start : start + 128]
    return total


def cost(microseconds, nbytes):
    return pl.CostEstimate(flops=int(microseconds * 1e3), bytes_accessed=nbytes // 1000, transcendentals=0)


def early_kernel(cot, down, attn, pick, d_act, d_att, cot_own, bias_sum):
    rows = cot[...]
    d_act[...] = dot(down[...], rows, NT).astype(BF16)
    d_att[...] = dot(attn[...], rows, NT).astype(BF16)
    own = dot(pick[...], rows, NT)
    cot_own[...] = own.astype(BF16)

    @pl.when(pl.program_id(0) == 0)
    def _():
        bias_sum[...] = jnp.zeros_like(bias_sum)

    bias_sum[...] += fold_lanes(own)


def early_call(cot, down, attn, pick, block=512):
    tokens, width = cot.shape
    seqs = tokens // LEN
    hidden, part = down.shape[0], attn.shape[0]
    steps = LEN // block
    fixed = lambda i: (0, 0)
    by_seq = lambda i: (i // steps, 0, i % steps)
    return pl.pallas_call(
        early_kernel,
        grid=(tokens // block,),
        in_specs=[
            pl.BlockSpec((block, width), lambda i: (i, 0)),
            pl.BlockSpec((hidden, width), fixed),
            pl.BlockSpec((part, width), fixed),
            pl.BlockSpec((part, width), fixed),
        ],
        out_specs=[
            pl.BlockSpec((None, hidden, block), by_seq),
            pl.BlockSpec((None, part, block), by_seq),
            pl.BlockSpec((part, block), lambda i: (0, i)),
            pl.BlockSpec((part, 128), fixed),
        ],
        out_shape=[
            jax.ShapeDtypeStruct((seqs, hidden, LEN), BF16),
            jax.ShapeDtypeStruct((seqs, part, LEN), BF16),
            jax.ShapeDtypeStruct((part, tokens), BF16),
            jax.ShapeDtypeStruct((part, 128), F32),
        ],
        cost_estimate=cost(10, 12_000_000),
        name="early",
    )(cot, down, attn, pick)


def mlp_kernel(
    place, own, flip_y, flip_c, flip_cy, gain_own, gain_y, gain_c, gain_cy, up_t, up_bias, d_act, cot,
    normed, active, d_pre, stats, bias_sum, gain_all, down_grad, up_grad, low, high
):
    pieces = (own, flip_y, flip_c, flip_cy)
    part = own.shape[0]
    width = part * 4
    first = pl.program_id(0) == 0
    last = pl.program_id(0) == pl.num_programs(0) - 1

    @pl.when(first)
    def _():
        bias_sum[...] = jnp.zeros_like(bias_sum)
        low[...] = jnp.zeros_like(low)
        high[...] = jnp.zeros_like(high)
        for slot, piece in enumerate((gain_own, gain_y, gain_c, gain_cy)):
            gain_all[pl.ds(pl.multiple_of(place[slot], part), part), :] = piece[...].astype(F32)

    total = 0.0
    squares = 0.0
    for piece in pieces:
        rows = piece[...].astype(F32)
        total = total + jnp.sum(rows, axis=0, keepdims=True)
        squares = squares + jnp.sum(rows * rows, axis=0, keepdims=True)
    mean = total * (1.0 / width)
    scale = lax.rsqrt(squares * (1.0 / width) - mean * mean + EPSILON)
    stats[0:1, :] = mean
    stats[1:2, :] = scale
    stats[2:8, :] = jnp.zeros((6, stats.shape[1]), F32)
    for slot, piece in enumerate(pieces):
        rows = piece[...].astype(F32)
        here = pl.ds(pl.multiple_of(place[slot], part), part)
        normed[here, :] = ((rows - mean) * scale * gain_all[here, :1]).astype(BF16)

    c0 = 0.7978845608028654
    c1 = 0.044715 * c0
    def lift(start):
        here = slice(start, start + 256)
        return dot(up_t[here, :], normed[...]) + up_bias[here, :]

    ahead = lift(0)
    for start in range(0, up_t.shape[0], 256):
        here = slice(start, start + 256)
        pre = ahead
        if start + 256 < up_t.shape[0]:
            ahead = lift(start + 256)
        square = pre * pre
        half = 0.5 * jnp.tanh(pre * (c0 + c1 * square)) + 0.5
        act = (pre * half).astype(BF16)
        active[here, :] = act
        slope = half + pre * (half - half * half) * (2.0 * c0 + 6.0 * c1 * square)
        grad = (d_act[here, :].astype(F32) * slope).astype(BF16)
        d_pre[here, :] = grad
        bias_sum[here, :] += fold_lanes(grad.astype(F32))
        low[here, :] += dot(act, cot[...])
        high[:, here] += dot(normed[...], grad, NT)

    @pl.when(last)
    def _():
        down_grad[...] = low[...].astype(BF16)
        up_grad[...] = high[...].astype(BF16)


def mlp_call(place, pieces, gains, up_t, up_bias, d_act, cot, block=512):
    part, tokens = pieces[0].shape
    width = 4 * part
    seqs, hidden, _ = d_act.shape
    steps = LEN // block
    lanes = lambda i, *_: (0, i)
    by_seq = lambda i, *_: (i // steps, 0, i % steps)
    fixed = lambda i, *_: (0, 0)
    grid_spec = pltpu.PrefetchScalarGridSpec(
        num_scalar_prefetch=1,
        grid=(tokens // block,),
        in_specs=[pl.BlockSpec((part, block), lanes)] * 4
        + [pl.BlockSpec((part, 128), fixed)] * 4
        + [
            pl.BlockSpec((hidden, width), fixed),
            pl.BlockSpec((hidden, 1), fixed),
            pl.BlockSpec((None, hidden, block), by_seq),
            pl.BlockSpec((block, width), lambda i, *_: (i, 0)),
        ],
        out_specs=[
            pl.BlockSpec((None, width, block), by_seq),
            pl.BlockSpec((None, hidden, block), by_seq),
            pl.BlockSpec((None, hidden, block), by_seq),
            pl.BlockSpec((8, block), lanes),
            pl.BlockSpec((hidden, 128), fixed),
            pl.BlockSpec((width, 128), fixed),
            pl.BlockSpec((hidden, width), fixed),
            pl.BlockSpec((width, hidden), fixed),
        ],
        scratch_shapes=[pltpu.VMEM((hidden, width), F32), pltpu.VMEM((width, hidden), F32)],
    )
    return pl.pallas_call(
        mlp_kernel,
        grid_spec=grid_spec,
        out_shape=[
            jax.ShapeDtypeStruct((seqs, width, LEN), BF16),
            jax.ShapeDtypeStruct((seqs, hidden, LEN), BF16),
            jax.ShapeDtypeStruct((seqs, hidden, LEN), BF16),
            jax.ShapeDtypeStruct((8, tokens), F32),
            jax.ShapeDtypeStruct((hidden, 128), F32),
            jax.ShapeDtypeStruct((width, 128), F32),
            jax.ShapeDtypeStruct((hidden, width), BF16),
            jax.ShapeDtypeStruct((width, hidden), BF16),
        ],
        cost_estimate=cost(20, 30_000_000),
        name="mlp",
    )(place, *pieces, *gains, up_t, up_bias, d_act, cot)


def attention_kernel(last, seq, first, count, normed, mixed_t, d_att, mask_q, mask_k, gains, cot_hbm, *rest):
    if seq:
        before_hbm, rest = rest[0], rest[1:]
    (
        attended, d_mixed, gain_sum, norm_row, grads, qkv, qx, kx, vn, kt, vt, es, ps, oa, dqa, dka, dva, cot, before, cot_sem,
        before_sem,
    ) = rest
    part = attended.shape[0]
    heads = part // DH
    inv_dh = 1.0 / DH
    copies = [pltpu.make_async_copy(cot_hbm.at[pl.ds(seq * LEN, LEN), :], cot, cot_sem)]
    if seq:
        copies.append(pltpu.make_async_copy(before_hbm, before, before_sem))
    for copy in copies:
        copy.start()

    qkv[...] = dot(mixed_t[...], normed[...])

    def unit(start):
        raw = qkv[start : start + DH, :]
        shifted = raw - jnp.sum(raw, axis=0, keepdims=True) * inv_dh
        scale = lax.rsqrt(jnp.sum(shifted * shifted, axis=0, keepdims=True) * inv_dh + EPSILON)
        return shifted * scale, scale

    zeros = jnp.zeros((128 - DH - IMAGE_SLOTS, LEN), BF16)
    for head in range(heads):
        rows = slice(head * DH, (head + 1) * DH)
        query, _ = unit(head * DH)
        query = (query * (gains[rows, :] * 0.125)).astype(BF16)
        qx[head] = jnp.concatenate([query, mask_q[...], zeros], axis=0)
        key, _ = unit(part + head * DH)
        key = (key * gains[part + head * DH : part + (head + 1) * DH, :]).astype(BF16)
        kt[rows, :] = key
        kx[head] = jnp.concatenate([key, mask_k[...], zeros], axis=0).T
        value = qkv[2 * part + head * DH : 2 * part + (head + 1) * DH, :].astype(BF16)
        vt[rows, :] = value
        vn[head] = value.T
    dka[...] = jnp.zeros_like(dka)
    dva[...] = jnp.zeros_like(dva)

    def query_block(ib, _):
        i0 = pl.multiple_of(ib * BI, BI)
        icols = pl.ds(i0, BI)
        base = first[ib]
        trips = count[ib]

        def scores(j, carry):
            j0 = pl.multiple_of((base + j) * BJ, BJ)
            slot = pl.multiple_of(j * BJ, BJ)
            out = []
            for head in range(heads):
                rows = slice(head * DH, (head + 1) * DH)
                e = jnp.exp(dot(kx[head, pl.ds(j0, BJ), :], qx[head, :, icols]))
                p = dot(vn[head, pl.ds(j0, BJ), :], d_att[rows, icols])
                es[head, pl.ds(slot, BJ), :] = e
                ps[head, pl.ds(slot, BJ), :] = p
                out.append(carry[2 * head] + jnp.sum(e.reshape(BJ // 8, 8, BI), axis=0))
                out.append(carry[2 * head + 1] + jnp.sum((e * p).reshape(BJ // 8, 8, BI), axis=0))
            return tuple(out)

        sums = lax.fori_loop(0, trips, scores, tuple(jnp.zeros((8, BI), F32) for _ in range(2 * heads)))
        inverse = []
        inner = []
        for head in range(heads):
            inv = 1.0 / jnp.sum(sums[2 * head], axis=0, keepdims=True)
            inverse.append(inv)
            inner.append(jnp.sum(sums[2 * head + 1], axis=0, keepdims=True) * inv)
        oa[...] = jnp.zeros_like(oa)
        dqa[:, icols] = jnp.zeros((part, BI), F32)

        def row_grads(j, _):
            j0 = pl.multiple_of((base + j) * BJ, BJ)
            slot = pl.multiple_of(j * BJ, BJ)
            jcols = pl.ds(j0, BJ)
            for head in range(heads):
                rows = slice(head * DH, (head + 1) * DH)
                w = es[head, pl.ds(slot, BJ), :] * inverse[head]
                d = (w * (ps[head, pl.ds(slot, BJ), :] - inner[head])).astype(BF16)
                w = w.astype(BF16)
                oa[rows, :] += dot(vt[rows, jcols], w)
                dqa[rows, icols] += dot(kt[rows, jcols], d)
                dva[rows, jcols] += dot(d_att[rows, icols], w, NT)
                dka[rows, jcols] += dot(qx[head, :DH, icols], d, NT)
            return 0

        lax.fori_loop(0, trips, row_grads, 0)
        attended[:, icols] = oa[...].astype(BF16)
        return 0

    lax.fori_loop(0, LEN // BI, query_block, 0)

    for source, offset, factor in ((dqa, 0, 0.125), (dka, part, 1.0)):
        for head in range(heads):
            start = offset + head * DH
            u, scale = unit(start)
            e = source[head * DH : (head + 1) * DH, :] * factor
            gain_sum[start : start + DH, :] = fold_lanes(e * u)
            f = e * gains[start : start + DH, :]
            mean_f = jnp.sum(f, axis=0, keepdims=True) * inv_dh
            mean_fu = jnp.sum(f * u, axis=0, keepdims=True) * inv_dh
            d_mixed[start : start + DH, :] = ((f - mean_f - u * mean_fu) * scale).astype(BF16)
    d_mixed[2 * part :, :] = dva[...].astype(BF16)

    for copy in copies:
        copy.wait()
    split = 3 * part
    for rows, value in (
        (slice(0, split), dot(d_mixed[...], normed[...], NT)),
        (slice(split, split + part), dot(attended[...], cot[...])),
    ):
        if seq:
            value = value + before[rows, :]
        if last and rows.start == 0:
            norm_row[...] = jnp.sum(value * mixed_t[...].astype(F32), axis=0, keepdims=True)
        grads[rows, :] = value.astype(grads.dtype)
    if not last:
        norm_row[...] = jnp.zeros_like(norm_row)


def attention_call(first, count, normed, mixed_t, d_att, mask_q, mask_k, gains, cot, before, seq, last):
    seqs, part, _ = d_att.shape
    width = normed.shape[1]
    heads = part // DH
    once = lambda i, *_: (0, 0)
    ours = lambda i, *_: (seq, 0, 0)
    grid_spec = pltpu.PrefetchScalarGridSpec(
        num_scalar_prefetch=2,
        grid=(1,),
        in_specs=[
            pl.BlockSpec((None, width, LEN), ours),
            pl.BlockSpec((3 * part, width), once),
            pl.BlockSpec((None, part, LEN), ours),
            pl.BlockSpec((None, IMAGE_SLOTS, LEN), ours),
            pl.BlockSpec((None, IMAGE_SLOTS, LEN), ours),
            pl.BlockSpec((2 * part, 1), once),
            ANY,
        ]
        + [ANY] * len(before),
        out_specs=[
            pl.BlockSpec((part, LEN), once),
            pl.BlockSpec((3 * part, LEN), once),
            pl.BlockSpec((2 * part, 128), once),
            pl.BlockSpec((1, width), once),
            pl.BlockSpec((4 * part, width), once),
        ],
        scratch_shapes=[
            pltpu.VMEM((3 * part, LEN), F32),
            pltpu.VMEM((heads, 128, LEN), BF16),
            pltpu.VMEM((heads, LEN, 128), BF16),
            pltpu.VMEM((heads, LEN, DH), BF16),
            pltpu.VMEM((part, LEN), BF16),
            pltpu.VMEM((part, LEN), BF16),
            pltpu.VMEM((heads, LEN, BI), F32),
            pltpu.VMEM((heads, LEN, BI), F32),
            pltpu.VMEM((part, BI), F32),
            pltpu.VMEM((part, LEN), F32),
            pltpu.VMEM((part, LEN), F32),
            pltpu.VMEM((part, LEN), F32),
            pltpu.VMEM((LEN, width), BF16),
            pltpu.VMEM((4 * part, width), F32),
            pltpu.SemaphoreType.DMA(()),
            pltpu.SemaphoreType.DMA(()),
        ],
    )
    return pl.pallas_call(
        functools.partial(attention_kernel, last, seq),
        grid_spec=grid_spec,
        out_shape=[
            jax.ShapeDtypeStruct((part, LEN), BF16),
            jax.ShapeDtypeStruct((3 * part, LEN), BF16),
            jax.ShapeDtypeStruct((2 * part, 128), F32),
            jax.ShapeDtypeStruct((1, width), F32),
            jax.ShapeDtypeStruct((4 * part, width), BF16 if last else F32),
        ],
        cost_estimate=cost(18, 5_000_000),
        name="attention",
    )(first, count, normed, mixed_t, d_att, mask_q, mask_k, gains, cot, *before)


def project_kernel(
    shard, active, attended, d_pre, d_mixed, normed, down_t, attn_t, up, mixed, gain, keep, send
):
    me = shard[0]
    part = attended.shape[0]
    out = dot(down_t[...], active[...]) + dot(attn_t[...], attended[...])
    grad = dot(up[...], d_pre[...]) + dot(mixed[...], d_mixed[...])
    product = grad * normed[...].astype(F32)
    sums = []
    for row in (jnp.sum(grad * gain[:, :1], axis=0, keepdims=True), jnp.sum(product, axis=0, keepdims=True)):
        high = row.astype(BF16)
        sums += [high, (row - high.astype(F32)).astype(BF16)]
    sums = jnp.concatenate(sums + [jnp.zeros((SUM_ROWS - 4, sums[0].shape[1]), BF16)], axis=0)
    for target in (keep, send):
        for slot in range(2):
            target[slot, 2 * part :, :] = sums
    for index in range(4):
        rows = slice(index * part, (index + 1) * part)
        away = jnp.bitwise_xor(me, index)
        slot = away // 2

        @pl.when(away % 2 == 0)
        def _():
            keep[slot, :part, :] = out[rows].astype(BF16)
            keep[slot, part : 2 * part, :] = grad[rows].astype(BF16)

        @pl.when(away % 2 == 1)
        def _():
            send[slot, :part, :] = out[rows].astype(BF16)
            send[slot, part : 2 * part, :] = grad[rows].astype(BF16)


def project_call(shard, active, attended, d_pre, d_mixed, normed, down_t, attn_t, up, mixed, gain, seq, block=256):
    width, hidden = down_t.shape
    part = attended.shape[0]
    steps = LEN // block
    lanes = lambda i, *_: (0, i)
    ours = lambda i, *_: (seq, 0, i)
    fixed = lambda i, *_: (0, 0)
    rows = 2 * part + SUM_ROWS
    grid_spec = pltpu.PrefetchScalarGridSpec(
        num_scalar_prefetch=1,
        grid=(steps,),
        in_specs=[
            pl.BlockSpec((None, hidden, block), ours),
            pl.BlockSpec((part, block), lanes),
            pl.BlockSpec((None, hidden, block), ours),
            pl.BlockSpec((3 * part, block), lanes),
            pl.BlockSpec((None, width, block), ours),
            pl.BlockSpec((width, hidden), fixed),
            pl.BlockSpec((width, part), fixed),
            pl.BlockSpec((width, hidden), fixed),
            pl.BlockSpec((width, 3 * part), fixed),
            pl.BlockSpec((width, 128), fixed),
        ],
        out_specs=[
            pl.BlockSpec((2, rows, block), lambda i, *_: (0, 0, i)),
            pl.BlockSpec((2, rows, block), lambda i, *_: (0, 0, i)),
        ],
    )
    return pl.pallas_call(
        project_kernel,
        grid_spec=grid_spec,
        out_shape=[
            jax.ShapeDtypeStruct((2, rows, LEN), BF16),
            jax.ShapeDtypeStruct((2, rows, LEN), BF16),
        ],
        cost_estimate=cost(8, 16_000_000),
        name="project",
    )(shard, active, attended, d_pre, d_mixed, normed, down_t, attn_t, up, mixed, gain)


def finish_kernel(keep, from_core, from_y, own_t, cot, stats, gain, bias, *rest):
    block_out, token_grad = rest[-2:]
    part = own_t.shape[0]
    inv_width = 0.25 / part
    total = keep[...].astype(F32) + from_core[...].astype(F32) + from_y[...].astype(F32)
    own = own_t[...].astype(F32)
    block_out[...] = (own + total[:part] + bias[...]).astype(BF16)
    grad = total[part : 2 * part]
    sums = total[2 * part :]
    mean = stats[0:1, :]
    scale = stats[1:2, :]
    hat = (own - mean) * scale
    inner = grad * gain[...] - (sums[0:1] + sums[1:2]) * inv_width - hat * ((sums[2:3] + sums[3:4]) * inv_width)
    token_grad[...] = cot[...].astype(F32) + inner * scale


def finish_call(keep, from_core, from_y, own_t, cot, stats, gain, bias, before, seq, block=512):
    part, tokens = own_t.shape
    steps = LEN // block
    fixed = lambda i: (0, 0)
    packed = pl.BlockSpec((None, 2 * part + SUM_ROWS, block), lambda i: (0, 0, i))
    ours = lambda i: (0, seq * steps + i)
    here = pl.BlockSpec((part, block), ours)
    return pl.pallas_call(
        finish_kernel,
        grid=(steps,),
        in_specs=[
            packed, packed, packed,
            here, here,
            pl.BlockSpec((8, block), ours),
            pl.BlockSpec((part, 1), fixed),
            pl.BlockSpec((part, 1), fixed),
        ]
        + [ANY] * len(before),
        out_specs=[here, here],
        out_shape=[
            jax.ShapeDtypeStruct((part, tokens), BF16),
            jax.ShapeDtypeStruct((part, tokens), F32),
        ],
        input_output_aliases={8 + i: i for i in range(len(before))},
        cost_estimate=cost(3, 5_000_000),
        name="finish",
    )(keep, from_core, from_y, own_t, cot, stats, gain, bias, *before)


def flip(value, axis, size, bit):
    return lax.ppermute(value, axis, [(i, i ^ bit) for i in range(size)])


def tie(*trees):
    return lax.optimization_barrier(trees)


class SumOverDp:
    def __init__(self, value, size, index, turn):
        self.size, self.index = size, index
        bits = [1 << i for i in range(size.bit_length() - 1)]
        bits = bits[turn:] + bits[:turn]
        self.steps = [("sum", bit) for bit in bits] + [("join", bit) for bit in reversed(bits)]
        self.prepare(value, None)

    def prepare(self, held, arrived):
        def part(which, half):
            rows = lax.dynamic_slice_in_dim(held, which * half, half, 0)
            if arrived is None:
                return rows
            came = lax.dynamic_slice_in_dim(arrived, which * half, half, 0)
            return (rows.astype(F32) + came.astype(F32)).astype(BF16)

        rows = held.shape[0]
        if self.steps and self.steps[0][0] == "sum":
            side = self.side(self.steps[0][1])
            self.send, self.keep = part(1 - side, rows // 2), part(side, rows // 2)
        else:
            self.keep = part(0, rows)
            self.send = self.keep

    def side(self, bit):
        return (self.index & bit) // bit

    def more(self):
        return bool(self.steps)

    def move(self, send):
        return flip(send, "dp", self.size, self.steps[0][1])

    def take(self, arrived):
        kind, bit = self.steps.pop(0)
        if kind == "sum":
            self.prepare(self.keep, arrived)
            return
        self.keep = jnp.where(
            self.side(bit) == 1,
            jnp.concatenate([arrived, self.keep], axis=0),
            jnp.concatenate([self.keep, arrived], axis=0),
        )
        self.send = self.keep


class SwapOverDp:
    def __init__(self, value, size):
        self.size = size
        self.send = value
        self.steps = ["sum", "join"]

    def more(self):
        return bool(self.steps)

    def move(self, send):
        return lax.all_to_all(send, "dp", 0, 0, tiled=True)

    def take(self, arrived):
        if self.steps.pop(0) == "sum":
            shares = arrived.reshape(self.size, -1, arrived.shape[1]).astype(F32)
            total = jnp.sum(shares, axis=0).astype(BF16)
            self.send = jnp.broadcast_to(total[None], (self.size,) + total.shape).reshape(arrived.shape)
        else:
            self.keep = arrived


class ScatterOverMp:
    def __init__(self, keep, send):
        self.keep, self.send = keep, send
        self.bits = [1, 2]

    def more(self):
        return bool(self.bits)

    def move(self, send):
        return flip(send, "mp", 4, self.bits[0])

    def take(self, arrived):
        bit = self.bits.pop(0)
        if bit == 1:
            self.from_core = arrived
            self.send = (self.keep[1].astype(F32) + arrived[1].astype(F32)).astype(BF16)[None]
        else:
            self.from_y = arrived


class ShortSums:
    def __init__(self, keep, send, rest, size):
        self.keep, self.send, self.rest, self.size = keep, send, rest, size
        self.steps = [("mp", 1), ("mp", 2)] + [("dp", 1 << i) for i in range(size.bit_length() - 1)]

    def more(self):
        return bool(self.steps)

    def move(self, send):
        axis, bit = self.steps[0]
        return flip(send, axis, 4 if axis == "mp" else self.size, bit)

    def take(self, arrived):
        axis, bit = self.steps.pop(0)
        if (axis, bit) == ("mp", 1):
            both = self.keep + arrived
            self.norm, self.send = both[0], both[1]
            return
        if axis == "mp":
            self.send = jnp.concatenate([self.norm + arrived, self.rest])
        else:
            self.send = self.send + arrived
        size = self.norm.shape[0]
        self.norm, self.rest = self.send[:size], self.send[size:]


def launch(movers, inputs):
    movers = [m for m in movers if m.more()]
    inputs, sends = tie(inputs, [m.send for m in movers])
    return inputs, [(m, m.move(s)) for m, s in zip(movers, sends)]


def land(flights, outputs):
    outputs, arrivals = tie(outputs, [f[1] for f in flights])
    for (mover, _), arrived in zip(flights, arrivals):
        mover.take(arrived)
    return outputs


def body(
    dp_size,
    tokens,
    image_ids,
    norm_gain,
    qkv_weight,
    qk_gain,
    attn_weight,
    up_weight,
    up_bias,
    down_weight,
    down_bias,
    cotangent,
):
    part = tokens.shape[1]
    width = cotangent.shape[1]
    seqs = image_ids.shape[0]
    me = lax.axis_index("mp")
    dp = lax.axis_index("dp")
    shard = me.astype(jnp.int32)[None]
    place = jnp.bitwise_xor(shard, jnp.array([0, 2, 1, 3], jnp.int32)) * part

    own_t = tokens.T
    from_y = flip(own_t, "mp", 4, 2)
    gain_own = jnp.broadcast_to(norm_gain[:, None], (part, 128))
    gain_y = flip(gain_own, "mp", 4, 2)
    gains = (gain_own, gain_y, flip(gain_own, "mp", 4, 1), flip(gain_y, "mp", 4, 1))

    mixed_t = jnp.transpose(qkv_weight, (1, 2, 0)).reshape(3 * part, width)
    mixed = mixed_t.T
    up_t = up_weight.T
    down_t = down_weight.T
    attn_t = attn_weight.T
    up_bias_col = up_bias.astype(F32)[:, None]
    head_gains = qk_gain.astype(F32).reshape(2 * part, 1)

    slots = jnp.arange(IMAGE_SLOTS, dtype=jnp.int32)[None, :, None]
    same = image_ids[:, None, :] == slots
    mask_q = same.astype(BF16)
    mask_k = jnp.where(same | (slots >= 8), 0.0, -PENALTY).astype(BF16)
    block_first = image_ids[:, ::BI]
    block_last = image_ids[:, BI - 1 :: BI]
    starts = jnp.sum(image_ids[:, None, :] < block_first[:, :, None], axis=2, dtype=jnp.int32)
    ends = jnp.sum(image_ids[:, None, :] <= block_last[:, :, None], axis=2, dtype=jnp.int32)
    first = starts // BJ
    count = (ends + BJ - 1) // BJ - first

    pick = (jnp.arange(part)[:, None] + me * part == jnp.arange(width)[None, :]).astype(BF16)
    d_act, d_att, cot_own, cot_sum = early_call(cotangent, down_weight, attn_weight, pick)
    gain_bias = down_bias.astype(F32)[:, None]
    gain_col = norm_gain.astype(F32)[:, None]
    prepared = (
        d_act, d_att, mixed_t, mixed, up_t, down_t, attn_t, up_bias_col, head_gains, mask_q, mask_k, first, count,
        gain_bias, gain_col,
    )
    prepared, from_y = tie(prepared, from_y)
    (
        d_act, d_att, mixed_t, mixed, up_t, down_t, attn_t, up_bias_col, head_gains, mask_q, mask_k, first, count,
        gain_bias, gain_col,
    ) = prepared
    pieces = (own_t, from_y, flip(own_t, "mp", 4, 1), flip(from_y, "mp", 4, 1))
    normed, active, d_pre, stats, upbias_part, gain_all, down_part, up_part = mlp_call(
        place, pieces, gains, up_t, up_bias_col, d_act, cotangent
    )
    down_sum = SumOverDp(down_part, dp_size, dp, 0)
    up_sum = SwapOverDp(up_part, dp_size)

    heads_out = []
    before = ()
    qk_part = 0.0
    held = []
    for seq in range(seqs):
        along = [down_sum] + ([up_sum] if not held else [])
        (states, before), flights = launch(along, (normed, before))
        *out, qk, norm_row, total = attention_call(
            first[seq], count[seq], states, mixed_t, d_att, mask_q, mask_k, head_gains, cotangent, before, seq,
            seq == seqs - 1,
        )
        ending = held + [f for f in flights if f[0] is down_sum]
        held = [f for f in flights if f[0] is up_sum]
        out, qk, norm_row, total = land(ending, (out, qk, norm_row, total))
        heads_out.append(out)
        before = (total,)
        qk_part = qk_part + qk
    mix_sum = SwapOverDp(before[0], dp_size)

    norm_vec = norm_row[0] + jnp.sum(up_part.astype(F32) * up_weight.astype(F32), axis=1)
    norm_parts = norm_vec.reshape(4, part)
    norm_parts = [lax.dynamic_index_in_dim(norm_parts, jnp.bitwise_xor(me, m), 0, False) for m in range(4)]
    short = ShortSums(
        jnp.stack([norm_parts[0], norm_parts[2]]),
        jnp.stack([norm_parts[1], norm_parts[3]]),
        jnp.concatenate([jnp.sum(qk_part, axis=1), jnp.sum(upbias_part, axis=1), jnp.sum(cot_sum, axis=1)]),
        dp_size,
    )

    def project(seq, work):
        attended, d_mixed = work
        return project_call(
            shard, active, attended, d_pre, d_mixed, normed, down_t, attn_t, up_weight, mixed, gain_all, seq
        )

    scatters = []
    mixing = []
    for seq in range(seqs):
        along = [down_sum, short] + [m for m in scatters if m.more()]
        if seq == 0:
            along.append(mix_sum)
        work, flights = launch(along, heads_out[seq])
        keep, send = project(seq, work)
        now = [f for f in flights if f[0] is not mix_sum]
        mixing += [f for f in flights if f[0] is mix_sum]
        if seq == 1:
            now += held
            held = []
        keep, send = land(now, (keep, send))
        scatters.append(ScatterOverMp(keep, send))

    finished = ()
    done = set()

    def finish_ready(finished):
        for seq, scatter in enumerate(scatters):
            if not scatter.more() and seq not in done:
                done.add(seq)
                finished = finish_call(
                    scatter.keep, scatter.from_core, scatter.from_y, own_t, cot_own, stats, gain_col, gain_bias,
                    finished, seq,
                )
        return finished

    flying = held + mixing
    while True:
        busy = [f[0] for f in flying]
        ready = [m for m in scatters + [down_sum, short, up_sum, mix_sum] if m.more() and m not in busy]
        finished, flights = launch(ready, finished)
        flying = flying + flights
        if not flying:
            break
        finished = finish_ready(finished)
        small = [f for f in flying if f[0] is short or f[0] in scatters and len(f[0].bits) == 2]
        sums = [f for f in flying if f[0] in (mix_sum, up_sum, down_sum)]
        moving = [f for f in flying if f[0] in scatters and len(f[0].bits) == 1]
        first_swap = [f for f in sums if len(f[0].steps) == 2]
        if small:
            now = small
        elif moving and (len(moving) > 1 or not first_swap):
            now = moving[:1]
        else:
            now = first_swap or sums
        finished = land(now, finished)
        flying = [f for f in flying if f not in now]
    finished = finish_ready(finished)
    block_out, token_grad = finished
    block_out, token_grad = block_out.T, token_grad.T
    mixed_grad = mix_sum.keep.astype(F32)
    qkv_grad = jnp.transpose(mixed_grad[: 3 * part].reshape(3, part, width), (2, 0, 1))

    gain_grad = short.norm / norm_gain.astype(F32)
    rest = short.rest
    split = 2 * part + up_weight.shape[1]
    return (
        block_out,
        token_grad,
        gain_grad,
        qkv_grad,
        rest[: 2 * part].reshape(2, part),
        mixed_grad[3 * part :],
        up_sum.keep.astype(F32),
        rest[2 * part : split],
        down_sum.keep.astype(F32),
        rest[split:],
    )


def solution(mesh):
    in_specs = (
        P("dp", "mp"),
        P("dp", None),
        P("mp"),
        P(None, None, "mp"),
        P(None, "mp"),
        P("mp", None),
        P(None, "mp"),
        P("mp"),
        P("mp", None),
        P("mp"),
        P("dp", None),
    )
    out_specs = (
        P("dp", "mp"),
        P("dp", "mp"),
        P("mp"),
        P(None, None, "mp"),
        P(None, "mp"),
        P("mp", None),
        P(None, "mp"),
        P("mp"),
        P("mp", None),
        P("mp"),
    )
    run = functools.partial(body, mesh.shape["dp"])
    return jax.shard_map(run, mesh=mesh, in_specs=in_specs, out_specs=out_specs, check_vma=False)
```

```python
import functools

import jax
import jax.numpy as jnp
from jax import lax
from jax.experimental import pallas as pl
from jax.experimental.pallas import tpu as pltpu
from jax.sharding import PartitionSpec as P

DH = 64
LEN = 1024
EPSILON = 1e-06
IMAGE_SLOTS = 16
PENALTY = 1024.0
BI = 256
BJ = 256
SUM_ROWS = 16
F32 = jnp.float32
BF16 = jnp.bfloat16

NN = (((1,), (0,)), ((), ()))
NT = (((1,), (1,)), ((), ()))
ANY = pl.BlockSpec(memory_space=pl.ANY)


def dot(left, right, dims=NN):
    return lax.dot_general(left, right, dims, preferred_element_type=F32)


def fold_lanes(rows):
    total = rows[:, :128]
    for start in range(128, rows.shape[1], 128):
        total = total + rows[:, start : start + 128]
    return total


def cost(microseconds, nbytes):
    return pl.CostEstimate(flops=int(microseconds * 1e3), bytes_accessed=nbytes // 1000, transcendentals=0)


def early_kernel(cot, down, attn, pick, d_act, d_att, cot_own, bias_sum):
    rows = cot[...]
    d_act[...] = dot(down[...], rows, NT).astype(BF16)
    d_att[...] = dot(attn[...], rows, NT).astype(BF16)
    own = dot(pick[...], rows, NT)
    cot_own[...] = own.astype(BF16)

    @pl.when(pl.program_id(0) == 0)
    def _():
        bias_sum[...] = jnp.zeros_like(bias_sum)

    bias_sum[...] += fold_lanes(own)


def early_call(cot, down, attn, pick, block=512):
    tokens, width = cot.shape
    seqs = tokens // LEN
    hidden, part = down.shape[0], attn.shape[0]
    steps = LEN // block
    fixed = lambda i: (0, 0)
    by_seq = lambda i: (i // steps, 0, i % steps)
    return pl.pallas_call(
        early_kernel,
        grid=(tokens // block,),
        in_specs=[
            pl.BlockSpec((block, width), lambda i: (i, 0)),
            pl.BlockSpec((hidden, width), fixed),
            pl.BlockSpec((part, width), fixed),
            pl.BlockSpec((part, width), fixed),
        ],
        out_specs=[
            pl.BlockSpec((None, hidden, block), by_seq),
            pl.BlockSpec((None, part, block), by_seq),
            pl.BlockSpec((part, block), lambda i: (0, i)),
            pl.BlockSpec((part, 128), fixed),
        ],
        out_shape=[
            jax.ShapeDtypeStruct((seqs, hidden, LEN), BF16),
            jax.ShapeDtypeStruct((seqs, part, LEN), BF16),
            jax.ShapeDtypeStruct((part, tokens), BF16),
            jax.ShapeDtypeStruct((part, 128), F32),
        ],
        cost_estimate=cost(10, 12_000_000),
        name="early",
    )(cot, down, attn, pick)


def mlp_kernel(
    pieces_order, place, own, flip_y, flip_c, flip_cy, gain_own, gain_y, gain_c, gain_cy, up_t, up_bias, d_act, cot, up,
    normed, active, d_pre, stats, bias_sum, gain_all, up_row, grads, low, high
):
    pieces = (own, flip_y, flip_c, flip_cy)
    part = own.shape[0]
    width = part * 4
    first = pl.program_id(0) == 0
    last = pl.program_id(0) == pl.num_programs(0) - 1

    @pl.when(first)
    def _():
        bias_sum[...] = jnp.zeros_like(bias_sum)
        low[...] = jnp.zeros_like(low)
        high[...] = jnp.zeros_like(high)
        for slot, piece in enumerate((gain_own, gain_y, gain_c, gain_cy)):
            gain_all[pl.ds(pl.multiple_of(place[slot], part), part), :] = piece[...].astype(F32)

    total = 0.0
    squares = 0.0
    for piece in pieces:
        rows = piece[...].astype(F32)
        total = total + jnp.sum(rows, axis=0, keepdims=True)
        squares = squares + jnp.sum(rows * rows, axis=0, keepdims=True)
    mean = total * (1.0 / width)
    scale = lax.rsqrt(squares * (1.0 / width) - mean * mean + EPSILON)
    stats[0:1, :] = mean
    stats[1:2, :] = scale
    stats[2:8, :] = jnp.zeros((6, stats.shape[1]), F32)
    for slot, piece in enumerate(pieces):
        rows = piece[...].astype(F32)
        here = pl.ds(pl.multiple_of(place[slot], part), part)
        normed[here, :] = ((rows - mean) * scale * gain_all[here, :1]).astype(BF16)

    c0 = 0.7978845608028654
    c1 = 0.044715 * c0
    def lift(start):
        here = slice(start, start + 256)
        return dot(up_t[here, :], normed[...]) + up_bias[here, :]

    ahead = lift(0)
    for start in range(0, up_t.shape[0], 256):
        here = slice(start, start + 256)
        pre = ahead
        if start + 256 < up_t.shape[0]:
            ahead = lift(start + 256)
        square = pre * pre
        half = 0.5 * jnp.tanh(pre * (c0 + c1 * square)) + 0.5
        act = (pre * half).astype(BF16)
        active[here, :] = act
        slope = half + pre * (half - half * half) * (2.0 * c0 + 6.0 * c1 * square)
        grad = (d_act[here, :].astype(F32) * slope).astype(BF16)
        d_pre[here, :] = grad
        bias_sum[here, :] += fold_lanes(grad.astype(F32))
        low[here, :] += dot(act, cot[...])
        high[:, here] += dot(normed[...], grad, NT)

    @pl.when(last)
    def _():
        up_row[...] = fold_lanes(high[...] * up[...].astype(F32))
        half = low.shape[0]
        size = grads.shape[0] // len(pieces_order)
        for slot, piece in enumerate(pieces_order):
            source, start = (low, piece * size) if piece * size < half else (high, piece * size - half)
            grads[slot * size : (slot + 1) * size, :] = source[start : start + size, :].astype(BF16)


def mlp_call(pieces_order, place, pieces, gains, up_t, up_bias, d_act, cot, up, block=512):
    part, tokens = pieces[0].shape
    width = 4 * part
    seqs, hidden, _ = d_act.shape
    steps = LEN // block
    lanes = lambda i, *_: (0, i)
    by_seq = lambda i, *_: (i // steps, 0, i % steps)
    fixed = lambda i, *_: (0, 0)
    grid_spec = pltpu.PrefetchScalarGridSpec(
        num_scalar_prefetch=1,
        grid=(tokens // block,),
        in_specs=[pl.BlockSpec((part, block), lanes)] * 4
        + [pl.BlockSpec((part, 128), fixed)] * 4
        + [
            pl.BlockSpec((hidden, width), fixed),
            pl.BlockSpec((hidden, 1), fixed),
            pl.BlockSpec((None, hidden, block), by_seq),
            pl.BlockSpec((block, width), lambda i, *_: (i, 0)),
            pl.BlockSpec((width, hidden), fixed),
        ],
        out_specs=[
            pl.BlockSpec((None, width, block), by_seq),
            pl.BlockSpec((None, hidden, block), by_seq),
            pl.BlockSpec((None, hidden, block), by_seq),
            pl.BlockSpec((8, block), lanes),
            pl.BlockSpec((hidden, 128), fixed),
            pl.BlockSpec((width, 128), fixed),
            pl.BlockSpec((width, 128), fixed),
            pl.BlockSpec((hidden + width, width), fixed),
        ],
        scratch_shapes=[pltpu.VMEM((hidden, width), F32), pltpu.VMEM((width, hidden), F32)],
    )
    assert hidden == width
    return pl.pallas_call(
        functools.partial(mlp_kernel, pieces_order),
        grid_spec=grid_spec,
        out_shape=[
            jax.ShapeDtypeStruct((seqs, width, LEN), BF16),
            jax.ShapeDtypeStruct((seqs, hidden, LEN), BF16),
            jax.ShapeDtypeStruct((seqs, hidden, LEN), BF16),
            jax.ShapeDtypeStruct((8, tokens), F32),
            jax.ShapeDtypeStruct((hidden, 128), F32),
            jax.ShapeDtypeStruct((width, 128), F32),
            jax.ShapeDtypeStruct((width, 128), F32),
            jax.ShapeDtypeStruct((hidden + width, width), BF16),
        ],
        cost_estimate=cost(20, 30_000_000),
        name="mlp",
    )(place, *pieces, *gains, up_t, up_bias, d_act, cot, up)


def attention_kernel(last, seq, first, count, normed, mixed_t, d_att, mask_q, mask_k, gains, cot_hbm, *rest):
    if seq:
        before_hbm, rest = rest[0], rest[1:]
    (
        attended, d_mixed, gain_sum, norm_row, grads, qkv, qx, kx, vn, kt, vt, es, ps, oa, dqa, dka, dva, cot, before, cot_sem,
        before_sem,
    ) = rest
    part = attended.shape[0]
    heads = part // DH
    inv_dh = 1.0 / DH
    copies = [pltpu.make_async_copy(cot_hbm.at[pl.ds(seq * LEN, LEN), :], cot, cot_sem)]
    if seq:
        copies.append(pltpu.make_async_copy(before_hbm, before, before_sem))
    for copy in copies:
        copy.start()

    qkv[...] = dot(mixed_t[...], normed[...])

    def unit(start):
        raw = qkv[start : start + DH, :]
        shifted = raw - jnp.sum(raw, axis=0, keepdims=True) * inv_dh
        scale = lax.rsqrt(jnp.sum(shifted * shifted, axis=0, keepdims=True) * inv_dh + EPSILON)
        return shifted * scale, scale

    zeros = jnp.zeros((128 - DH - IMAGE_SLOTS, LEN), BF16)
    for head in range(heads):
        rows = slice(head * DH, (head + 1) * DH)
        query, _ = unit(head * DH)
        query = (query * (gains[rows, :] * 0.125)).astype(BF16)
        qx[head] = jnp.concatenate([query, mask_q[...], zeros], axis=0)
        key, _ = unit(part + head * DH)
        key = (key * gains[part + head * DH : part + (head + 1) * DH, :]).astype(BF16)
        kt[rows, :] = key
        kx[head] = jnp.concatenate([key, mask_k[...], zeros], axis=0).T
        value = qkv[2 * part + head * DH : 2 * part + (head + 1) * DH, :].astype(BF16)
        vt[rows, :] = value
        vn[head] = value.T
    dka[...] = jnp.zeros_like(dka)
    dva[...] = jnp.zeros_like(dva)

    def query_block(ib, _):
        i0 = pl.multiple_of(ib * BI, BI)
        icols = pl.ds(i0, BI)
        base = first[ib]
        trips = count[ib]

        def scores(j, carry):
            j0 = pl.multiple_of((base + j) * BJ, BJ)
            slot = pl.multiple_of(j * BJ, BJ)
            out = []
            for head in range(heads):
                rows = slice(head * DH, (head + 1) * DH)
                e = jnp.exp(dot(kx[head, pl.ds(j0, BJ), :], qx[head, :, icols]))
                p = dot(vn[head, pl.ds(j0, BJ), :], d_att[rows, icols])
                es[head, pl.ds(slot, BJ), :] = e
                ps[head, pl.ds(slot, BJ), :] = p
                out.append(carry[2 * head] + jnp.sum(e.reshape(BJ // 8, 8, BI), axis=0))
                out.append(carry[2 * head + 1] + jnp.sum((e * p).reshape(BJ // 8, 8, BI), axis=0))
            return tuple(out)

        sums = lax.fori_loop(0, trips, scores, tuple(jnp.zeros((8, BI), F32) for _ in range(2 * heads)))
        inverse = []
        inner = []
        for head in range(heads):
            inv = 1.0 / jnp.sum(sums[2 * head], axis=0, keepdims=True)
            inverse.append(inv)
            inner.append(jnp.sum(sums[2 * head + 1], axis=0, keepdims=True) * inv)
        oa[...] = jnp.zeros_like(oa)
        dqa[:, icols] = jnp.zeros((part, BI), F32)

        def row_grads(j, _):
            j0 = pl.multiple_of((base + j) * BJ, BJ)
            slot = pl.multiple_of(j * BJ, BJ)
            jcols = pl.ds(j0, BJ)
            for head in range(heads):
                rows = slice(head * DH, (head + 1) * DH)
                w = es[head, pl.ds(slot, BJ), :] * inverse[head]
                d = (w * (ps[head, pl.ds(slot, BJ), :] - inner[head])).astype(BF16)
                w = w.astype(BF16)
                oa[rows, :] += dot(vt[rows, jcols], w)
                dqa[rows, icols] += dot(kt[rows, jcols], d)
                dva[rows, jcols] += dot(d_att[rows, icols], w, NT)
                dka[rows, jcols] += dot(qx[head, :DH, icols], d, NT)
            return 0

        lax.fori_loop(0, trips, row_grads, 0)
        attended[:, icols] = oa[...].astype(BF16)
        return 0

    lax.fori_loop(0, LEN // BI, query_block, 0)

    for source, offset, factor in ((dqa, 0, 0.125), (dka, part, 1.0)):
        for head in range(heads):
            start = offset + head * DH
            u, scale = unit(start)
            e = source[head * DH : (head + 1) * DH, :] * factor
            gain_sum[start : start + DH, :] = fold_lanes(e * u)
            f = e * gains[start : start + DH, :]
            mean_f = jnp.sum(f, axis=0, keepdims=True) * inv_dh
            mean_fu = jnp.sum(f * u, axis=0, keepdims=True) * inv_dh
            d_mixed[start : start + DH, :] = ((f - mean_f - u * mean_fu) * scale).astype(BF16)
    d_mixed[2 * part :, :] = dva[...].astype(BF16)

    for copy in copies:
        copy.wait()
    split = 3 * part
    for rows, value in (
        (slice(0, split), dot(d_mixed[...], normed[...], NT)),
        (slice(split, split + part), dot(attended[...], cot[...])),
    ):
        if seq:
            value = value + before[rows, :]
        if last and rows.start == 0:
            norm_row[...] = jnp.sum(value * mixed_t[...].astype(F32), axis=0, keepdims=True)
        grads[rows, :] = value.astype(grads.dtype)
    if not last:
        norm_row[...] = jnp.zeros_like(norm_row)


def attention_call(first, count, normed, mixed_t, d_att, mask_q, mask_k, gains, cot, before, seq, last):
    seqs, part, _ = d_att.shape
    width = normed.shape[1]
    heads = part // DH
    once = lambda i, *_: (0, 0)
    ours = lambda i, *_: (seq, 0, 0)
    grid_spec = pltpu.PrefetchScalarGridSpec(
        num_scalar_prefetch=2,
        grid=(1,),
        in_specs=[
            pl.BlockSpec((None, width, LEN), ours),
            pl.BlockSpec((3 * part, width), once),
            pl.BlockSpec((None, part, LEN), ours),
            pl.BlockSpec((None, IMAGE_SLOTS, LEN), ours),
            pl.BlockSpec((None, IMAGE_SLOTS, LEN), ours),
            pl.BlockSpec((2 * part, 1), once),
            ANY,
        ]
        + [ANY] * len(before),
        out_specs=[
            pl.BlockSpec((part, LEN), once),
            pl.BlockSpec((3 * part, LEN), once),
            pl.BlockSpec((2 * part, 128), once),
            pl.BlockSpec((1, width), once),
            pl.BlockSpec((4 * part, width), once),
        ],
        scratch_shapes=[
            pltpu.VMEM((3 * part, LEN), F32),
            pltpu.VMEM((heads, 128, LEN), BF16),
            pltpu.VMEM((heads, LEN, 128), BF16),
            pltpu.VMEM((heads, LEN, DH), BF16),
            pltpu.VMEM((part, LEN), BF16),
            pltpu.VMEM((part, LEN), BF16),
            pltpu.VMEM((heads, LEN, BI), F32),
            pltpu.VMEM((heads, LEN, BI), F32),
            pltpu.VMEM((part, BI), F32),
            pltpu.VMEM((part, LEN), F32),
            pltpu.VMEM((part, LEN), F32),
            pltpu.VMEM((part, LEN), F32),
            pltpu.VMEM((LEN, width), BF16),
            pltpu.VMEM((4 * part, width), F32),
            pltpu.SemaphoreType.DMA(()),
            pltpu.SemaphoreType.DMA(()),
        ],
    )
    return pl.pallas_call(
        functools.partial(attention_kernel, last, seq),
        grid_spec=grid_spec,
        out_shape=[
            jax.ShapeDtypeStruct((part, LEN), BF16),
            jax.ShapeDtypeStruct((3 * part, LEN), BF16),
            jax.ShapeDtypeStruct((2 * part, 128), F32),
            jax.ShapeDtypeStruct((1, width), F32),
            jax.ShapeDtypeStruct((4 * part, width), BF16 if last else F32),
        ],
        cost_estimate=cost(18, 5_000_000),
        name="attention",
    )(first, count, normed, mixed_t, d_att, mask_q, mask_k, gains, cot, *before)


def project_kernel(
    shard, active, attended, d_pre, d_mixed, normed, down_t, attn_t, up, mixed, gain, keep, send
):
    me = shard[0]
    part = attended.shape[0]
    out = dot(down_t[...], active[...]) + dot(attn_t[...], attended[...])
    grad = dot(up[...], d_pre[...]) + dot(mixed[...], d_mixed[...])
    product = grad * normed[...].astype(F32)
    sums = []
    for row in (jnp.sum(grad * gain[:, :1], axis=0, keepdims=True), jnp.sum(product, axis=0, keepdims=True)):
        high = row.astype(BF16)
        sums += [high, (row - high.astype(F32)).astype(BF16)]
    sums = jnp.concatenate(sums + [jnp.zeros((SUM_ROWS - 4, sums[0].shape[1]), BF16)], axis=0)
    for target in (keep, send):
        for slot in range(2):
            target[slot, 2 * part :, :] = sums
    for index in range(4):
        rows = slice(index * part, (index + 1) * part)
        away = jnp.bitwise_xor(me, index)
        slot = away // 2

        @pl.when(away % 2 == 0)
        def _():
            keep[slot, :part, :] = out[rows].astype(BF16)
            keep[slot, part : 2 * part, :] = grad[rows].astype(BF16)

        @pl.when(away % 2 == 1)
        def _():
            send[slot, :part, :] = out[rows].astype(BF16)
            send[slot, part : 2 * part, :] = grad[rows].astype(BF16)


def project_call(shard, active, attended, d_pre, d_mixed, normed, down_t, attn_t, up, mixed, gain, seq, block=256):
    width, hidden = down_t.shape
    part = attended.shape[0]
    steps = LEN // block
    lanes = lambda i, *_: (0, i)
    ours = lambda i, *_: (seq, 0, i)
    fixed = lambda i, *_: (0, 0)
    rows = 2 * part + SUM_ROWS
    grid_spec = pltpu.PrefetchScalarGridSpec(
        num_scalar_prefetch=1,
        grid=(steps,),
        in_specs=[
            pl.BlockSpec((None, hidden, block), ours),
            pl.BlockSpec((part, block), lanes),
            pl.BlockSpec((None, hidden, block), ours),
            pl.BlockSpec((3 * part, block), lanes),
            pl.BlockSpec((None, width, block), ours),
            pl.BlockSpec((width, hidden), fixed),
            pl.BlockSpec((width, part), fixed),
            pl.BlockSpec((width, hidden), fixed),
            pl.BlockSpec((width, 3 * part), fixed),
            pl.BlockSpec((width, 128), fixed),
        ],
        out_specs=[
            pl.BlockSpec((2, rows, block), lambda i, *_: (0, 0, i)),
            pl.BlockSpec((2, rows, block), lambda i, *_: (0, 0, i)),
        ],
    )
    return pl.pallas_call(
        project_kernel,
        grid_spec=grid_spec,
        out_shape=[
            jax.ShapeDtypeStruct((2, rows, LEN), BF16),
            jax.ShapeDtypeStruct((2, rows, LEN), BF16),
        ],
        cost_estimate=cost(8, 16_000_000),
        name="project",
    )(shard, active, attended, d_pre, d_mixed, normed, down_t, attn_t, up, mixed, gain)


def finish_kernel(keep, from_core, from_y, own_t, cot, stats, gain, bias, *rest):
    block_out, token_grad = rest[-2:]
    part = own_t.shape[0]
    inv_width = 0.25 / part
    total = keep[...].astype(F32) + from_core[...].astype(F32) + from_y[...].astype(F32)
    own = own_t[...].astype(F32)
    block_out[...] = (own + total[:part] + bias[...]).astype(BF16)
    grad = total[part : 2 * part]
    sums = total[2 * part :]
    mean = stats[0:1, :]
    scale = stats[1:2, :]
    hat = (own - mean) * scale
    inner = grad * gain[...] - (sums[0:1] + sums[1:2]) * inv_width - hat * ((sums[2:3] + sums[3:4]) * inv_width)
    token_grad[...] = cot[...].astype(F32) + inner * scale


def finish_call(keep, from_core, from_y, own_t, cot, stats, gain, bias, before, seq, block=512):
    part, tokens = own_t.shape
    steps = LEN // block
    fixed = lambda i: (0, 0)
    packed = pl.BlockSpec((None, 2 * part + SUM_ROWS, block), lambda i: (0, 0, i))
    ours = lambda i: (0, seq * steps + i)
    here = pl.BlockSpec((part, block), ours)
    return pl.pallas_call(
        finish_kernel,
        grid=(steps,),
        in_specs=[
            packed, packed, packed,
            here, here,
            pl.BlockSpec((8, block), ours),
            pl.BlockSpec((part, 1), fixed),
            pl.BlockSpec((part, 1), fixed),
        ]
        + [ANY] * len(before),
        out_specs=[here, here],
        out_shape=[
            jax.ShapeDtypeStruct((part, tokens), BF16),
            jax.ShapeDtypeStruct((part, tokens), F32),
        ],
        input_output_aliases={8 + i: i for i in range(len(before))},
        cost_estimate=cost(3, 5_000_000),
        name="finish",
    )(keep, from_core, from_y, own_t, cot, stats, gain, bias, *before)


def flip(value, axis, size, bit):
    return lax.ppermute(value, axis, [(i, i ^ bit) for i in range(size)])


def tie(*trees):
    return lax.optimization_barrier(trees)


def piece_order(size):
    bits = size.bit_length() - 1
    return [sum(((i >> b) & 1) << (bits - 1 - b) for b in range(bits)) for i in range(size)]


class SumOverDp:
    def __init__(self, value, size, index):
        self.size, self.index = size, index
        self.send = value
        self.steps = ["sum"] + [1 << i for i in reversed(range(size.bit_length() - 1))]

    def more(self):
        return bool(self.steps)

    def move(self, send):
        if self.steps[0] == "sum":
            return lax.all_to_all(send, "dp", 0, 0, tiled=True)
        return flip(send, "dp", self.size, self.steps[0])

    def take(self, arrived):
        step = self.steps.pop(0)
        if step == "sum":
            shares = arrived.reshape(self.size, -1, arrived.shape[1]).astype(F32)
            self.keep = jnp.sum(shares, axis=0).astype(BF16)
        else:
            self.keep = jnp.where(
                (self.index & step) > 0,
                jnp.concatenate([arrived, self.keep], axis=0),
                jnp.concatenate([self.keep, arrived], axis=0),
            )
        self.send = self.keep


class SwapOverDp:
    def __init__(self, value, size):
        self.size = size
        self.send = value
        self.steps = ["sum", "join"]

    def more(self):
        return bool(self.steps)

    def move(self, send):
        return lax.all_to_all(send, "dp", 0, 0, tiled=True)

    def take(self, arrived):
        if self.steps.pop(0) == "sum":
            shares = arrived.reshape(self.size, -1, arrived.shape[1]).astype(F32)
            total = jnp.sum(shares, axis=0).astype(BF16)
            self.send = jnp.broadcast_to(total[None], (self.size,) + total.shape).reshape(arrived.shape)
        else:
            self.keep = arrived


class ScatterOverMp:
    def __init__(self, keep, send):
        self.keep, self.send = keep, send
        self.bits = [1, 2]

    def more(self):
        return bool(self.bits)

    def move(self, send):
        return flip(send, "mp", 4, self.bits[0])

    def take(self, arrived):
        bit = self.bits.pop(0)
        if bit == 1:
            self.from_core = arrived
            self.send = (self.keep[1].astype(F32) + arrived[1].astype(F32)).astype(BF16)[None]
        else:
            self.from_y = arrived


class ShortSums:
    def __init__(self, keep, send, rest, size):
        self.keep, self.send, self.rest, self.size = keep, send, rest, size
        self.steps = [("mp", 1), ("mp", 2)] + [("dp", 1 << i) for i in range(size.bit_length() - 1)]

    def more(self):
        return bool(self.steps)

    def move(self, send):
        axis, bit = self.steps[0]
        return flip(send, axis, 4 if axis == "mp" else self.size, bit)

    def take(self, arrived):
        axis, bit = self.steps.pop(0)
        if (axis, bit) == ("mp", 1):
            both = self.keep + arrived
            self.norm, self.send = both[0], both[1]
            return
        if axis == "mp":
            self.send = jnp.concatenate([self.norm + arrived, self.rest])
        else:
            self.send = self.send + arrived
        size = self.norm.shape[0]
        self.norm, self.rest = self.send[:size], self.send[size:]


def launch(movers, inputs):
    movers = [m for m in movers if m.more()]
    inputs, sends = tie(inputs, [m.send for m in movers])
    return inputs, [(m, m.move(s)) for m, s in zip(movers, sends)]


def land(flights, outputs):
    outputs, arrivals = tie(outputs, [f[1] for f in flights])
    for (mover, _), arrived in zip(flights, arrivals):
        mover.take(arrived)
    return outputs


def body(
    dp_size,
    tokens,
    image_ids,
    norm_gain,
    qkv_weight,
    qk_gain,
    attn_weight,
    up_weight,
    up_bias,
    down_weight,
    down_bias,
    cotangent,
):
    part = tokens.shape[1]
    width = cotangent.shape[1]
    seqs = image_ids.shape[0]
    me = lax.axis_index("mp")
    dp = lax.axis_index("dp")
    shard = me.astype(jnp.int32)[None]
    place = jnp.bitwise_xor(shard, jnp.array([0, 2, 1, 3], jnp.int32)) * part

    own_t = tokens.T
    from_y = flip(own_t, "mp", 4, 2)
    gain_own = jnp.broadcast_to(norm_gain[:, None], (part, 128))
    gain_y = flip(gain_own, "mp", 4, 2)
    gains = (gain_own, gain_y, flip(gain_own, "mp", 4, 1), flip(gain_y, "mp", 4, 1))

    mixed_t = jnp.transpose(qkv_weight, (1, 2, 0)).reshape(3 * part, width)
    mixed = mixed_t.T
    up_t = up_weight.T
    down_t = down_weight.T
    attn_t = attn_weight.T
    up_bias_col = up_bias.astype(F32)[:, None]
    head_gains = qk_gain.astype(F32).reshape(2 * part, 1)

    slots = jnp.arange(IMAGE_SLOTS, dtype=jnp.int32)[None, :, None]
    same = image_ids[:, None, :] == slots
    mask_q = same.astype(BF16)
    mask_k = jnp.where(same | (slots >= 8), 0.0, -PENALTY).astype(BF16)
    block_first = image_ids[:, ::BI]
    block_last = image_ids[:, BI - 1 :: BI]
    starts = jnp.sum(image_ids[:, None, :] < block_first[:, :, None], axis=2, dtype=jnp.int32)
    ends = jnp.sum(image_ids[:, None, :] <= block_last[:, :, None], axis=2, dtype=jnp.int32)
    first = starts // BJ
    count = (ends + BJ - 1) // BJ - first

    pick = (jnp.arange(part)[:, None] + me * part == jnp.arange(width)[None, :]).astype(BF16)
    d_act, d_att, cot_own, cot_sum = early_call(cotangent, down_weight, attn_weight, pick)
    gain_bias = down_bias.astype(F32)[:, None]
    gain_col = norm_gain.astype(F32)[:, None]
    prepared = (
        d_act, d_att, mixed_t, mixed, up_t, down_t, attn_t, up_bias_col, head_gains, mask_q, mask_k, first, count,
        gain_bias, gain_col,
    )
    prepared, from_y = tie(prepared, from_y)
    (
        d_act, d_att, mixed_t, mixed, up_t, down_t, attn_t, up_bias_col, head_gains, mask_q, mask_k, first, count,
        gain_bias, gain_col,
    ) = prepared
    pieces = (own_t, from_y, flip(own_t, "mp", 4, 1), flip(from_y, "mp", 4, 1))
    normed, active, d_pre, stats, upbias_part, gain_all, up_row, mlp_part = mlp_call(
        tuple(piece_order(dp_size)), place, pieces, gains, up_t, up_bias_col, d_act, cotangent, up_weight
    )
    mlp_sum = SumOverDp(mlp_part, dp_size, dp)

    heads_out = []
    before = ()
    qk_part = 0.0
    (states,), flights = launch([mlp_sum], (normed,))
    for seq in range(seqs):
        *out, qk, norm_row, total = attention_call(
            first[seq], count[seq], states, mixed_t, d_att, mask_q, mask_k, head_gains, cotangent, before, seq,
            seq == seqs - 1,
        )
        heads_out.append(out)
        before = (total,)
        qk_part = qk_part + qk
    heads_out, before, qk_part, norm_row = land(flights, (heads_out, before, qk_part, norm_row))
    mix_sum = SwapOverDp(before[0], dp_size)

    norm_vec = norm_row[0] + jnp.sum(up_row, axis=1)
    norm_parts = norm_vec.reshape(4, part)
    norm_parts = [lax.dynamic_index_in_dim(norm_parts, jnp.bitwise_xor(me, m), 0, False) for m in range(4)]
    short = ShortSums(
        jnp.stack([norm_parts[0], norm_parts[2]]),
        jnp.stack([norm_parts[1], norm_parts[3]]),
        jnp.concatenate([jnp.sum(qk_part, axis=1), jnp.sum(upbias_part, axis=1), jnp.sum(cot_sum, axis=1)]),
        dp_size,
    )

    def project(seq, work):
        attended, d_mixed = work
        return project_call(
            shard, active, attended, d_pre, d_mixed, normed, down_t, attn_t, up_weight, mixed, gain_all, seq
        )

    scatters = []
    mixing = []
    for seq in range(seqs):
        along = [mlp_sum, short] + [m for m in scatters if m.more()]
        if seq == 0:
            along.append(mix_sum)
        work, flights = launch(along, heads_out[seq])
        keep, send = project(seq, work)
        later = [f for f in flights if f[0] is mix_sum or f[0] is mlp_sum and seq == 2]
        now = [f for f in flights if f not in later]
        if seq == 2:
            now += mixing
            mixing = []
        mixing += later
        keep, send = land(now, (keep, send))
        scatters.append(ScatterOverMp(keep, send))

    finished = ()
    done = set()

    def finish_ready(finished):
        for seq, scatter in enumerate(scatters):
            if not scatter.more() and seq not in done:
                done.add(seq)
                finished = finish_call(
                    scatter.keep, scatter.from_core, scatter.from_y, own_t, cot_own, stats, gain_col, gain_bias,
                    finished, seq,
                )
        return finished

    flying = mixing
    while True:
        busy = [f[0] for f in flying]
        ready = [m for m in scatters + [short, mlp_sum, mix_sum] if m.more() and m not in busy]
        finished, flights = launch(ready, finished)
        flying = flying + flights
        if not flying:
            break
        finished = finish_ready(finished)
        small = [f for f in flying if f[0] is short or f[0] in scatters and len(f[0].bits) == 2]
        sums = [f for f in flying if f[0] in (mix_sum, mlp_sum)]
        moving = [f for f in flying if f[0] in scatters and len(f[0].bits) == 1]
        first_swap = [f for f in sums if f[0] is mlp_sum or len(f[0].steps) == 2]
        if small:
            now = small
        elif moving and (len(moving) > 1 or not first_swap):
            now = moving[:1]
        else:
            now = first_swap or sums
        finished = land(now, finished)
        flying = [f for f in flying if f not in now]
    finished = finish_ready(finished)
    block_out, token_grad = finished
    block_out, token_grad = block_out.T, token_grad.T
    mixed_grad = mix_sum.keep.astype(F32)
    qkv_grad = jnp.transpose(mixed_grad[: 3 * part].reshape(3, part, width), (2, 0, 1))

    gain_grad = short.norm / norm_gain.astype(F32)
    rest = short.rest
    split = 2 * part + up_weight.shape[1]
    return (
        block_out,
        token_grad,
        gain_grad,
        qkv_grad,
        rest[: 2 * part].reshape(2, part),
        mixed_grad[3 * part :],
        mlp_sum.keep[up_weight.shape[1] :].astype(F32),
        rest[2 * part : split],
        mlp_sum.keep[: up_weight.shape[1]].astype(F32),
        rest[split:],
    )


def solution(mesh):
    in_specs = (
        P("dp", "mp"),
        P("dp", None),
        P("mp"),
        P(None, None, "mp"),
        P(None, "mp"),
        P("mp", None),
        P(None, "mp"),
        P("mp"),
        P("mp", None),
        P("mp"),
        P("dp", None),
    )
    out_specs = (
        P("dp", "mp"),
        P("dp", "mp"),
        P("mp"),
        P(None, None, "mp"),
        P(None, "mp"),
        P("mp", None),
        P(None, "mp"),
        P("mp"),
        P("mp", None),
        P("mp"),
    )
    run = functools.partial(body, mesh.shape["dp"])
    return jax.shard_map(run, mesh=mesh, in_specs=in_specs, out_specs=out_specs, check_vma=False)
```

```python
import functools

import jax
import jax.numpy as jnp
from jax import lax
from jax.experimental import pallas as pl
from jax.experimental.pallas import tpu as pltpu
from jax.sharding import PartitionSpec as P

DH = 64
LEN = 1024
EPSILON = 1e-06
IMAGE_SLOTS = 16
PENALTY = 1024.0
BI = 256
BJ = 256
SUM_ROWS = 16
F32 = jnp.float32
BF16 = jnp.bfloat16

NN = (((1,), (0,)), ((), ()))
NT = (((1,), (1,)), ((), ()))
ANY = pl.BlockSpec(memory_space=pl.ANY)


def dot(left, right, dims=NN):
    return lax.dot_general(left, right, dims, preferred_element_type=F32)


def fold_lanes(rows):
    total = rows[:, :128]
    for start in range(128, rows.shape[1], 128):
        total = total + rows[:, start : start + 128]
    return total


def cost(microseconds, nbytes):
    return pl.CostEstimate(flops=int(microseconds * 1e3), bytes_accessed=nbytes // 1000, transcendentals=0)


def early_kernel(cot, down, attn, pick, d_act, d_att, cot_own, bias_sum):
    rows = cot[...]
    d_act[...] = dot(down[...], rows, NT).astype(BF16)
    d_att[...] = dot(attn[...], rows, NT).astype(BF16)
    own = dot(pick[...], rows, NT)
    cot_own[...] = own.astype(BF16)

    @pl.when(pl.program_id(0) == 0)
    def _():
        bias_sum[...] = jnp.zeros_like(bias_sum)

    bias_sum[...] += fold_lanes(own)


def early_call(cot, down, attn, pick, block=512):
    tokens, width = cot.shape
    seqs = tokens // LEN
    hidden, part = down.shape[0], attn.shape[0]
    steps = LEN // block
    fixed = lambda i: (0, 0)
    by_seq = lambda i: (i // steps, 0, i % steps)
    return pl.pallas_call(
        early_kernel,
        grid=(tokens // block,),
        in_specs=[
            pl.BlockSpec((block, width), lambda i: (i, 0)),
            pl.BlockSpec((hidden, width), fixed),
            pl.BlockSpec((part, width), fixed),
            pl.BlockSpec((part, width), fixed),
        ],
        out_specs=[
            pl.BlockSpec((None, hidden, block), by_seq),
            pl.BlockSpec((None, part, block), by_seq),
            pl.BlockSpec((part, block), lambda i: (0, i)),
            pl.BlockSpec((part, 128), fixed),
        ],
        out_shape=[
            jax.ShapeDtypeStruct((seqs, hidden, LEN), BF16),
            jax.ShapeDtypeStruct((seqs, part, LEN), BF16),
            jax.ShapeDtypeStruct((part, tokens), BF16),
            jax.ShapeDtypeStruct((part, 128), F32),
        ],
        cost_estimate=cost(10, 12_000_000),
        name="early",
    )(cot, down, attn, pick)


def mlp_kernel(
    pieces_order, place, own, flip_y, flip_c, flip_cy, gain_own, gain_y, gain_c, gain_cy, up_t, up_bias, d_act, cot, up,
    normed, active, d_pre, stats, bias_sum, gain_all, up_row, grads, low, high
):
    pieces = (own, flip_y, flip_c, flip_cy)
    part = own.shape[0]
    width = part * 4
    first = pl.program_id(0) == 0
    last = pl.program_id(0) == pl.num_programs(0) - 1

    @pl.when(first)
    def _():
        bias_sum[...] = jnp.zeros_like(bias_sum)
        low[...] = jnp.zeros_like(low)
        high[...] = jnp.zeros_like(high)
        for slot, piece in enumerate((gain_own, gain_y, gain_c, gain_cy)):
            gain_all[pl.ds(pl.multiple_of(place[slot], part), part), :] = piece[...].astype(F32)

    total = 0.0
    squares = 0.0
    for piece in pieces:
        rows = piece[...].astype(F32)
        total = total + jnp.sum(rows, axis=0, keepdims=True)
        squares = squares + jnp.sum(rows * rows, axis=0, keepdims=True)
    mean = total * (1.0 / width)
    scale = lax.rsqrt(squares * (1.0 / width) - mean * mean + EPSILON)
    stats[0:1, :] = mean
    stats[1:2, :] = scale
    stats[2:8, :] = jnp.zeros((6, stats.shape[1]), F32)
    for slot, piece in enumerate(pieces):
        rows = piece[...].astype(F32)
        here = pl.ds(pl.multiple_of(place[slot], part), part)
        normed[here, :] = ((rows - mean) * scale * gain_all[here, :1]).astype(BF16)

    c0 = 0.7978845608028654
    c1 = 0.044715 * c0
    def lift(start):
        here = slice(start, start + 256)
        return dot(up_t[here, :], normed[...]) + up_bias[here, :1].astype(F32)

    ahead = lift(0)
    for start in range(0, up_t.shape[0], 256):
        here = slice(start, start + 256)
        pre = ahead
        if start + 256 < up_t.shape[0]:
            ahead = lift(start + 256)
        square = pre * pre
        half = 0.5 * jnp.tanh(pre * (c0 + c1 * square)) + 0.5
        act = (pre * half).astype(BF16)
        active[here, :] = act
        slope = half + pre * (half - half * half) * (2.0 * c0 + 6.0 * c1 * square)
        grad = (d_act[here, :].astype(F32) * slope).astype(BF16)
        d_pre[here, :] = grad
        bias_sum[here, :] += fold_lanes(grad.astype(F32))
        low[here, :] += dot(act, cot[...])
        high[:, here] += dot(normed[...], grad, NT)

    @pl.when(last)
    def _():
        up_row[...] = fold_lanes(high[...] * up[...].astype(F32))
        half = low.shape[0]
        size = grads.shape[0] // len(pieces_order)
        for slot, piece in enumerate(pieces_order):
            source, start = (low, piece * size) if piece * size < half else (high, piece * size - half)
            grads[slot * size : (slot + 1) * size, :] = source[start : start + size, :].astype(BF16)


def mlp_call(pieces_order, place, pieces, gains, up_t, up_bias, d_act, cot, up, block=512):
    part, tokens = pieces[0].shape
    width = 4 * part
    seqs, hidden, _ = d_act.shape
    steps = LEN // block
    lanes = lambda i, *_: (0, i)
    by_seq = lambda i, *_: (i // steps, 0, i % steps)
    fixed = lambda i, *_: (0, 0)
    grid_spec = pltpu.PrefetchScalarGridSpec(
        num_scalar_prefetch=1,
        grid=(tokens // block,),
        in_specs=[pl.BlockSpec((part, block), lanes)] * 4
        + [pl.BlockSpec((part, 128), fixed)] * 4
        + [
            pl.BlockSpec((hidden, width), fixed),
            pl.BlockSpec((hidden, 128), fixed),
            pl.BlockSpec((None, hidden, block), by_seq),
            pl.BlockSpec((block, width), lambda i, *_: (i, 0)),
            pl.BlockSpec((width, hidden), fixed),
        ],
        out_specs=[
            pl.BlockSpec((None, width, block), by_seq),
            pl.BlockSpec((None, hidden, block), by_seq),
            pl.BlockSpec((None, hidden, block), by_seq),
            pl.BlockSpec((8, block), lanes),
            pl.BlockSpec((hidden, 128), fixed),
            pl.BlockSpec((width, 128), fixed),
            pl.BlockSpec((width, 128), fixed),
            pl.BlockSpec((hidden + width, width), fixed),
        ],
        scratch_shapes=[pltpu.VMEM((hidden, width), F32), pltpu.VMEM((width, hidden), F32)],
    )
    assert hidden == width
    return pl.pallas_call(
        functools.partial(mlp_kernel, pieces_order),
        grid_spec=grid_spec,
        out_shape=[
            jax.ShapeDtypeStruct((seqs, width, LEN), BF16),
            jax.ShapeDtypeStruct((seqs, hidden, LEN), BF16),
            jax.ShapeDtypeStruct((seqs, hidden, LEN), BF16),
            jax.ShapeDtypeStruct((8, tokens), F32),
            jax.ShapeDtypeStruct((hidden, 128), F32),
            jax.ShapeDtypeStruct((width, 128), F32),
            jax.ShapeDtypeStruct((width, 128), F32),
            jax.ShapeDtypeStruct((hidden + width, width), BF16),
        ],
        cost_estimate=cost(20, 30_000_000),
        name="mlp",
    )(place, *pieces, *gains, up_t, up_bias, d_act, cot, up)


def attention_kernel(
    first, count, normed, mixed_t, d_att, mask_q, mask_k, gains, cot, attended, d_mixed, gain_sum, norm_row, grads,
    total, qkv, qx, kx, vn, kt, vt, es, ps, oa, dqa, dka, dva
):
    seq = pl.program_id(0)
    last = seq == pl.num_programs(0) - 1
    part = attended.shape[0]
    heads = part // DH
    inv_dh = 1.0 / DH

    @pl.when(seq == 0)
    def _():
        total[...] = jnp.zeros_like(total)
        gain_sum[...] = jnp.zeros_like(gain_sum)

    qkv[...] = dot(mixed_t[...], normed[...])

    def unit(start):
        raw = qkv[start : start + DH, :]
        shifted = raw - jnp.sum(raw, axis=0, keepdims=True) * inv_dh
        scale = lax.rsqrt(jnp.sum(shifted * shifted, axis=0, keepdims=True) * inv_dh + EPSILON)
        return shifted * scale, scale

    zeros = jnp.zeros((128 - DH - IMAGE_SLOTS, LEN), BF16)
    for head in range(heads):
        rows = slice(head * DH, (head + 1) * DH)
        query, _ = unit(head * DH)
        query = (query * (gains[rows, :1] * 0.125)).astype(BF16)
        qx[head] = jnp.concatenate([query, mask_q[...], zeros], axis=0)
        key, _ = unit(part + head * DH)
        key = (key * gains[part + head * DH : part + (head + 1) * DH, :1]).astype(BF16)
        kt[rows, :] = key
        kx[head] = jnp.concatenate([key, mask_k[...], zeros], axis=0).T
        value = qkv[2 * part + head * DH : 2 * part + (head + 1) * DH, :].astype(BF16)
        vt[rows, :] = value
        vn[head] = value.T
    dka[...] = jnp.zeros_like(dka)
    dva[...] = jnp.zeros_like(dva)

    def query_block(ib, _):
        i0 = pl.multiple_of(ib * BI, BI)
        icols = pl.ds(i0, BI)
        base = first[seq * (LEN // BI) + ib]
        trips = count[seq * (LEN // BI) + ib]

        def scores(j, carry):
            j0 = pl.multiple_of((base + j) * BJ, BJ)
            slot = pl.multiple_of(j * BJ, BJ)
            out = []
            for head in range(heads):
                rows = slice(head * DH, (head + 1) * DH)
                e = jnp.exp(dot(kx[head, pl.ds(j0, BJ), :], qx[head, :, icols]))
                p = dot(vn[head, pl.ds(j0, BJ), :], d_att[rows, icols])
                es[head, pl.ds(slot, BJ), :] = e
                ps[head, pl.ds(slot, BJ), :] = p
                out.append(carry[2 * head] + jnp.sum(e.reshape(BJ // 8, 8, BI), axis=0))
                out.append(carry[2 * head + 1] + jnp.sum((e * p).reshape(BJ // 8, 8, BI), axis=0))
            return tuple(out)

        sums = lax.fori_loop(0, trips, scores, tuple(jnp.zeros((8, BI), F32) for _ in range(2 * heads)))
        inverse = []
        inner = []
        for head in range(heads):
            inv = 1.0 / jnp.sum(sums[2 * head], axis=0, keepdims=True)
            inverse.append(inv)
            inner.append(jnp.sum(sums[2 * head + 1], axis=0, keepdims=True) * inv)
        oa[...] = jnp.zeros_like(oa)
        dqa[:, icols] = jnp.zeros((part, BI), F32)

        def row_grads(j, _):
            j0 = pl.multiple_of((base + j) * BJ, BJ)
            slot = pl.multiple_of(j * BJ, BJ)
            jcols = pl.ds(j0, BJ)
            for head in range(heads):
                rows = slice(head * DH, (head + 1) * DH)
                w = es[head, pl.ds(slot, BJ), :] * inverse[head]
                d = (w * (ps[head, pl.ds(slot, BJ), :] - inner[head])).astype(BF16)
                w = w.astype(BF16)
                oa[rows, :] += dot(vt[rows, jcols], w)
                dqa[rows, icols] += dot(kt[rows, jcols], d)
                dva[rows, jcols] += dot(d_att[rows, icols], w, NT)
                dka[rows, jcols] += dot(qx[head, :DH, icols], d, NT)
            return 0

        lax.fori_loop(0, trips, row_grads, 0)
        attended[:, icols] = oa[...].astype(BF16)
        return 0

    lax.fori_loop(0, LEN // BI, query_block, 0)

    for source, offset, factor in ((dqa, 0, 0.125), (dka, part, 1.0)):
        for head in range(heads):
            start = offset + head * DH
            u, scale = unit(start)
            e = source[head * DH : (head + 1) * DH, :] * factor
            gain_sum[start : start + DH, :] += fold_lanes(e * u)
            f = e * gains[start : start + DH, :1]
            mean_f = jnp.sum(f, axis=0, keepdims=True) * inv_dh
            mean_fu = jnp.sum(f * u, axis=0, keepdims=True) * inv_dh
            d_mixed[start : start + DH, :] = ((f - mean_f - u * mean_fu) * scale).astype(BF16)
    d_mixed[2 * part :, :] = dva[...].astype(BF16)

    split = 3 * part
    total[:split, :] += dot(d_mixed[...], normed[...], NT)
    total[split:, :] += dot(attended[...], cot[...])

    @pl.when(last)
    def _():
        norm_row[...] = jnp.sum(total[:split, :] * mixed_t[...].astype(F32), axis=0, keepdims=True)
        grads[...] = total[...].astype(BF16)


def attention_call(first, count, normed, mixed_t, d_att, mask_q, mask_k, gains, cot):
    seqs, part, _ = d_att.shape
    width = normed.shape[1]
    heads = part // DH
    fixed = lambda i, *_: (0, 0)
    by_seq = lambda i, *_: (i, 0, 0)
    grid_spec = pltpu.PrefetchScalarGridSpec(
        num_scalar_prefetch=2,
        grid=(seqs,),
        in_specs=[
            pl.BlockSpec((None, width, LEN), by_seq),
            pl.BlockSpec((3 * part, width), fixed),
            pl.BlockSpec((None, part, LEN), by_seq),
            pl.BlockSpec((None, IMAGE_SLOTS, LEN), by_seq),
            pl.BlockSpec((None, IMAGE_SLOTS, LEN), by_seq),
            pl.BlockSpec((2 * part, 128), fixed),
            pl.BlockSpec((LEN, width), lambda i, *_: (i, 0)),
        ],
        out_specs=[
            pl.BlockSpec((None, part, LEN), by_seq),
            pl.BlockSpec((None, 3 * part, LEN), by_seq),
            pl.BlockSpec((2 * part, 128), fixed),
            pl.BlockSpec((1, width), fixed),
            pl.BlockSpec((4 * part, width), fixed),
        ],
        scratch_shapes=[
            pltpu.VMEM((4 * part, width), F32),
            pltpu.VMEM((3 * part, LEN), F32),
            pltpu.VMEM((heads, 128, LEN), BF16),
            pltpu.VMEM((heads, LEN, 128), BF16),
            pltpu.VMEM((heads, LEN, DH), BF16),
            pltpu.VMEM((part, LEN), BF16),
            pltpu.VMEM((part, LEN), BF16),
            pltpu.VMEM((heads, LEN, BI), F32),
            pltpu.VMEM((heads, LEN, BI), F32),
            pltpu.VMEM((part, BI), F32),
            pltpu.VMEM((part, LEN), F32),
            pltpu.VMEM((part, LEN), F32),
            pltpu.VMEM((part, LEN), F32),
        ],
    )
    return pl.pallas_call(
        attention_kernel,
        grid_spec=grid_spec,
        out_shape=[
            jax.ShapeDtypeStruct((seqs, part, LEN), BF16),
            jax.ShapeDtypeStruct((seqs, 3 * part, LEN), BF16),
            jax.ShapeDtypeStruct((2 * part, 128), F32),
            jax.ShapeDtypeStruct((1, width), F32),
            jax.ShapeDtypeStruct((4 * part, width), BF16),
        ],
        cost_estimate=cost(18, 5_000_000),
        name="attention",
    )(first, count, normed, mixed_t, d_att, mask_q, mask_k, gains, cot)


def project_kernel(
    shard, active, attended, d_pre, d_mixed, normed, down_t, attn_t, up, mixed, gain, keep, send
):
    me = shard[0]
    part = attended.shape[0]
    out = dot(down_t[...], active[...]) + dot(attn_t[...], attended[...])
    grad = dot(up[...], d_pre[...]) + dot(mixed[...], d_mixed[...])
    product = grad * normed[...].astype(F32)
    sums = []
    for row in (jnp.sum(grad * gain[:, :1], axis=0, keepdims=True), jnp.sum(product, axis=0, keepdims=True)):
        high = row.astype(BF16)
        sums += [high, (row - high.astype(F32)).astype(BF16)]
    sums = jnp.concatenate(sums + [jnp.zeros((SUM_ROWS - 4, sums[0].shape[1]), BF16)], axis=0)
    for target in (keep, send):
        for slot in range(2):
            target[slot, 2 * part :, :] = sums
    for index in range(4):
        rows = slice(index * part, (index + 1) * part)
        away = jnp.bitwise_xor(me, index)
        slot = away // 2

        @pl.when(away % 2 == 0)
        def _():
            keep[slot, :part, :] = out[rows].astype(BF16)
            keep[slot, part : 2 * part, :] = grad[rows].astype(BF16)

        @pl.when(away % 2 == 1)
        def _():
            send[slot, :part, :] = out[rows].astype(BF16)
            send[slot, part : 2 * part, :] = grad[rows].astype(BF16)


def project_call(shard, active, attended, d_pre, d_mixed, normed, down_t, attn_t, up, mixed, gain, begin, size, block=256):
    width, hidden = down_t.shape
    part = attended.shape[1]
    steps = LEN // block
    ours = lambda i, *_: (begin + i // steps, 0, i % steps)
    out = lambda i, *_: (i // steps, 0, 0, i % steps)
    fixed = lambda i, *_: (0, 0)
    rows = 2 * part + SUM_ROWS
    grid_spec = pltpu.PrefetchScalarGridSpec(
        num_scalar_prefetch=1,
        grid=(size * steps,),
        in_specs=[
            pl.BlockSpec((None, hidden, block), ours),
            pl.BlockSpec((None, part, block), ours),
            pl.BlockSpec((None, hidden, block), ours),
            pl.BlockSpec((None, 3 * part, block), ours),
            pl.BlockSpec((None, width, block), ours),
            pl.BlockSpec((width, hidden), fixed),
            pl.BlockSpec((width, part), fixed),
            pl.BlockSpec((width, hidden), fixed),
            pl.BlockSpec((width, 3 * part), fixed),
            pl.BlockSpec((width, 128), fixed),
        ],
        out_specs=[
            pl.BlockSpec((None, 2, rows, block), out),
            pl.BlockSpec((None, 2, rows, block), out),
        ],
    )
    return pl.pallas_call(
        project_kernel,
        grid_spec=grid_spec,
        out_shape=[
            jax.ShapeDtypeStruct((size, 2, rows, LEN), BF16),
            jax.ShapeDtypeStruct((size, 2, rows, LEN), BF16),
        ],
        cost_estimate=cost(8, 16_000_000),
        name="project",
    )(shard, active, attended, d_pre, d_mixed, normed, down_t, attn_t, up, mixed, gain)


def finish_kernel(keep, from_core, from_y, own_t, cot, stats, gain, bias, *rest):
    block_out, token_grad = rest[-2:]
    part = own_t.shape[0]
    inv_width = 0.25 / part
    total = keep[...].astype(F32) + from_core[...].astype(F32) + from_y[...].astype(F32)
    own = own_t[...].astype(F32)
    block_out[...] = (own + total[:part] + bias[:, :1].astype(F32)).astype(BF16)
    grad = total[part : 2 * part]
    sums = total[2 * part :]
    mean = stats[0:1, :]
    scale = stats[1:2, :]
    hat = (own - mean) * scale
    inner = grad * gain[:, :1].astype(F32) - (sums[0:1] + sums[1:2]) * inv_width - hat * ((sums[2:3] + sums[3:4]) * inv_width)
    token_grad[...] = cot[...].astype(F32) + inner * scale


def finish_call(keep, from_core, from_y, own_t, cot, stats, gain, bias, before, begin, block=512):
    part, tokens = own_t.shape
    steps = LEN // block
    size = keep.shape[0]
    fixed = lambda i: (0, 0)
    packed = pl.BlockSpec((None, None, 2 * part + SUM_ROWS, block), lambda i: (i // steps, 0, 0, i % steps))
    ours = lambda i: (0, begin * steps + i)
    here = pl.BlockSpec((part, block), ours)
    return pl.pallas_call(
        finish_kernel,
        grid=(size * steps,),
        in_specs=[
            packed, packed, packed,
            here, here,
            pl.BlockSpec((8, block), ours),
            pl.BlockSpec((part, 128), fixed),
            pl.BlockSpec((part, 128), fixed),
        ]
        + [ANY] * len(before),
        out_specs=[here, here],
        out_shape=[
            jax.ShapeDtypeStruct((part, tokens), BF16),
            jax.ShapeDtypeStruct((part, tokens), F32),
        ],
        input_output_aliases={8 + i: i for i in range(len(before))},
        cost_estimate=cost(3, 5_000_000),
        name="finish",
    )(keep, from_core, from_y, own_t, cot, stats, gain, bias, *before)


def flip(value, axis, size, bit):
    return lax.ppermute(value, axis, [(i, i ^ bit) for i in range(size)])


def tie(*trees):
    return lax.optimization_barrier(trees)


def piece_order(size):
    bits = size.bit_length() - 1
    return [sum(((i >> b) & 1) << (bits - 1 - b) for b in range(bits)) for i in range(size)]


class SumOverDp:
    def __init__(self, value, size, index):
        self.size, self.index = size, index
        self.send = value
        self.steps = ["sum"] + [1 << i for i in reversed(range(size.bit_length() - 1))]

    def more(self):
        return bool(self.steps)

    def move(self, send):
        if self.steps[0] == "sum":
            return lax.all_to_all(send, "dp", 0, 0, tiled=True)
        return flip(send, "dp", self.size, self.steps[0])

    def take(self, arrived):
        step = self.steps.pop(0)
        if step == "sum":
            shares = arrived.reshape(self.size, -1, arrived.shape[1]).astype(F32)
            self.keep = jnp.sum(shares, axis=0).astype(BF16)
        else:
            self.keep = jnp.where(
                (self.index & step) > 0,
                jnp.concatenate([arrived, self.keep], axis=0),
                jnp.concatenate([self.keep, arrived], axis=0),
            )
        self.send = self.keep


class ChainOverDp:
    def __init__(self, value, size, index):
        self.size, self.index = size, index
        bits = [1 << i for i in range(size.bit_length() - 1)]
        self.steps = [("sum", bit) for bit in bits] + [("join", bit) for bit in reversed(bits)]
        self.prepare(value, None)

    def prepare(self, held, arrived):
        def part(which, half):
            rows = lax.dynamic_slice_in_dim(held, which * half, half, 0)
            if arrived is None:
                return rows
            came = lax.dynamic_slice_in_dim(arrived, which * half, half, 0)
            return (rows.astype(F32) + came.astype(F32)).astype(BF16)

        rows = held.shape[0]
        if self.steps and self.steps[0][0] == "sum":
            side = ((self.index & self.steps[0][1]) > 0).astype(jnp.int32)
            self.send, self.keep = part(1 - side, rows // 2), part(side, rows // 2)
        else:
            self.keep = part(0, rows)
            self.send = self.keep

    def more(self):
        return bool(self.steps)

    def move(self, send):
        return flip(send, "dp", self.size, self.steps[0][1])

    def take(self, arrived):
        kind, bit = self.steps.pop(0)
        if kind == "sum":
            self.prepare(self.keep, arrived)
            return
        self.keep = jnp.where(
            (self.index & bit) > 0,
            jnp.concatenate([arrived, self.keep], axis=0),
            jnp.concatenate([self.keep, arrived], axis=0),
        )
        self.send = self.keep


class ScatterOverMp:
    def __init__(self, keep, send):
        self.keep, self.send = keep, send
        self.bits = [1, 2]

    def more(self):
        return bool(self.bits)

    def move(self, send):
        return flip(send, "mp", 4, self.bits[0])

    def take(self, arrived):
        bit = self.bits.pop(0)
        if bit == 1:
            self.from_core = arrived
            self.send = (self.keep[:, 1:].astype(F32) + arrived[:, 1:].astype(F32)).astype(BF16)
        else:
            self.from_y = arrived


class ShortSums:
    def __init__(self, keep, send, rest, size):
        self.keep, self.send, self.rest, self.size = keep, send, rest, size
        self.steps = [("mp", 1), ("mp", 2)] + [("dp", 1 << i) for i in range(size.bit_length() - 1)]

    def more(self):
        return bool(self.steps)

    def move(self, send):
        axis, bit = self.steps[0]
        return flip(send, axis, 4 if axis == "mp" else self.size, bit)

    def take(self, arrived):
        axis, bit = self.steps.pop(0)
        if (axis, bit) == ("mp", 1):
            both = self.keep + arrived
            self.norm, self.send = both[0], both[1]
            return
        if axis == "mp":
            self.send = jnp.concatenate([self.norm + arrived, self.rest])
        else:
            self.send = self.send + arrived
        size = self.norm.shape[0]
        self.norm, self.rest = self.send[:size], self.send[size:]


def launch(movers, inputs):
    movers = [m for m in movers if m.more()]
    inputs, sends = tie(inputs, [m.send for m in movers])
    return inputs, [(m, m.move(s)) for m, s in zip(movers, sends)]


def land(flights, outputs):
    outputs, arrivals = tie(outputs, [f[1] for f in flights])
    for (mover, _), arrived in zip(flights, arrivals):
        mover.take(arrived)
    return outputs


def body(
    dp_size,
    tokens,
    image_ids,
    norm_gain,
    qkv_weight,
    qk_gain,
    attn_weight,
    up_weight,
    up_bias,
    down_weight,
    down_bias,
    cotangent,
):
    part = tokens.shape[1]
    width = cotangent.shape[1]
    seqs = image_ids.shape[0]
    me = lax.axis_index("mp")
    dp = lax.axis_index("dp")
    shard = me.astype(jnp.int32)[None]
    place = jnp.bitwise_xor(shard, jnp.array([0, 2, 1, 3], jnp.int32)) * part

    own_t = tokens.T
    from_y = flip(own_t, "mp", 4, 2)
    gain_own = jnp.broadcast_to(norm_gain[:, None], (part, 128))
    gain_y = flip(gain_own, "mp", 4, 2)
    gains = (gain_own, gain_y, flip(gain_own, "mp", 4, 1), flip(gain_y, "mp", 4, 1))

    mixed_t = jnp.transpose(qkv_weight, (1, 2, 0)).reshape(3 * part, width)
    mixed = mixed_t.T
    up_t = up_weight.T
    down_t = down_weight.T
    attn_t = attn_weight.T
    def column(vector):
        return jnp.broadcast_to(vector[:, None], (vector.shape[0], 128))

    up_bias_col = column(up_bias)
    head_gains = column(qk_gain.astype(F32).reshape(2 * part))

    slots = jnp.arange(IMAGE_SLOTS, dtype=jnp.int32)[None, :, None]
    same = image_ids[:, None, :] == slots
    mask_q = same.astype(BF16)
    mask_k = jnp.where(same | (slots >= 8), 0.0, -PENALTY).astype(BF16)
    block_first = image_ids[:, ::BI]
    block_last = image_ids[:, BI - 1 :: BI]
    starts = jnp.sum(image_ids[:, None, :] < block_first[:, :, None], axis=2, dtype=jnp.int32)
    ends = jnp.sum(image_ids[:, None, :] <= block_last[:, :, None], axis=2, dtype=jnp.int32)
    first = (starts // BJ).reshape(-1)
    count = ((ends + BJ - 1) // BJ).reshape(-1) - first

    pick = (jnp.arange(part)[:, None] + me * part == jnp.arange(width)[None, :]).astype(BF16)
    d_act, d_att, cot_own, cot_sum = early_call(cotangent, down_weight, attn_weight, pick)
    bias_col = column(down_bias)
    prepared = (
        d_act, d_att, mixed_t, mixed, up_t, down_t, attn_t, up_bias_col, head_gains, mask_q, mask_k, first, count,
        bias_col,
    )
    prepared, from_y = tie(prepared, from_y)
    (
        d_act, d_att, mixed_t, mixed, up_t, down_t, attn_t, up_bias_col, head_gains, mask_q, mask_k, first, count,
        bias_col,
    ) = prepared
    pieces = (own_t, from_y, flip(own_t, "mp", 4, 1), flip(from_y, "mp", 4, 1))
    normed, active, d_pre, stats, upbias_part, gain_all, up_row, mlp_part = mlp_call(
        tuple(piece_order(dp_size)), place, pieces, gains, up_t, up_bias_col, d_act, cotangent, up_weight
    )
    mlp_sum = SumOverDp(mlp_part, dp_size, dp)

    (states,), flights = launch([mlp_sum], (normed,))
    attended, d_mixed, qk_part, norm_row, mix_part = land(
        flights,
        attention_call(first, count, states, mixed_t, d_att, mask_q, mask_k, head_gains, cotangent),
    )
    mix_sum = ChainOverDp(mix_part, dp_size, dp)

    norm_vec = norm_row[0] + jnp.sum(up_row, axis=1)
    norm_parts = norm_vec.reshape(4, part)
    norm_parts = [lax.dynamic_index_in_dim(norm_parts, jnp.bitwise_xor(me, m), 0, False) for m in range(4)]
    short = ShortSums(
        jnp.stack([norm_parts[0], norm_parts[2]]),
        jnp.stack([norm_parts[1], norm_parts[3]]),
        jnp.concatenate([jnp.sum(qk_part, axis=1), jnp.sum(upbias_part, axis=1), jnp.sum(cot_sum, axis=1)]),
        dp_size,
    )

    runs = [(0, seqs - 1), (seqs - 1, 1)] if seqs > 1 else [(0, 1)]
    scatters = []
    for begin, size in runs:
        along = [mix_sum, mlp_sum, short] + [m for m in scatters if m.more()]
        (att, dm), flights = launch(along, (attended, d_mixed))
        sent = project_call(
            shard, active, att, d_pre, dm, normed, down_t, attn_t, up_weight, mixed, gain_all, begin, size
        )
        keep, send = land(flights, sent)
        scatters.append(ScatterOverMp(keep, send))

    finished = ()
    done = set()

    def finish_ready(finished):
        for (begin, _), scatter in zip(runs, scatters):
            if not scatter.more() and begin not in done:
                done.add(begin)
                finished = finish_call(
                    scatter.keep, scatter.from_core, scatter.from_y, own_t, cot_own, stats, gain_own, bias_col,
                    finished, begin,
                )
        return finished

    flying = []
    while True:
        busy = [f[0] for f in flying]
        ready = [m for m in scatters + [short, mlp_sum, mix_sum] if m.more() and m not in busy]
        finished, flights = launch(ready, finished)
        flying = flying + flights
        if not flying:
            break
        finished = finish_ready(finished)
        near = [f for f in flying if f[0] in scatters and len(f[0].bits) == 2]
        across = [f for f in flying if f[0] in scatters and len(f[0].bits) == 1]
        chain = [f for f in flying if f[0] is mix_sum]
        rest = [f for f in flying if f[0] is short]
        wide = [f for f in flying if f[0] is mlp_sum]
        left = len(mix_sum.steps)
        if near:
            now = near + chain + rest
        elif left == 2:
            now = chain + across[:1] + wide + rest
        elif left == 1:
            now = across[:1] + wide + rest or chain
        else:
            now = chain + rest or flying
        finished = land(now, finished)
        flying = [f for f in flying if f not in now]
    finished = finish_ready(finished)
    block_out, token_grad = finished
    block_out, token_grad = block_out.T, token_grad.T
    mixed_grad = mix_sum.keep.astype(F32)
    qkv_grad = jnp.transpose(mixed_grad[: 3 * part].reshape(3, part, width), (2, 0, 1))

    gain_grad = short.norm / norm_gain.astype(F32)
    rest = short.rest
    split = 2 * part + up_weight.shape[1]
    return (
        block_out,
        token_grad,
        gain_grad,
        qkv_grad,
        rest[: 2 * part].reshape(2, part),
        mixed_grad[3 * part :],
        mlp_sum.keep[up_weight.shape[1] :].astype(F32),
        rest[2 * part : split],
        mlp_sum.keep[: up_weight.shape[1]].astype(F32),
        rest[split:],
    )


def solution(mesh):
    in_specs = (
        P("dp", "mp"),
        P("dp", None),
        P("mp"),
        P(None, None, "mp"),
        P(None, "mp"),
        P("mp", None),
        P(None, "mp"),
        P("mp"),
        P("mp", None),
        P("mp"),
        P("dp", None),
    )
    out_specs = (
        P("dp", "mp"),
        P("dp", "mp"),
        P("mp"),
        P(None, None, "mp"),
        P(None, "mp"),
        P("mp", None),
        P(None, "mp"),
        P("mp"),
        P("mp", None),
        P("mp"),
    )
    run = functools.partial(body, mesh.shape["dp"])
    return jax.shard_map(run, mesh=mesh, in_specs=in_specs, out_specs=out_specs, check_vma=False)
```

```python
import functools

import jax
import jax.numpy as jnp
from jax import lax
from jax.experimental import pallas as pl
from jax.experimental.pallas import tpu as pltpu
from jax.sharding import PartitionSpec as P

DH = 64
LEN = 1024
EPSILON = 1e-06
IMAGE_SLOTS = 16
PENALTY = 1024.0
BI = 256
BJ = 256
SUM_ROWS = 16
F32 = jnp.float32
BF16 = jnp.bfloat16

NN = (((1,), (0,)), ((), ()))
NT = (((1,), (1,)), ((), ()))
ANY = pl.BlockSpec(memory_space=pl.ANY)


def dot(left, right, dims=NN):
    return lax.dot_general(left, right, dims, preferred_element_type=F32)


def fold_lanes(rows):
    total = rows[:, :128]
    for start in range(128, rows.shape[1], 128):
        total = total + rows[:, start : start + 128]
    return total


def cost(microseconds, nbytes):
    return pl.CostEstimate(flops=int(microseconds * 1e3), bytes_accessed=nbytes // 1000, transcendentals=0)


def early_kernel(cot, down, attn, pick, d_act, d_att, cot_own, bias_sum):
    rows = cot[...]
    d_act[...] = dot(down[...], rows, NT).astype(BF16)
    d_att[...] = dot(attn[...], rows, NT).astype(BF16)
    own = dot(pick[...], rows, NT)
    cot_own[...] = own.astype(BF16)

    @pl.when(pl.program_id(0) == 0)
    def _():
        bias_sum[...] = jnp.zeros_like(bias_sum)

    bias_sum[...] += fold_lanes(own)


def early_call(cot, down, attn, pick, block=512):
    tokens, width = cot.shape
    seqs = tokens // LEN
    hidden, part = down.shape[0], attn.shape[0]
    steps = LEN // block
    fixed = lambda i: (0, 0)
    by_seq = lambda i: (i // steps, 0, i % steps)
    return pl.pallas_call(
        early_kernel,
        grid=(tokens // block,),
        in_specs=[
            pl.BlockSpec((block, width), lambda i: (i, 0)),
            pl.BlockSpec((hidden, width), fixed),
            pl.BlockSpec((part, width), fixed),
            pl.BlockSpec((part, width), fixed),
        ],
        out_specs=[
            pl.BlockSpec((None, hidden, block), by_seq),
            pl.BlockSpec((None, part, block), by_seq),
            pl.BlockSpec((part, block), lambda i: (0, i)),
            pl.BlockSpec((part, 128), fixed),
        ],
        out_shape=[
            jax.ShapeDtypeStruct((seqs, hidden, LEN), BF16),
            jax.ShapeDtypeStruct((seqs, part, LEN), BF16),
            jax.ShapeDtypeStruct((part, tokens), BF16),
            jax.ShapeDtypeStruct((part, 128), F32),
        ],
        cost_estimate=cost(10, 12_000_000),
        name="early",
    )(cot, down, attn, pick)


def mlp_kernel(
    pieces_order, place, own, flip_y, flip_c, flip_cy, gain_own, gain_y, gain_c, gain_cy, up_t, up_bias, d_act, cot, up,
    normed, active, d_pre, stats, bias_sum, gain_all, up_row, grads, low, high
):
    pieces = (own, flip_y, flip_c, flip_cy)
    part = own.shape[0]
    width = part * 4
    first = pl.program_id(0) == 0
    last = pl.program_id(0) == pl.num_programs(0) - 1

    @pl.when(first)
    def _():
        bias_sum[...] = jnp.zeros_like(bias_sum)
        low[...] = jnp.zeros_like(low)
        high[...] = jnp.zeros_like(high)
        for slot, piece in enumerate((gain_own, gain_y, gain_c, gain_cy)):
            gain_all[pl.ds(pl.multiple_of(place[slot], part), part), :] = piece[...].astype(F32)

    total = 0.0
    squares = 0.0
    for piece in pieces:
        rows = piece[...].astype(F32)
        total = total + jnp.sum(rows, axis=0, keepdims=True)
        squares = squares + jnp.sum(rows * rows, axis=0, keepdims=True)
    mean = total * (1.0 / width)
    scale = lax.rsqrt(squares * (1.0 / width) - mean * mean + EPSILON)
    stats[0:1, :] = mean
    stats[1:2, :] = scale
    stats[2:8, :] = jnp.zeros((6, stats.shape[1]), F32)
    for slot, piece in enumerate(pieces):
        rows = piece[...].astype(F32)
        here = pl.ds(pl.multiple_of(place[slot], part), part)
        normed[here, :] = ((rows - mean) * scale * gain_all[here, :1]).astype(BF16)

    c0 = 0.7978845608028654
    c1 = 0.044715 * c0
    def lift(start):
        here = slice(start, start + 256)
        return dot(up_t[here, :], normed[...]) + up_bias[here, :1].astype(F32)

    ahead = lift(0)
    for start in range(0, up_t.shape[0], 256):
        here = slice(start, start + 256)
        pre = ahead
        if start + 256 < up_t.shape[0]:
            ahead = lift(start + 256)
        square = pre * pre
        half = 0.5 * jnp.tanh(pre * (c0 + c1 * square)) + 0.5
        act = (pre * half).astype(BF16)
        active[here, :] = act
        slope = half + pre * (half - half * half) * (2.0 * c0 + 6.0 * c1 * square)
        grad = (d_act[here, :].astype(F32) * slope).astype(BF16)
        d_pre[here, :] = grad
        bias_sum[here, :] += fold_lanes(grad.astype(F32))
        low[here, :] += dot(act, cot[...])
        high[:, here] += dot(normed[...], grad, NT)

    @pl.when(last)
    def _():
        up_row[...] = fold_lanes(high[...] * up[...].astype(F32))
        half = low.shape[0]
        size = grads.shape[0] // len(pieces_order)
        for slot, piece in enumerate(pieces_order):
            source, start = (low, piece * size) if piece * size < half else (high, piece * size - half)
            grads[slot * size : (slot + 1) * size, :] = source[start : start + size, :].astype(BF16)


def mlp_call(pieces_order, place, pieces, gains, up_t, up_bias, d_act, cot, up, block=512):
    part, tokens = pieces[0].shape
    width = 4 * part
    seqs, hidden, _ = d_act.shape
    steps = LEN // block
    lanes = lambda i, *_: (0, i)
    by_seq = lambda i, *_: (i // steps, 0, i % steps)
    fixed = lambda i, *_: (0, 0)
    grid_spec = pltpu.PrefetchScalarGridSpec(
        num_scalar_prefetch=1,
        grid=(tokens // block,),
        in_specs=[pl.BlockSpec((part, block), lanes)] * 4
        + [pl.BlockSpec((part, 128), fixed)] * 4
        + [
            pl.BlockSpec((hidden, width), fixed),
            pl.BlockSpec((hidden, 128), fixed),
            pl.BlockSpec((None, hidden, block), by_seq),
            pl.BlockSpec((block, width), lambda i, *_: (i, 0)),
            pl.BlockSpec((width, hidden), fixed),
        ],
        out_specs=[
            pl.BlockSpec((None, width, block), by_seq),
            pl.BlockSpec((None, hidden, block), by_seq),
            pl.BlockSpec((None, hidden, block), by_seq),
            pl.BlockSpec((8, block), lanes),
            pl.BlockSpec((hidden, 128), fixed),
            pl.BlockSpec((width, 128), fixed),
            pl.BlockSpec((width, 128), fixed),
            pl.BlockSpec((hidden + width, width), fixed),
        ],
        scratch_shapes=[pltpu.VMEM((hidden, width), F32), pltpu.VMEM((width, hidden), F32)],
    )
    assert hidden == width
    return pl.pallas_call(
        functools.partial(mlp_kernel, pieces_order),
        grid_spec=grid_spec,
        out_shape=[
            jax.ShapeDtypeStruct((seqs, width, LEN), BF16),
            jax.ShapeDtypeStruct((seqs, hidden, LEN), BF16),
            jax.ShapeDtypeStruct((seqs, hidden, LEN), BF16),
            jax.ShapeDtypeStruct((8, tokens), F32),
            jax.ShapeDtypeStruct((hidden, 128), F32),
            jax.ShapeDtypeStruct((width, 128), F32),
            jax.ShapeDtypeStruct((width, 128), F32),
            jax.ShapeDtypeStruct((hidden + width, width), BF16),
        ],
        cost_estimate=cost(20, 30_000_000),
        name="mlp",
    )(place, *pieces, *gains, up_t, up_bias, d_act, cot, up)


def attention_kernel(
    first, count, normed, mixed_t, d_att, mask_q, mask_k, gains, cot, attended, d_mixed, gain_sum, norm_row, grads,
    total, qkv, qx, kx, vn, kt, vt, es, ps, oa, dqa, dka, dva
):
    seq = pl.program_id(0)
    last = seq == pl.num_programs(0) - 1
    part = attended.shape[0]
    heads = part // DH
    inv_dh = 1.0 / DH

    @pl.when(seq == 0)
    def _():
        total[...] = jnp.zeros_like(total)
        gain_sum[...] = jnp.zeros_like(gain_sum)

    qkv[...] = dot(mixed_t[...], normed[...])

    def unit(start):
        raw = qkv[start : start + DH, :]
        shifted = raw - jnp.sum(raw, axis=0, keepdims=True) * inv_dh
        scale = lax.rsqrt(jnp.sum(shifted * shifted, axis=0, keepdims=True) * inv_dh + EPSILON)
        return shifted * scale, scale

    zeros = jnp.zeros((128 - DH - IMAGE_SLOTS, LEN), BF16)
    for head in range(heads):
        rows = slice(head * DH, (head + 1) * DH)
        query, _ = unit(head * DH)
        query = (query * (gains[rows, :1] * 0.125)).astype(BF16)
        qx[head] = jnp.concatenate([query, mask_q[...], zeros], axis=0)
        key, _ = unit(part + head * DH)
        key = (key * gains[part + head * DH : part + (head + 1) * DH, :1]).astype(BF16)
        kt[rows, :] = key
        kx[head] = jnp.concatenate([key, mask_k[...], zeros], axis=0).T
        value = qkv[2 * part + head * DH : 2 * part + (head + 1) * DH, :].astype(BF16)
        vt[rows, :] = value
        vn[head] = value.T
    dka[...] = jnp.zeros_like(dka)
    dva[...] = jnp.zeros_like(dva)

    def query_block(ib, _):
        i0 = pl.multiple_of(ib * BI, BI)
        icols = pl.ds(i0, BI)
        base = first[seq * (LEN // BI) + ib]
        trips = count[seq * (LEN // BI) + ib]

        def scores(j, carry):
            j0 = pl.multiple_of((base + j) * BJ, BJ)
            slot = pl.multiple_of(j * BJ, BJ)
            out = []
            for head in range(heads):
                rows = slice(head * DH, (head + 1) * DH)
                e = jnp.exp(dot(kx[head, pl.ds(j0, BJ), :], qx[head, :, icols]))
                p = dot(vn[head, pl.ds(j0, BJ), :], d_att[rows, icols])
                es[head, pl.ds(slot, BJ), :] = e
                ps[head, pl.ds(slot, BJ), :] = p
                out.append(carry[2 * head] + jnp.sum(e.reshape(BJ // 8, 8, BI), axis=0))
                out.append(carry[2 * head + 1] + jnp.sum((e * p).reshape(BJ // 8, 8, BI), axis=0))
            return tuple(out)

        sums = lax.fori_loop(0, trips, scores, tuple(jnp.zeros((8, BI), F32) for _ in range(2 * heads)))
        inverse = []
        inner = []
        for head in range(heads):
            inv = 1.0 / jnp.sum(sums[2 * head], axis=0, keepdims=True)
            inverse.append(inv)
            inner.append(jnp.sum(sums[2 * head + 1], axis=0, keepdims=True) * inv)
        oa[...] = jnp.zeros_like(oa)
        dqa[:, icols] = jnp.zeros((part, BI), F32)

        def row_grads(j, _):
            j0 = pl.multiple_of((base + j) * BJ, BJ)
            slot = pl.multiple_of(j * BJ, BJ)
            jcols = pl.ds(j0, BJ)
            for head in range(heads):
                rows = slice(head * DH, (head + 1) * DH)
                w = es[head, pl.ds(slot, BJ), :] * inverse[head]
                d = (w * (ps[head, pl.ds(slot, BJ), :] - inner[head])).astype(BF16)
                w = w.astype(BF16)
                oa[rows, :] += dot(vt[rows, jcols], w)
                dqa[rows, icols] += dot(kt[rows, jcols], d)
                dva[rows, jcols] += dot(d_att[rows, icols], w, NT)
                dka[rows, jcols] += dot(qx[head, :DH, icols], d, NT)
            return 0

        lax.fori_loop(0, trips, row_grads, 0)
        attended[:, icols] = oa[...].astype(BF16)
        return 0

    lax.fori_loop(0, LEN // BI, query_block, 0)

    for source, offset, factor in ((dqa, 0, 0.125), (dka, part, 1.0)):
        for head in range(heads):
            start = offset + head * DH
            u, scale = unit(start)
            e = source[head * DH : (head + 1) * DH, :] * factor
            gain_sum[start : start + DH, :] += fold_lanes(e * u)
            f = e * gains[start : start + DH, :1]
            mean_f = jnp.sum(f, axis=0, keepdims=True) * inv_dh
            mean_fu = jnp.sum(f * u, axis=0, keepdims=True) * inv_dh
            d_mixed[start : start + DH, :] = ((f - mean_f - u * mean_fu) * scale).astype(BF16)
    d_mixed[2 * part :, :] = dva[...].astype(BF16)

    split = 3 * part
    total[:split, :] += dot(d_mixed[...], normed[...], NT)
    total[split:, :] += dot(attended[...], cot[...])

    @pl.when(last)
    def _():
        norm_row[...] = jnp.sum(total[:split, :] * mixed_t[...].astype(F32), axis=0, keepdims=True)
        grads[...] = total[...].astype(BF16)


def attention_call(first, count, normed, mixed_t, d_att, mask_q, mask_k, gains, cot):
    seqs, part, _ = d_att.shape
    width = normed.shape[1]
    heads = part // DH
    fixed = lambda i, *_: (0, 0)
    by_seq = lambda i, *_: (i, 0, 0)
    grid_spec = pltpu.PrefetchScalarGridSpec(
        num_scalar_prefetch=2,
        grid=(seqs,),
        in_specs=[
            pl.BlockSpec((None, width, LEN), by_seq),
            pl.BlockSpec((3 * part, width), fixed),
            pl.BlockSpec((None, part, LEN), by_seq),
            pl.BlockSpec((None, IMAGE_SLOTS, LEN), by_seq),
            pl.BlockSpec((None, IMAGE_SLOTS, LEN), by_seq),
            pl.BlockSpec((2 * part, 128), fixed),
            pl.BlockSpec((LEN, width), lambda i, *_: (i, 0)),
        ],
        out_specs=[
            pl.BlockSpec((None, part, LEN), by_seq),
            pl.BlockSpec((None, 3 * part, LEN), by_seq),
            pl.BlockSpec((2 * part, 128), fixed),
            pl.BlockSpec((1, width), fixed),
            pl.BlockSpec((4 * part, width), fixed),
        ],
        scratch_shapes=[
            pltpu.VMEM((4 * part, width), F32),
            pltpu.VMEM((3 * part, LEN), F32),
            pltpu.VMEM((heads, 128, LEN), BF16),
            pltpu.VMEM((heads, LEN, 128), BF16),
            pltpu.VMEM((heads, LEN, DH), BF16),
            pltpu.VMEM((part, LEN), BF16),
            pltpu.VMEM((part, LEN), BF16),
            pltpu.VMEM((heads, LEN, BI), F32),
            pltpu.VMEM((heads, LEN, BI), F32),
            pltpu.VMEM((part, BI), F32),
            pltpu.VMEM((part, LEN), F32),
            pltpu.VMEM((part, LEN), F32),
            pltpu.VMEM((part, LEN), F32),
        ],
    )
    return pl.pallas_call(
        attention_kernel,
        grid_spec=grid_spec,
        out_shape=[
            jax.ShapeDtypeStruct((seqs, part, LEN), BF16),
            jax.ShapeDtypeStruct((seqs, 3 * part, LEN), BF16),
            jax.ShapeDtypeStruct((2 * part, 128), F32),
            jax.ShapeDtypeStruct((1, width), F32),
            jax.ShapeDtypeStruct((4 * part, width), BF16),
        ],
        cost_estimate=cost(18, 5_000_000),
        name="attention",
    )(first, count, normed, mixed_t, d_att, mask_q, mask_k, gains, cot)


def project_kernel(
    shard, active, attended, d_pre, d_mixed, normed, down_t, attn_t, up, mixed, gain, keep, send
):
    me = shard[0]
    part = attended.shape[0]
    out = dot(down_t[...], active[...]) + dot(attn_t[...], attended[...])
    grad = dot(up[...], d_pre[...]) + dot(mixed[...], d_mixed[...])
    product = grad * normed[...].astype(F32)
    sums = []
    for row in (jnp.sum(grad * gain[:, :1], axis=0, keepdims=True), jnp.sum(product, axis=0, keepdims=True)):
        high = row.astype(BF16)
        sums += [high, (row - high.astype(F32)).astype(BF16)]
    sums = jnp.concatenate(sums + [jnp.zeros((SUM_ROWS - 4, sums[0].shape[1]), BF16)], axis=0)
    for target in (keep, send):
        for slot in range(2):
            target[slot, 2 * part :, :] = sums
    for index in range(4):
        rows = slice(index * part, (index + 1) * part)
        away = jnp.bitwise_xor(me, index)
        slot = away // 2

        @pl.when(away % 2 == 0)
        def _():
            keep[slot, :part, :] = out[rows].astype(BF16)
            keep[slot, part : 2 * part, :] = grad[rows].astype(BF16)

        @pl.when(away % 2 == 1)
        def _():
            send[slot, :part, :] = out[rows].astype(BF16)
            send[slot, part : 2 * part, :] = grad[rows].astype(BF16)


def project_call(shard, active, attended, d_pre, d_mixed, normed, down_t, attn_t, up, mixed, gain, begin, size, block=256):
    width, hidden = down_t.shape
    part = attended.shape[1]
    steps = LEN // block
    ours = lambda i, *_: (begin + i // steps, 0, i % steps)
    out = lambda i, *_: (i // steps, 0, 0, i % steps)
    fixed = lambda i, *_: (0, 0)
    rows = 2 * part + SUM_ROWS
    grid_spec = pltpu.PrefetchScalarGridSpec(
        num_scalar_prefetch=1,
        grid=(size * steps,),
        in_specs=[
            pl.BlockSpec((None, hidden, block), ours),
            pl.BlockSpec((None, part, block), ours),
            pl.BlockSpec((None, hidden, block), ours),
            pl.BlockSpec((None, 3 * part, block), ours),
            pl.BlockSpec((None, width, block), ours),
            pl.BlockSpec((width, hidden), fixed),
            pl.BlockSpec((width, part), fixed),
            pl.BlockSpec((width, hidden), fixed),
            pl.BlockSpec((width, 3 * part), fixed),
            pl.BlockSpec((width, 128), fixed),
        ],
        out_specs=[
            pl.BlockSpec((None, 2, rows, block), out),
            pl.BlockSpec((None, 2, rows, block), out),
        ],
    )
    return pl.pallas_call(
        project_kernel,
        grid_spec=grid_spec,
        out_shape=[
            jax.ShapeDtypeStruct((size, 2, rows, LEN), BF16),
            jax.ShapeDtypeStruct((size, 2, rows, LEN), BF16),
        ],
        cost_estimate=cost(8, 16_000_000),
        name="project",
    )(shard, active, attended, d_pre, d_mixed, normed, down_t, attn_t, up, mixed, gain)


def finish_kernel(keep, from_core, from_y, own_t, cot, stats, gain, bias, *rest):
    block_out, token_grad = rest[-2:]
    part = own_t.shape[0]
    inv_width = 0.25 / part
    total = keep[...].astype(F32) + from_core[...].astype(F32) + from_y[...].astype(F32)
    own = own_t[...].astype(F32)
    block_out[...] = (own + total[:part] + bias[:, :1].astype(F32)).astype(BF16)
    grad = total[part : 2 * part]
    sums = total[2 * part :]
    mean = stats[0:1, :]
    scale = stats[1:2, :]
    hat = (own - mean) * scale
    inner = grad * gain[:, :1].astype(F32) - (sums[0:1] + sums[1:2]) * inv_width - hat * ((sums[2:3] + sums[3:4]) * inv_width)
    token_grad[...] = cot[...].astype(F32) + inner * scale


def finish_call(keep, from_core, from_y, own_t, cot, stats, gain, bias, before, begin, block=512):
    part, tokens = own_t.shape
    steps = LEN // block
    size = keep.shape[0]
    fixed = lambda i: (0, 0)
    packed = pl.BlockSpec((None, None, 2 * part + SUM_ROWS, block), lambda i: (i // steps, 0, 0, i % steps))
    ours = lambda i: (0, begin * steps + i)
    here = pl.BlockSpec((part, block), ours)
    return pl.pallas_call(
        finish_kernel,
        grid=(size * steps,),
        in_specs=[
            packed, packed, packed,
            here, here,
            pl.BlockSpec((8, block), ours),
            pl.BlockSpec((part, 128), fixed),
            pl.BlockSpec((part, 128), fixed),
        ]
        + [ANY] * len(before),
        out_specs=[here, here],
        out_shape=[
            jax.ShapeDtypeStruct((part, tokens), BF16),
            jax.ShapeDtypeStruct((part, tokens), F32),
        ],
        input_output_aliases={8 + i: i for i in range(len(before))},
        cost_estimate=cost(3, 5_000_000),
        name="finish",
    )(keep, from_core, from_y, own_t, cot, stats, gain, bias, *before)


def flip(value, axis, size, bit):
    return lax.ppermute(value, axis, [(i, i ^ bit) for i in range(size)])


def tie(*trees):
    return lax.optimization_barrier(trees)


def piece_order(size):
    bits = size.bit_length() - 1
    return [sum(((i >> b) & 1) << (bits - 1 - b) for b in range(bits)) for i in range(size)]


class SumOverDp:
    def __init__(self, value, size, index):
        self.size, self.index = size, index
        self.send = value
        self.steps = ["sum"] + [1 << i for i in reversed(range(size.bit_length() - 1))]

    def more(self):
        return bool(self.steps)

    def move(self, send):
        if self.steps[0] == "sum":
            return lax.all_to_all(send, "dp", 0, 0, tiled=True)
        return flip(send, "dp", self.size, self.steps[0])

    def take(self, arrived):
        step = self.steps.pop(0)
        if step == "sum":
            shares = arrived.reshape(self.size, -1, arrived.shape[1]).astype(F32)
            self.keep = jnp.sum(shares, axis=0).astype(BF16)
        else:
            self.keep = jnp.where(
                (self.index & step) > 0,
                jnp.concatenate([arrived, self.keep], axis=0),
                jnp.concatenate([self.keep, arrived], axis=0),
            )
        self.send = self.keep


class ChainOverDp:
    def __init__(self, value, size, index):
        self.size, self.index = size, index
        bits = [1 << i for i in range(size.bit_length() - 1)]
        self.steps = [("sum", bit) for bit in bits] + [("join", bit) for bit in reversed(bits)]
        self.prepare(value, None)

    def prepare(self, held, arrived):
        def part(which, half):
            rows = lax.dynamic_slice_in_dim(held, which * half, half, 0)
            if arrived is None:
                return rows
            came = lax.dynamic_slice_in_dim(arrived, which * half, half, 0)
            return (rows.astype(F32) + came.astype(F32)).astype(BF16)

        rows = held.shape[0]
        if self.steps and self.steps[0][0] == "sum":
            side = ((self.index & self.steps[0][1]) > 0).astype(jnp.int32)
            self.send, self.keep = part(1 - side, rows // 2), part(side, rows // 2)
        else:
            self.keep = part(0, rows)
            self.send = self.keep

    def more(self):
        return bool(self.steps)

    def move(self, send):
        return flip(send, "dp", self.size, self.steps[0][1])

    def take(self, arrived):
        kind, bit = self.steps.pop(0)
        if kind == "sum":
            self.prepare(self.keep, arrived)
            return
        self.keep = jnp.where(
            (self.index & bit) > 0,
            jnp.concatenate([arrived, self.keep], axis=0),
            jnp.concatenate([self.keep, arrived], axis=0),
        )
        self.send = self.keep


class ScatterOverMp:
    def __init__(self, keep, send):
        self.keep, self.send = keep, send
        self.bits = [1, 2]

    def more(self):
        return bool(self.bits)

    def move(self, send):
        return flip(send, "mp", 4, self.bits[0])

    def take(self, arrived):
        bit = self.bits.pop(0)
        if bit == 1:
            self.from_core = arrived
            self.send = (self.keep[:, 1:].astype(F32) + arrived[:, 1:].astype(F32)).astype(BF16)
        else:
            self.from_y = arrived


class ShortSums:
    def __init__(self, keep, send, rest, size):
        self.keep, self.send, self.rest, self.size = keep, send, rest, size
        self.steps = [("mp", 1), ("mp", 2)] + [("dp", 1 << i) for i in range(size.bit_length() - 1)]

    def more(self):
        return bool(self.steps)

    def move(self, send):
        axis, bit = self.steps[0]
        return flip(send, axis, 4 if axis == "mp" else self.size, bit)

    def take(self, arrived):
        axis, bit = self.steps.pop(0)
        if (axis, bit) == ("mp", 1):
            both = self.keep + arrived
            self.norm, self.send = both[0], both[1]
            return
        if axis == "mp":
            self.send = jnp.concatenate([self.norm + arrived, self.rest])
        else:
            self.send = self.send + arrived
        size = self.norm.shape[0]
        self.norm, self.rest = self.send[:size], self.send[size:]


def launch(movers, inputs):
    movers = [m for m in movers if m.more()]
    inputs, sends = tie(inputs, [m.send for m in movers])
    return inputs, [(m, m.move(s)) for m, s in zip(movers, sends)]


def land(flights, outputs):
    outputs, arrivals = tie(outputs, [f[1] for f in flights])
    for (mover, _), arrived in zip(flights, arrivals):
        mover.take(arrived)
    return outputs


def body(
    dp_size,
    tokens,
    image_ids,
    norm_gain,
    qkv_weight,
    qk_gain,
    attn_weight,
    up_weight,
    up_bias,
    down_weight,
    down_bias,
    cotangent,
):
    part = tokens.shape[1]
    width = cotangent.shape[1]
    seqs = image_ids.shape[0]
    me = lax.axis_index("mp")
    dp = lax.axis_index("dp")
    shard = me.astype(jnp.int32)[None]
    place = jnp.bitwise_xor(shard, jnp.array([0, 2, 1, 3], jnp.int32)) * part

    own_t = tokens.T
    from_y = flip(own_t, "mp", 4, 2)
    gain_own = jnp.broadcast_to(norm_gain[:, None], (part, 128))
    gain_y = flip(gain_own, "mp", 4, 2)
    gains = (gain_own, gain_y, flip(gain_own, "mp", 4, 1), flip(gain_y, "mp", 4, 1))

    mixed_t = jnp.transpose(qkv_weight, (1, 2, 0)).reshape(3 * part, width)
    mixed = mixed_t.T
    up_t = up_weight.T
    down_t = down_weight.T
    attn_t = attn_weight.T
    def column(vector):
        return jnp.broadcast_to(vector[:, None], (vector.shape[0], 128))

    up_bias_col = column(up_bias)
    head_gains = column(qk_gain.astype(F32).reshape(2 * part))

    slots = jnp.arange(IMAGE_SLOTS, dtype=jnp.int32)[None, :, None]
    same = image_ids[:, None, :] == slots
    mask_q = same.astype(BF16)
    mask_k = jnp.where(same | (slots >= 8), 0.0, -PENALTY).astype(BF16)
    block_first = image_ids[:, ::BI]
    block_last = image_ids[:, BI - 1 :: BI]
    starts = jnp.sum(image_ids[:, None, :] < block_first[:, :, None], axis=2, dtype=jnp.int32)
    ends = jnp.sum(image_ids[:, None, :] <= block_last[:, :, None], axis=2, dtype=jnp.int32)
    first = (starts // BJ).reshape(-1)
    count = ((ends + BJ - 1) // BJ).reshape(-1) - first

    pick = (jnp.arange(part)[:, None] + me * part == jnp.arange(width)[None, :]).astype(BF16)
    d_act, d_att, cot_own, cot_sum = early_call(cotangent, down_weight, attn_weight, pick)
    bias_col = column(down_bias)
    prepared = (
        d_act, d_att, mixed_t, mixed, up_t, down_t, attn_t, up_bias_col, head_gains, mask_q, mask_k, first, count,
        bias_col,
    )
    prepared, from_y = tie(prepared, from_y)
    (
        d_act, d_att, mixed_t, mixed, up_t, down_t, attn_t, up_bias_col, head_gains, mask_q, mask_k, first, count,
        bias_col,
    ) = prepared
    pieces = (own_t, from_y, flip(own_t, "mp", 4, 1), flip(from_y, "mp", 4, 1))
    normed, active, d_pre, stats, upbias_part, gain_all, up_row, mlp_part = mlp_call(
        tuple(piece_order(dp_size)), place, pieces, gains, up_t, up_bias_col, d_act, cotangent, up_weight
    )
    mlp_sum = SumOverDp(mlp_part, dp_size, dp)

    (states,), flying = launch([mlp_sum], (normed,))
    attended, d_mixed, qk_part, norm_row, mix_part = attention_call(
        first, count, states, mixed_t, d_att, mask_q, mask_k, head_gains, cotangent
    )
    mix_sum = ChainOverDp(mix_part, dp_size, dp)

    norm_vec = norm_row[0] + jnp.sum(up_row, axis=1)
    norm_parts = norm_vec.reshape(4, part)
    norm_parts = [lax.dynamic_index_in_dim(norm_parts, jnp.bitwise_xor(me, m), 0, False) for m in range(4)]
    short = ShortSums(
        jnp.stack([norm_parts[0], norm_parts[2]]),
        jnp.stack([norm_parts[1], norm_parts[3]]),
        jnp.concatenate([jnp.sum(qk_part, axis=1), jnp.sum(upbias_part, axis=1), jnp.sum(cot_sum, axis=1)]),
        dp_size,
    )

    runs = [(seq, 1) for seq in range(seqs)]
    scatters = []
    for begin, size in runs:
        busy = [f[0] for f in flying]
        along = [m for m in [mix_sum, mlp_sum, short] + scatters if m.more() and m not in busy]
        (att, dm), flights = launch(along, (attended, d_mixed))
        flying = flying + flights
        sent = project_call(
            shard, active, att, d_pre, dm, normed, down_t, attn_t, up_weight, mixed, gain_all, begin, size
        )
        late = [f for f in flights if begin == 0 and f[0] is mix_sum]
        keep, send = land([f for f in flying if f not in late], sent)
        flying = late
        scatters.append(ScatterOverMp(keep, send))

    finished = ()
    done = set()

    def finish_ready(finished):
        for (begin, _), scatter in zip(runs, scatters):
            if not scatter.more() and begin not in done:
                done.add(begin)
                finished = finish_call(
                    scatter.keep, scatter.from_core, scatter.from_y, own_t, cot_own, stats, gain_own, bias_col,
                    finished, begin,
                )
        return finished

    rounds = 0
    while True:
        busy = [f[0] for f in flying]
        rounds += 1
        ready = [m for m in [mix_sum] + scatters + [short, mlp_sum] if m.more() and m not in busy]
        ready = [m for m in ready if m is not mlp_sum or rounds > 1]
        finished, flights = launch(ready, finished)
        flying = flying + flights
        if not flying:
            break
        finished = finish_ready(finished)
        near = [f for f in flying if f[0] in scatters and len(f[0].bits) == 2]
        across = [f for f in flying if f[0] in scatters and len(f[0].bits) == 1]
        chain = [f for f in flying if f[0] is mix_sum]
        rest = [f for f in flying if f[0] is short]
        wide = [f for f in flying if f[0] is mlp_sum]
        left = len(mix_sum.steps)
        if near:
            now = near + chain + rest
        elif left == 2:
            now = chain + across[:1] + wide + rest
        elif left == 1:
            now = across + wide + rest + chain
        else:
            now = chain + rest or flying
        finished = land(now, finished)
        flying = [f for f in flying if f not in now]
    finished = finish_ready(finished)
    block_out, token_grad = finished
    block_out, token_grad = block_out.T, token_grad.T
    mixed_grad = mix_sum.keep.astype(F32)
    qkv_grad = jnp.transpose(mixed_grad[: 3 * part].reshape(3, part, width), (2, 0, 1))

    gain_grad = short.norm / norm_gain.astype(F32)
    rest = short.rest
    split = 2 * part + up_weight.shape[1]
    return (
        block_out,
        token_grad,
        gain_grad,
        qkv_grad,
        rest[: 2 * part].reshape(2, part),
        mixed_grad[3 * part :],
        mlp_sum.keep[up_weight.shape[1] :].astype(F32),
        rest[2 * part : split],
        mlp_sum.keep[: up_weight.shape[1]].astype(F32),
        rest[split:],
    )


def solution(mesh):
    in_specs = (
        P("dp", "mp"),
        P("dp", None),
        P("mp"),
        P(None, None, "mp"),
        P(None, "mp"),
        P("mp", None),
        P(None, "mp"),
        P("mp"),
        P("mp", None),
        P("mp"),
        P("dp", None),
    )
    out_specs = (
        P("dp", "mp"),
        P("dp", "mp"),
        P("mp"),
        P(None, None, "mp"),
        P(None, "mp"),
        P("mp", None),
        P(None, "mp"),
        P("mp"),
        P("mp", None),
        P("mp"),
    )
    run = functools.partial(body, mesh.shape["dp"])
    return jax.shard_map(run, mesh=mesh, in_specs=in_specs, out_specs=out_specs, check_vma=False)
```

```python
import functools

import jax
import jax.numpy as jnp
from jax import lax
from jax.experimental import pallas as pl
from jax.experimental.pallas import tpu as pltpu
from jax.sharding import PartitionSpec as P

DH = 64
LEN = 1024
EPSILON = 1e-06
IMAGE_SLOTS = 16
PENALTY = 1024.0
BI = 256
BJ = 256
SUM_ROWS = 16
F32 = jnp.float32
BF16 = jnp.bfloat16

NN = (((1,), (0,)), ((), ()))
NT = (((1,), (1,)), ((), ()))
ANY = pl.BlockSpec(memory_space=pl.ANY)


def dot(left, right, dims=NN):
    return lax.dot_general(left, right, dims, preferred_element_type=F32)


def fold_lanes(rows):
    total = rows[:, :128]
    for start in range(128, rows.shape[1], 128):
        total = total + rows[:, start : start + 128]
    return total


def cost(microseconds, nbytes):
    return pl.CostEstimate(flops=int(microseconds * 1e3), bytes_accessed=nbytes // 1000, transcendentals=0)


def early_kernel(cot, down, attn, pick, d_act, d_att, cot_own, bias_sum):
    rows = cot[...]
    d_act[...] = dot(down[...], rows, NT).astype(BF16)
    d_att[...] = dot(attn[...], rows, NT).astype(BF16)
    own = dot(pick[...], rows, NT)
    cot_own[...] = own.astype(BF16)

    @pl.when(pl.program_id(0) == 0)
    def _():
        bias_sum[...] = jnp.zeros_like(bias_sum)

    bias_sum[...] += fold_lanes(own)


def early_call(cot, down, attn, pick, block=512):
    tokens, width = cot.shape
    seqs = tokens // LEN
    hidden, part = down.shape[0], attn.shape[0]
    steps = LEN // block
    fixed = lambda i: (0, 0)
    by_seq = lambda i: (i // steps, 0, i % steps)
    return pl.pallas_call(
        early_kernel,
        grid=(tokens // block,),
        in_specs=[
            pl.BlockSpec((block, width), lambda i: (i, 0)),
            pl.BlockSpec((hidden, width), fixed),
            pl.BlockSpec((part, width), fixed),
            pl.BlockSpec((part, width), fixed),
        ],
        out_specs=[
            pl.BlockSpec((None, hidden, block), by_seq),
            pl.BlockSpec((None, part, block), by_seq),
            pl.BlockSpec((part, block), lambda i: (0, i)),
            pl.BlockSpec((part, 128), fixed),
        ],
        out_shape=[
            jax.ShapeDtypeStruct((seqs, hidden, LEN), BF16),
            jax.ShapeDtypeStruct((seqs, part, LEN), BF16),
            jax.ShapeDtypeStruct((part, tokens), BF16),
            jax.ShapeDtypeStruct((part, 128), F32),
        ],
        cost_estimate=cost(10, 12_000_000),
        name="early",
    )(cot, down, attn, pick)


def mlp_kernel(
    pieces_order, place, own, flip_y, flip_c, flip_cy, gain_own, gain_y, gain_c, gain_cy, up_t, up_bias, d_act, cot, up,
    normed, active, d_pre, stats, bias_sum, gain_all, up_row, grads, low, high
):
    pieces = (own, flip_y, flip_c, flip_cy)
    part = own.shape[0]
    width = part * 4
    first = pl.program_id(0) == 0
    last = pl.program_id(0) == pl.num_programs(0) - 1

    @pl.when(first)
    def _():
        bias_sum[...] = jnp.zeros_like(bias_sum)
        low[...] = jnp.zeros_like(low)
        high[...] = jnp.zeros_like(high)
        for slot, piece in enumerate((gain_own, gain_y, gain_c, gain_cy)):
            gain_all[pl.ds(pl.multiple_of(place[slot], part), part), :] = piece[...].astype(F32)

    total = 0.0
    squares = 0.0
    for piece in pieces:
        rows = piece[...].astype(F32)
        total = total + jnp.sum(rows, axis=0, keepdims=True)
        squares = squares + jnp.sum(rows * rows, axis=0, keepdims=True)
    mean = total * (1.0 / width)
    scale = lax.rsqrt(squares * (1.0 / width) - mean * mean + EPSILON)
    stats[0:1, :] = mean
    stats[1:2, :] = scale
    stats[2:8, :] = jnp.zeros((6, stats.shape[1]), F32)
    for slot, piece in enumerate(pieces):
        rows = piece[...].astype(F32)
        here = pl.ds(pl.multiple_of(place[slot], part), part)
        normed[here, :] = ((rows - mean) * scale * gain_all[here, :1]).astype(BF16)

    c0 = 0.7978845608028654
    c1 = 0.044715 * c0
    def lift(start):
        here = slice(start, start + 256)
        return dot(up_t[here, :], normed[...]) + up_bias[here, :1].astype(F32)

    ahead = lift(0)
    for start in range(0, up_t.shape[0], 256):
        here = slice(start, start + 256)
        pre = ahead
        if start + 256 < up_t.shape[0]:
            ahead = lift(start + 256)
        square = pre * pre
        half = 0.5 * jnp.tanh(pre * (c0 + c1 * square)) + 0.5
        act = (pre * half).astype(BF16)
        active[here, :] = act
        slope = half + pre * (half - half * half) * (2.0 * c0 + 6.0 * c1 * square)
        grad = (d_act[here, :].astype(F32) * slope).astype(BF16)
        d_pre[here, :] = grad
        bias_sum[here, :] += fold_lanes(grad.astype(F32))
        low[here, :] += dot(act, cot[...])
        high[:, here] += dot(normed[...], grad, NT)

    @pl.when(last)
    def _():
        up_row[...] = fold_lanes(high[...] * up[...].astype(F32))
        half = low.shape[0]
        size = grads.shape[0] // len(pieces_order)
        for slot, piece in enumerate(pieces_order):
            source, start = (low, piece * size) if piece * size < half else (high, piece * size - half)
            grads[slot * size : (slot + 1) * size, :] = source[start : start + size, :].astype(BF16)


def mlp_call(pieces_order, place, pieces, gains, up_t, up_bias, d_act, cot, up, block=512):
    part, tokens = pieces[0].shape
    width = 4 * part
    seqs, hidden, _ = d_act.shape
    steps = LEN // block
    lanes = lambda i, *_: (0, i)
    by_seq = lambda i, *_: (i // steps, 0, i % steps)
    fixed = lambda i, *_: (0, 0)
    grid_spec = pltpu.PrefetchScalarGridSpec(
        num_scalar_prefetch=1,
        grid=(tokens // block,),
        in_specs=[pl.BlockSpec((part, block), lanes)] * 4
        + [pl.BlockSpec((part, 128), fixed)] * 4
        + [
            pl.BlockSpec((hidden, width), fixed),
            pl.BlockSpec((hidden, 128), fixed),
            pl.BlockSpec((None, hidden, block), by_seq),
            pl.BlockSpec((block, width), lambda i, *_: (i, 0)),
            pl.BlockSpec((width, hidden), fixed),
        ],
        out_specs=[
            pl.BlockSpec((None, width, block), by_seq),
            pl.BlockSpec((None, hidden, block), by_seq),
            pl.BlockSpec((None, hidden, block), by_seq),
            pl.BlockSpec((8, block), lanes),
            pl.BlockSpec((hidden, 128), fixed),
            pl.BlockSpec((width, 128), fixed),
            pl.BlockSpec((width, 128), fixed),
            pl.BlockSpec((hidden + width, width), fixed),
        ],
        scratch_shapes=[pltpu.VMEM((hidden, width), F32), pltpu.VMEM((width, hidden), F32)],
    )
    assert hidden == width
    return pl.pallas_call(
        functools.partial(mlp_kernel, pieces_order),
        grid_spec=grid_spec,
        out_shape=[
            jax.ShapeDtypeStruct((seqs, width, LEN), BF16),
            jax.ShapeDtypeStruct((seqs, hidden, LEN), BF16),
            jax.ShapeDtypeStruct((seqs, hidden, LEN), BF16),
            jax.ShapeDtypeStruct((8, tokens), F32),
            jax.ShapeDtypeStruct((hidden, 128), F32),
            jax.ShapeDtypeStruct((width, 128), F32),
            jax.ShapeDtypeStruct((width, 128), F32),
            jax.ShapeDtypeStruct((hidden + width, width), BF16),
        ],
        cost_estimate=cost(20, 30_000_000),
        name="mlp",
    )(place, *pieces, *gains, up_t, up_bias, d_act, cot, up)


def attention_kernel(
    first, count, normed, mixed_t, d_att, mask_q, mask_k, gains, cot, attended, d_mixed, gain_sum, norm_row, grads,
    total, qkv, qx, kx, vn, kt, vt, es, ps, dqa, dka, dva
):
    seq = pl.program_id(0)
    last = seq == pl.num_programs(0) - 1
    part = attended.shape[0]
    heads = part // DH
    inv_dh = 1.0 / DH

    @pl.when(seq == 0)
    def _():
        total[...] = jnp.zeros_like(total)
        gain_sum[...] = jnp.zeros_like(gain_sum)

    qkv[...] = dot(mixed_t[...], normed[...])

    def unit(start):
        raw = qkv[start : start + DH, :]
        shifted = raw - jnp.sum(raw, axis=0, keepdims=True) * inv_dh
        scale = lax.rsqrt(jnp.sum(shifted * shifted, axis=0, keepdims=True) * inv_dh + EPSILON)
        return shifted * scale, scale

    zeros = jnp.zeros((128 - DH - IMAGE_SLOTS, LEN), BF16)
    for head in range(heads):
        rows = slice(head * DH, (head + 1) * DH)
        query, _ = unit(head * DH)
        query = (query * (gains[rows, :1] * 0.125)).astype(BF16)
        qx[head] = jnp.concatenate([query, mask_q[...], zeros], axis=0)
        key, _ = unit(part + head * DH)
        key = (key * gains[part + head * DH : part + (head + 1) * DH, :1]).astype(BF16)
        kt[rows, :] = key
        kx[head] = jnp.concatenate([key, mask_k[...], zeros], axis=0).T
        value = qkv[2 * part + head * DH : 2 * part + (head + 1) * DH, :].astype(BF16)
        vt[rows, :] = value
        vn[head] = value.T
    dka[...] = jnp.zeros_like(dka)
    dva[...] = jnp.zeros_like(dva)

    def straight(trips, i0, base):
        icols = pl.ds(i0, BI)
        places = [pl.ds(pl.multiple_of(base + j * BJ, 128), BJ) for j in range(trips)]

        def scores(head, j, sums):
            rows = slice(head * DH, (head + 1) * DH)
            e = jnp.exp(dot(kx[head, places[j], :], qx[head, :, icols]))
            p = dot(vn[head, places[j], :], d_att[rows, icols])
            es[head % 2, j * BJ : (j + 1) * BJ, :] = e
            ps[head % 2, j * BJ : (j + 1) * BJ, :] = p
            more = (jnp.sum(e, axis=0, keepdims=True), jnp.sum(e * p, axis=0, keepdims=True))
            return more if sums is None else (sums[0] + more[0], sums[1] + more[1])

        def row_grads(head, j, inverse, inner, held):
            rows = slice(head * DH, (head + 1) * DH)
            w = es[head % 2, j * BJ : (j + 1) * BJ, :] * inverse
            d = (w * (ps[head % 2, j * BJ : (j + 1) * BJ, :] - inner)).astype(BF16)
            w = w.astype(BF16)
            out = dot(vt[rows, places[j]], w)
            query = dot(kt[rows, places[j]], d)
            dva[rows, places[j]] += dot(d_att[rows, icols], w, NT)
            dka[rows, places[j]] += dot(qx[head, :DH, icols], d, NT)
            return (out, query) if held is None else (held[0] + out, held[1] + query)

        sums = None
        for j in range(trips):
            sums = scores(0, j, sums)
        for head in range(heads):
            rows = slice(head * DH, (head + 1) * DH)
            inverse = 1.0 / sums[0]
            inner = sums[1] * inverse
            held = following = None
            for j in range(trips):
                if head + 1 < heads:
                    following = scores(head + 1, j, following)
                held = row_grads(head, j, inverse, inner, held)
            attended[rows, icols] = held[0].astype(BF16)
            dqa[rows, icols] = held[1]
            sums = following

    def query_block(ib, _):
        i0 = pl.multiple_of(ib * BI, BI)
        base = first[seq * (LEN // BI) + ib] * 128
        trips = count[seq * (LEN // BI) + ib]
        for number in range(1, LEN // BJ + 1):
            pl.when(trips == number)(functools.partial(straight, number, i0, base))
        return 0

    lax.fori_loop(0, LEN // BI, query_block, 0)

    for source, offset, factor in ((dqa, 0, 0.125), (dka, part, 1.0)):
        for head in range(heads):
            start = offset + head * DH
            u, scale = unit(start)
            e = source[head * DH : (head + 1) * DH, :] * factor
            gain_sum[start : start + DH, :] += fold_lanes(e * u)
            f = e * gains[start : start + DH, :1]
            mean_f = jnp.sum(f, axis=0, keepdims=True) * inv_dh
            mean_fu = jnp.sum(f * u, axis=0, keepdims=True) * inv_dh
            d_mixed[start : start + DH, :] = ((f - mean_f - u * mean_fu) * scale).astype(BF16)
    d_mixed[2 * part :, :] = dva[...].astype(BF16)

    split = 3 * part
    total[:split, :] += dot(d_mixed[...], normed[...], NT)
    total[split:, :] += dot(attended[...], cot[...])

    @pl.when(last)
    def _():
        norm_row[...] = jnp.sum(total[:split, :] * mixed_t[...].astype(F32), axis=0, keepdims=True)
        grads[...] = total[...].astype(BF16)


def attention_call(first, count, normed, mixed_t, d_att, mask_q, mask_k, gains, cot):
    seqs, part, _ = d_att.shape
    width = normed.shape[1]
    heads = part // DH
    fixed = lambda i, *_: (0, 0)
    by_seq = lambda i, *_: (i, 0, 0)
    grid_spec = pltpu.PrefetchScalarGridSpec(
        num_scalar_prefetch=2,
        grid=(seqs,),
        in_specs=[
            pl.BlockSpec((None, width, LEN), by_seq),
            pl.BlockSpec((3 * part, width), fixed),
            pl.BlockSpec((None, part, LEN), by_seq),
            pl.BlockSpec((None, IMAGE_SLOTS, LEN), by_seq),
            pl.BlockSpec((None, IMAGE_SLOTS, LEN), by_seq),
            pl.BlockSpec((2 * part, 128), fixed),
            pl.BlockSpec((LEN, width), lambda i, *_: (i, 0)),
        ],
        out_specs=[
            pl.BlockSpec((None, part, LEN), by_seq),
            pl.BlockSpec((None, 3 * part, LEN), by_seq),
            pl.BlockSpec((2 * part, 128), fixed),
            pl.BlockSpec((1, width), fixed),
            pl.BlockSpec((4 * part, width), fixed),
        ],
        scratch_shapes=[
            pltpu.VMEM((4 * part, width), F32),
            pltpu.VMEM((3 * part, LEN), F32),
            pltpu.VMEM((heads, 128, LEN), BF16),
            pltpu.VMEM((heads, LEN, 128), BF16),
            pltpu.VMEM((heads, LEN, DH), BF16),
            pltpu.VMEM((part, LEN), BF16),
            pltpu.VMEM((part, LEN), BF16),
            pltpu.VMEM((2, LEN, BI), F32),
            pltpu.VMEM((2, LEN, BI), F32),
            pltpu.VMEM((part, LEN), F32),
            pltpu.VMEM((part, LEN), F32),
            pltpu.VMEM((part, LEN), F32),
        ],
    )
    return pl.pallas_call(
        attention_kernel,
        grid_spec=grid_spec,
        out_shape=[
            jax.ShapeDtypeStruct((seqs, part, LEN), BF16),
            jax.ShapeDtypeStruct((seqs, 3 * part, LEN), BF16),
            jax.ShapeDtypeStruct((2 * part, 128), F32),
            jax.ShapeDtypeStruct((1, width), F32),
            jax.ShapeDtypeStruct((4 * part, width), BF16),
        ],
        cost_estimate=cost(18, 5_000_000),
        name="attention",
    )(first, count, normed, mixed_t, d_att, mask_q, mask_k, gains, cot)


def project_kernel(
    shard, active, attended, d_pre, d_mixed, normed, down_t, attn_t, up, mixed, gain, keep, send
):
    me = shard[0]
    part = attended.shape[0]
    out = dot(down_t[...], active[...]) + dot(attn_t[...], attended[...])
    grad = dot(up[...], d_pre[...]) + dot(mixed[...], d_mixed[...])
    product = grad * normed[...].astype(F32)
    sums = []
    for row in (jnp.sum(grad * gain[:, :1], axis=0, keepdims=True), jnp.sum(product, axis=0, keepdims=True)):
        high = row.astype(BF16)
        sums += [high, (row - high.astype(F32)).astype(BF16)]
    sums = jnp.concatenate(sums + [jnp.zeros((SUM_ROWS - 4, sums[0].shape[1]), BF16)], axis=0)
    for target in (keep, send):
        for slot in range(2):
            target[slot, 2 * part :, :] = sums
    for index in range(4):
        rows = slice(index * part, (index + 1) * part)
        away = jnp.bitwise_xor(me, index)
        slot = away // 2

        @pl.when(away % 2 == 0)
        def _():
            keep[slot, :part, :] = out[rows].astype(BF16)
            keep[slot, part : 2 * part, :] = grad[rows].astype(BF16)

        @pl.when(away % 2 == 1)
        def _():
            send[slot, :part, :] = out[rows].astype(BF16)
            send[slot, part : 2 * part, :] = grad[rows].astype(BF16)


def project_call(shard, active, attended, d_pre, d_mixed, normed, down_t, attn_t, up, mixed, gain, begin, size, block=256):
    width, hidden = down_t.shape
    part = attended.shape[1]
    steps = LEN // block
    ours = lambda i, *_: (begin + i // steps, 0, i % steps)
    out = lambda i, *_: (i // steps, 0, 0, i % steps)
    fixed = lambda i, *_: (0, 0)
    rows = 2 * part + SUM_ROWS
    grid_spec = pltpu.PrefetchScalarGridSpec(
        num_scalar_prefetch=1,
        grid=(size * steps,),
        in_specs=[
            pl.BlockSpec((None, hidden, block), ours),
            pl.BlockSpec((None, part, block), ours),
            pl.BlockSpec((None, hidden, block), ours),
            pl.BlockSpec((None, 3 * part, block), ours),
            pl.BlockSpec((None, width, block), ours),
            pl.BlockSpec((width, hidden), fixed),
            pl.BlockSpec((width, part), fixed),
            pl.BlockSpec((width, hidden), fixed),
            pl.BlockSpec((width, 3 * part), fixed),
            pl.BlockSpec((width, 128), fixed),
        ],
        out_specs=[
            pl.BlockSpec((None, 2, rows, block), out),
            pl.BlockSpec((None, 2, rows, block), out),
        ],
    )
    return pl.pallas_call(
        project_kernel,
        grid_spec=grid_spec,
        out_shape=[
            jax.ShapeDtypeStruct((size, 2, rows, LEN), BF16),
            jax.ShapeDtypeStruct((size, 2, rows, LEN), BF16),
        ],
        cost_estimate=cost(8, 16_000_000),
        name="project",
    )(shard, active, attended, d_pre, d_mixed, normed, down_t, attn_t, up, mixed, gain)


def finish_kernel(keep, from_core, from_y, own_t, cot, stats, gain, bias, *rest):
    block_out, token_grad = rest[-2:]
    part = own_t.shape[0]
    inv_width = 0.25 / part
    total = keep[...].astype(F32) + from_core[...].astype(F32) + from_y[...].astype(F32)
    own = own_t[...].astype(F32)
    block_out[...] = (own + total[:part] + bias[:, :1].astype(F32)).astype(BF16)
    grad = total[part : 2 * part]
    sums = total[2 * part :]
    mean = stats[0:1, :]
    scale = stats[1:2, :]
    hat = (own - mean) * scale
    inner = grad * gain[:, :1].astype(F32) - (sums[0:1] + sums[1:2]) * inv_width - hat * ((sums[2:3] + sums[3:4]) * inv_width)
    token_grad[...] = cot[...].astype(F32) + inner * scale


def finish_call(keep, from_core, from_y, own_t, cot, stats, gain, bias, before, begin, block=512):
    part, tokens = own_t.shape
    steps = LEN // block
    size = keep.shape[0]
    fixed = lambda i: (0, 0)
    packed = pl.BlockSpec((None, None, 2 * part + SUM_ROWS, block), lambda i: (i // steps, 0, 0, i % steps))
    ours = lambda i: (0, begin * steps + i)
    here = pl.BlockSpec((part, block), ours)
    return pl.pallas_call(
        finish_kernel,
        grid=(size * steps,),
        in_specs=[
            packed, packed, packed,
            here, here,
            pl.BlockSpec((8, block), ours),
            pl.BlockSpec((part, 128), fixed),
            pl.BlockSpec((part, 128), fixed),
        ]
        + [ANY] * len(before),
        out_specs=[here, here],
        out_shape=[
            jax.ShapeDtypeStruct((part, tokens), BF16),
            jax.ShapeDtypeStruct((part, tokens), F32),
        ],
        input_output_aliases={8 + i: i for i in range(len(before))},
        cost_estimate=cost(3, 5_000_000),
        name="finish",
    )(keep, from_core, from_y, own_t, cot, stats, gain, bias, *before)


def flip(value, axis, size, bit):
    return lax.ppermute(value, axis, [(i, i ^ bit) for i in range(size)])


def tie(*trees):
    return lax.optimization_barrier(trees)


def piece_order(size):
    bits = size.bit_length() - 1
    return [sum(((i >> b) & 1) << (bits - 1 - b) for b in range(bits)) for i in range(size)]


class SumOverDp:
    def __init__(self, value, size, index):
        self.size, self.index = size, index
        self.send = value
        self.steps = ["sum"] + [1 << i for i in reversed(range(size.bit_length() - 1))]

    def more(self):
        return bool(self.steps)

    def move(self, send):
        if self.steps[0] == "sum":
            return lax.all_to_all(send, "dp", 0, 0, tiled=True)
        return flip(send, "dp", self.size, self.steps[0])

    def take(self, arrived):
        step = self.steps.pop(0)
        if step == "sum":
            shares = arrived.reshape(self.size, -1, arrived.shape[1]).astype(F32)
            self.keep = jnp.sum(shares, axis=0).astype(BF16)
        else:
            self.keep = jnp.where(
                (self.index & step) > 0,
                jnp.concatenate([arrived, self.keep], axis=0),
                jnp.concatenate([self.keep, arrived], axis=0),
            )
        self.send = self.keep


class ChainOverDp:
    def __init__(self, value, size, index):
        self.size, self.index = size, index
        bits = [1 << i for i in range(size.bit_length() - 1)]
        self.steps = [("sum", bit) for bit in bits] + [("join", bit) for bit in reversed(bits)]
        self.prepare(value, None)

    def prepare(self, held, arrived):
        def part(which, half):
            rows = lax.dynamic_slice_in_dim(held, which * half, half, 0)
            if arrived is None:
                return rows
            came = lax.dynamic_slice_in_dim(arrived, which * half, half, 0)
            return (rows.astype(F32) + came.astype(F32)).astype(BF16)

        rows = held.shape[0]
        if self.steps and self.steps[0][0] == "sum":
            side = ((self.index & self.steps[0][1]) > 0).astype(jnp.int32)
            self.send, self.keep = part(1 - side, rows // 2), part(side, rows // 2)
        else:
            self.keep = part(0, rows)
            self.send = self.keep

    def more(self):
        return bool(self.steps)

    def move(self, send):
        return flip(send, "dp", self.size, self.steps[0][1])

    def take(self, arrived):
        kind, bit = self.steps.pop(0)
        if kind == "sum":
            self.prepare(self.keep, arrived)
            return
        self.keep = jnp.where(
            (self.index & bit) > 0,
            jnp.concatenate([arrived, self.keep], axis=0),
            jnp.concatenate([self.keep, arrived], axis=0),
        )
        self.send = self.keep


class ScatterOverMp:
    def __init__(self, keep, send):
        self.keep, self.send = keep, send
        self.bits = [1, 2]

    def more(self):
        return bool(self.bits)

    def move(self, send):
        return flip(send, "mp", 4, self.bits[0])

    def take(self, arrived):
        bit = self.bits.pop(0)
        if bit == 1:
            self.from_core = arrived
            self.send = (self.keep[:, 1:].astype(F32) + arrived[:, 1:].astype(F32)).astype(BF16)
        else:
            self.from_y = arrived


class ShortSums:
    def __init__(self, keep, send, rest, size):
        self.keep, self.send, self.rest, self.size = keep, send, rest, size
        self.steps = [("mp", 1), ("mp", 2)] + [("dp", 1 << i) for i in range(size.bit_length() - 1)]

    def more(self):
        return bool(self.steps)

    def move(self, send):
        axis, bit = self.steps[0]
        return flip(send, axis, 4 if axis == "mp" else self.size, bit)

    def take(self, arrived):
        axis, bit = self.steps.pop(0)
        if (axis, bit) == ("mp", 1):
            both = self.keep + arrived
            self.norm, self.send = both[0], both[1]
            return
        if axis == "mp":
            self.send = jnp.concatenate([self.norm + arrived, self.rest])
        else:
            self.send = self.send + arrived
        size = self.norm.shape[0]
        self.norm, self.rest = self.send[:size], self.send[size:]


def launch(movers, inputs):
    movers = [m for m in movers if m.more()]
    inputs, sends = tie(inputs, [m.send for m in movers])
    return inputs, [(m, m.move(s)) for m, s in zip(movers, sends)]


def land(flights, outputs):
    outputs, arrivals = tie(outputs, [f[1] for f in flights])
    for (mover, _), arrived in zip(flights, arrivals):
        mover.take(arrived)
    return outputs


def body(
    dp_size,
    tokens,
    image_ids,
    norm_gain,
    qkv_weight,
    qk_gain,
    attn_weight,
    up_weight,
    up_bias,
    down_weight,
    down_bias,
    cotangent,
):
    part = tokens.shape[1]
    width = cotangent.shape[1]
    seqs = image_ids.shape[0]
    me = lax.axis_index("mp")
    dp = lax.axis_index("dp")
    shard = me.astype(jnp.int32)[None]
    place = jnp.bitwise_xor(shard, jnp.array([0, 2, 1, 3], jnp.int32)) * part

    own_t = tokens.T
    from_y = flip(own_t, "mp", 4, 2)
    gain_own = jnp.broadcast_to(norm_gain[:, None], (part, 128))
    gain_y = flip(gain_own, "mp", 4, 2)
    gain_c = flip(gain_own, "mp", 4, 1)

    mixed_t = jnp.transpose(qkv_weight, (1, 2, 0)).reshape(3 * part, width)
    mixed = mixed_t.T
    up_t = up_weight.T
    down_t = down_weight.T
    attn_t = attn_weight.T
    def column(vector):
        return jnp.broadcast_to(vector[:, None], (vector.shape[0], 128))

    up_bias_col = column(up_bias)
    head_gains = column(qk_gain.astype(F32).reshape(2 * part))

    slots = jnp.arange(IMAGE_SLOTS, dtype=jnp.int32)[None, :, None]
    same = image_ids[:, None, :] == slots
    mask_q = same.astype(BF16)
    mask_k = jnp.where(same | (slots >= 8), 0.0, -PENALTY).astype(BF16)
    block_first = image_ids[:, ::BI]
    block_last = image_ids[:, BI - 1 :: BI]
    starts = jnp.sum(image_ids[:, None, :] < block_first[:, :, None], axis=2, dtype=jnp.int32)
    ends = jnp.sum(image_ids[:, None, :] <= block_last[:, :, None], axis=2, dtype=jnp.int32)
    first = starts // 128
    count = ((ends + 127) // 128 - first + BJ // 128 - 1) // (BJ // 128)
    first = jnp.minimum(first, (LEN - count * BJ) // 128).reshape(-1)
    count = count.reshape(-1)

    pick = (jnp.arange(part)[:, None] + me * part == jnp.arange(width)[None, :]).astype(BF16)
    d_act, d_att, cot_own, cot_sum = early_call(cotangent, down_weight, attn_weight, pick)
    bias_col = column(down_bias)
    prepared = (
        d_act, d_att, mixed_t, mixed, up_t, down_t, attn_t, up_bias_col, head_gains, mask_q, mask_k, first, count,
        bias_col,
    )
    prepared, (from_y, gain_y, gain_c) = tie(prepared, (from_y, gain_y, gain_c))
    gains = (gain_own, gain_y, gain_c, flip(gain_y, "mp", 4, 1))
    (
        d_act, d_att, mixed_t, mixed, up_t, down_t, attn_t, up_bias_col, head_gains, mask_q, mask_k, first, count,
        bias_col,
    ) = prepared
    pieces = (own_t, from_y, flip(own_t, "mp", 4, 1), flip(from_y, "mp", 4, 1))
    normed, active, d_pre, stats, upbias_part, gain_all, up_row, mlp_part = mlp_call(
        tuple(piece_order(dp_size)), place, pieces, gains, up_t, up_bias_col, d_act, cotangent, up_weight
    )
    mlp_sum = SumOverDp(mlp_part, dp_size, dp)

    (states,), flying = launch([mlp_sum], (normed,))
    attended, d_mixed, qk_part, norm_row, mix_part = attention_call(
        first, count, states, mixed_t, d_att, mask_q, mask_k, head_gains, cotangent
    )
    mix_sum = ChainOverDp(mix_part, dp_size, dp)

    norm_vec = norm_row[0] + jnp.sum(up_row, axis=1)
    norm_parts = norm_vec.reshape(4, part)
    norm_parts = [lax.dynamic_index_in_dim(norm_parts, jnp.bitwise_xor(me, m), 0, False) for m in range(4)]
    short = ShortSums(
        jnp.stack([norm_parts[0], norm_parts[2]]),
        jnp.stack([norm_parts[1], norm_parts[3]]),
        jnp.concatenate([jnp.sum(qk_part, axis=1), jnp.sum(upbias_part, axis=1), jnp.sum(cot_sum, axis=1)]),
        dp_size,
    )

    runs = [(seq, 1) for seq in range(seqs)]
    scatters = []
    for begin, size in runs:
        busy = [f[0] for f in flying]
        along = [m for m in [mix_sum, mlp_sum, short] + scatters if m.more() and m not in busy]
        (att, dm), flights = launch(along, (attended, d_mixed))
        flying = flying + flights
        sent = project_call(
            shard, active, att, d_pre, dm, normed, down_t, attn_t, up_weight, mixed, gain_all, begin, size
        )
        late = [f for f in flights if begin == 0 and f[0] is mix_sum]
        keep, send = land([f for f in flying if f not in late], sent)
        flying = late
        scatters.append(ScatterOverMp(keep, send))

    finished = ()
    done = set()

    def finish_ready(finished):
        for (begin, _), scatter in zip(runs, scatters):
            if not scatter.more() and begin not in done:
                done.add(begin)
                finished = finish_call(
                    scatter.keep, scatter.from_core, scatter.from_y, own_t, cot_own, stats, gain_own, bias_col,
                    finished, begin,
                )
        return finished

    rounds = 0
    while True:
        busy = [f[0] for f in flying]
        rounds += 1
        ready = [m for m in [mix_sum] + scatters + [short, mlp_sum] if m.more() and m not in busy]
        ready = [m for m in ready if m is not mlp_sum or rounds > 1]
        finished, flights = launch(ready, finished)
        flying = flying + flights
        if not flying:
            break
        finished = finish_ready(finished)
        near = [f for f in flying if f[0] in scatters and len(f[0].bits) == 2]
        across = [f for f in flying if f[0] in scatters and len(f[0].bits) == 1]
        chain = [f for f in flying if f[0] is mix_sum]
        rest = [f for f in flying if f[0] is short]
        wide = [f for f in flying if f[0] is mlp_sum]
        left = len(mix_sum.steps)
        if near:
            now = near + chain + rest
        elif left == 2:
            now = chain + across[:1] + wide + rest
        elif left == 1:
            now = across + wide + rest + chain
        else:
            now = chain + rest or flying
        finished = land(now, finished)
        flying = [f for f in flying if f not in now]
    finished = finish_ready(finished)
    block_out, token_grad = finished
    block_out, token_grad = block_out.T, token_grad.T
    mixed_grad = mix_sum.keep.astype(F32)
    qkv_grad = jnp.transpose(mixed_grad[: 3 * part].reshape(3, part, width), (2, 0, 1))

    gain_grad = short.norm / norm_gain.astype(F32)
    rest = short.rest
    split = 2 * part + up_weight.shape[1]
    return (
        block_out,
        token_grad,
        gain_grad,
        qkv_grad,
        rest[: 2 * part].reshape(2, part),
        mixed_grad[3 * part :],
        mlp_sum.keep[up_weight.shape[1] :].astype(F32),
        rest[2 * part : split],
        mlp_sum.keep[: up_weight.shape[1]].astype(F32),
        rest[split:],
    )


def solution(mesh):
    in_specs = (
        P("dp", "mp"),
        P("dp", None),
        P("mp"),
        P(None, None, "mp"),
        P(None, "mp"),
        P("mp", None),
        P(None, "mp"),
        P("mp"),
        P("mp", None),
        P("mp"),
        P("dp", None),
    )
    out_specs = (
        P("dp", "mp"),
        P("dp", "mp"),
        P("mp"),
        P(None, None, "mp"),
        P(None, "mp"),
        P("mp", None),
        P(None, "mp"),
        P("mp"),
        P("mp", None),
        P("mp"),
    )
    run = functools.partial(body, mesh.shape["dp"])
    return jax.shard_map(run, mesh=mesh, in_specs=in_specs, out_specs=out_specs, check_vma=False)
```

```python
import functools

import jax
import jax.numpy as jnp
from jax import lax
from jax.experimental import pallas as pl
from jax.experimental.pallas import tpu as pltpu
from jax.sharding import PartitionSpec as P

DH = 64
LEN = 1024
EPSILON = 1e-06
IMAGE_SLOTS = 16
PENALTY = 1024.0
BI = 256
BJ = 256
SUM_ROWS = 16
F32 = jnp.float32
BF16 = jnp.bfloat16

NN = (((1,), (0,)), ((), ()))
NT = (((1,), (1,)), ((), ()))
ANY = pl.BlockSpec(memory_space=pl.ANY)


def dot(left, right, dims=NN):
    return lax.dot_general(left, right, dims, preferred_element_type=F32)


def fold_lanes(rows):
    total = rows[:, :128]
    for start in range(128, rows.shape[1], 128):
        total = total + rows[:, start : start + 128]
    return total


def cost(microseconds, nbytes):
    return pl.CostEstimate(flops=int(microseconds * 1e3), bytes_accessed=nbytes // 1000, transcendentals=0)


def early_kernel(cot, down, attn, pick, d_act, d_att, cot_own, bias_sum):
    rows = cot[...]
    d_act[...] = dot(down[...], rows, NT).astype(BF16)
    d_att[...] = dot(attn[...], rows, NT).astype(BF16)
    own = dot(pick[...], rows, NT)
    cot_own[...] = own.astype(BF16)

    @pl.when(pl.program_id(0) == 0)
    def _():
        bias_sum[...] = jnp.zeros_like(bias_sum)

    bias_sum[...] += fold_lanes(own)


def early_call(cot, down, attn, pick, block=512):
    tokens, width = cot.shape
    seqs = tokens // LEN
    hidden, part = down.shape[0], attn.shape[0]
    steps = LEN // block
    fixed = lambda i: (0, 0)
    by_seq = lambda i: (i // steps, 0, i % steps)
    return pl.pallas_call(
        early_kernel,
        grid=(tokens // block,),
        in_specs=[
            pl.BlockSpec((block, width), lambda i: (i, 0)),
            pl.BlockSpec((hidden, width), fixed),
            pl.BlockSpec((part, width), fixed),
            pl.BlockSpec((part, width), fixed),
        ],
        out_specs=[
            pl.BlockSpec((None, hidden, block), by_seq),
            pl.BlockSpec((None, part, block), by_seq),
            pl.BlockSpec((part, block), lambda i: (0, i)),
            pl.BlockSpec((part, 128), fixed),
        ],
        out_shape=[
            jax.ShapeDtypeStruct((seqs, hidden, LEN), BF16),
            jax.ShapeDtypeStruct((seqs, part, LEN), BF16),
            jax.ShapeDtypeStruct((part, tokens), BF16),
            jax.ShapeDtypeStruct((part, 128), F32),
        ],
        cost_estimate=cost(10, 12_000_000),
        name="early",
    )(cot, down, attn, pick)


def mlp_kernel(
    pieces_order, place, own, flip_y, flip_c, flip_cy, gain_own, gain_y, gain_c, gain_cy, up_t, up_bias, d_act, cot, up,
    normed, active, d_pre, stats, bias_sum, gain_all, up_row, grads, low, high
):
    pieces = (own, flip_y, flip_c, flip_cy)
    part = own.shape[0]
    width = part * 4
    first = pl.program_id(0) == 0
    last = pl.program_id(0) == pl.num_programs(0) - 1

    @pl.when(first)
    def _():
        bias_sum[...] = jnp.zeros_like(bias_sum)
        low[...] = jnp.zeros_like(low)
        high[...] = jnp.zeros_like(high)
        for slot, piece in enumerate((gain_own, gain_y, gain_c, gain_cy)):
            gain_all[pl.ds(pl.multiple_of(place[slot], part), part), :] = piece[...].astype(F32)

    total = 0.0
    squares = 0.0
    for piece in pieces:
        rows = piece[...].astype(F32)
        total = total + jnp.sum(rows, axis=0, keepdims=True)
        squares = squares + jnp.sum(rows * rows, axis=0, keepdims=True)
    mean = total * (1.0 / width)
    scale = lax.rsqrt(squares * (1.0 / width) - mean * mean + EPSILON)
    stats[0:1, :] = mean
    stats[1:2, :] = scale
    stats[2:8, :] = jnp.zeros((6, stats.shape[1]), F32)
    for slot, piece in enumerate(pieces):
        rows = piece[...].astype(F32)
        here = pl.ds(pl.multiple_of(place[slot], part), part)
        normed[here, :] = ((rows - mean) * scale * gain_all[here, :1]).astype(BF16)

    c0 = 0.7978845608028654
    c1 = 0.044715 * c0
    def lift(start):
        here = slice(start, start + 256)
        return dot(up_t[here, :], normed[...]) + up_bias[here, :1].astype(F32)

    ahead = lift(0)
    for start in range(0, up_t.shape[0], 256):
        here = slice(start, start + 256)
        pre = ahead
        if start + 256 < up_t.shape[0]:
            ahead = lift(start + 256)
        square = pre * pre
        half = 0.5 * jnp.tanh(pre * (c0 + c1 * square)) + 0.5
        act = (pre * half).astype(BF16)
        active[here, :] = act
        slope = half + pre * (half - half * half) * (2.0 * c0 + 6.0 * c1 * square)
        grad = (d_act[here, :].astype(F32) * slope).astype(BF16)
        d_pre[here, :] = grad
        bias_sum[here, :] += fold_lanes(grad.astype(F32))
        low[here, :] += dot(act, cot[...])
        high[:, here] += dot(normed[...], grad, NT)

    @pl.when(last)
    def _():
        up_row[...] = fold_lanes(high[...] * up[...].astype(F32))
        half = low.shape[0]
        size = grads.shape[0] // len(pieces_order)
        for slot, piece in enumerate(pieces_order):
            source, start = (low, piece * size) if piece * size < half else (high, piece * size - half)
            grads[slot * size : (slot + 1) * size, :] = source[start : start + size, :].astype(BF16)


def mlp_call(pieces_order, place, pieces, gains, up_t, up_bias, d_act, cot, up, block=512):
    part, tokens = pieces[0].shape
    width = 4 * part
    seqs, hidden, _ = d_act.shape
    steps = LEN // block
    lanes = lambda i, *_: (0, i)
    by_seq = lambda i, *_: (i // steps, 0, i % steps)
    fixed = lambda i, *_: (0, 0)
    grid_spec = pltpu.PrefetchScalarGridSpec(
        num_scalar_prefetch=1,
        grid=(tokens // block,),
        in_specs=[pl.BlockSpec((part, block), lanes)] * 4
        + [pl.BlockSpec((part, 128), fixed)] * 4
        + [
            pl.BlockSpec((hidden, width), fixed),
            pl.BlockSpec((hidden, 128), fixed),
            pl.BlockSpec((None, hidden, block), by_seq),
            pl.BlockSpec((block, width), lambda i, *_: (i, 0)),
            pl.BlockSpec((width, hidden), fixed),
        ],
        out_specs=[
            pl.BlockSpec((None, width, block), by_seq),
            pl.BlockSpec((None, hidden, block), by_seq),
            pl.BlockSpec((None, hidden, block), by_seq),
            pl.BlockSpec((8, block), lanes),
            pl.BlockSpec((hidden, 128), fixed),
            pl.BlockSpec((width, 128), fixed),
            pl.BlockSpec((width, 128), fixed),
            pl.BlockSpec((hidden + width, width), fixed),
        ],
        scratch_shapes=[pltpu.VMEM((hidden, width), F32), pltpu.VMEM((width, hidden), F32)],
    )
    assert hidden == width
    return pl.pallas_call(
        functools.partial(mlp_kernel, pieces_order),
        grid_spec=grid_spec,
        out_shape=[
            jax.ShapeDtypeStruct((seqs, width, LEN), BF16),
            jax.ShapeDtypeStruct((seqs, hidden, LEN), BF16),
            jax.ShapeDtypeStruct((seqs, hidden, LEN), BF16),
            jax.ShapeDtypeStruct((8, tokens), F32),
            jax.ShapeDtypeStruct((hidden, 128), F32),
            jax.ShapeDtypeStruct((width, 128), F32),
            jax.ShapeDtypeStruct((width, 128), F32),
            jax.ShapeDtypeStruct((hidden + width, width), BF16),
        ],
        cost_estimate=cost(20, 30_000_000),
        name="mlp",
    )(place, *pieces, *gains, up_t, up_bias, d_act, cot, up)


def attention_kernel(
    first, count, normed, mixed_t, d_att, mask_q, mask_k, gains, cot, attended, d_mixed, gain_sum, norm_row, grads,
    total, qkv, qx, kx, vn, kt, vt, es, ps, dqa, dka, dva
):
    seq = pl.program_id(0)
    last = seq == pl.num_programs(0) - 1
    part = attended.shape[0]
    heads = part // DH
    inv_dh = 1.0 / DH

    @pl.when(seq == 0)
    def _():
        total[...] = jnp.zeros_like(total)
        gain_sum[...] = jnp.zeros_like(gain_sum)

    qkv[...] = dot(mixed_t[...], normed[...])

    def unit(start):
        raw = qkv[start : start + DH, :]
        shifted = raw - jnp.sum(raw, axis=0, keepdims=True) * inv_dh
        scale = lax.rsqrt(jnp.sum(shifted * shifted, axis=0, keepdims=True) * inv_dh + EPSILON)
        return shifted * scale, scale

    zeros = jnp.zeros((128 - DH - IMAGE_SLOTS, LEN), BF16)
    for head in range(heads):
        rows = slice(head * DH, (head + 1) * DH)
        query, _ = unit(head * DH)
        query = (query * (gains[rows, :1] * 0.125)).astype(BF16)
        qx[head] = jnp.concatenate([query, mask_q[...], zeros], axis=0)
        key, _ = unit(part + head * DH)
        key = (key * gains[part + head * DH : part + (head + 1) * DH, :1]).astype(BF16)
        kt[rows, :] = key
        kx[head] = jnp.concatenate([key, mask_k[...], zeros], axis=0).T
        value = qkv[2 * part + head * DH : 2 * part + (head + 1) * DH, :].astype(BF16)
        vt[rows, :] = value
        vn[head] = value.T
    dka[...] = jnp.zeros_like(dka)
    dva[...] = jnp.zeros_like(dva)

    def straight(trips, i0, base):
        icols = pl.ds(i0, BI)
        places = [pl.ds(pl.multiple_of(base + j * BJ, 128), BJ) for j in range(trips)]

        def scores(head, j, sums):
            rows = slice(head * DH, (head + 1) * DH)
            e = jnp.exp(dot(kx[head, places[j], :], qx[head, :, icols]))
            p = dot(vn[head, places[j], :], d_att[rows, icols])
            es[head % 2, j * BJ : (j + 1) * BJ, :] = e
            ps[head % 2, j * BJ : (j + 1) * BJ, :] = p
            more = (jnp.sum(e, axis=0, keepdims=True), jnp.sum(e * p, axis=0, keepdims=True))
            return more if sums is None else (sums[0] + more[0], sums[1] + more[1])

        def row_grads(head, j, inverse, inner, held):
            rows = slice(head * DH, (head + 1) * DH)
            w = es[head % 2, j * BJ : (j + 1) * BJ, :] * inverse
            d = (w * (ps[head % 2, j * BJ : (j + 1) * BJ, :] - inner)).astype(BF16)
            w = w.astype(BF16)
            out = dot(vt[rows, places[j]], w)
            query = dot(kt[rows, places[j]], d)
            dva[rows, places[j]] += dot(d_att[rows, icols], w, NT)
            dka[rows, places[j]] += dot(qx[head, :DH, icols], d, NT)
            return (out, query) if held is None else (held[0] + out, held[1] + query)

        sums = None
        for j in range(trips):
            sums = scores(0, j, sums)
        for head in range(heads):
            rows = slice(head * DH, (head + 1) * DH)
            inverse = 1.0 / sums[0]
            inner = sums[1] * inverse
            held = following = None
            for j in range(trips):
                if head + 1 < heads:
                    following = scores(head + 1, j, following)
                held = row_grads(head, j, inverse, inner, held)
            attended[rows, icols] = held[0].astype(BF16)
            dqa[rows, icols] = held[1]
            sums = following

    def query_block(ib, _):
        i0 = pl.multiple_of(ib * BI, BI)
        base = first[seq * (LEN // BI) + ib] * 128
        trips = count[seq * (LEN // BI) + ib]
        for number in range(1, LEN // BJ + 1):
            pl.when(trips == number)(functools.partial(straight, number, i0, base))
        return 0

    lax.fori_loop(0, LEN // BI, query_block, 0)

    for source, offset, factor in ((dqa, 0, 0.125), (dka, part, 1.0)):
        for head in range(heads):
            start = offset + head * DH
            u, scale = unit(start)
            e = source[head * DH : (head + 1) * DH, :] * factor
            gain_sum[start : start + DH, :] += fold_lanes(e * u)
            f = e * gains[start : start + DH, :1]
            mean_f = jnp.sum(f, axis=0, keepdims=True) * inv_dh
            mean_fu = jnp.sum(f * u, axis=0, keepdims=True) * inv_dh
            d_mixed[start : start + DH, :] = ((f - mean_f - u * mean_fu) * scale).astype(BF16)
    d_mixed[2 * part :, :] = dva[...].astype(BF16)

    split = 3 * part
    total[:split, :] += dot(d_mixed[...], normed[...], NT)
    total[split:, :] += dot(attended[...], cot[...])

    @pl.when(last)
    def _():
        norm_row[...] = jnp.sum(total[:split, :] * mixed_t[...].astype(F32), axis=0, keepdims=True)
        grads[...] = total[...].astype(BF16)


def attention_call(first, count, normed, mixed_t, d_att, mask_q, mask_k, gains, cot):
    seqs, part, _ = d_att.shape
    width = normed.shape[1]
    heads = part // DH
    fixed = lambda i, *_: (0, 0)
    by_seq = lambda i, *_: (i, 0, 0)
    grid_spec = pltpu.PrefetchScalarGridSpec(
        num_scalar_prefetch=2,
        grid=(seqs,),
        in_specs=[
            pl.BlockSpec((None, width, LEN), by_seq),
            pl.BlockSpec((3 * part, width), fixed),
            pl.BlockSpec((None, part, LEN), by_seq),
            pl.BlockSpec((None, IMAGE_SLOTS, LEN), by_seq),
            pl.BlockSpec((None, IMAGE_SLOTS, LEN), by_seq),
            pl.BlockSpec((2 * part, 128), fixed),
            pl.BlockSpec((LEN, width), lambda i, *_: (i, 0)),
        ],
        out_specs=[
            pl.BlockSpec((None, part, LEN), by_seq),
            pl.BlockSpec((None, 3 * part, LEN), by_seq),
            pl.BlockSpec((2 * part, 128), fixed),
            pl.BlockSpec((1, width), fixed),
            pl.BlockSpec((4 * part, width), fixed),
        ],
        scratch_shapes=[
            pltpu.VMEM((4 * part, width), F32),
            pltpu.VMEM((3 * part, LEN), F32),
            pltpu.VMEM((heads, 128, LEN), BF16),
            pltpu.VMEM((heads, LEN, 128), BF16),
            pltpu.VMEM((heads, LEN, DH), BF16),
            pltpu.VMEM((part, LEN), BF16),
            pltpu.VMEM((part, LEN), BF16),
            pltpu.VMEM((2, LEN, BI), F32),
            pltpu.VMEM((2, LEN, BI), F32),
            pltpu.VMEM((part, LEN), F32),
            pltpu.VMEM((part, LEN), F32),
            pltpu.VMEM((part, LEN), F32),
        ],
    )
    return pl.pallas_call(
        attention_kernel,
        grid_spec=grid_spec,
        out_shape=[
            jax.ShapeDtypeStruct((seqs, part, LEN), BF16),
            jax.ShapeDtypeStruct((seqs, 3 * part, LEN), BF16),
            jax.ShapeDtypeStruct((2 * part, 128), F32),
            jax.ShapeDtypeStruct((1, width), F32),
            jax.ShapeDtypeStruct((4 * part, width), BF16),
        ],
        cost_estimate=cost(18, 5_000_000),
        name="attention",
    )(first, count, normed, mixed_t, d_att, mask_q, mask_k, gains, cot)


def project_kernel(
    shard, active, attended, d_pre, d_mixed, normed, down_t, attn_t, up, mixed, gain, keep, send
):
    me = shard[0]
    part = attended.shape[0]
    out = dot(down_t[...], active[...]) + dot(attn_t[...], attended[...])
    grad = dot(up[...], d_pre[...]) + dot(mixed[...], d_mixed[...])
    product = grad * normed[...].astype(F32)
    sums = []
    for row in (jnp.sum(grad * gain[:, :1], axis=0, keepdims=True), jnp.sum(product, axis=0, keepdims=True)):
        high = row.astype(BF16)
        sums += [high, (row - high.astype(F32)).astype(BF16)]
    sums = jnp.concatenate(sums + [jnp.zeros((SUM_ROWS - 4, sums[0].shape[1]), BF16)], axis=0)
    for target in (keep, send):
        for slot in range(2):
            target[slot, 2 * part :, :] = sums
    for index in range(4):
        rows = slice(index * part, (index + 1) * part)
        away = jnp.bitwise_xor(me, index)
        slot = away // 2

        @pl.when(away % 2 == 0)
        def _():
            keep[slot, :part, :] = out[rows].astype(BF16)
            keep[slot, part : 2 * part, :] = grad[rows].astype(BF16)

        @pl.when(away % 2 == 1)
        def _():
            send[slot, :part, :] = out[rows].astype(BF16)
            send[slot, part : 2 * part, :] = grad[rows].astype(BF16)


def project_call(shard, active, attended, d_pre, d_mixed, normed, down_t, attn_t, up, mixed, gain, begin, size, block=256):
    width, hidden = down_t.shape
    part = attended.shape[1]
    steps = LEN // block
    ours = lambda i, *_: (begin + i // steps, 0, i % steps)
    out = lambda i, *_: (i // steps, 0, 0, i % steps)
    fixed = lambda i, *_: (0, 0)
    rows = 2 * part + SUM_ROWS
    grid_spec = pltpu.PrefetchScalarGridSpec(
        num_scalar_prefetch=1,
        grid=(size * steps,),
        in_specs=[
            pl.BlockSpec((None, hidden, block), ours),
            pl.BlockSpec((None, part, block), ours),
            pl.BlockSpec((None, hidden, block), ours),
            pl.BlockSpec((None, 3 * part, block), ours),
            pl.BlockSpec((None, width, block), ours),
            pl.BlockSpec((width, hidden), fixed),
            pl.BlockSpec((width, part), fixed),
            pl.BlockSpec((width, hidden), fixed),
            pl.BlockSpec((width, 3 * part), fixed),
            pl.BlockSpec((width, 128), fixed),
        ],
        out_specs=[
            pl.BlockSpec((None, 2, rows, block), out),
            pl.BlockSpec((None, 2, rows, block), out),
        ],
    )
    return pl.pallas_call(
        project_kernel,
        grid_spec=grid_spec,
        out_shape=[
            jax.ShapeDtypeStruct((size, 2, rows, LEN), BF16),
            jax.ShapeDtypeStruct((size, 2, rows, LEN), BF16),
        ],
        cost_estimate=cost(8, 16_000_000),
        name="project",
    )(shard, active, attended, d_pre, d_mixed, normed, down_t, attn_t, up, mixed, gain)


def finish_kernel(keep, from_core, from_y, own_t, cot, stats, gain, bias, *rest):
    block_out, token_grad = rest[-2:]
    part = own_t.shape[0]
    inv_width = 0.25 / part
    total = keep[...].astype(F32) + from_core[...].astype(F32) + from_y[...].astype(F32)
    own = own_t[...].astype(F32)
    block_out[...] = (own + total[:part] + bias[:, :1].astype(F32)).astype(BF16)
    grad = total[part : 2 * part]
    sums = total[2 * part :]
    mean = stats[0:1, :]
    scale = stats[1:2, :]
    hat = (own - mean) * scale
    inner = grad * gain[:, :1].astype(F32) - (sums[0:1] + sums[1:2]) * inv_width - hat * ((sums[2:3] + sums[3:4]) * inv_width)
    token_grad[...] = cot[...].astype(F32) + inner * scale


def finish_call(keep, from_core, from_y, own_t, cot, stats, gain, bias, before, begin, block=256):
    part, tokens = own_t.shape
    steps = LEN // block
    size = keep.shape[0]
    fixed = lambda i: (0, 0)
    packed = pl.BlockSpec((None, None, 2 * part + SUM_ROWS, block), lambda i: (i // steps, 0, 0, i % steps))
    ours = lambda i: (0, begin * steps + i)
    here = pl.BlockSpec((part, block), ours)
    return pl.pallas_call(
        finish_kernel,
        grid=(size * steps,),
        in_specs=[
            packed, packed, packed,
            here, here,
            pl.BlockSpec((8, block), ours),
            pl.BlockSpec((part, 128), fixed),
            pl.BlockSpec((part, 128), fixed),
        ]
        + [ANY] * len(before),
        out_specs=[here, here],
        out_shape=[
            jax.ShapeDtypeStruct((part, tokens), BF16),
            jax.ShapeDtypeStruct((part, tokens), F32),
        ],
        input_output_aliases={8 + i: i for i in range(len(before))},
        cost_estimate=cost(3, 5_000_000),
        name="finish",
    )(keep, from_core, from_y, own_t, cot, stats, gain, bias, *before)


def flip(value, axis, size, bit):
    return lax.ppermute(value, axis, [(i, i ^ bit) for i in range(size)])


def tie(*trees):
    return lax.optimization_barrier(trees)


def piece_order(size):
    bits = size.bit_length() - 1
    return [sum(((i >> b) & 1) << (bits - 1 - b) for b in range(bits)) for i in range(size)]


class SumOverDp:
    def __init__(self, value, size, index):
        self.size, self.index = size, index
        self.send = value
        self.steps = ["sum"] + [1 << i for i in reversed(range(size.bit_length() - 1))]

    def more(self):
        return bool(self.steps)

    def move(self, send):
        if self.steps[0] == "sum":
            return lax.all_to_all(send, "dp", 0, 0, tiled=True)
        return flip(send, "dp", self.size, self.steps[0])

    def take(self, arrived):
        step = self.steps.pop(0)
        if step == "sum":
            shares = arrived.reshape(self.size, -1, arrived.shape[1]).astype(F32)
            self.keep = jnp.sum(shares, axis=0).astype(BF16)
        else:
            self.keep = jnp.where(
                (self.index & step) > 0,
                jnp.concatenate([arrived, self.keep], axis=0),
                jnp.concatenate([self.keep, arrived], axis=0),
            )
        self.send = self.keep


class ChainOverDp:
    def __init__(self, value, size, index):
        self.size, self.index = size, index
        bits = [1 << i for i in range(size.bit_length() - 1)]
        self.steps = [("sum", bit) for bit in bits] + [("join", bit) for bit in reversed(bits)]
        self.prepare(value, None)

    def prepare(self, held, arrived):
        def part(which, half):
            rows = lax.dynamic_slice_in_dim(held, which * half, half, 0)
            if arrived is None:
                return rows
            came = lax.dynamic_slice_in_dim(arrived, which * half, half, 0)
            return (rows.astype(F32) + came.astype(F32)).astype(BF16)

        rows = held.shape[0]
        if self.steps and self.steps[0][0] == "sum":
            side = ((self.index & self.steps[0][1]) > 0).astype(jnp.int32)
            self.send, self.keep = part(1 - side, rows // 2), part(side, rows // 2)
        else:
            self.keep = part(0, rows)
            self.send = self.keep

    def more(self):
        return bool(self.steps)

    def move(self, send):
        return flip(send, "dp", self.size, self.steps[0][1])

    def take(self, arrived):
        kind, bit = self.steps.pop(0)
        if kind == "sum":
            self.prepare(self.keep, arrived)
            return
        self.keep = jnp.where(
            (self.index & bit) > 0,
            jnp.concatenate([arrived, self.keep], axis=0),
            jnp.concatenate([self.keep, arrived], axis=0),
        )
        self.send = self.keep


class ScatterOverMp:
    def __init__(self, keep, send):
        self.keep, self.send = keep, send
        self.bits = [1, 2]

    def more(self):
        return bool(self.bits)

    def move(self, send):
        return flip(send, "mp", 4, self.bits[0])

    def take(self, arrived):
        bit = self.bits.pop(0)
        if bit == 1:
            self.from_core = arrived
            self.send = (self.keep[:, 1:].astype(F32) + arrived[:, 1:].astype(F32)).astype(BF16)
        else:
            self.from_y = arrived


class ShortSums:
    def __init__(self, keep, send, rest, size):
        self.keep, self.send, self.rest, self.size = keep, send, rest, size
        self.steps = [("mp", 1), ("mp", 2)] + [("dp", 1 << i) for i in range(size.bit_length() - 1)]

    def more(self):
        return bool(self.steps)

    def move(self, send):
        axis, bit = self.steps[0]
        return flip(send, axis, 4 if axis == "mp" else self.size, bit)

    def take(self, arrived):
        axis, bit = self.steps.pop(0)
        if (axis, bit) == ("mp", 1):
            both = self.keep + arrived
            self.norm, self.send = both[0], both[1]
            return
        if axis == "mp":
            self.send = jnp.concatenate([self.norm + arrived, self.rest])
        else:
            self.send = self.send + arrived
        size = self.norm.shape[0]
        self.norm, self.rest = self.send[:size], self.send[size:]


def launch(movers, inputs):
    movers = [m for m in movers if m.more()]
    inputs, sends = tie(inputs, [m.send for m in movers])
    return inputs, [(m, m.move(s)) for m, s in zip(movers, sends)]


def land(flights, outputs):
    outputs, arrivals = tie(outputs, [f[1] for f in flights])
    for (mover, _), arrived in zip(flights, arrivals):
        mover.take(arrived)
    return outputs


def body(
    dp_size,
    tokens,
    image_ids,
    norm_gain,
    qkv_weight,
    qk_gain,
    attn_weight,
    up_weight,
    up_bias,
    down_weight,
    down_bias,
    cotangent,
):
    part = tokens.shape[1]
    width = cotangent.shape[1]
    seqs = image_ids.shape[0]
    me = lax.axis_index("mp")
    dp = lax.axis_index("dp")
    shard = me.astype(jnp.int32)[None]
    place = jnp.bitwise_xor(shard, jnp.array([0, 2, 1, 3], jnp.int32)) * part

    own_t = tokens.T
    from_y = flip(own_t, "mp", 4, 2)
    gain_own = jnp.broadcast_to(norm_gain[:, None], (part, 128))
    gain_y = flip(gain_own, "mp", 4, 2)
    gain_c = flip(gain_own, "mp", 4, 1)

    mixed_t = jnp.transpose(qkv_weight, (1, 2, 0)).reshape(3 * part, width)
    mixed = mixed_t.T
    up_t = up_weight.T
    down_t = down_weight.T
    attn_t = attn_weight.T
    def column(vector):
        return jnp.broadcast_to(vector[:, None], (vector.shape[0], 128))

    up_bias_col = column(up_bias)
    head_gains = column(qk_gain.astype(F32).reshape(2 * part))

    slots = jnp.arange(IMAGE_SLOTS, dtype=jnp.int32)[None, :, None]
    same = image_ids[:, None, :] == slots
    mask_q = same.astype(BF16)
    mask_k = jnp.where(same | (slots >= 8), 0.0, -PENALTY).astype(BF16)
    block_first = image_ids[:, ::BI]
    block_last = image_ids[:, BI - 1 :: BI]
    starts = jnp.sum(image_ids[:, None, :] < block_first[:, :, None], axis=2, dtype=jnp.int32)
    ends = jnp.sum(image_ids[:, None, :] <= block_last[:, :, None], axis=2, dtype=jnp.int32)
    first = starts // 128
    count = ((ends + 127) // 128 - first + BJ // 128 - 1) // (BJ // 128)
    first = jnp.minimum(first, (LEN - count * BJ) // 128).reshape(-1)
    count = count.reshape(-1)

    pick = (jnp.arange(part)[:, None] + me * part == jnp.arange(width)[None, :]).astype(BF16)
    d_act, d_att, cot_own, cot_sum = early_call(cotangent, down_weight, attn_weight, pick)
    bias_col = column(down_bias)
    prepared = (
        d_act, d_att, mixed_t, mixed, up_t, down_t, attn_t, up_bias_col, head_gains, mask_q, mask_k, first, count,
        bias_col,
    )
    prepared, (from_y, gain_y, gain_c) = tie(prepared, (from_y, gain_y, gain_c))
    gains = (gain_own, gain_y, gain_c, flip(gain_y, "mp", 4, 1))
    (
        d_act, d_att, mixed_t, mixed, up_t, down_t, attn_t, up_bias_col, head_gains, mask_q, mask_k, first, count,
        bias_col,
    ) = prepared
    pieces = (own_t, from_y, flip(own_t, "mp", 4, 1), flip(from_y, "mp", 4, 1))
    normed, active, d_pre, stats, upbias_part, gain_all, up_row, mlp_part = mlp_call(
        tuple(piece_order(dp_size)), place, pieces, gains, up_t, up_bias_col, d_act, cotangent, up_weight
    )
    mlp_sum = SumOverDp(mlp_part, dp_size, dp)

    (states,), flying = launch([mlp_sum], (normed,))
    attended, d_mixed, qk_part, norm_row, mix_part = attention_call(
        first, count, states, mixed_t, d_att, mask_q, mask_k, head_gains, cotangent
    )
    mix_sum = ChainOverDp(mix_part, dp_size, dp)

    norm_vec = norm_row[0] + jnp.sum(up_row, axis=1)
    norm_parts = norm_vec.reshape(4, part)
    norm_parts = [lax.dynamic_index_in_dim(norm_parts, jnp.bitwise_xor(me, m), 0, False) for m in range(4)]
    short = ShortSums(
        jnp.stack([norm_parts[0], norm_parts[2]]),
        jnp.stack([norm_parts[1], norm_parts[3]]),
        jnp.concatenate([jnp.sum(qk_part, axis=1), jnp.sum(upbias_part, axis=1), jnp.sum(cot_sum, axis=1)]),
        dp_size,
    )

    runs = [(seq, 1) for seq in range(seqs)]
    scatters = []
    for begin, size in runs:
        busy = [f[0] for f in flying]
        along = [m for m in [mix_sum, mlp_sum, short] + scatters if m.more() and m not in busy]
        (att, dm), flights = launch(along, (attended, d_mixed))
        flying = flying + flights
        sent = project_call(
            shard, active, att, d_pre, dm, normed, down_t, attn_t, up_weight, mixed, gain_all, begin, size
        )
        late = [f for f in flights if begin == 0 and f[0] is mix_sum]
        keep, send = land([f for f in flying if f not in late], sent)
        flying = late
        scatters.append(ScatterOverMp(keep, send))

    finished = ()
    wide_grads = ()
    done = set()

    def finish_ready(finished):
        for (begin, _), scatter in zip(runs, scatters):
            if not scatter.more() and begin not in done:
                done.add(begin)
                finished = finish_call(
                    scatter.keep, scatter.from_core, scatter.from_y, own_t, cot_own, stats, gain_own, bias_col,
                    finished, begin,
                )
        return finished

    while True:
        busy = [f[0] for f in flying]
        ready = [m for m in [mix_sum] + scatters + [short, mlp_sum] if m.more() and m not in busy]
        finished, flights = launch(ready, finished)
        flying = flying + flights
        if not flying:
            break
        finished = finish_ready(finished)
        near = [f for f in flying if f[0] in scatters and len(f[0].bits) == 2]
        across = [f for f in flying if f[0] in scatters and len(f[0].bits) == 1]
        chain = [f for f in flying if f[0] is mix_sum]
        rest = [f for f in flying if f[0] is short]
        wide = [f for f in flying if f[0] is mlp_sum]
        left = len(mix_sum.steps)
        if near:
            now = near + chain + rest
        elif left == 2:
            now = chain + across[:1] + wide + rest
        elif left == 1:
            now = across + wide + rest or chain
        else:
            now = chain + rest or flying
        finished, wide_grads = land(now, (finished, wide_grads))
        flying = [f for f in flying if f not in now]
        if not mlp_sum.more() and not wide_grads:
            split = up_weight.shape[1]
            wide_grads = (mlp_sum.keep[:split].astype(F32), mlp_sum.keep[split:].astype(F32))
    finished = finish_ready(finished)
    block_out, token_grad = finished
    block_out, token_grad = block_out.T, token_grad.T
    mixed_grad = mix_sum.keep.astype(F32)
    qkv_grad = jnp.transpose(mixed_grad[: 3 * part].reshape(3, part, width), (2, 0, 1))

    gain_grad = short.norm / norm_gain.astype(F32)
    rest = short.rest
    split = 2 * part + up_weight.shape[1]
    return (
        block_out,
        token_grad,
        gain_grad,
        qkv_grad,
        rest[: 2 * part].reshape(2, part),
        mixed_grad[3 * part :],
        wide_grads[1],
        rest[2 * part : split],
        wide_grads[0],
        rest[split:],
    )


def solution(mesh):
    in_specs = (
        P("dp", "mp"),
        P("dp", None),
        P("mp"),
        P(None, None, "mp"),
        P(None, "mp"),
        P("mp", None),
        P(None, "mp"),
        P("mp"),
        P("mp", None),
        P("mp"),
        P("dp", None),
    )
    out_specs = (
        P("dp", "mp"),
        P("dp", "mp"),
        P("mp"),
        P(None, None, "mp"),
        P(None, "mp"),
        P("mp", None),
        P(None, "mp"),
        P("mp"),
        P("mp", None),
        P("mp"),
    )
    run = functools.partial(body, mesh.shape["dp"])
    return jax.shard_map(run, mesh=mesh, in_specs=in_specs, out_specs=out_specs, check_vma=False)
```

```python
import functools

import jax
import jax.numpy as jnp
from jax import lax
from jax.experimental import pallas as pl
from jax.experimental.pallas import tpu as pltpu
from jax.sharding import PartitionSpec as P

DH = 64
LEN = 1024
EPSILON = 1e-06
IMAGE_SLOTS = 16
PENALTY = 1024.0
BI = 256
BJ = 256
SUM_ROWS = 16
F32 = jnp.float32
BF16 = jnp.bfloat16

NN = (((1,), (0,)), ((), ()))
NT = (((1,), (1,)), ((), ()))
ANY = pl.BlockSpec(memory_space=pl.ANY)


def dot(left, right, dims=NN):
    return lax.dot_general(left, right, dims, preferred_element_type=F32)


def fold_lanes(rows):
    total = rows[:, :128]
    for start in range(128, rows.shape[1], 128):
        total = total + rows[:, start : start + 128]
    return total


def cost(microseconds, nbytes):
    return pl.CostEstimate(flops=int(microseconds * 1e3), bytes_accessed=nbytes // 1000, transcendentals=0)


def early_kernel(cot, down, attn, pick, d_act, d_att, cot_own, bias_sum):
    rows = cot[...]
    d_act[...] = dot(down[...], rows, NT).astype(BF16)
    d_att[...] = dot(attn[...], rows, NT).astype(BF16)
    own = dot(pick[...], rows, NT)
    cot_own[...] = own.astype(BF16)

    @pl.when(pl.program_id(0) == 0)
    def _():
        bias_sum[...] = jnp.zeros_like(bias_sum)

    bias_sum[...] += fold_lanes(own)


def early_call(cot, down, attn, pick, block=512):
    tokens, width = cot.shape
    seqs = tokens // LEN
    hidden, part = down.shape[0], attn.shape[0]
    steps = LEN // block
    fixed = lambda i: (0, 0)
    by_seq = lambda i: (i // steps, 0, i % steps)
    return pl.pallas_call(
        early_kernel,
        grid=(tokens // block,),
        in_specs=[
            pl.BlockSpec((block, width), lambda i: (i, 0)),
            pl.BlockSpec((hidden, width), fixed),
            pl.BlockSpec((part, width), fixed),
            pl.BlockSpec((part, width), fixed),
        ],
        out_specs=[
            pl.BlockSpec((None, hidden, block), by_seq),
            pl.BlockSpec((None, part, block), by_seq),
            pl.BlockSpec((part, block), lambda i: (0, i)),
            pl.BlockSpec((part, 128), fixed),
        ],
        out_shape=[
            jax.ShapeDtypeStruct((seqs, hidden, LEN), BF16),
            jax.ShapeDtypeStruct((seqs, part, LEN), BF16),
            jax.ShapeDtypeStruct((part, tokens), BF16),
            jax.ShapeDtypeStruct((part, 128), F32),
        ],
        cost_estimate=cost(10, 12_000_000),
        name="early",
    )(cot, down, attn, pick)


def mlp_kernel(
    pieces_order, opening, closing, place, own, flip_y, flip_c, flip_cy, gain_own, gain_y, gain_c, gain_cy, up_t, up_bias,
    d_act, cot, *rest
):
    if closing:
        up, rest = rest[0], rest[1:]
    if not opening:
        held, rest = rest[4:6], rest[6:]
    normed, active, d_pre, stats, bias_sum, gain_all, *rest = rest
    if closing:
        up_row, grads, low, high, low_sem, high_sem = rest
    else:
        low, high = rest
    pieces = (own, flip_y, flip_c, flip_cy)
    part = own.shape[0]
    width = part * 4
    first = pl.program_id(0) == 0
    last = pl.program_id(0) == pl.num_programs(0) - 1
    copies = []
    if not opening:
        copies = [
            pltpu.make_async_copy(held[0], low, low_sem),
            pltpu.make_async_copy(held[1], high, high_sem),
        ]

    @pl.when(first)
    def _():
        for copy in copies:
            copy.start()
        bias_sum[...] = jnp.zeros_like(bias_sum)
        if opening:
            low[...] = jnp.zeros_like(low)
            high[...] = jnp.zeros_like(high)
        for slot, piece in enumerate((gain_own, gain_y, gain_c, gain_cy)):
            gain_all[pl.ds(pl.multiple_of(place[slot], part), part), :] = piece[...].astype(F32)

    total = 0.0
    squares = 0.0
    for piece in pieces:
        rows = piece[...].astype(F32)
        total = total + jnp.sum(rows, axis=0, keepdims=True)
        squares = squares + jnp.sum(rows * rows, axis=0, keepdims=True)
    mean = total * (1.0 / width)
    scale = lax.rsqrt(squares * (1.0 / width) - mean * mean + EPSILON)
    stats[0:1, :] = mean
    stats[1:2, :] = scale
    stats[2:8, :] = jnp.zeros((6, stats.shape[1]), F32)
    for slot, piece in enumerate(pieces):
        rows = piece[...].astype(F32)
        here = pl.ds(pl.multiple_of(place[slot], part), part)
        normed[here, :] = ((rows - mean) * scale * gain_all[here, :1]).astype(BF16)

    c0 = 0.7978845608028654
    c1 = 0.044715 * c0
    def lift(start):
        here = slice(start, start + 256)
        return dot(up_t[here, :], normed[...]) + up_bias[here, :1].astype(F32)

    ahead = lift(0)
    if copies:

        @pl.when(first)
        def _():
            for copy in copies:
                copy.wait()

    for start in range(0, up_t.shape[0], 256):
        here = slice(start, start + 256)
        pre = ahead
        if start + 256 < up_t.shape[0]:
            ahead = lift(start + 256)
        square = pre * pre
        half = 0.5 * jnp.tanh(pre * (c0 + c1 * square)) + 0.5
        act = (pre * half).astype(BF16)
        active[here, :] = act
        slope = half + pre * (half - half * half) * (2.0 * c0 + 6.0 * c1 * square)
        grad = (d_act[here, :].astype(F32) * slope).astype(BF16)
        d_pre[here, :] = grad
        bias_sum[here, :] += fold_lanes(grad.astype(F32))
        low[here, :] += dot(act, cot[...])
        high[:, here] += dot(normed[...], grad, NT)

    if not closing:
        return

    @pl.when(last)
    def _():
        up_row[...] = fold_lanes(high[...] * up[...].astype(F32))
        half = low.shape[0]
        size = grads.shape[0] // len(pieces_order)
        for slot, piece in enumerate(pieces_order):
            source, start = (low, piece * size) if piece * size < half else (high, piece * size - half)
            grads[slot * size : (slot + 1) * size, :] = source[start : start + size, :].astype(BF16)


def mlp_call(pieces_order, place, pieces, gains, up_t, up_bias, d_act, cot, up, before, held, begin, block=512):
    part = pieces[0].shape[0]
    width = 4 * part
    seqs, hidden, _ = d_act.shape
    assert hidden == width
    steps = LEN // block
    grid = pieces[0].shape[1] // block
    opening = begin == 0
    closing = begin + grid // steps == seqs
    lanes = lambda i, *_: (0, i)
    tokens = lambda i, *_: (0, begin * steps + i)
    by_seq = lambda i, *_: (begin + i // steps, 0, i % steps)
    fixed = lambda i, *_: (0, 0)
    square = jax.ShapeDtypeStruct((hidden, width), F32)
    in_specs = (
        [pl.BlockSpec((part, block), lanes)] * 4
        + [pl.BlockSpec((part, 128), fixed)] * 4
        + [
            pl.BlockSpec((hidden, width), fixed),
            pl.BlockSpec((hidden, 128), fixed),
            pl.BlockSpec((None, hidden, block), by_seq),
            pl.BlockSpec((block, width), lambda i, *_: (begin * steps + i, 0)),
        ]
        + ([pl.BlockSpec((width, hidden), fixed)] if closing else [])
    )
    out_specs = [
        pl.BlockSpec((None, width, block), by_seq),
        pl.BlockSpec((None, hidden, block), by_seq),
        pl.BlockSpec((None, hidden, block), by_seq),
        pl.BlockSpec((8, block), tokens),
        pl.BlockSpec((hidden, 128), fixed),
        pl.BlockSpec((width, 128), fixed),
    ]
    out_shape = [
        jax.ShapeDtypeStruct((seqs, width, LEN), BF16),
        jax.ShapeDtypeStruct((seqs, hidden, LEN), BF16),
        jax.ShapeDtypeStruct((seqs, hidden, LEN), BF16),
        jax.ShapeDtypeStruct((8, seqs * LEN), F32),
        jax.ShapeDtypeStruct((hidden, 128), F32),
        jax.ShapeDtypeStruct((width, 128), F32),
    ]
    scratch = []
    if closing:
        out_specs += [pl.BlockSpec((width, 128), fixed), pl.BlockSpec((hidden + width, width), fixed)]
        out_shape += [
            jax.ShapeDtypeStruct((width, 128), F32),
            jax.ShapeDtypeStruct((hidden + width, width), BF16),
        ]
        scratch = [pltpu.VMEM(square.shape, F32)] * 2 + [pltpu.SemaphoreType.DMA(())] * 2
    else:
        out_specs += [pl.BlockSpec(square.shape, fixed)] * 2
        out_shape += [square] * 2
    extra = [*before, *held]
    grid_spec = pltpu.PrefetchScalarGridSpec(
        num_scalar_prefetch=1,
        grid=(grid,),
        in_specs=in_specs + [ANY] * len(extra),
        out_specs=out_specs,
        scratch_shapes=scratch,
    )
    start = 1 + len(in_specs)
    return pl.pallas_call(
        functools.partial(mlp_kernel, pieces_order, opening, closing),
        grid_spec=grid_spec,
        out_shape=out_shape,
        input_output_aliases={start + i: i for i in range(len(before))},
        cost_estimate=cost(20, 30_000_000),
        name="mlp",
    )(place, *pieces, *gains, up_t, up_bias, d_act, cot, *([up] if closing else []), *extra)


def attention_kernel(
    first, count, normed, mixed_t, d_att, mask_q, mask_k, gains, cot, attended, d_mixed, gain_sum, norm_row, grads,
    total, qkv, qx, kx, vn, kt, vt, es, ps, dqa, dka, dva
):
    seq = pl.program_id(0)
    last = seq == pl.num_programs(0) - 1
    part = attended.shape[0]
    heads = part // DH
    inv_dh = 1.0 / DH

    @pl.when(seq == 0)
    def _():
        total[...] = jnp.zeros_like(total)
        gain_sum[...] = jnp.zeros_like(gain_sum)

    qkv[...] = dot(mixed_t[...], normed[...])

    def unit(start):
        raw = qkv[start : start + DH, :]
        shifted = raw - jnp.sum(raw, axis=0, keepdims=True) * inv_dh
        scale = lax.rsqrt(jnp.sum(shifted * shifted, axis=0, keepdims=True) * inv_dh + EPSILON)
        return shifted * scale, scale

    zeros = jnp.zeros((128 - DH - IMAGE_SLOTS, LEN), BF16)
    for head in range(heads):
        rows = slice(head * DH, (head + 1) * DH)
        query, _ = unit(head * DH)
        query = (query * (gains[rows, :1] * 0.125)).astype(BF16)
        qx[head] = jnp.concatenate([query, mask_q[...], zeros], axis=0)
        key, _ = unit(part + head * DH)
        key = (key * gains[part + head * DH : part + (head + 1) * DH, :1]).astype(BF16)
        kt[rows, :] = key
        kx[head] = jnp.concatenate([key, mask_k[...], zeros], axis=0).T
        value = qkv[2 * part + head * DH : 2 * part + (head + 1) * DH, :].astype(BF16)
        vt[rows, :] = value
        vn[head] = value.T
    dka[...] = jnp.zeros_like(dka)
    dva[...] = jnp.zeros_like(dva)

    def straight(trips, i0, base):
        icols = pl.ds(i0, BI)
        places = [pl.ds(pl.multiple_of(base + j * BJ, 128), BJ) for j in range(trips)]

        def scores(head, j, sums):
            rows = slice(head * DH, (head + 1) * DH)
            e = jnp.exp(dot(kx[head, places[j], :], qx[head, :, icols]))
            p = dot(vn[head, places[j], :], d_att[rows, icols])
            es[head % 2, j * BJ : (j + 1) * BJ, :] = e
            ps[head % 2, j * BJ : (j + 1) * BJ, :] = p
            more = (jnp.sum(e, axis=0, keepdims=True), jnp.sum(e * p, axis=0, keepdims=True))
            return more if sums is None else (sums[0] + more[0], sums[1] + more[1])

        def row_grads(head, j, inverse, inner, held):
            rows = slice(head * DH, (head + 1) * DH)
            w = es[head % 2, j * BJ : (j + 1) * BJ, :] * inverse
            d = (w * (ps[head % 2, j * BJ : (j + 1) * BJ, :] - inner)).astype(BF16)
            w = w.astype(BF16)
            out = dot(vt[rows, places[j]], w)
            query = dot(kt[rows, places[j]], d)
            dva[rows, places[j]] += dot(d_att[rows, icols], w, NT)
            dka[rows, places[j]] += dot(qx[head, :DH, icols], d, NT)
            return (out, query) if held is None else (held[0] + out, held[1] + query)

        sums = None
        for j in range(trips):
            sums = scores(0, j, sums)
        for head in range(heads):
            rows = slice(head * DH, (head + 1) * DH)
            inverse = 1.0 / sums[0]
            inner = sums[1] * inverse
            held = following = None
            for j in range(trips):
                if head + 1 < heads:
                    following = scores(head + 1, j, following)
                held = row_grads(head, j, inverse, inner, held)
            attended[rows, icols] = held[0].astype(BF16)
            dqa[rows, icols] = held[1]
            sums = following

    def query_block(ib, _):
        i0 = pl.multiple_of(ib * BI, BI)
        base = first[seq * (LEN // BI) + ib] * 128
        trips = count[seq * (LEN // BI) + ib]
        for number in range(1, LEN // BJ + 1):
            pl.when(trips == number)(functools.partial(straight, number, i0, base))
        return 0

    lax.fori_loop(0, LEN // BI, query_block, 0)

    for source, offset, factor in ((dqa, 0, 0.125), (dka, part, 1.0)):
        for head in range(heads):
            start = offset + head * DH
            u, scale = unit(start)
            e = source[head * DH : (head + 1) * DH, :] * factor
            gain_sum[start : start + DH, :] += fold_lanes(e * u)
            f = e * gains[start : start + DH, :1]
            mean_f = jnp.sum(f, axis=0, keepdims=True) * inv_dh
            mean_fu = jnp.sum(f * u, axis=0, keepdims=True) * inv_dh
            d_mixed[start : start + DH, :] = ((f - mean_f - u * mean_fu) * scale).astype(BF16)
    d_mixed[2 * part :, :] = dva[...].astype(BF16)

    split = 3 * part
    total[:split, :] += dot(d_mixed[...], normed[...], NT)
    total[split:, :] += dot(attended[...], cot[...])

    @pl.when(last)
    def _():
        norm_row[...] = jnp.sum(total[:split, :] * mixed_t[...].astype(F32), axis=0, keepdims=True)
        grads[...] = total[...].astype(BF16)


def attention_call(first, count, normed, mixed_t, d_att, mask_q, mask_k, gains, cot):
    seqs, part, _ = d_att.shape
    width = normed.shape[1]
    heads = part // DH
    fixed = lambda i, *_: (0, 0)
    by_seq = lambda i, *_: (i, 0, 0)
    grid_spec = pltpu.PrefetchScalarGridSpec(
        num_scalar_prefetch=2,
        grid=(seqs,),
        in_specs=[
            pl.BlockSpec((None, width, LEN), by_seq),
            pl.BlockSpec((3 * part, width), fixed),
            pl.BlockSpec((None, part, LEN), by_seq),
            pl.BlockSpec((None, IMAGE_SLOTS, LEN), by_seq),
            pl.BlockSpec((None, IMAGE_SLOTS, LEN), by_seq),
            pl.BlockSpec((2 * part, 128), fixed),
            pl.BlockSpec((LEN, width), lambda i, *_: (i, 0)),
        ],
        out_specs=[
            pl.BlockSpec((None, part, LEN), by_seq),
            pl.BlockSpec((None, 3 * part, LEN), by_seq),
            pl.BlockSpec((2 * part, 128), fixed),
            pl.BlockSpec((1, width), fixed),
            pl.BlockSpec((4 * part, width), fixed),
        ],
        scratch_shapes=[
            pltpu.VMEM((4 * part, width), F32),
            pltpu.VMEM((3 * part, LEN), F32),
            pltpu.VMEM((heads, 128, LEN), BF16),
            pltpu.VMEM((heads, LEN, 128), BF16),
            pltpu.VMEM((heads, LEN, DH), BF16),
            pltpu.VMEM((part, LEN), BF16),
            pltpu.VMEM((part, LEN), BF16),
            pltpu.VMEM((2, LEN, BI), F32),
            pltpu.VMEM((2, LEN, BI), F32),
            pltpu.VMEM((part, LEN), F32),
            pltpu.VMEM((part, LEN), F32),
            pltpu.VMEM((part, LEN), F32),
        ],
    )
    return pl.pallas_call(
        attention_kernel,
        grid_spec=grid_spec,
        out_shape=[
            jax.ShapeDtypeStruct((seqs, part, LEN), BF16),
            jax.ShapeDtypeStruct((seqs, 3 * part, LEN), BF16),
            jax.ShapeDtypeStruct((2 * part, 128), F32),
            jax.ShapeDtypeStruct((1, width), F32),
            jax.ShapeDtypeStruct((4 * part, width), BF16),
        ],
        cost_estimate=cost(18, 5_000_000),
        name="attention",
    )(first, count, normed, mixed_t, d_att, mask_q, mask_k, gains, cot)


def project_kernel(
    shard, active, attended, d_pre, d_mixed, normed, down_t, attn_t, up, mixed, gain, keep, send
):
    me = shard[0]
    part = attended.shape[0]
    out = dot(down_t[...], active[...]) + dot(attn_t[...], attended[...])
    grad = dot(up[...], d_pre[...]) + dot(mixed[...], d_mixed[...])
    product = grad * normed[...].astype(F32)
    sums = []
    for row in (jnp.sum(grad * gain[:, :1], axis=0, keepdims=True), jnp.sum(product, axis=0, keepdims=True)):
        high = row.astype(BF16)
        sums += [high, (row - high.astype(F32)).astype(BF16)]
    sums = jnp.concatenate(sums + [jnp.zeros((SUM_ROWS - 4, sums[0].shape[1]), BF16)], axis=0)
    for target in (keep, send):
        for slot in range(2):
            target[slot, 2 * part :, :] = sums
    for index in range(4):
        rows = slice(index * part, (index + 1) * part)
        away = jnp.bitwise_xor(me, index)
        slot = away // 2

        @pl.when(away % 2 == 0)
        def _():
            keep[slot, :part, :] = out[rows].astype(BF16)
            keep[slot, part : 2 * part, :] = grad[rows].astype(BF16)

        @pl.when(away % 2 == 1)
        def _():
            send[slot, :part, :] = out[rows].astype(BF16)
            send[slot, part : 2 * part, :] = grad[rows].astype(BF16)


def project_call(shard, active, attended, d_pre, d_mixed, normed, down_t, attn_t, up, mixed, gain, begin, size, block=256):
    width, hidden = down_t.shape
    part = attended.shape[1]
    steps = LEN // block
    ours = lambda i, *_: (begin + i // steps, 0, i % steps)
    out = lambda i, *_: (i // steps, 0, 0, i % steps)
    fixed = lambda i, *_: (0, 0)
    rows = 2 * part + SUM_ROWS
    grid_spec = pltpu.PrefetchScalarGridSpec(
        num_scalar_prefetch=1,
        grid=(size * steps,),
        in_specs=[
            pl.BlockSpec((None, hidden, block), ours),
            pl.BlockSpec((None, part, block), ours),
            pl.BlockSpec((None, hidden, block), ours),
            pl.BlockSpec((None, 3 * part, block), ours),
            pl.BlockSpec((None, width, block), ours),
            pl.BlockSpec((width, hidden), fixed),
            pl.BlockSpec((width, part), fixed),
            pl.BlockSpec((width, hidden), fixed),
            pl.BlockSpec((width, 3 * part), fixed),
            pl.BlockSpec((width, 128), fixed),
        ],
        out_specs=[
            pl.BlockSpec((None, 2, rows, block), out),
            pl.BlockSpec((None, 2, rows, block), out),
        ],
    )
    return pl.pallas_call(
        project_kernel,
        grid_spec=grid_spec,
        out_shape=[
            jax.ShapeDtypeStruct((size, 2, rows, LEN), BF16),
            jax.ShapeDtypeStruct((size, 2, rows, LEN), BF16),
        ],
        cost_estimate=cost(8, 16_000_000),
        name="project",
    )(shard, active, attended, d_pre, d_mixed, normed, down_t, attn_t, up, mixed, gain)


def finish_kernel(keep, from_core, from_y, own_t, cot, stats, gain, bias, *rest):
    block_out, token_grad = rest[-2:]
    part = own_t.shape[0]
    inv_width = 0.25 / part
    total = keep[...].astype(F32) + from_core[...].astype(F32) + from_y[...].astype(F32)
    own = own_t[...].astype(F32)
    block_out[...] = (own + total[:part] + bias[:, :1].astype(F32)).astype(BF16)
    grad = total[part : 2 * part]
    sums = total[2 * part :]
    mean = stats[0:1, :]
    scale = stats[1:2, :]
    hat = (own - mean) * scale
    inner = grad * gain[:, :1].astype(F32) - (sums[0:1] + sums[1:2]) * inv_width - hat * ((sums[2:3] + sums[3:4]) * inv_width)
    token_grad[...] = cot[...].astype(F32) + inner * scale


def finish_call(keep, from_core, from_y, own_t, cot, stats, gain, bias, before, begin, block=512):
    part, tokens = own_t.shape
    steps = LEN // block
    size = keep.shape[0]
    fixed = lambda i: (0, 0)
    packed = pl.BlockSpec((None, None, 2 * part + SUM_ROWS, block), lambda i: (i // steps, 0, 0, i % steps))
    ours = lambda i: (0, begin * steps + i)
    here = pl.BlockSpec((part, block), ours)
    return pl.pallas_call(
        finish_kernel,
        grid=(size * steps,),
        in_specs=[
            packed, packed, packed,
            here, here,
            pl.BlockSpec((8, block), ours),
            pl.BlockSpec((part, 128), fixed),
            pl.BlockSpec((part, 128), fixed),
        ]
        + [ANY] * len(before),
        out_specs=[here, here],
        out_shape=[
            jax.ShapeDtypeStruct((part, tokens), BF16),
            jax.ShapeDtypeStruct((part, tokens), F32),
        ],
        input_output_aliases={8 + i: i for i in range(len(before))},
        cost_estimate=cost(3, 5_000_000),
        name="finish",
    )(keep, from_core, from_y, own_t, cot, stats, gain, bias, *before)


def flip(value, axis, size, bit):
    return lax.ppermute(value, axis, [(i, i ^ bit) for i in range(size)])


def tie(*trees):
    return lax.optimization_barrier(trees)


def piece_order(size):
    bits = size.bit_length() - 1
    return [sum(((i >> b) & 1) << (bits - 1 - b) for b in range(bits)) for i in range(size)]


class SumOverDp:
    def __init__(self, value, size, index):
        self.size, self.index = size, index
        self.send = value
        self.steps = ["sum"] + [1 << i for i in reversed(range(size.bit_length() - 1))]

    def more(self):
        return bool(self.steps)

    def move(self, send):
        if self.steps[0] == "sum":
            return lax.all_to_all(send, "dp", 0, 0, tiled=True)
        return flip(send, "dp", self.size, self.steps[0])

    def take(self, arrived):
        step = self.steps.pop(0)
        if step == "sum":
            shares = arrived.reshape(self.size, -1, arrived.shape[1]).astype(F32)
            self.keep = jnp.sum(shares, axis=0).astype(BF16)
        else:
            self.keep = jnp.where(
                (self.index & step) > 0,
                jnp.concatenate([arrived, self.keep], axis=0),
                jnp.concatenate([self.keep, arrived], axis=0),
            )
        self.send = self.keep


class ChainOverDp:
    def __init__(self, value, size, index):
        self.size, self.index = size, index
        bits = [1 << i for i in range(size.bit_length() - 1)]
        self.steps = [("sum", bit) for bit in bits] + [("join", bit) for bit in reversed(bits)]
        self.prepare(value, None)

    def prepare(self, held, arrived):
        def part(which, half):
            rows = lax.dynamic_slice_in_dim(held, which * half, half, 0)
            if arrived is None:
                return rows
            came = lax.dynamic_slice_in_dim(arrived, which * half, half, 0)
            return (rows.astype(F32) + came.astype(F32)).astype(BF16)

        rows = held.shape[0]
        if self.steps and self.steps[0][0] == "sum":
            side = ((self.index & self.steps[0][1]) > 0).astype(jnp.int32)
            self.send, self.keep = part(1 - side, rows // 2), part(side, rows // 2)
        else:
            self.keep = part(0, rows)
            self.send = self.keep

    def more(self):
        return bool(self.steps)

    def move(self, send):
        return flip(send, "dp", self.size, self.steps[0][1])

    def take(self, arrived):
        kind, bit = self.steps.pop(0)
        if kind == "sum":
            self.prepare(self.keep, arrived)
            return
        self.keep = jnp.where(
            (self.index & bit) > 0,
            jnp.concatenate([arrived, self.keep], axis=0),
            jnp.concatenate([self.keep, arrived], axis=0),
        )
        self.send = self.keep


class ScatterOverMp:
    def __init__(self, keep, send):
        self.keep, self.send = keep, send
        self.bits = [1, 2]

    def more(self):
        return bool(self.bits)

    def move(self, send):
        return flip(send, "mp", 4, self.bits[0])

    def take(self, arrived):
        bit = self.bits.pop(0)
        if bit == 1:
            self.from_core = arrived
            self.send = (self.keep[:, 1:].astype(F32) + arrived[:, 1:].astype(F32)).astype(BF16)
        else:
            self.from_y = arrived


class ShortSums:
    def __init__(self, keep, send, rest, size):
        self.keep, self.send, self.rest, self.size = keep, send, rest, size
        self.steps = [("mp", 1), ("mp", 2)] + [("dp", 1 << i) for i in range(size.bit_length() - 1)]

    def more(self):
        return bool(self.steps)

    def move(self, send):
        axis, bit = self.steps[0]
        return flip(send, axis, 4 if axis == "mp" else self.size, bit)

    def take(self, arrived):
        axis, bit = self.steps.pop(0)
        if (axis, bit) == ("mp", 1):
            both = self.keep + arrived
            self.norm, self.send = both[0], both[1]
            return
        if axis == "mp":
            self.send = jnp.concatenate([self.norm + arrived, self.rest])
        else:
            self.send = self.send + arrived
        size = self.norm.shape[0]
        self.norm, self.rest = self.send[:size], self.send[size:]


def launch(movers, inputs):
    movers = [m for m in movers if m.more()]
    inputs, sends = tie(inputs, [m.send for m in movers])
    return inputs, [(m, m.move(s)) for m, s in zip(movers, sends)]


def land(flights, outputs):
    outputs, arrivals = tie(outputs, [f[1] for f in flights])
    for (mover, _), arrived in zip(flights, arrivals):
        mover.take(arrived)
    return outputs


def body(
    dp_size,
    tokens,
    image_ids,
    norm_gain,
    qkv_weight,
    qk_gain,
    attn_weight,
    up_weight,
    up_bias,
    down_weight,
    down_bias,
    cotangent,
):
    part = tokens.shape[1]
    width = cotangent.shape[1]
    seqs = image_ids.shape[0]
    me = lax.axis_index("mp")
    dp = lax.axis_index("dp")
    shard = me.astype(jnp.int32)[None]
    place = jnp.bitwise_xor(shard, jnp.array([0, 2, 1, 3], jnp.int32)) * part

    own_t = tokens.T
    cuts = [(0, 1), (1, seqs)] if seqs > 1 else [(0, seqs)]
    owns = [own_t[:, lo * LEN : hi * LEN] for lo, hi in cuts]
    across = [flip(own, "mp", 4, 2) for own in owns]
    gain_own = jnp.broadcast_to(norm_gain[:, None], (part, 128))
    gain_y = flip(gain_own, "mp", 4, 2)
    gain_c = flip(gain_own, "mp", 4, 1)

    def column(vector):
        return jnp.broadcast_to(vector[:, None], (vector.shape[0], 128))

    def prepare(qkv_weight, down_weight, attn_weight, qk_gain, down_bias, image_ids):
        mixed_t = jnp.transpose(qkv_weight, (1, 2, 0)).reshape(3 * part, width)
        slots = jnp.arange(IMAGE_SLOTS, dtype=jnp.int32)[None, :, None]
        same = image_ids[:, None, :] == slots
        mask_q = same.astype(BF16)
        mask_k = jnp.where(same | (slots >= 8), 0.0, -PENALTY).astype(BF16)
        block_first = image_ids[:, ::BI]
        block_last = image_ids[:, BI - 1 :: BI]
        starts = jnp.sum(image_ids[:, None, :] < block_first[:, :, None], axis=2, dtype=jnp.int32)
        ends = jnp.sum(image_ids[:, None, :] <= block_last[:, :, None], axis=2, dtype=jnp.int32)
        first = starts // 128
        count = ((ends + 127) // 128 - first + BJ // 128 - 1) // (BJ // 128)
        first = jnp.minimum(first, (LEN - count * BJ) // 128)
        head_gains = column(qk_gain.astype(F32).reshape(2 * part))
        return (
            mixed_t, mixed_t.T, down_weight.T, attn_weight.T, head_gains, column(down_bias), mask_q, mask_k,
            first.reshape(-1), count.reshape(-1),
        )

    pick = (jnp.arange(part)[:, None] + me * part == jnp.arange(width)[None, :]).astype(BF16)
    d_act, d_att, cot_own, cot_sum = early_call(cotangent, down_weight, attn_weight, pick)
    (d_act, up_t, up_bias_col), (across[0], gain_y, gain_c) = tie(
        (d_act, up_weight.T, column(up_bias)), (across[0], gain_y, gain_c)
    )
    gains = (gain_own, gain_y, gain_c, flip(gain_y, "mp", 4, 1))
    before = held = ()
    bias_parts = 0.0
    for number, (lo, _) in enumerate(cuts):
        own, from_y = owns[number], across[number]
        pieces = (own, from_y, flip(own, "mp", 4, 1), flip(from_y, "mp", 4, 1))
        if number == 1:
            prepared, pieces = tie(prepared, pieces)
        *before, bias_part, gain_all, left, right = mlp_call(
            tuple(piece_order(dp_size)), place, pieces, gains, up_t, up_bias_col, d_act, cotangent, up_weight, before,
            held, lo,
        )
        held = (left, right)
        bias_parts = bias_parts + bias_part
        if number == 0:
            (before, held), raw = tie(
                (before, held), (qkv_weight, down_weight, attn_weight, qk_gain, down_bias, image_ids)
            )
            prepared = prepare(*raw)
        if number + 1 < len(cuts):
            (before, held), across[number + 1] = tie((before, held), across[number + 1])
    mixed_t, mixed, down_t, attn_t, head_gains, bias_col, mask_q, mask_k, first, count = prepared
    normed, active, d_pre, stats = before
    up_row, mlp_part = held
    mlp_sum = SumOverDp(mlp_part, dp_size, dp)

    (states,), flying = launch([mlp_sum], (normed,))
    attended, d_mixed, qk_part, norm_row, mix_part = attention_call(
        first, count, states, mixed_t, d_att, mask_q, mask_k, head_gains, cotangent
    )
    mix_sum = ChainOverDp(mix_part, dp_size, dp)

    norm_vec = norm_row[0] + jnp.sum(up_row, axis=1)
    norm_parts = norm_vec.reshape(4, part)
    norm_parts = [lax.dynamic_index_in_dim(norm_parts, jnp.bitwise_xor(me, m), 0, False) for m in range(4)]
    short = ShortSums(
        jnp.stack([norm_parts[0], norm_parts[2]]),
        jnp.stack([norm_parts[1], norm_parts[3]]),
        jnp.concatenate([jnp.sum(qk_part, axis=1), jnp.sum(bias_parts, axis=1), jnp.sum(cot_sum, axis=1)]),
        dp_size,
    )

    runs = [(seq, 1) for seq in range(seqs)]
    scatters = []
    for begin, size in runs:
        busy = [f[0] for f in flying]
        along = [m for m in [mix_sum, mlp_sum, short] + scatters if m.more() and m not in busy]
        (att, dm), flights = launch(along, (attended, d_mixed))
        flying = flying + flights
        sent = project_call(
            shard, active, att, d_pre, dm, normed, down_t, attn_t, up_weight, mixed, gain_all, begin, size
        )
        late = [f for f in flights if begin == 0 and f[0] is mix_sum]
        keep, send = land([f for f in flying if f not in late], sent)
        flying = late
        scatters.append(ScatterOverMp(keep, send))

    finished = ()
    wide_grads = ()
    done = set()

    def finish_ready(finished):
        for (begin, _), scatter in zip(runs, scatters):
            if not scatter.more() and begin not in done:
                done.add(begin)
                finished = finish_call(
                    scatter.keep, scatter.from_core, scatter.from_y, own_t, cot_own, stats, gain_own, bias_col,
                    finished, begin,
                )
        return finished

    while True:
        busy = [f[0] for f in flying]
        ready = [m for m in [mix_sum] + scatters + [short, mlp_sum] if m.more() and m not in busy]
        finished, flights = launch(ready, finished)
        flying = flying + flights
        if not flying:
            break
        finished = finish_ready(finished)
        near = [f for f in flying if f[0] in scatters and len(f[0].bits) == 2]
        across = [f for f in flying if f[0] in scatters and len(f[0].bits) == 1]
        chain = [f for f in flying if f[0] is mix_sum]
        rest = [f for f in flying if f[0] is short]
        wide = [f for f in flying if f[0] is mlp_sum]
        left = len(mix_sum.steps)
        if near:
            now = near + chain + rest
        elif left == 2:
            now = chain + across[:1] + wide + rest
        elif left == 1:
            now = across + wide + rest or chain
        else:
            now = chain + rest or flying
        finished, wide_grads = land(now, (finished, wide_grads))
        flying = [f for f in flying if f not in now]
        if not mlp_sum.more() and not wide_grads:
            split = up_weight.shape[1]
            wide_grads = (mlp_sum.keep[:split].astype(F32), mlp_sum.keep[split:].astype(F32))
    finished = finish_ready(finished)
    block_out, token_grad = finished
    block_out, token_grad = block_out.T, token_grad.T
    mixed_grad = mix_sum.keep.astype(F32)
    qkv_grad = jnp.transpose(mixed_grad[: 3 * part].reshape(3, part, width), (2, 0, 1))

    gain_grad = short.norm / norm_gain.astype(F32)
    rest = short.rest
    split = 2 * part + up_weight.shape[1]
    return (
        block_out,
        token_grad,
        gain_grad,
        qkv_grad,
        rest[: 2 * part].reshape(2, part),
        mixed_grad[3 * part :],
        wide_grads[1],
        rest[2 * part : split],
        wide_grads[0],
        rest[split:],
    )


def solution(mesh):
    in_specs = (
        P("dp", "mp"),
        P("dp", None),
        P("mp"),
        P(None, None, "mp"),
        P(None, "mp"),
        P("mp", None),
        P(None, "mp"),
        P("mp"),
        P("mp", None),
        P("mp"),
        P("dp", None),
    )
    out_specs = (
        P("dp", "mp"),
        P("dp", "mp"),
        P("mp"),
        P(None, None, "mp"),
        P(None, "mp"),
        P("mp", None),
        P(None, "mp"),
        P("mp"),
        P("mp", None),
        P("mp"),
    )
    run = functools.partial(body, mesh.shape["dp"])
    return jax.shard_map(run, mesh=mesh, in_specs=in_specs, out_specs=out_specs, check_vma=False)
```

```python
import functools

import jax
import jax.numpy as jnp
from jax import lax
from jax.experimental import pallas as pl
from jax.experimental.pallas import tpu as pltpu
from jax.sharding import PartitionSpec as P

DH = 64
LEN = 1024
EPSILON = 1e-06
IMAGE_SLOTS = 16
PENALTY = 1024.0
BI = 256
BJ = 256
SUM_ROWS = 16
F32 = jnp.float32
BF16 = jnp.bfloat16

NN = (((1,), (0,)), ((), ()))
NT = (((1,), (1,)), ((), ()))
ANY = pl.BlockSpec(memory_space=pl.ANY)


def dot(left, right, dims=NN):
    return lax.dot_general(left, right, dims, preferred_element_type=F32)


def fold_lanes(rows):
    total = rows[:, :128]
    for start in range(128, rows.shape[1], 128):
        total = total + rows[:, start : start + 128]
    return total


def cost(microseconds, nbytes):
    return pl.CostEstimate(flops=int(microseconds * 1e3), bytes_accessed=nbytes // 1000, transcendentals=0)


def early_kernel(cot, down, attn, pick, d_act, d_att, cot_own, bias_sum):
    rows = cot[...]
    d_act[...] = dot(down[...], rows, NT).astype(BF16)
    d_att[...] = dot(attn[...], rows, NT).astype(BF16)
    own = dot(pick[...], rows, NT)
    cot_own[...] = own.astype(BF16)

    @pl.when(pl.program_id(0) == 0)
    def _():
        bias_sum[...] = jnp.zeros_like(bias_sum)

    bias_sum[...] += fold_lanes(own)


def early_call(cot, down, attn, pick, block=512):
    tokens, width = cot.shape
    seqs = tokens // LEN
    hidden, part = down.shape[0], attn.shape[0]
    steps = LEN // block
    fixed = lambda i: (0, 0)
    by_seq = lambda i: (i // steps, 0, i % steps)
    return pl.pallas_call(
        early_kernel,
        grid=(tokens // block,),
        in_specs=[
            pl.BlockSpec((block, width), lambda i: (i, 0)),
            pl.BlockSpec((hidden, width), fixed),
            pl.BlockSpec((part, width), fixed),
            pl.BlockSpec((part, width), fixed),
        ],
        out_specs=[
            pl.BlockSpec((None, hidden, block), by_seq),
            pl.BlockSpec((None, part, block), by_seq),
            pl.BlockSpec((part, block), lambda i: (0, i)),
            pl.BlockSpec((part, 128), fixed),
        ],
        out_shape=[
            jax.ShapeDtypeStruct((seqs, hidden, LEN), BF16),
            jax.ShapeDtypeStruct((seqs, part, LEN), BF16),
            jax.ShapeDtypeStruct((part, tokens), BF16),
            jax.ShapeDtypeStruct((part, 128), F32),
        ],
        cost_estimate=cost(10, 12_000_000),
        name="early",
    )(cot, down, attn, pick)


def mlp_kernel(
    pieces_order, place, own, flip_y, flip_c, flip_cy, gain_own, gain_y, gain_c, gain_cy, up_t, up_bias, d_act, cot, up,
    normed, active, d_pre, stats, bias_sum, gain_all, up_row, grads, low, high
):
    pieces = (own, flip_y, flip_c, flip_cy)
    part = own.shape[0]
    width = part * 4
    first = pl.program_id(0) == 0
    last = pl.program_id(0) == pl.num_programs(0) - 1

    @pl.when(first)
    def _():
        bias_sum[...] = jnp.zeros_like(bias_sum)
        low[...] = jnp.zeros_like(low)
        high[...] = jnp.zeros_like(high)
        for slot, piece in enumerate((gain_own, gain_y, gain_c, gain_cy)):
            gain_all[pl.ds(pl.multiple_of(place[slot], part), part), :] = piece[...].astype(F32)

    total = 0.0
    squares = 0.0
    for piece in pieces:
        rows = piece[...].astype(F32)
        total = total + jnp.sum(rows, axis=0, keepdims=True)
        squares = squares + jnp.sum(rows * rows, axis=0, keepdims=True)
    mean = total * (1.0 / width)
    scale = lax.rsqrt(squares * (1.0 / width) - mean * mean + EPSILON)
    stats[0:1, :] = mean
    stats[1:2, :] = scale
    stats[2:8, :] = jnp.zeros((6, stats.shape[1]), F32)
    for slot, piece in enumerate(pieces):
        rows = piece[...].astype(F32)
        here = pl.ds(pl.multiple_of(place[slot], part), part)
        normed[here, :] = ((rows - mean) * scale * gain_all[here, :1]).astype(BF16)

    c0 = 0.7978845608028654
    c1 = 0.044715 * c0
    def lift(start):
        here = slice(start, start + 256)
        return dot(up_t[here, :], normed[...]) + up_bias[here, :1].astype(F32)

    ahead = lift(0)
    for start in range(0, up_t.shape[0], 256):
        here = slice(start, start + 256)
        pre = ahead
        if start + 256 < up_t.shape[0]:
            ahead = lift(start + 256)
        square = pre * pre
        half = 0.5 * jnp.tanh(pre * (c0 + c1 * square)) + 0.5
        act = (pre * half).astype(BF16)
        active[here, :] = act
        slope = half + pre * (half - half * half) * (2.0 * c0 + 6.0 * c1 * square)
        grad = (d_act[here, :].astype(F32) * slope).astype(BF16)
        d_pre[here, :] = grad
        bias_sum[here, :] += fold_lanes(grad.astype(F32))
        low[here, :] += dot(act, cot[...])
        high[:, here] += dot(normed[...], grad, NT)

    @pl.when(last)
    def _():
        up_row[...] = fold_lanes(high[...] * up[...].astype(F32))
        half = low.shape[0]
        size = grads.shape[0] // len(pieces_order)
        for slot, piece in enumerate(pieces_order):
            source, start = (low, piece * size) if piece * size < half else (high, piece * size - half)
            grads[slot * size : (slot + 1) * size, :] = source[start : start + size, :].astype(BF16)


def mlp_call(pieces_order, place, pieces, gains, up_t, up_bias, d_act, cot, up, block=512):
    part, tokens = pieces[0].shape
    width = 4 * part
    seqs, hidden, _ = d_act.shape
    steps = LEN // block
    lanes = lambda i, *_: (0, i)
    by_seq = lambda i, *_: (i // steps, 0, i % steps)
    fixed = lambda i, *_: (0, 0)
    grid_spec = pltpu.PrefetchScalarGridSpec(
        num_scalar_prefetch=1,
        grid=(tokens // block,),
        in_specs=[pl.BlockSpec((part, block), lanes)] * 4
        + [pl.BlockSpec((part, 128), fixed)] * 4
        + [
            pl.BlockSpec((hidden, width), fixed),
            pl.BlockSpec((hidden, 128), fixed),
            pl.BlockSpec((None, hidden, block), by_seq),
            pl.BlockSpec((block, width), lambda i, *_: (i, 0)),
            pl.BlockSpec((width, hidden), fixed),
        ],
        out_specs=[
            pl.BlockSpec((None, width, block), by_seq),
            pl.BlockSpec((None, hidden, block), by_seq),
            pl.BlockSpec((None, hidden, block), by_seq),
            pl.BlockSpec((8, block), lanes),
            pl.BlockSpec((hidden, 128), fixed),
            pl.BlockSpec((width, 128), fixed),
            pl.BlockSpec((width, 128), fixed),
            pl.BlockSpec((hidden + width, width), fixed),
        ],
        scratch_shapes=[pltpu.VMEM((hidden, width), F32), pltpu.VMEM((width, hidden), F32)],
    )
    assert hidden == width
    return pl.pallas_call(
        functools.partial(mlp_kernel, pieces_order),
        grid_spec=grid_spec,
        out_shape=[
            jax.ShapeDtypeStruct((seqs, width, LEN), BF16),
            jax.ShapeDtypeStruct((seqs, hidden, LEN), BF16),
            jax.ShapeDtypeStruct((seqs, hidden, LEN), BF16),
            jax.ShapeDtypeStruct((8, tokens), F32),
            jax.ShapeDtypeStruct((hidden, 128), F32),
            jax.ShapeDtypeStruct((width, 128), F32),
            jax.ShapeDtypeStruct((width, 128), F32),
            jax.ShapeDtypeStruct((hidden + width, width), BF16),
        ],
        cost_estimate=cost(20, 30_000_000),
        name="mlp",
    )(place, *pieces, *gains, up_t, up_bias, d_act, cot, up)


def attention_kernel(
    first, count, normed, mixed_t, d_att, mask_q, mask_k, gains, cot, attended, d_mixed, gain_sum, norm_row, grads,
    total, qkv, qx, kx, vn, kt, vt, es, ps, dqa, dka, dva
):
    seq = pl.program_id(0)
    last = seq == pl.num_programs(0) - 1
    part = attended.shape[0]
    heads = part // DH
    inv_dh = 1.0 / DH

    @pl.when(seq == 0)
    def _():
        total[...] = jnp.zeros_like(total)
        gain_sum[...] = jnp.zeros_like(gain_sum)

    qkv[...] = dot(mixed_t[...], normed[...])

    def unit(start):
        raw = qkv[start : start + DH, :]
        shifted = raw - jnp.sum(raw, axis=0, keepdims=True) * inv_dh
        scale = lax.rsqrt(jnp.sum(shifted * shifted, axis=0, keepdims=True) * inv_dh + EPSILON)
        return shifted * scale, scale

    zeros = jnp.zeros((128 - DH - IMAGE_SLOTS, LEN), BF16)
    for head in range(heads):
        rows = slice(head * DH, (head + 1) * DH)
        query, _ = unit(head * DH)
        query = (query * (gains[rows, :1] * 0.125)).astype(BF16)
        qx[head] = jnp.concatenate([query, mask_q[...], zeros], axis=0)
        key, _ = unit(part + head * DH)
        key = (key * gains[part + head * DH : part + (head + 1) * DH, :1]).astype(BF16)
        kt[rows, :] = key
        kx[head] = jnp.concatenate([key, mask_k[...], zeros], axis=0).T
        value = qkv[2 * part + head * DH : 2 * part + (head + 1) * DH, :].astype(BF16)
        vt[rows, :] = value
        vn[head] = value.T
    dka[...] = jnp.zeros_like(dka)
    dva[...] = jnp.zeros_like(dva)

    def straight(units, i0, base):
        icols = pl.ds(i0, BI)
        edges = [(at, min(BJ, units * 128 - at)) for at in range(0, units * 128, BJ)]
        trips = len(edges)
        spots = [slice(at, at + size) for at, size in edges]
        places = [pl.ds(pl.multiple_of(base + at, 128), size) for at, size in edges]

        def scores(head, j, sums):
            rows = slice(head * DH, (head + 1) * DH)
            e = jnp.exp(dot(kx[head, places[j], :], qx[head, :, icols]))
            p = dot(vn[head, places[j], :], d_att[rows, icols])
            es[head % 2, spots[j], :] = e
            ps[head % 2, spots[j], :] = p
            more = (jnp.sum(e, axis=0, keepdims=True), jnp.sum(e * p, axis=0, keepdims=True))
            return more if sums is None else (sums[0] + more[0], sums[1] + more[1])

        def row_grads(head, j, inverse, inner, held):
            rows = slice(head * DH, (head + 1) * DH)
            w = es[head % 2, spots[j], :] * inverse
            d = (w * (ps[head % 2, spots[j], :] - inner)).astype(BF16)
            w = w.astype(BF16)
            out = dot(vt[rows, places[j]], w)
            query = dot(kt[rows, places[j]], d)
            dva[rows, places[j]] += dot(d_att[rows, icols], w, NT)
            dka[rows, places[j]] += dot(qx[head, :DH, icols], d, NT)
            return (out, query) if held is None else (held[0] + out, held[1] + query)

        sums = None
        for j in range(trips):
            sums = scores(0, j, sums)
        for head in range(heads):
            rows = slice(head * DH, (head + 1) * DH)
            inverse = 1.0 / sums[0]
            inner = sums[1] * inverse
            held = following = None
            for j in range(trips):
                if head + 1 < heads:
                    following = scores(head + 1, j, following)
                held = row_grads(head, j, inverse, inner, held)
            attended[rows, icols] = held[0].astype(BF16)
            dqa[rows, icols] = held[1]
            sums = following

    def query_block(ib, _):
        i0 = pl.multiple_of(ib * BI, BI)
        base = first[seq * (LEN // BI) + ib] * 128
        trips = count[seq * (LEN // BI) + ib]
        for number in range(BI // 128, LEN // 128 + 1):
            pl.when(trips == number)(functools.partial(straight, number, i0, base))
        return 0

    lax.fori_loop(0, LEN // BI, query_block, 0)

    for source, offset, factor in ((dqa, 0, 0.125), (dka, part, 1.0)):
        for head in range(heads):
            start = offset + head * DH
            u, scale = unit(start)
            e = source[head * DH : (head + 1) * DH, :] * factor
            gain_sum[start : start + DH, :] += fold_lanes(e * u)
            f = e * gains[start : start + DH, :1]
            mean_f = jnp.sum(f, axis=0, keepdims=True) * inv_dh
            mean_fu = jnp.sum(f * u, axis=0, keepdims=True) * inv_dh
            d_mixed[start : start + DH, :] = ((f - mean_f - u * mean_fu) * scale).astype(BF16)
    d_mixed[2 * part :, :] = dva[...].astype(BF16)

    split = 3 * part
    total[:split, :] += dot(d_mixed[...], normed[...], NT)
    total[split:, :] += dot(attended[...], cot[...])

    @pl.when(last)
    def _():
        norm_row[...] = jnp.sum(total[:split, :] * mixed_t[...].astype(F32), axis=0, keepdims=True)
        grads[...] = total[...].astype(BF16)


def attention_call(first, count, normed, mixed_t, d_att, mask_q, mask_k, gains, cot):
    seqs, part, _ = d_att.shape
    width = normed.shape[1]
    heads = part // DH
    fixed = lambda i, *_: (0, 0)
    by_seq = lambda i, *_: (i, 0, 0)
    grid_spec = pltpu.PrefetchScalarGridSpec(
        num_scalar_prefetch=2,
        grid=(seqs,),
        in_specs=[
            pl.BlockSpec((None, width, LEN), by_seq),
            pl.BlockSpec((3 * part, width), fixed),
            pl.BlockSpec((None, part, LEN), by_seq),
            pl.BlockSpec((None, IMAGE_SLOTS, LEN), by_seq),
            pl.BlockSpec((None, IMAGE_SLOTS, LEN), by_seq),
            pl.BlockSpec((2 * part, 128), fixed),
            pl.BlockSpec((LEN, width), lambda i, *_: (i, 0)),
        ],
        out_specs=[
            pl.BlockSpec((None, part, LEN), by_seq),
            pl.BlockSpec((None, 3 * part, LEN), by_seq),
            pl.BlockSpec((2 * part, 128), fixed),
            pl.BlockSpec((1, width), fixed),
            pl.BlockSpec((4 * part, width), fixed),
        ],
        scratch_shapes=[
            pltpu.VMEM((4 * part, width), F32),
            pltpu.VMEM((3 * part, LEN), F32),
            pltpu.VMEM((heads, 128, LEN), BF16),
            pltpu.VMEM((heads, LEN, 128), BF16),
            pltpu.VMEM((heads, LEN, DH), BF16),
            pltpu.VMEM((part, LEN), BF16),
            pltpu.VMEM((part, LEN), BF16),
            pltpu.VMEM((2, LEN, BI), F32),
            pltpu.VMEM((2, LEN, BI), F32),
            pltpu.VMEM((part, LEN), F32),
            pltpu.VMEM((part, LEN), F32),
            pltpu.VMEM((part, LEN), F32),
        ],
    )
    return pl.pallas_call(
        attention_kernel,
        grid_spec=grid_spec,
        out_shape=[
            jax.ShapeDtypeStruct((seqs, part, LEN), BF16),
            jax.ShapeDtypeStruct((seqs, 3 * part, LEN), BF16),
            jax.ShapeDtypeStruct((2 * part, 128), F32),
            jax.ShapeDtypeStruct((1, width), F32),
            jax.ShapeDtypeStruct((4 * part, width), BF16),
        ],
        cost_estimate=cost(18, 5_000_000),
        name="attention",
    )(first, count, normed, mixed_t, d_att, mask_q, mask_k, gains, cot)


def project_kernel(
    shard, active, attended, d_pre, d_mixed, normed, down_t, attn_t, up, mixed, gain, keep, send
):
    me = shard[0]
    part = attended.shape[0]
    out = dot(down_t[...], active[...]) + dot(attn_t[...], attended[...])
    grad = dot(up[...], d_pre[...]) + dot(mixed[...], d_mixed[...])
    product = grad * normed[...].astype(F32)
    sums = []
    for row in (jnp.sum(grad * gain[:, :1], axis=0, keepdims=True), jnp.sum(product, axis=0, keepdims=True)):
        high = row.astype(BF16)
        sums += [high, (row - high.astype(F32)).astype(BF16)]
    sums = jnp.concatenate(sums + [jnp.zeros((SUM_ROWS - 4, sums[0].shape[1]), BF16)], axis=0)
    for target in (keep, send):
        for slot in range(2):
            target[slot, 2 * part :, :] = sums
    for index in range(4):
        rows = slice(index * part, (index + 1) * part)
        away = jnp.bitwise_xor(me, index)
        slot = away // 2

        @pl.when(away % 2 == 0)
        def _():
            keep[slot, :part, :] = out[rows].astype(BF16)
            keep[slot, part : 2 * part, :] = grad[rows].astype(BF16)

        @pl.when(away % 2 == 1)
        def _():
            send[slot, :part, :] = out[rows].astype(BF16)
            send[slot, part : 2 * part, :] = grad[rows].astype(BF16)


def project_call(shard, active, attended, d_pre, d_mixed, normed, down_t, attn_t, up, mixed, gain, begin, size, block=256):
    width, hidden = down_t.shape
    part = attended.shape[1]
    steps = LEN // block
    ours = lambda i, *_: (begin + i // steps, 0, i % steps)
    out = lambda i, *_: (i // steps, 0, 0, i % steps)
    fixed = lambda i, *_: (0, 0)
    rows = 2 * part + SUM_ROWS
    grid_spec = pltpu.PrefetchScalarGridSpec(
        num_scalar_prefetch=1,
        grid=(size * steps,),
        in_specs=[
            pl.BlockSpec((None, hidden, block), ours),
            pl.BlockSpec((None, part, block), ours),
            pl.BlockSpec((None, hidden, block), ours),
            pl.BlockSpec((None, 3 * part, block), ours),
            pl.BlockSpec((None, width, block), ours),
            pl.BlockSpec((width, hidden), fixed),
            pl.BlockSpec((width, part), fixed),
            pl.BlockSpec((width, hidden), fixed),
            pl.BlockSpec((width, 3 * part), fixed),
            pl.BlockSpec((width, 128), fixed),
        ],
        out_specs=[
            pl.BlockSpec((None, 2, rows, block), out),
            pl.BlockSpec((None, 2, rows, block), out),
        ],
    )
    return pl.pallas_call(
        project_kernel,
        grid_spec=grid_spec,
        out_shape=[
            jax.ShapeDtypeStruct((size, 2, rows, LEN), BF16),
            jax.ShapeDtypeStruct((size, 2, rows, LEN), BF16),
        ],
        cost_estimate=cost(8, 16_000_000),
        name="project",
    )(shard, active, attended, d_pre, d_mixed, normed, down_t, attn_t, up, mixed, gain)


def finish_kernel(keep, from_core, from_y, own_t, cot, stats, gain, bias, *rest):
    block_out, token_grad = rest[-2:]
    part = own_t.shape[0]
    inv_width = 0.25 / part
    total = keep[...].astype(F32) + from_core[...].astype(F32) + from_y[...].astype(F32)
    own = own_t[...].astype(F32)
    block_out[...] = (own + total[:part] + bias[:, :1].astype(F32)).astype(BF16)
    grad = total[part : 2 * part]
    sums = total[2 * part :]
    mean = stats[0:1, :]
    scale = stats[1:2, :]
    hat = (own - mean) * scale
    inner = grad * gain[:, :1].astype(F32) - (sums[0:1] + sums[1:2]) * inv_width - hat * ((sums[2:3] + sums[3:4]) * inv_width)
    token_grad[...] = cot[...].astype(F32) + inner * scale


def finish_call(keep, from_core, from_y, own_t, cot, stats, gain, bias, before, begin, block=512):
    part, tokens = own_t.shape
    steps = LEN // block
    size = keep.shape[0]
    fixed = lambda i: (0, 0)
    packed = pl.BlockSpec((None, None, 2 * part + SUM_ROWS, block), lambda i: (i // steps, 0, 0, i % steps))
    ours = lambda i: (0, begin * steps + i)
    here = pl.BlockSpec((part, block), ours)
    return pl.pallas_call(
        finish_kernel,
        grid=(size * steps,),
        in_specs=[
            packed, packed, packed,
            here, here,
            pl.BlockSpec((8, block), ours),
            pl.BlockSpec((part, 128), fixed),
            pl.BlockSpec((part, 128), fixed),
        ]
        + [ANY] * len(before),
        out_specs=[here, here],
        out_shape=[
            jax.ShapeDtypeStruct((part, tokens), BF16),
            jax.ShapeDtypeStruct((part, tokens), F32),
        ],
        input_output_aliases={8 + i: i for i in range(len(before))},
        cost_estimate=cost(3, 5_000_000),
        name="finish",
    )(keep, from_core, from_y, own_t, cot, stats, gain, bias, *before)


def flip(value, axis, size, bit):
    return lax.ppermute(value, axis, [(i, i ^ bit) for i in range(size)])


def tie(*trees):
    return lax.optimization_barrier(trees)


def joined(swap, held, arrived):
    return jnp.where(
        swap, jnp.concatenate([arrived, held], axis=0), jnp.concatenate([held, arrived], axis=0)
    )


def piece_order(size):
    bits = size.bit_length() - 1
    return [sum(((i >> b) & 1) << (bits - 1 - b) for b in range(bits)) for i in range(size)]


class SumOverDp:
    def __init__(self, value, size, index):
        self.size, self.index = size, index
        self.send = value
        self.steps = ["sum"] + [1 << i for i in reversed(range(size.bit_length() - 1))]

    def more(self):
        return bool(self.steps)

    def move(self, send):
        if self.steps[0] == "sum":
            return lax.all_to_all(send, "dp", 0, 0, tiled=True)
        return flip(send, "dp", self.size, self.steps[0])

    def take(self, arrived):
        step = self.steps.pop(0)
        if step == "sum":
            shares = arrived.reshape(self.size, -1, arrived.shape[1]).astype(F32)
            self.keep = jnp.sum(shares, axis=0).astype(BF16)
        else:
            self.last = ((self.index & step) > 0, self.keep, arrived)
            self.keep = joined(*self.last)
        self.send = self.keep


class ChainOverDp:
    def __init__(self, value, size, index):
        self.size, self.index = size, index
        bits = [1 << i for i in range(size.bit_length() - 1)]
        self.steps = [("sum", bit) for bit in bits] + [("join", bit) for bit in reversed(bits)]
        self.prepare(value, None)

    def prepare(self, held, arrived):
        def part(which, half):
            rows = lax.dynamic_slice_in_dim(held, which * half, half, 0)
            if arrived is None:
                return rows
            came = lax.dynamic_slice_in_dim(arrived, which * half, half, 0)
            return (rows.astype(F32) + came.astype(F32)).astype(BF16)

        rows = held.shape[0]
        if self.steps and self.steps[0][0] == "sum":
            side = ((self.index & self.steps[0][1]) > 0).astype(jnp.int32)
            self.send, self.keep = part(1 - side, rows // 2), part(side, rows // 2)
        else:
            self.keep = part(0, rows)
            self.send = self.keep

    def more(self):
        return bool(self.steps)

    def move(self, send):
        return flip(send, "dp", self.size, self.steps[0][1])

    def take(self, arrived):
        kind, bit = self.steps.pop(0)
        if kind == "sum":
            self.prepare(self.keep, arrived)
            return
        self.last = ((self.index & bit) > 0, self.keep, arrived)
        self.keep = self.send = joined(*self.last)


class ScatterOverMp:
    def __init__(self, keep, send):
        self.keep, self.send = keep, send
        self.bits = [1, 2]

    def more(self):
        return bool(self.bits)

    def move(self, send):
        return flip(send, "mp", 4, self.bits[0])

    def take(self, arrived):
        bit = self.bits.pop(0)
        if bit == 1:
            self.from_core = arrived
            self.send = (self.keep[:, 1:].astype(F32) + arrived[:, 1:].astype(F32)).astype(BF16)
        else:
            self.from_y = arrived


class ShortSums:
    def __init__(self, keep, send, rest, size):
        self.keep, self.send, self.rest, self.size = keep, send, rest, size
        self.steps = [("mp", 1), ("mp", 2)] + [("dp", 1 << i) for i in range(size.bit_length() - 1)]

    def more(self):
        return bool(self.steps)

    def move(self, send):
        axis, bit = self.steps[0]
        return flip(send, axis, 4 if axis == "mp" else self.size, bit)

    def take(self, arrived):
        axis, bit = self.steps.pop(0)
        if (axis, bit) == ("mp", 1):
            both = self.keep + arrived
            self.norm, self.send = both[0], both[1]
            return
        if axis == "mp":
            self.send = jnp.concatenate([self.norm + arrived, self.rest])
        else:
            self.send = self.send + arrived
        size = self.norm.shape[0]
        self.norm, self.rest = self.send[:size], self.send[size:]


def launch(movers, inputs):
    movers = [m for m in movers if m.more()]
    inputs, sends = tie(inputs, [m.send for m in movers])
    return inputs, [(m, m.move(s)) for m, s in zip(movers, sends)]


def land(flights, outputs):
    outputs, arrivals = tie(outputs, [f[1] for f in flights])
    for (mover, _), arrived in zip(flights, arrivals):
        mover.take(arrived)
    return outputs


def body(
    dp_size,
    tokens,
    image_ids,
    norm_gain,
    qkv_weight,
    qk_gain,
    attn_weight,
    up_weight,
    up_bias,
    down_weight,
    down_bias,
    cotangent,
):
    part = tokens.shape[1]
    width = cotangent.shape[1]
    seqs = image_ids.shape[0]
    me = lax.axis_index("mp")
    dp = lax.axis_index("dp")
    shard = me.astype(jnp.int32)[None]
    place = jnp.bitwise_xor(shard, jnp.array([0, 2, 1, 3], jnp.int32)) * part

    own_t = tokens.T
    from_y = flip(own_t, "mp", 4, 2)
    gain_own = jnp.broadcast_to(norm_gain[:, None], (part, 128))
    gain_y = flip(gain_own, "mp", 4, 2)
    gain_c = flip(gain_own, "mp", 4, 1)

    mixed_t = jnp.transpose(qkv_weight, (1, 2, 0)).reshape(3 * part, width)
    mixed = mixed_t.T
    up_t = up_weight.T
    down_t = down_weight.T
    attn_t = attn_weight.T
    def column(vector):
        return jnp.broadcast_to(vector[:, None], (vector.shape[0], 128))

    columns = (column(up_bias), column(qk_gain.astype(F32).reshape(2 * part)), column(down_bias))

    slots = jnp.arange(IMAGE_SLOTS, dtype=jnp.int32)[None, :, None]
    same = image_ids[:, None, :] == slots
    mask_q = same.astype(BF16)
    mask_k = jnp.where(same | (slots >= 8), 0.0, -PENALTY).astype(BF16)
    block_first = image_ids[:, ::BI]
    block_last = image_ids[:, BI - 1 :: BI]
    starts = jnp.sum(image_ids[:, None, :] < block_first[:, :, None], axis=2, dtype=jnp.int32)
    ends = jnp.sum(image_ids[:, None, :] <= block_last[:, :, None], axis=2, dtype=jnp.int32)
    first = starts // 128
    count = ((ends + 127) // 128 - first).reshape(-1)
    first = first.reshape(-1)

    pick = (jnp.arange(part)[:, None] + me * part == jnp.arange(width)[None, :]).astype(BF16)
    pick, place, columns, (gain_y, gain_c) = tie(pick, place, columns, (gain_y, gain_c))
    up_bias_col, head_gains, bias_col = columns
    gain_cy = flip(gain_y, "mp", 4, 1)
    d_act, d_att, cot_own, cot_sum = early_call(cotangent, down_weight, attn_weight, pick)
    prepared = (
        d_act, d_att, mixed_t, mixed, up_t, down_t, attn_t, up_bias_col, head_gains, mask_q, mask_k, first, count,
        bias_col,
    )
    prepared, (from_y, gain_cy) = tie(prepared, (from_y, gain_cy))
    gains = (gain_own, gain_y, gain_c, gain_cy)
    (
        d_act, d_att, mixed_t, mixed, up_t, down_t, attn_t, up_bias_col, head_gains, mask_q, mask_k, first, count,
        bias_col,
    ) = prepared
    pieces = (own_t, from_y, flip(own_t, "mp", 4, 1), flip(from_y, "mp", 4, 1))
    normed, active, d_pre, stats, upbias_part, gain_all, up_row, mlp_part = mlp_call(
        tuple(piece_order(dp_size)), place, pieces, gains, up_t, up_bias_col, d_act, cotangent, up_weight
    )
    mlp_sum = SumOverDp(mlp_part, dp_size, dp)

    (states,), flying = launch([mlp_sum], (normed,))
    attended, d_mixed, qk_part, norm_row, mix_part = attention_call(
        first, count, states, mixed_t, d_att, mask_q, mask_k, head_gains, cotangent
    )
    mix_sum = ChainOverDp(mix_part, dp_size, dp)

    norm_vec = norm_row[0] + jnp.sum(up_row, axis=1)
    norm_parts = norm_vec.reshape(4, part)
    norm_parts = [lax.dynamic_index_in_dim(norm_parts, jnp.bitwise_xor(me, m), 0, False) for m in range(4)]
    short = ShortSums(
        jnp.stack([norm_parts[0], norm_parts[2]]),
        jnp.stack([norm_parts[1], norm_parts[3]]),
        jnp.concatenate([jnp.sum(qk_part, axis=1), jnp.sum(upbias_part, axis=1), jnp.sum(cot_sum, axis=1)]),
        dp_size,
    )

    runs = [(seq, 1) for seq in range(seqs)]
    scatters = []
    for begin, size in runs:
        busy = [f[0] for f in flying]
        along = [m for m in [mix_sum, mlp_sum, short] + scatters if m.more() and m not in busy]
        (att, dm), flights = launch(along, (attended, d_mixed))
        flying = flying + flights
        sent = project_call(
            shard, active, att, d_pre, dm, normed, down_t, attn_t, up_weight, mixed, gain_all, begin, size
        )
        late = [f for f in flights if begin == 0 and f[0] is mix_sum]
        keep, send = land([f for f in flying if f not in late], sent)
        flying = late
        scatters.append(ScatterOverMp(keep, send))

    finished = ()
    wide_grads = ()
    done = set()

    def finish_ready(finished):
        for (begin, _), scatter in zip(runs, scatters):
            if not scatter.more() and begin not in done:
                done.add(begin)
                finished = finish_call(
                    scatter.keep, scatter.from_core, scatter.from_y, own_t, cot_own, stats, gain_own, bias_col,
                    finished, begin,
                )
        return finished

    while True:
        busy = [f[0] for f in flying]
        ready = [m for m in [mix_sum] + scatters + [short, mlp_sum] if m.more() and m not in busy]
        finished, flights = launch(ready, finished)
        flying = flying + flights
        if not flying:
            break
        finished = finish_ready(finished)
        near = [f for f in flying if f[0] in scatters and len(f[0].bits) == 2]
        across = [f for f in flying if f[0] in scatters and len(f[0].bits) == 1]
        chain = [f for f in flying if f[0] is mix_sum]
        rest = [f for f in flying if f[0] is short]
        wide = [f for f in flying if f[0] is mlp_sum]
        left = len(mix_sum.steps)
        if near:
            now = near + chain + rest
        elif left == 2:
            now = chain + across[:1] + wide + rest
        elif left == 1:
            now = across + wide + rest or chain
        else:
            now = chain + rest or flying
        finished, wide_grads = land(now, (finished, wide_grads))
        flying = [f for f in flying if f not in now]
        if not mlp_sum.more() and not wide_grads:
            swap, held, arrived = mlp_sum.last
            wide_grads = (
                jnp.where(swap, arrived, held).astype(F32),
                jnp.where(swap, held, arrived).astype(F32),
            )
    finished = finish_ready(finished)
    block_out, token_grad = finished
    block_out, token_grad = block_out.T, token_grad.T
    swap, held, arrived = mix_sum.last
    left = 3 * part - held.shape[0]
    qkv_rows = joined(swap, held, arrived)[: 3 * part].astype(F32)
    attn_grad = jnp.where(swap, held[left:], arrived[left:]).astype(F32)
    qkv_grad = jnp.transpose(qkv_rows.reshape(3, part, width), (2, 0, 1))

    gain_grad = short.norm / norm_gain.astype(F32)
    rest = short.rest
    split = 2 * part + up_weight.shape[1]
    return (
        block_out,
        token_grad,
        gain_grad,
        qkv_grad,
        rest[: 2 * part].reshape(2, part),
        attn_grad,
        wide_grads[1],
        rest[2 * part : split],
        wide_grads[0],
        rest[split:],
    )


def solution(mesh):
    in_specs = (
        P("dp", "mp"),
        P("dp", None),
        P("mp"),
        P(None, None, "mp"),
        P(None, "mp"),
        P("mp", None),
        P(None, "mp"),
        P("mp"),
        P("mp", None),
        P("mp"),
        P("dp", None),
    )
    out_specs = (
        P("dp", "mp"),
        P("dp", "mp"),
        P("mp"),
        P(None, None, "mp"),
        P(None, "mp"),
        P("mp", None),
        P(None, "mp"),
        P("mp"),
        P("mp", None),
        P("mp"),
    )
    run = functools.partial(body, mesh.shape["dp"])
    return jax.shard_map(run, mesh=mesh, in_specs=in_specs, out_specs=out_specs, check_vma=False)
```

```python
import functools

import jax
import jax.numpy as jnp
from jax import lax
from jax.experimental import pallas as pl
from jax.experimental.pallas import tpu as pltpu
from jax.sharding import PartitionSpec as P

DH = 64
LEN = 1024
EPSILON = 1e-06
IMAGE_SLOTS = 16
PENALTY = 1024.0
BI = 256
BJ = 256
SUM_ROWS = 16
F32 = jnp.float32
BF16 = jnp.bfloat16

NN = (((1,), (0,)), ((), ()))
NT = (((1,), (1,)), ((), ()))
TN = (((0,), (0,)), ((), ()))
ANY = pl.BlockSpec(memory_space=pl.ANY)


def dot(left, right, dims=NN):
    return lax.dot_general(left, right, dims, preferred_element_type=F32)


def fold_lanes(rows):
    total = rows[:, :128]
    for start in range(128, rows.shape[1], 128):
        total = total + rows[:, start : start + 128]
    return total


def cost(microseconds, nbytes):
    return pl.CostEstimate(flops=int(microseconds * 1e3), bytes_accessed=nbytes // 1000, transcendentals=0)


def early_kernel(cot, down, attn, pick, d_act, d_att, cot_own, bias_sum):
    rows = cot[...]
    d_act[...] = dot(down[...], rows, NT).astype(BF16)
    d_att[...] = dot(attn[...], rows, NT).astype(BF16)
    own = dot(pick[...], rows, NT)
    cot_own[...] = own.astype(BF16)

    @pl.when(pl.program_id(0) == 0)
    def _():
        bias_sum[...] = jnp.zeros_like(bias_sum)

    bias_sum[...] += fold_lanes(own)


def early_call(cot, down, attn, pick, block=512):
    tokens, width = cot.shape
    seqs = tokens // LEN
    hidden, part = down.shape[0], attn.shape[0]
    steps = LEN // block
    fixed = lambda i: (0, 0)
    by_seq = lambda i: (i // steps, 0, i % steps)
    return pl.pallas_call(
        early_kernel,
        grid=(tokens // block,),
        in_specs=[
            pl.BlockSpec((block, width), lambda i: (i, 0)),
            pl.BlockSpec((hidden, width), fixed),
            pl.BlockSpec((part, width), fixed),
            pl.BlockSpec((part, width), fixed),
        ],
        out_specs=[
            pl.BlockSpec((None, hidden, block), by_seq),
            pl.BlockSpec((None, part, block), by_seq),
            pl.BlockSpec((part, block), lambda i: (0, i)),
            pl.BlockSpec((part, 128), fixed),
        ],
        out_shape=[
            jax.ShapeDtypeStruct((seqs, hidden, LEN), BF16),
            jax.ShapeDtypeStruct((seqs, part, LEN), BF16),
            jax.ShapeDtypeStruct((part, tokens), BF16),
            jax.ShapeDtypeStruct((part, 128), F32),
        ],
        cost_estimate=cost(10, 12_000_000),
        name="early",
    )(cot, down, attn, pick)


def mlp_kernel(
    pieces_order, place, own, flip_y, flip_c, flip_cy, gain_own, gain_y, gain_c, gain_cy, up, up_bias, d_act, cot,
    normed, active, d_pre, stats, bias_sum, gain_all, up_row, grads, low, high
):
    pieces = (own, flip_y, flip_c, flip_cy)
    part = own.shape[0]
    width = part * 4
    first = pl.program_id(0) == 0
    last = pl.program_id(0) == pl.num_programs(0) - 1

    @pl.when(first)
    def _():
        bias_sum[...] = jnp.zeros_like(bias_sum)
        low[...] = jnp.zeros_like(low)
        high[...] = jnp.zeros_like(high)
        for slot, piece in enumerate((gain_own, gain_y, gain_c, gain_cy)):
            gain_all[pl.ds(pl.multiple_of(place[slot], part), part), :] = piece[...].astype(F32)

    total = 0.0
    squares = 0.0
    for piece in pieces:
        rows = piece[...].astype(F32)
        total = total + jnp.sum(rows, axis=0, keepdims=True)
        squares = squares + jnp.sum(rows * rows, axis=0, keepdims=True)
    mean = total * (1.0 / width)
    scale = lax.rsqrt(squares * (1.0 / width) - mean * mean + EPSILON)
    stats[0:1, :] = mean
    stats[1:2, :] = scale
    stats[2:8, :] = jnp.zeros((6, stats.shape[1]), F32)
    for slot, piece in enumerate(pieces):
        rows = piece[...].astype(F32)
        here = pl.ds(pl.multiple_of(place[slot], part), part)
        normed[here, :] = ((rows - mean) * scale * gain_all[here, :1]).astype(BF16)

    c0 = 0.7978845608028654
    c1 = 0.044715 * c0
    def lift(start):
        here = slice(start, start + 256)
        return dot(up[:, here], normed[...], TN) + up_bias[here, :1].astype(F32)

    ahead = lift(0)
    for start in range(0, up.shape[1], 256):
        here = slice(start, start + 256)
        pre = ahead
        if start + 256 < up.shape[1]:
            ahead = lift(start + 256)
        square = pre * pre
        half = 0.5 * jnp.tanh(pre * (c0 + c1 * square)) + 0.5
        act = (pre * half).astype(BF16)
        active[here, :] = act
        slope = half + pre * (half - half * half) * (2.0 * c0 + 6.0 * c1 * square)
        grad = (d_act[here, :].astype(F32) * slope).astype(BF16)
        d_pre[here, :] = grad
        bias_sum[here, :] += fold_lanes(grad.astype(F32))
        low[here, :] += dot(act, cot[...])
        high[:, here] += dot(normed[...], grad, NT)

    @pl.when(last)
    def _():
        up_row[...] = fold_lanes(high[...] * up[...].astype(F32))
        half = low.shape[0]
        size = grads.shape[0] // len(pieces_order)
        for slot, piece in enumerate(pieces_order):
            source, start = (low, piece * size) if piece * size < half else (high, piece * size - half)
            grads[slot * size : (slot + 1) * size, :] = source[start : start + size, :].astype(BF16)


def mlp_call(pieces_order, place, pieces, gains, up, up_bias, d_act, cot, block=512):
    part, tokens = pieces[0].shape
    width = 4 * part
    seqs, hidden, _ = d_act.shape
    steps = LEN // block
    lanes = lambda i, *_: (0, i)
    by_seq = lambda i, *_: (i // steps, 0, i % steps)
    fixed = lambda i, *_: (0, 0)
    grid_spec = pltpu.PrefetchScalarGridSpec(
        num_scalar_prefetch=1,
        grid=(tokens // block,),
        in_specs=[pl.BlockSpec((part, block), lanes)] * 4
        + [pl.BlockSpec((part, 128), fixed)] * 4
        + [
            pl.BlockSpec((width, hidden), fixed),
            pl.BlockSpec((hidden, 128), fixed),
            pl.BlockSpec((None, hidden, block), by_seq),
            pl.BlockSpec((block, width), lambda i, *_: (i, 0)),
        ],
        out_specs=[
            pl.BlockSpec((None, width, block), by_seq),
            pl.BlockSpec((None, hidden, block), by_seq),
            pl.BlockSpec((None, hidden, block), by_seq),
            pl.BlockSpec((8, block), lanes),
            pl.BlockSpec((hidden, 128), fixed),
            pl.BlockSpec((width, 128), fixed),
            pl.BlockSpec((width, 128), fixed),
            pl.BlockSpec((hidden + width, width), fixed),
        ],
        scratch_shapes=[pltpu.VMEM((hidden, width), F32), pltpu.VMEM((width, hidden), F32)],
    )
    assert hidden == width
    return pl.pallas_call(
        functools.partial(mlp_kernel, pieces_order),
        grid_spec=grid_spec,
        out_shape=[
            jax.ShapeDtypeStruct((seqs, width, LEN), BF16),
            jax.ShapeDtypeStruct((seqs, hidden, LEN), BF16),
            jax.ShapeDtypeStruct((seqs, hidden, LEN), BF16),
            jax.ShapeDtypeStruct((8, tokens), F32),
            jax.ShapeDtypeStruct((hidden, 128), F32),
            jax.ShapeDtypeStruct((width, 128), F32),
            jax.ShapeDtypeStruct((width, 128), F32),
            jax.ShapeDtypeStruct((hidden + width, width), BF16),
        ],
        cost_estimate=cost(20, 30_000_000),
        name="mlp",
    )(place, *pieces, *gains, up, up_bias, d_act, cot)


def attention_kernel(
    first, count, normed, mixed_t, d_att, mask_q, mask_k, gains, cot, attended, d_mixed, gain_sum, norm_row, grads,
    total, qkv, qx, kx, vn, kt, vt, es, ps, dqa, dka, dva
):
    seq = pl.program_id(0)
    last = seq == pl.num_programs(0) - 1
    part = attended.shape[0]
    heads = part // DH
    inv_dh = 1.0 / DH

    @pl.when(seq == 0)
    def _():
        total[...] = jnp.zeros_like(total)
        gain_sum[...] = jnp.zeros_like(gain_sum)

    qkv[...] = dot(mixed_t[...], normed[...])

    def unit(start):
        raw = qkv[start : start + DH, :]
        shifted = raw - jnp.sum(raw, axis=0, keepdims=True) * inv_dh
        scale = lax.rsqrt(jnp.sum(shifted * shifted, axis=0, keepdims=True) * inv_dh + EPSILON)
        return shifted * scale, scale

    zeros = jnp.zeros((128 - DH - IMAGE_SLOTS, LEN), BF16)
    for head in range(heads):
        rows = slice(head * DH, (head + 1) * DH)
        query, _ = unit(head * DH)
        query = (query * (gains[rows, :1] * 0.125)).astype(BF16)
        qx[head] = jnp.concatenate([query, mask_q[...], zeros], axis=0)
        key, _ = unit(part + head * DH)
        key = (key * gains[part + head * DH : part + (head + 1) * DH, :1]).astype(BF16)
        kt[rows, :] = key
        kx[head] = jnp.concatenate([key, mask_k[...], zeros], axis=0).T
        value = qkv[2 * part + head * DH : 2 * part + (head + 1) * DH, :].astype(BF16)
        vt[rows, :] = value
        vn[head] = value.T
    dka[...] = jnp.zeros_like(dka)
    dva[...] = jnp.zeros_like(dva)

    def straight(units, i0, base):
        icols = pl.ds(i0, BI)
        edges = [(at, min(BJ, units * 128 - at)) for at in range(0, units * 128, BJ)]
        trips = len(edges)
        spots = [slice(at, at + size) for at, size in edges]
        places = [pl.ds(pl.multiple_of(base + at, 128), size) for at, size in edges]

        def scores(head, j, sums):
            rows = slice(head * DH, (head + 1) * DH)
            e = jnp.exp(dot(kx[head, places[j], :], qx[head, :, icols]))
            p = dot(vn[head, places[j], :], d_att[rows, icols])
            es[head % 2, spots[j], :] = e
            ps[head % 2, spots[j], :] = p
            more = (jnp.sum(e, axis=0, keepdims=True), jnp.sum(e * p, axis=0, keepdims=True))
            return more if sums is None else (sums[0] + more[0], sums[1] + more[1])

        def row_grads(head, j, inverse, inner, held):
            rows = slice(head * DH, (head + 1) * DH)
            w = es[head % 2, spots[j], :] * inverse
            d = (w * (ps[head % 2, spots[j], :] - inner)).astype(BF16)
            w = w.astype(BF16)
            out = dot(vt[rows, places[j]], w)
            query = dot(kt[rows, places[j]], d)
            dva[rows, places[j]] += dot(d_att[rows, icols], w, NT)
            dka[rows, places[j]] += dot(qx[head, :DH, icols], d, NT)
            return (out, query) if held is None else (held[0] + out, held[1] + query)

        sums = None
        for j in range(trips):
            sums = scores(0, j, sums)
        for head in range(heads):
            rows = slice(head * DH, (head + 1) * DH)
            inverse = 1.0 / sums[0]
            inner = sums[1] * inverse
            held = following = None
            for j in range(trips):
                if head + 1 < heads:
                    following = scores(head + 1, j, following)
                held = row_grads(head, j, inverse, inner, held)
            attended[rows, icols] = held[0].astype(BF16)
            dqa[rows, icols] = held[1]
            sums = following

    def query_block(ib, _):
        i0 = pl.multiple_of(ib * BI, BI)
        base = first[seq * (LEN // BI) + ib] * 128
        trips = count[seq * (LEN // BI) + ib]
        for number in range(BI // 128, LEN // 128 + 1):
            pl.when(trips == number)(functools.partial(straight, number, i0, base))
        return 0

    lax.fori_loop(0, LEN // BI, query_block, 0)

    for source, offset, factor in ((dqa, 0, 0.125), (dka, part, 1.0)):
        for head in range(heads):
            start = offset + head * DH
            u, scale = unit(start)
            e = source[head * DH : (head + 1) * DH, :] * factor
            gain_sum[start : start + DH, :] += fold_lanes(e * u)
            f = e * gains[start : start + DH, :1]
            mean_f = jnp.sum(f, axis=0, keepdims=True) * inv_dh
            mean_fu = jnp.sum(f * u, axis=0, keepdims=True) * inv_dh
            d_mixed[start : start + DH, :] = ((f - mean_f - u * mean_fu) * scale).astype(BF16)
    d_mixed[2 * part :, :] = dva[...].astype(BF16)

    split = 3 * part
    total[:split, :] += dot(d_mixed[...], normed[...], NT)
    total[split:, :] += dot(attended[...], cot[...])

    @pl.when(last)
    def _():
        norm_row[...] = jnp.sum(total[:split, :] * mixed_t[...].astype(F32), axis=0, keepdims=True)
        grads[...] = total[...].astype(BF16)


def attention_call(first, count, normed, mixed_t, d_att, mask_q, mask_k, gains, cot):
    seqs, part, _ = d_att.shape
    width = normed.shape[1]
    heads = part // DH
    fixed = lambda i, *_: (0, 0)
    by_seq = lambda i, *_: (i, 0, 0)
    grid_spec = pltpu.PrefetchScalarGridSpec(
        num_scalar_prefetch=2,
        grid=(seqs,),
        in_specs=[
            pl.BlockSpec((None, width, LEN), by_seq),
            pl.BlockSpec((3 * part, width), fixed),
            pl.BlockSpec((None, part, LEN), by_seq),
            pl.BlockSpec((None, IMAGE_SLOTS, LEN), by_seq),
            pl.BlockSpec((None, IMAGE_SLOTS, LEN), by_seq),
            pl.BlockSpec((2 * part, 128), fixed),
            pl.BlockSpec((LEN, width), lambda i, *_: (i, 0)),
        ],
        out_specs=[
            pl.BlockSpec((None, part, LEN), by_seq),
            pl.BlockSpec((None, 3 * part, LEN), by_seq),
            pl.BlockSpec((2 * part, 128), fixed),
            pl.BlockSpec((1, width), fixed),
            pl.BlockSpec((4 * part, width), fixed),
        ],
        scratch_shapes=[
            pltpu.VMEM((4 * part, width), F32),
            pltpu.VMEM((3 * part, LEN), F32),
            pltpu.VMEM((heads, 128, LEN), BF16),
            pltpu.VMEM((heads, LEN, 128), BF16),
            pltpu.VMEM((heads, LEN, DH), BF16),
            pltpu.VMEM((part, LEN), BF16),
            pltpu.VMEM((part, LEN), BF16),
            pltpu.VMEM((2, LEN, BI), F32),
            pltpu.VMEM((2, LEN, BI), F32),
            pltpu.VMEM((part, LEN), F32),
            pltpu.VMEM((part, LEN), F32),
            pltpu.VMEM((part, LEN), F32),
        ],
    )
    return pl.pallas_call(
        attention_kernel,
        grid_spec=grid_spec,
        out_shape=[
            jax.ShapeDtypeStruct((seqs, part, LEN), BF16),
            jax.ShapeDtypeStruct((seqs, 3 * part, LEN), BF16),
            jax.ShapeDtypeStruct((2 * part, 128), F32),
            jax.ShapeDtypeStruct((1, width), F32),
            jax.ShapeDtypeStruct((4 * part, width), BF16),
        ],
        cost_estimate=cost(18, 5_000_000),
        name="attention",
    )(first, count, normed, mixed_t, d_att, mask_q, mask_k, gains, cot)


def project_kernel(
    shard, active, attended, d_pre, d_mixed, normed, down, attn, up, mixed_t, gain, keep, send
):
    me = shard[0]
    part = attended.shape[0]
    out = dot(down[...], active[...], TN) + dot(attn[...], attended[...], TN)
    grad = dot(up[...], d_pre[...]) + dot(mixed_t[...], d_mixed[...], TN)
    product = grad * normed[...].astype(F32)
    sums = []
    for row in (jnp.sum(grad * gain[:, :1], axis=0, keepdims=True), jnp.sum(product, axis=0, keepdims=True)):
        high = row.astype(BF16)
        sums += [high, (row - high.astype(F32)).astype(BF16)]
    sums = jnp.concatenate(sums + [jnp.zeros((SUM_ROWS - 4, sums[0].shape[1]), BF16)], axis=0)
    for target in (keep, send):
        for slot in range(2):
            target[slot, 2 * part :, :] = sums
    for index in range(4):
        rows = slice(index * part, (index + 1) * part)
        away = jnp.bitwise_xor(me, index)
        slot = away // 2

        @pl.when(away % 2 == 0)
        def _():
            keep[slot, :part, :] = out[rows].astype(BF16)
            keep[slot, part : 2 * part, :] = grad[rows].astype(BF16)

        @pl.when(away % 2 == 1)
        def _():
            send[slot, :part, :] = out[rows].astype(BF16)
            send[slot, part : 2 * part, :] = grad[rows].astype(BF16)


def project_call(shard, active, attended, d_pre, d_mixed, normed, down, attn, up, mixed_t, gain, begin, size, block=256):
    hidden, width = down.shape
    part = attended.shape[1]
    steps = LEN // block
    ours = lambda i, *_: (begin + i // steps, 0, i % steps)
    out = lambda i, *_: (i // steps, 0, 0, i % steps)
    fixed = lambda i, *_: (0, 0)
    rows = 2 * part + SUM_ROWS
    grid_spec = pltpu.PrefetchScalarGridSpec(
        num_scalar_prefetch=1,
        grid=(size * steps,),
        in_specs=[
            pl.BlockSpec((None, hidden, block), ours),
            pl.BlockSpec((None, part, block), ours),
            pl.BlockSpec((None, hidden, block), ours),
            pl.BlockSpec((None, 3 * part, block), ours),
            pl.BlockSpec((None, width, block), ours),
            pl.BlockSpec((hidden, width), fixed),
            pl.BlockSpec((part, width), fixed),
            pl.BlockSpec((width, hidden), fixed),
            pl.BlockSpec((3 * part, width), fixed),
            pl.BlockSpec((width, 128), fixed),
        ],
        out_specs=[
            pl.BlockSpec((None, 2, rows, block), out),
            pl.BlockSpec((None, 2, rows, block), out),
        ],
    )
    return pl.pallas_call(
        project_kernel,
        grid_spec=grid_spec,
        out_shape=[
            jax.ShapeDtypeStruct((size, 2, rows, LEN), BF16),
            jax.ShapeDtypeStruct((size, 2, rows, LEN), BF16),
        ],
        cost_estimate=cost(8, 16_000_000),
        name="project",
    )(shard, active, attended, d_pre, d_mixed, normed, down, attn, up, mixed_t, gain)


def finish_kernel(keep, from_core, from_y, own_t, cot, stats, gain, bias, *rest):
    block_out, token_grad = rest[-2:]
    part = own_t.shape[0]
    inv_width = 0.25 / part
    total = keep[...].astype(F32) + from_core[...].astype(F32) + from_y[...].astype(F32)
    own = own_t[...].astype(F32)
    block_out[...] = (own + total[:part] + bias[:, :1].astype(F32)).astype(BF16)
    grad = total[part : 2 * part]
    sums = total[2 * part :]
    mean = stats[0:1, :]
    scale = stats[1:2, :]
    hat = (own - mean) * scale
    inner = grad * gain[:, :1].astype(F32) - (sums[0:1] + sums[1:2]) * inv_width - hat * ((sums[2:3] + sums[3:4]) * inv_width)
    token_grad[...] = cot[...].astype(F32) + inner * scale


def finish_call(keep, from_core, from_y, own_t, cot, stats, gain, bias, before, begin, block=512):
    part, tokens = own_t.shape
    steps = LEN // block
    size = keep.shape[0]
    fixed = lambda i: (0, 0)
    packed = pl.BlockSpec((None, None, 2 * part + SUM_ROWS, block), lambda i: (i // steps, 0, 0, i % steps))
    ours = lambda i: (0, begin * steps + i)
    here = pl.BlockSpec((part, block), ours)
    return pl.pallas_call(
        finish_kernel,
        grid=(size * steps,),
        in_specs=[
            packed, packed, packed,
            here, here,
            pl.BlockSpec((8, block), ours),
            pl.BlockSpec((part, 128), fixed),
            pl.BlockSpec((part, 128), fixed),
        ]
        + [ANY] * len(before),
        out_specs=[here, here],
        out_shape=[
            jax.ShapeDtypeStruct((part, tokens), BF16),
            jax.ShapeDtypeStruct((part, tokens), F32),
        ],
        input_output_aliases={8 + i: i for i in range(len(before))},
        cost_estimate=cost(3, 5_000_000),
        name="finish",
    )(keep, from_core, from_y, own_t, cot, stats, gain, bias, *before)


def flip(value, axis, size, bit):
    return lax.ppermute(value, axis, [(i, i ^ bit) for i in range(size)])


def tie(*trees):
    return lax.optimization_barrier(trees)


def joined(swap, held, arrived):
    return jnp.where(
        swap, jnp.concatenate([arrived, held], axis=0), jnp.concatenate([held, arrived], axis=0)
    )


def piece_order(size):
    bits = size.bit_length() - 1
    return [sum(((i >> b) & 1) << (bits - 1 - b) for b in range(bits)) for i in range(size)]


class SumOverDp:
    def __init__(self, value, size, index):
        self.size, self.index = size, index
        self.send = value
        self.steps = ["sum"] + [1 << i for i in reversed(range(size.bit_length() - 1))]

    def more(self):
        return bool(self.steps)

    def move(self, send):
        if self.steps[0] == "sum":
            return lax.all_to_all(send, "dp", 0, 0, tiled=True)
        return flip(send, "dp", self.size, self.steps[0])

    def take(self, arrived):
        step = self.steps.pop(0)
        if step == "sum":
            shares = arrived.reshape(self.size, -1, arrived.shape[1]).astype(F32)
            self.keep = jnp.sum(shares, axis=0).astype(BF16)
        else:
            self.last = ((self.index & step) > 0, self.keep, arrived)
            self.keep = joined(*self.last)
        self.send = self.keep


class ChainOverDp:
    def __init__(self, value, size, index):
        self.size, self.index = size, index
        bits = [1 << i for i in range(size.bit_length() - 1)]
        self.steps = [("sum", bit) for bit in bits] + [("join", bit) for bit in reversed(bits)]
        self.prepare(value, None)

    def prepare(self, held, arrived):
        def part(which, half):
            rows = lax.dynamic_slice_in_dim(held, which * half, half, 0)
            if arrived is None:
                return rows
            came = lax.dynamic_slice_in_dim(arrived, which * half, half, 0)
            return (rows.astype(F32) + came.astype(F32)).astype(BF16)

        rows = held.shape[0]
        if self.steps and self.steps[0][0] == "sum":
            side = ((self.index & self.steps[0][1]) > 0).astype(jnp.int32)
            self.send, self.keep = part(1 - side, rows // 2), part(side, rows // 2)
        else:
            self.keep = part(0, rows)
            self.send = self.keep

    def more(self):
        return bool(self.steps)

    def move(self, send):
        return flip(send, "dp", self.size, self.steps[0][1])

    def take(self, arrived):
        kind, bit = self.steps.pop(0)
        if kind == "sum":
            self.prepare(self.keep, arrived)
            return
        self.last = ((self.index & bit) > 0, self.keep, arrived)
        self.keep = self.send = joined(*self.last)


class ScatterOverMp:
    def __init__(self, keep, send):
        self.keep, self.send = keep, send
        self.bits = [1, 2]

    def more(self):
        return bool(self.bits)

    def move(self, send):
        return flip(send, "mp", 4, self.bits[0])

    def take(self, arrived):
        bit = self.bits.pop(0)
        if bit == 1:
            self.from_core = arrived
            self.send = (self.keep[:, 1:].astype(F32) + arrived[:, 1:].astype(F32)).astype(BF16)
        else:
            self.from_y = arrived


def land_then(flights, final, outputs):
    outputs = land(flights, outputs)
    movers = [f[0] for f in flights]
    outputs, sends = land(final, (outputs, [m.send for m in movers]))
    for mover, send in zip(movers, sends):
        mover.send = send
    return outputs


class ShortSums:
    def __init__(self, keep, send, rest, size):
        self.keep, self.send, self.rest, self.size = keep, send, rest, size
        self.steps = [("mp", 1), ("mp", 2)] + [("dp", 1 << i) for i in range(size.bit_length() - 1)]

    def more(self):
        return bool(self.steps)

    def move(self, send):
        axis, bit = self.steps[0]
        return flip(send, axis, 4 if axis == "mp" else self.size, bit)

    def take(self, arrived):
        axis, bit = self.steps.pop(0)
        if (axis, bit) == ("mp", 1):
            both = self.keep + arrived
            self.norm, self.send = both[0], both[1]
            return
        if axis == "mp":
            self.send = jnp.concatenate([self.norm + arrived, self.rest])
        else:
            self.send = self.send + arrived
        size = self.norm.shape[0]
        self.norm, self.rest = self.send[:size], self.send[size:]


def launch(movers, inputs):
    movers = [m for m in movers if m.more()]
    inputs, sends = tie(inputs, [m.send for m in movers])
    return inputs, [(m, m.move(s)) for m, s in zip(movers, sends)]


def land(flights, outputs):
    outputs, arrivals = tie(outputs, [f[1] for f in flights])
    for (mover, _), arrived in zip(flights, arrivals):
        mover.take(arrived)
    return outputs


def body(
    dp_size,
    tokens,
    image_ids,
    norm_gain,
    qkv_weight,
    qk_gain,
    attn_weight,
    up_weight,
    up_bias,
    down_weight,
    down_bias,
    cotangent,
):
    part = tokens.shape[1]
    width = cotangent.shape[1]
    seqs = image_ids.shape[0]
    me = lax.axis_index("mp")
    dp = lax.axis_index("dp")
    shard = me.astype(jnp.int32)[None]
    place = jnp.bitwise_xor(shard, jnp.array([0, 2, 1, 3], jnp.int32)) * part

    own_t = tokens.T
    from_y = flip(own_t, "mp", 4, 2)
    gain_own = jnp.broadcast_to(norm_gain[:, None], (part, 128))
    gain_y = flip(gain_own, "mp", 4, 2)
    gain_c = flip(gain_own, "mp", 4, 1)

    mixed_t = jnp.transpose(qkv_weight, (1, 2, 0)).reshape(3 * part, width)
    def column(vector):
        return jnp.broadcast_to(vector[:, None], (vector.shape[0], 128))

    columns = (column(up_bias), column(qk_gain.astype(F32).reshape(2 * part)), column(down_bias))

    slots = jnp.arange(IMAGE_SLOTS, dtype=jnp.int32)[None, :, None]
    same = image_ids[:, None, :] == slots
    mask_q = same.astype(BF16)
    mask_k = jnp.where(same | (slots >= 8), 0.0, -PENALTY).astype(BF16)
    block_first = image_ids[:, ::BI]
    block_last = image_ids[:, BI - 1 :: BI]
    starts = jnp.sum(image_ids[:, None, :] < block_first[:, :, None], axis=2, dtype=jnp.int32)
    ends = jnp.sum(image_ids[:, None, :] <= block_last[:, :, None], axis=2, dtype=jnp.int32)
    first = starts // 128
    count = ((ends + 127) // 128 - first).reshape(-1)
    first = first.reshape(-1)

    pick = (jnp.arange(part)[:, None] + me * part == jnp.arange(width)[None, :]).astype(BF16)
    pick, place, columns, (gain_y, gain_c) = tie(pick, place, columns, (gain_y, gain_c))
    up_bias_col, head_gains, bias_col = columns
    gain_cy = flip(gain_y, "mp", 4, 1)
    d_act, d_att, cot_own, cot_sum = early_call(cotangent, down_weight, attn_weight, pick)
    prepared = (
        d_act, d_att, mixed_t, up_bias_col, head_gains, mask_q, mask_k, first, count,
        bias_col,
    )
    prepared, (from_y, gain_cy) = tie(prepared, (from_y, gain_cy))
    gains = (gain_own, gain_y, gain_c, gain_cy)
    (
        d_act, d_att, mixed_t, up_bias_col, head_gains, mask_q, mask_k, first, count,
        bias_col,
    ) = prepared
    pieces = (own_t, from_y, flip(own_t, "mp", 4, 1), flip(from_y, "mp", 4, 1))
    normed, active, d_pre, stats, upbias_part, gain_all, up_row, mlp_part = mlp_call(
        tuple(piece_order(dp_size)), place, pieces, gains, up_weight, up_bias_col, d_act, cotangent
    )
    mlp_sum = SumOverDp(mlp_part, dp_size, dp)

    (states,), flying = launch([mlp_sum], (normed,))
    attended, d_mixed, qk_part, norm_row, mix_part = attention_call(
        first, count, states, mixed_t, d_att, mask_q, mask_k, head_gains, cotangent
    )
    mix_sum = ChainOverDp(mix_part, dp_size, dp)

    norm_vec = norm_row[0] + jnp.sum(up_row, axis=1)
    norm_parts = norm_vec.reshape(4, part)
    norm_parts = [lax.dynamic_index_in_dim(norm_parts, jnp.bitwise_xor(me, m), 0, False) for m in range(4)]
    short = ShortSums(
        jnp.stack([norm_parts[0], norm_parts[2]]),
        jnp.stack([norm_parts[1], norm_parts[3]]),
        jnp.concatenate([jnp.sum(qk_part, axis=1), jnp.sum(upbias_part, axis=1), jnp.sum(cot_sum, axis=1)]),
        dp_size,
    )

    runs = [(seq, 1) for seq in range(seqs)]
    scatters = []
    for begin, size in runs:
        busy = [f[0] for f in flying]
        along = [m for m in [mix_sum, mlp_sum, short] + scatters if m.more() and m not in busy]
        (att, dm), flights = launch(along, (attended, d_mixed))
        flying = flying + flights
        sent = project_call(
            shard, active, att, d_pre, dm, normed, down_weight, attn_weight, up_weight, mixed_t, gain_all, begin, size
        )
        late = [f for f in flights if begin == 0 and f[0] is mix_sum]
        final = [f for f in flying if f[0] is mix_sum and f not in late]
        keep, send = land_then([f for f in flying if f not in late + final], final, sent)
        flying = late
        scatters.append(ScatterOverMp(keep, send))

    finished = ()
    wide_grads = ()
    done = set()

    def finish_ready(finished):
        for (begin, _), scatter in zip(runs, scatters):
            if not scatter.more() and begin not in done:
                done.add(begin)
                finished = finish_call(
                    scatter.keep, scatter.from_core, scatter.from_y, own_t, cot_own, stats, gain_own, bias_col,
                    finished, begin,
                )
        return finished

    while True:
        busy = [f[0] for f in flying]
        ready = [m for m in [mix_sum] + scatters + [short, mlp_sum] if m.more() and m not in busy]
        finished, flights = launch(ready, finished)
        flying = flying + flights
        if not flying:
            break
        finished = finish_ready(finished)
        near = [f for f in flying if f[0] in scatters and len(f[0].bits) == 2]
        across = [f for f in flying if f[0] in scatters and len(f[0].bits) == 1]
        chain = [f for f in flying if f[0] is mix_sum]
        rest = [f for f in flying if f[0] is short]
        wide = [f for f in flying if f[0] is mlp_sum]
        left = len(mix_sum.steps)
        if near:
            now = near + chain + rest
        elif left == 2:
            now = chain + across[:1] + wide + rest
        elif left == 1:
            now = across + wide + rest or chain
        else:
            now = chain + rest or flying
        final = [f for f in now if f[0] is mix_sum]
        finished, wide_grads = land_then([f for f in now if f not in final], final, (finished, wide_grads))
        flying = [f for f in flying if f not in now]
        if not mlp_sum.more() and not wide_grads:
            swap, held, arrived = mlp_sum.last
            wide_grads = (
                jnp.where(swap, arrived, held).astype(F32),
                jnp.where(swap, held, arrived).astype(F32),
            )
    finished = finish_ready(finished)
    block_out, token_grad = finished
    block_out, token_grad = block_out.T, token_grad.T
    swap, held, arrived = mix_sum.last
    left = 3 * part - held.shape[0]
    qkv_rows = joined(swap, held, arrived)[: 3 * part].astype(F32)
    attn_grad = jnp.where(swap, held[left:], arrived[left:]).astype(F32)
    qkv_grad = jnp.transpose(qkv_rows.reshape(3, part, width), (2, 0, 1))

    gain_grad = short.norm / norm_gain.astype(F32)
    rest = short.rest
    split = 2 * part + up_weight.shape[1]
    return (
        block_out,
        token_grad,
        gain_grad,
        qkv_grad,
        rest[: 2 * part].reshape(2, part),
        attn_grad,
        wide_grads[1],
        rest[2 * part : split],
        wide_grads[0],
        rest[split:],
    )


def solution(mesh):
    in_specs = (
        P("dp", "mp"),
        P("dp", None),
        P("mp"),
        P(None, None, "mp"),
        P(None, "mp"),
        P("mp", None),
        P(None, "mp"),
        P("mp"),
        P("mp", None),
        P("mp"),
        P("dp", None),
    )
    out_specs = (
        P("dp", "mp"),
        P("dp", "mp"),
        P("mp"),
        P(None, None, "mp"),
        P(None, "mp"),
        P("mp", None),
        P(None, "mp"),
        P("mp"),
        P("mp", None),
        P("mp"),
    )
    run = functools.partial(body, mesh.shape["dp"])
    return jax.shard_map(run, mesh=mesh, in_specs=in_specs, out_specs=out_specs, check_vma=False)
```

```python
import functools

import jax
import jax.numpy as jnp
from jax import lax
from jax.experimental import pallas as pl
from jax.experimental.pallas import tpu as pltpu
from jax.sharding import PartitionSpec as P

DH = 64
LEN = 1024
EPSILON = 1e-06
IMAGE_SLOTS = 16
PENALTY = 1024.0
BI = 256
BJ = 256
SUM_ROWS = 16
F32 = jnp.float32
BF16 = jnp.bfloat16

NN = (((1,), (0,)), ((), ()))
NT = (((1,), (1,)), ((), ()))
TN = (((0,), (0,)), ((), ()))
ANY = pl.BlockSpec(memory_space=pl.ANY)


def dot(left, right, dims=NN):
    return lax.dot_general(left, right, dims, preferred_element_type=F32)


def fold_lanes(rows):
    total = rows[:, :128]
    for start in range(128, rows.shape[1], 128):
        total = total + rows[:, start : start + 128]
    return total


def cost(microseconds, nbytes):
    return pl.CostEstimate(flops=int(microseconds * 1e3), bytes_accessed=nbytes // 1000, transcendentals=0)


def early_kernel(cot, down, attn, pick, d_act, d_att, cot_own, bias_sum):
    rows = cot[...]
    d_act[...] = dot(down[...], rows, NT).astype(BF16)
    d_att[...] = dot(attn[...], rows, NT).astype(BF16)
    own = dot(pick[...], rows, NT)
    cot_own[...] = own.astype(BF16)

    @pl.when(pl.program_id(0) == 0)
    def _():
        bias_sum[...] = jnp.zeros_like(bias_sum)

    bias_sum[...] += fold_lanes(own)


def early_call(cot, down, attn, pick, block=512):
    tokens, width = cot.shape
    seqs = tokens // LEN
    hidden, part = down.shape[0], attn.shape[0]
    steps = LEN // block
    fixed = lambda i: (0, 0)
    by_seq = lambda i: (i // steps, 0, i % steps)
    return pl.pallas_call(
        early_kernel,
        grid=(tokens // block,),
        in_specs=[
            pl.BlockSpec((block, width), lambda i: (i, 0)),
            pl.BlockSpec((hidden, width), fixed),
            pl.BlockSpec((part, width), fixed),
            pl.BlockSpec((part, width), fixed),
        ],
        out_specs=[
            pl.BlockSpec((None, hidden, block), by_seq),
            pl.BlockSpec((None, part, block), by_seq),
            pl.BlockSpec((part, block), lambda i: (0, i)),
            pl.BlockSpec((part, 128), fixed),
        ],
        out_shape=[
            jax.ShapeDtypeStruct((seqs, hidden, LEN), BF16),
            jax.ShapeDtypeStruct((seqs, part, LEN), BF16),
            jax.ShapeDtypeStruct((part, tokens), BF16),
            jax.ShapeDtypeStruct((part, 128), F32),
        ],
        cost_estimate=cost(10, 12_000_000),
        name="early",
    )(cot, down, attn, pick)


def mlp_kernel(
    pieces_order, place, own, flip_y, flip_c, flip_cy, gain_own, gain_y, gain_c, gain_cy, up, up_bias, d_act, cot,
    normed, active, d_pre, stats, bias_sum, gain_all, up_row, grads, low, high
):
    pieces = (own, flip_y, flip_c, flip_cy)
    part = own.shape[0]
    width = part * 4
    first = pl.program_id(0) == 0
    last = pl.program_id(0) == pl.num_programs(0) - 1

    @pl.when(first)
    def _():
        bias_sum[...] = jnp.zeros_like(bias_sum)
        low[...] = jnp.zeros_like(low)
        high[...] = jnp.zeros_like(high)
        for slot, piece in enumerate((gain_own, gain_y, gain_c, gain_cy)):
            gain_all[pl.ds(pl.multiple_of(place[slot], part), part), :] = piece[...].astype(F32)

    total = 0.0
    squares = 0.0
    for piece in pieces:
        rows = piece[...].astype(F32)
        total = total + jnp.sum(rows, axis=0, keepdims=True)
        squares = squares + jnp.sum(rows * rows, axis=0, keepdims=True)
    mean = total * (1.0 / width)
    scale = lax.rsqrt(squares * (1.0 / width) - mean * mean + EPSILON)
    stats[0:1, :] = mean
    stats[1:2, :] = scale
    stats[2:8, :] = jnp.zeros((6, stats.shape[1]), F32)
    for slot, piece in enumerate(pieces):
        rows = piece[...].astype(F32)
        here = pl.ds(pl.multiple_of(place[slot], part), part)
        normed[here, :] = ((rows - mean) * scale * gain_all[here, :1]).astype(BF16)

    c0 = 0.7978845608028654
    c1 = 0.044715 * c0
    def lift(start):
        here = slice(start, start + 256)
        return dot(up[:, here], normed[...], TN) + up_bias[here, :1].astype(F32)

    ahead = lift(0)
    for start in range(0, up.shape[1], 256):
        here = slice(start, start + 256)
        pre = ahead
        if start + 256 < up.shape[1]:
            ahead = lift(start + 256)
        square = pre * pre
        half = 0.5 * jnp.tanh(pre * (c0 + c1 * square)) + 0.5
        act = (pre * half).astype(BF16)
        active[here, :] = act
        slope = half + pre * (half - half * half) * (2.0 * c0 + 6.0 * c1 * square)
        grad = (d_act[here, :].astype(F32) * slope).astype(BF16)
        d_pre[here, :] = grad
        bias_sum[here, :] += fold_lanes(grad.astype(F32))
        low[here, :] += dot(act, cot[...])
        high[:, here] += dot(normed[...], grad, NT)

    @pl.when(last)
    def _():
        up_row[...] = fold_lanes(high[...] * up[...].astype(F32))
        half = low.shape[0]
        size = grads.shape[0] // len(pieces_order)
        for slot, piece in enumerate(pieces_order):
            source, start = (low, piece * size) if piece * size < half else (high, piece * size - half)
            grads[slot * size : (slot + 1) * size, :] = source[start : start + size, :].astype(BF16)


def mlp_call(pieces_order, place, pieces, gains, up, up_bias, d_act, cot, block=512):
    part, tokens = pieces[0].shape
    width = 4 * part
    seqs, hidden, _ = d_act.shape
    steps = LEN // block
    lanes = lambda i, *_: (0, i)
    by_seq = lambda i, *_: (i // steps, 0, i % steps)
    fixed = lambda i, *_: (0, 0)
    grid_spec = pltpu.PrefetchScalarGridSpec(
        num_scalar_prefetch=1,
        grid=(tokens // block,),
        in_specs=[pl.BlockSpec((part, block), lanes)] * 4
        + [pl.BlockSpec((part, 128), fixed)] * 4
        + [
            pl.BlockSpec((width, hidden), fixed),
            pl.BlockSpec((hidden, 128), fixed),
            pl.BlockSpec((None, hidden, block), by_seq),
            pl.BlockSpec((block, width), lambda i, *_: (i, 0)),
        ],
        out_specs=[
            pl.BlockSpec((None, width, block), by_seq),
            pl.BlockSpec((None, hidden, block), by_seq),
            pl.BlockSpec((None, hidden, block), by_seq),
            pl.BlockSpec((8, block), lanes),
            pl.BlockSpec((hidden, 128), fixed),
            pl.BlockSpec((width, 128), fixed),
            pl.BlockSpec((width, 128), fixed),
            pl.BlockSpec((hidden + width, width), fixed),
        ],
        scratch_shapes=[pltpu.VMEM((hidden, width), F32), pltpu.VMEM((width, hidden), F32)],
    )
    assert hidden == width
    return pl.pallas_call(
        functools.partial(mlp_kernel, pieces_order),
        grid_spec=grid_spec,
        out_shape=[
            jax.ShapeDtypeStruct((seqs, width, LEN), BF16),
            jax.ShapeDtypeStruct((seqs, hidden, LEN), BF16),
            jax.ShapeDtypeStruct((seqs, hidden, LEN), BF16),
            jax.ShapeDtypeStruct((8, tokens), F32),
            jax.ShapeDtypeStruct((hidden, 128), F32),
            jax.ShapeDtypeStruct((width, 128), F32),
            jax.ShapeDtypeStruct((width, 128), F32),
            jax.ShapeDtypeStruct((hidden + width, width), BF16),
        ],
        cost_estimate=cost(20, 30_000_000),
        name="mlp",
    )(place, *pieces, *gains, up, up_bias, d_act, cot)


def attention_kernel(
    first, count, normed, mixed_t, d_att, mask_q, mask_k, gains, cot, attended, d_mixed, gain_sum, norm_row, grads,
    total, qkv, qx, kx, vn, kt, vt, es, ps, dqa, dka, dva
):
    seq = pl.program_id(0)
    last = seq == pl.num_programs(0) - 1
    part = attended.shape[0]
    heads = part // DH
    inv_dh = 1.0 / DH

    @pl.when(seq == 0)
    def _():
        total[...] = jnp.zeros_like(total)
        gain_sum[...] = jnp.zeros_like(gain_sum)

    qkv[...] = dot(mixed_t[...], normed[...])

    def unit(start):
        raw = qkv[start : start + DH, :]
        shifted = raw - jnp.sum(raw, axis=0, keepdims=True) * inv_dh
        scale = lax.rsqrt(jnp.sum(shifted * shifted, axis=0, keepdims=True) * inv_dh + EPSILON)
        return shifted * scale, scale

    zeros = jnp.zeros((128 - DH - IMAGE_SLOTS, LEN), BF16)
    for head in range(heads):
        rows = slice(head * DH, (head + 1) * DH)
        query, _ = unit(head * DH)
        query = (query * (gains[rows, :1] * 0.125)).astype(BF16)
        qx[head] = jnp.concatenate([query, mask_q[...], zeros], axis=0)
        key, _ = unit(part + head * DH)
        key = (key * gains[part + head * DH : part + (head + 1) * DH, :1]).astype(BF16)
        kt[rows, :] = key
        kx[head] = jnp.concatenate([key, mask_k[...], zeros], axis=0).T
        value = qkv[2 * part + head * DH : 2 * part + (head + 1) * DH, :].astype(BF16)
        vt[rows, :] = value
        vn[head] = value.T
    dka[...] = jnp.zeros_like(dka)
    dva[...] = jnp.zeros_like(dva)

    def straight(units, i0, base):
        icols = pl.ds(i0, BI)
        edges = [(at, min(BJ, units * 128 - at)) for at in range(0, units * 128, BJ)]
        trips = len(edges)
        spots = [slice(at, at + size) for at, size in edges]
        places = [pl.ds(pl.multiple_of(base + at, 128), size) for at, size in edges]

        def scores(head, j, sums):
            rows = slice(head * DH, (head + 1) * DH)
            e = jnp.exp(dot(kx[head, places[j], :], qx[head, :, icols]))
            p = dot(vn[head, places[j], :], d_att[rows, icols])
            es[head % 2, spots[j], :] = e
            ps[head % 2, spots[j], :] = p
            more = (jnp.sum(e, axis=0, keepdims=True), jnp.sum(e * p, axis=0, keepdims=True))
            return more if sums is None else (sums[0] + more[0], sums[1] + more[1])

        def row_grads(head, j, inverse, inner, held):
            rows = slice(head * DH, (head + 1) * DH)
            w = es[head % 2, spots[j], :] * inverse
            d = (w * (ps[head % 2, spots[j], :] - inner)).astype(BF16)
            w = w.astype(BF16)
            out = dot(vt[rows, places[j]], w)
            query = dot(kt[rows, places[j]], d)
            dva[rows, places[j]] += dot(d_att[rows, icols], w, NT)
            dka[rows, places[j]] += dot(qx[head, :DH, icols], d, NT)
            return (out, query) if held is None else (held[0] + out, held[1] + query)

        sums = None
        for j in range(trips):
            sums = scores(0, j, sums)
        for head in range(heads):
            rows = slice(head * DH, (head + 1) * DH)
            inverse = 1.0 / sums[0]
            inner = sums[1] * inverse
            held = following = None
            for j in range(trips):
                if head + 1 < heads:
                    following = scores(head + 1, j, following)
                held = row_grads(head, j, inverse, inner, held)
            attended[rows, icols] = held[0].astype(BF16)
            dqa[rows, icols] = held[1]
            sums = following

    def query_block(ib, _):
        i0 = pl.multiple_of(ib * BI, BI)
        base = first[seq * (LEN // BI) + ib] * 128
        trips = count[seq * (LEN // BI) + ib]
        for number in range(BI // 128, LEN // 128 + 1):
            pl.when(trips == number)(functools.partial(straight, number, i0, base))
        return 0

    lax.fori_loop(0, LEN // BI, query_block, 0)

    for source, offset, factor in ((dqa, 0, 0.125), (dka, part, 1.0)):
        for head in range(heads):
            start = offset + head * DH
            u, scale = unit(start)
            e = source[head * DH : (head + 1) * DH, :] * factor
            gain_sum[start : start + DH, :] += fold_lanes(e * u)
            f = e * gains[start : start + DH, :1]
            mean_f = jnp.sum(f, axis=0, keepdims=True) * inv_dh
            mean_fu = jnp.sum(f * u, axis=0, keepdims=True) * inv_dh
            d_mixed[start : start + DH, :] = ((f - mean_f - u * mean_fu) * scale).astype(BF16)
    d_mixed[2 * part :, :] = dva[...].astype(BF16)

    split = 3 * part
    total[:split, :] += dot(d_mixed[...], normed[...], NT)
    total[split:, :] += dot(attended[...], cot[...])

    @pl.when(last)
    def _():
        norm_row[...] = jnp.sum(total[:split, :] * mixed_t[...].astype(F32), axis=0, keepdims=True)
        grads[...] = total[...].astype(BF16)


def attention_call(first, count, normed, mixed_t, d_att, mask_q, mask_k, gains, cot):
    seqs, part, _ = d_att.shape
    width = normed.shape[1]
    heads = part // DH
    fixed = lambda i, *_: (0, 0)
    by_seq = lambda i, *_: (i, 0, 0)
    grid_spec = pltpu.PrefetchScalarGridSpec(
        num_scalar_prefetch=2,
        grid=(seqs,),
        in_specs=[
            pl.BlockSpec((None, width, LEN), by_seq),
            pl.BlockSpec((3 * part, width), fixed),
            pl.BlockSpec((None, part, LEN), by_seq),
            pl.BlockSpec((None, IMAGE_SLOTS, LEN), by_seq),
            pl.BlockSpec((None, IMAGE_SLOTS, LEN), by_seq),
            pl.BlockSpec((2 * part, 128), fixed),
            pl.BlockSpec((LEN, width), lambda i, *_: (i, 0)),
        ],
        out_specs=[
            pl.BlockSpec((None, part, LEN), by_seq),
            pl.BlockSpec((None, 3 * part, LEN), by_seq),
            pl.BlockSpec((2 * part, 128), fixed),
            pl.BlockSpec((1, width), fixed),
            pl.BlockSpec((4 * part, width), fixed),
        ],
        scratch_shapes=[
            pltpu.VMEM((4 * part, width), F32),
            pltpu.VMEM((3 * part, LEN), F32),
            pltpu.VMEM((heads, 128, LEN), BF16),
            pltpu.VMEM((heads, LEN, 128), BF16),
            pltpu.VMEM((heads, LEN, DH), BF16),
            pltpu.VMEM((part, LEN), BF16),
            pltpu.VMEM((part, LEN), BF16),
            pltpu.VMEM((2, LEN, BI), F32),
            pltpu.VMEM((2, LEN, BI), F32),
            pltpu.VMEM((part, LEN), F32),
            pltpu.VMEM((part, LEN), F32),
            pltpu.VMEM((part, LEN), F32),
        ],
    )
    return pl.pallas_call(
        attention_kernel,
        grid_spec=grid_spec,
        out_shape=[
            jax.ShapeDtypeStruct((seqs, part, LEN), BF16),
            jax.ShapeDtypeStruct((seqs, 3 * part, LEN), BF16),
            jax.ShapeDtypeStruct((2 * part, 128), F32),
            jax.ShapeDtypeStruct((1, width), F32),
            jax.ShapeDtypeStruct((4 * part, width), BF16),
        ],
        cost_estimate=cost(18, 5_000_000),
        name="attention",
    )(first, count, normed, mixed_t, d_att, mask_q, mask_k, gains, cot)


def project_kernel(
    shard, active, attended, d_pre, d_mixed, normed, down, attn, up, mixed_t, gain, keep, send
):
    me = shard[0]
    part = attended.shape[0]
    out = dot(down[...], active[...], TN) + dot(attn[...], attended[...], TN)
    grad = dot(up[...], d_pre[...]) + dot(mixed_t[...], d_mixed[...], TN)
    product = grad * normed[...].astype(F32)
    sums = []
    for row in (jnp.sum(grad * gain[:, :1], axis=0, keepdims=True), jnp.sum(product, axis=0, keepdims=True)):
        high = row.astype(BF16)
        sums += [high, (row - high.astype(F32)).astype(BF16)]
    sums = jnp.concatenate(sums + [jnp.zeros((SUM_ROWS - 4, sums[0].shape[1]), BF16)], axis=0)
    for target in (keep, send):
        for slot in range(2):
            target[slot, 2 * part :, :] = sums
    for index in range(4):
        rows = slice(index * part, (index + 1) * part)
        away = jnp.bitwise_xor(me, index)
        slot = away // 2

        @pl.when(away % 2 == 0)
        def _():
            keep[slot, :part, :] = out[rows].astype(BF16)
            keep[slot, part : 2 * part, :] = grad[rows].astype(BF16)

        @pl.when(away % 2 == 1)
        def _():
            send[slot, :part, :] = out[rows].astype(BF16)
            send[slot, part : 2 * part, :] = grad[rows].astype(BF16)


def project_call(shard, active, attended, d_pre, d_mixed, normed, down, attn, up, mixed_t, gain, begin, size, block=256):
    hidden, width = down.shape
    part = attended.shape[1]
    steps = LEN // block
    ours = lambda i, *_: (begin + i // steps, 0, i % steps)
    out = lambda i, *_: (i // steps, 0, 0, i % steps)
    fixed = lambda i, *_: (0, 0)
    rows = 2 * part + SUM_ROWS
    grid_spec = pltpu.PrefetchScalarGridSpec(
        num_scalar_prefetch=1,
        grid=(size * steps,),
        in_specs=[
            pl.BlockSpec((None, hidden, block), ours),
            pl.BlockSpec((None, part, block), ours),
            pl.BlockSpec((None, hidden, block), ours),
            pl.BlockSpec((None, 3 * part, block), ours),
            pl.BlockSpec((None, width, block), ours),
            pl.BlockSpec((hidden, width), fixed),
            pl.BlockSpec((part, width), fixed),
            pl.BlockSpec((width, hidden), fixed),
            pl.BlockSpec((3 * part, width), fixed),
            pl.BlockSpec((width, 128), fixed),
        ],
        out_specs=[
            pl.BlockSpec((None, 2, rows, block), out),
            pl.BlockSpec((None, 2, rows, block), out),
        ],
    )
    return pl.pallas_call(
        project_kernel,
        grid_spec=grid_spec,
        out_shape=[
            jax.ShapeDtypeStruct((size, 2, rows, LEN), BF16),
            jax.ShapeDtypeStruct((size, 2, rows, LEN), BF16),
        ],
        cost_estimate=cost(8, 16_000_000),
        name="project",
    )(shard, active, attended, d_pre, d_mixed, normed, down, attn, up, mixed_t, gain)


def finish_kernel(keep, from_core, from_y, own_t, cot, stats, gain, bias, *rest):
    block_out, token_grad = rest[-2:]
    part = own_t.shape[0]
    inv_width = 0.25 / part
    total = keep[...].astype(F32) + from_core[...].astype(F32) + from_y[...].astype(F32)
    own = own_t[...].astype(F32)
    block_out[...] = (own + total[:part] + bias[:, :1].astype(F32)).astype(BF16)
    grad = total[part : 2 * part]
    sums = total[2 * part :]
    mean = stats[0:1, :]
    scale = stats[1:2, :]
    hat = (own - mean) * scale
    inner = grad * gain[:, :1].astype(F32) - (sums[0:1] + sums[1:2]) * inv_width - hat * ((sums[2:3] + sums[3:4]) * inv_width)
    token_grad[...] = cot[...].astype(F32) + inner * scale


def finish_call(keep, from_core, from_y, own_t, cot, stats, gain, bias, before, begin, block=512):
    part, tokens = own_t.shape
    steps = LEN // block
    size = keep.shape[0]
    fixed = lambda i: (0, 0)
    packed = pl.BlockSpec((None, None, 2 * part + SUM_ROWS, block), lambda i: (i // steps, 0, 0, i % steps))
    ours = lambda i: (0, begin * steps + i)
    here = pl.BlockSpec((part, block), ours)
    return pl.pallas_call(
        finish_kernel,
        grid=(size * steps,),
        in_specs=[
            packed, packed, packed,
            here, here,
            pl.BlockSpec((8, block), ours),
            pl.BlockSpec((part, 128), fixed),
            pl.BlockSpec((part, 128), fixed),
        ]
        + [ANY] * len(before),
        out_specs=[here, here],
        out_shape=[
            jax.ShapeDtypeStruct((part, tokens), BF16),
            jax.ShapeDtypeStruct((part, tokens), F32),
        ],
        input_output_aliases={8 + i: i for i in range(len(before))},
        cost_estimate=cost(3, 5_000_000),
        name="finish",
    )(keep, from_core, from_y, own_t, cot, stats, gain, bias, *before)


def flip(value, axis, size, bit):
    return lax.ppermute(value, axis, [(i, i ^ bit) for i in range(size)])


def tie(*trees):
    return lax.optimization_barrier(trees)


def joined(swap, held, arrived):
    return jnp.where(
        swap, jnp.concatenate([arrived, held], axis=0), jnp.concatenate([held, arrived], axis=0)
    )


def piece_order(size):
    bits = size.bit_length() - 1
    return [sum(((i >> b) & 1) << (bits - 1 - b) for b in range(bits)) for i in range(size)]


class SumOverDp:
    def __init__(self, value, size, index):
        self.size, self.index = size, index
        self.send = value
        self.steps = ["sum"] + [1 << i for i in reversed(range(size.bit_length() - 1))]

    def more(self):
        return bool(self.steps)

    def move(self, send):
        if self.steps[0] == "sum":
            return lax.all_to_all(send, "dp", 0, 0, tiled=True)
        return flip(send, "dp", self.size, self.steps[0])

    def take(self, arrived):
        step = self.steps.pop(0)
        if step == "sum":
            shares = arrived.reshape(self.size, -1, arrived.shape[1]).astype(F32)
            self.keep = jnp.sum(shares, axis=0).astype(BF16)
        else:
            self.last = ((self.index & step) > 0, self.keep, arrived)
            self.keep = joined(*self.last)
        self.send = self.keep


class ChainOverDp:
    def __init__(self, value, size, index):
        self.size, self.index = size, index
        bits = [1 << i for i in range(size.bit_length() - 1)]
        self.steps = [("sum", bit) for bit in bits] + [("join", bit) for bit in reversed(bits)]
        self.prepare(value, None)

    def prepare(self, held, arrived):
        def part(which, half):
            rows = lax.dynamic_slice_in_dim(held, which * half, half, 0)
            if arrived is None:
                return rows
            came = lax.dynamic_slice_in_dim(arrived, which * half, half, 0)
            return (rows.astype(F32) + came.astype(F32)).astype(BF16)

        rows = held.shape[0]
        if self.steps and self.steps[0][0] == "sum":
            side = ((self.index & self.steps[0][1]) > 0).astype(jnp.int32)
            self.send, self.keep = part(1 - side, rows // 2), part(side, rows // 2)
        else:
            self.keep = part(0, rows)
            self.send = self.keep

    def more(self):
        return bool(self.steps)

    def move(self, send):
        return flip(send, "dp", self.size, self.steps[0][1])

    def take(self, arrived):
        kind, bit = self.steps.pop(0)
        if kind == "sum":
            self.prepare(self.keep, arrived)
            return
        self.last = ((self.index & bit) > 0, self.keep, arrived)
        self.keep = self.send = joined(*self.last)


class ScatterOverMp:
    def __init__(self, keep, send):
        self.keep, self.send = keep, send
        self.bits = [1, 2]

    def more(self):
        return bool(self.bits)

    def move(self, send):
        return flip(send, "mp", 4, self.bits[0])

    def take(self, arrived):
        bit = self.bits.pop(0)
        if bit == 1:
            self.from_core = arrived
            self.send = (self.keep[:, 1:].astype(F32) + arrived[:, 1:].astype(F32)).astype(BF16)
        else:
            self.from_y = arrived


def land_in_turn(phases, outputs):
    movers = []
    for flights in phases:
        outputs, sends, arrivals = tie(outputs, [m.send for m in movers], [f[1] for f in flights])
        for mover, send in zip(movers, sends):
            mover.send = send
        for (mover, _), arrived in zip(flights, arrivals):
            mover.take(arrived)
        movers += [f[0] for f in flights]
    return outputs


class ShortSums:
    def __init__(self, keep, send, rest, size):
        self.keep, self.send, self.rest, self.size = keep, send, rest, size
        self.steps = [("mp", 1), ("mp", 2)] + [("dp", 1 << i) for i in range(size.bit_length() - 1)]

    def more(self):
        return bool(self.steps)

    def move(self, send):
        axis, bit = self.steps[0]
        return flip(send, axis, 4 if axis == "mp" else self.size, bit)

    def take(self, arrived):
        axis, bit = self.steps.pop(0)
        if (axis, bit) == ("mp", 1):
            both = self.keep + arrived
            self.norm, self.send = both[0], both[1]
            return
        if axis == "mp":
            self.send = jnp.concatenate([self.norm + arrived, self.rest])
        else:
            self.send = self.send + arrived
        size = self.norm.shape[0]
        self.norm, self.rest = self.send[:size], self.send[size:]


def launch(movers, inputs):
    movers = [m for m in movers if m.more()]
    inputs, sends = tie(inputs, [m.send for m in movers])
    return inputs, [(m, m.move(s)) for m, s in zip(movers, sends)]


def land(flights, outputs):
    outputs, arrivals = tie(outputs, [f[1] for f in flights])
    for (mover, _), arrived in zip(flights, arrivals):
        mover.take(arrived)
    return outputs


def body(
    dp_size,
    tokens,
    image_ids,
    norm_gain,
    qkv_weight,
    qk_gain,
    attn_weight,
    up_weight,
    up_bias,
    down_weight,
    down_bias,
    cotangent,
):
    part = tokens.shape[1]
    width = cotangent.shape[1]
    seqs = image_ids.shape[0]
    me = lax.axis_index("mp")
    dp = lax.axis_index("dp")
    shard = me.astype(jnp.int32)[None]
    place = jnp.bitwise_xor(shard, jnp.array([0, 2, 1, 3], jnp.int32)) * part

    own_t = tokens.T
    from_y = flip(own_t, "mp", 4, 2)
    gain_own = jnp.broadcast_to(norm_gain[:, None], (part, 128))
    gain_y = flip(gain_own, "mp", 4, 2)
    gain_c = flip(gain_own, "mp", 4, 1)

    mixed_t = jnp.transpose(qkv_weight, (1, 2, 0)).reshape(3 * part, width)
    def column(vector):
        return jnp.broadcast_to(vector[:, None], (vector.shape[0], 128))

    columns = (column(up_bias), column(qk_gain.astype(F32).reshape(2 * part)), column(down_bias))

    slots = jnp.arange(IMAGE_SLOTS, dtype=jnp.int32)[None, :, None]
    same = image_ids[:, None, :] == slots
    mask_q = same.astype(BF16)
    mask_k = jnp.where(same | (slots >= 8), 0.0, -PENALTY).astype(BF16)
    block_first = image_ids[:, ::BI]
    block_last = image_ids[:, BI - 1 :: BI]
    starts = jnp.sum(image_ids[:, None, :] < block_first[:, :, None], axis=2, dtype=jnp.int32)
    ends = jnp.sum(image_ids[:, None, :] <= block_last[:, :, None], axis=2, dtype=jnp.int32)
    first = starts // 128
    count = ((ends + 127) // 128 - first).reshape(-1)
    first = first.reshape(-1)

    pick = (jnp.arange(part)[:, None] + me * part == jnp.arange(width)[None, :]).astype(BF16)
    pick, place, columns, (gain_y, gain_c) = tie(pick, place, columns, (gain_y, gain_c))
    up_bias_col, head_gains, bias_col = columns
    gain_cy = flip(gain_y, "mp", 4, 1)
    d_act, d_att, cot_own, cot_sum = early_call(cotangent, down_weight, attn_weight, pick)
    prepared = (
        d_act, d_att, mixed_t, up_bias_col, head_gains, mask_q, mask_k, first, count,
        bias_col,
    )
    prepared, (from_y, gain_cy) = tie(prepared, (from_y, gain_cy))
    gains = (gain_own, gain_y, gain_c, gain_cy)
    (
        d_act, d_att, mixed_t, up_bias_col, head_gains, mask_q, mask_k, first, count,
        bias_col,
    ) = prepared
    pieces = (own_t, from_y, flip(own_t, "mp", 4, 1), flip(from_y, "mp", 4, 1))
    normed, active, d_pre, stats, upbias_part, gain_all, up_row, mlp_part = mlp_call(
        tuple(piece_order(dp_size)), place, pieces, gains, up_weight, up_bias_col, d_act, cotangent
    )
    mlp_sum = SumOverDp(mlp_part, dp_size, dp)

    (states,), flying = launch([mlp_sum], (normed,))
    attended, d_mixed, qk_part, norm_row, mix_part = attention_call(
        first, count, states, mixed_t, d_att, mask_q, mask_k, head_gains, cotangent
    )
    mix_sum = ChainOverDp(mix_part, dp_size, dp)

    norm_vec = norm_row[0] + jnp.sum(up_row, axis=1)
    norm_parts = norm_vec.reshape(4, part)
    norm_parts = [lax.dynamic_index_in_dim(norm_parts, jnp.bitwise_xor(me, m), 0, False) for m in range(4)]
    short = ShortSums(
        jnp.stack([norm_parts[0], norm_parts[2]]),
        jnp.stack([norm_parts[1], norm_parts[3]]),
        jnp.concatenate([jnp.sum(qk_part, axis=1), jnp.sum(upbias_part, axis=1), jnp.sum(cot_sum, axis=1)]),
        dp_size,
    )

    runs = [(seq, 1) for seq in range(seqs)]
    scatters = []
    for begin, size in runs:
        busy = [f[0] for f in flying]
        along = [m for m in [mix_sum, mlp_sum, short] + scatters if m.more() and m not in busy]
        (att, dm), flights = launch(along, (attended, d_mixed))
        flying = flying + flights
        sent = project_call(
            shard, active, att, d_pre, dm, normed, down_weight, attn_weight, up_weight, mixed_t, gain_all, begin, size
        )
        final = seqs - 1
        late = [f for f in flights if begin == 0 and f[0] is mix_sum or begin == final and f[0] is scatters[0]]
        wide = [f for f in flying if f[0] is mlp_sum]
        chain = [f for f in flying if f[0] is mix_sum and f not in late]
        quick = [f for f in flying if f not in late + wide + chain]
        keep, send = land_in_turn([quick, wide, chain], sent)
        if begin == final and begin > 0:
            _, ahead = launch([mix_sum], ())
            (keep, send), *_ = (land(late, (keep, send)),)
            late = ahead
        flying = late
        scatters.append(ScatterOverMp(keep, send))

    finished = ()
    wide_grads = ()
    done = set()

    def finish_ready(finished):
        for (begin, _), scatter in zip(runs, scatters):
            if not scatter.more() and begin not in done:
                done.add(begin)
                finished = finish_call(
                    scatter.keep, scatter.from_core, scatter.from_y, own_t, cot_own, stats, gain_own, bias_col,
                    finished, begin,
                )
        return finished

    while True:
        busy = [f[0] for f in flying]
        ready = [m for m in [mix_sum] + scatters + [short, mlp_sum] if m.more() and m not in busy]
        finished, flights = launch(ready, finished)
        flying = flying + flights
        if not flying:
            break
        finished = finish_ready(finished)
        near = [f for f in flying if f[0] in scatters and len(f[0].bits) == 2]
        across = [f for f in flying if f[0] in scatters and len(f[0].bits) == 1]
        chain = [f for f in flying if f[0] is mix_sum]
        rest = [f for f in flying if f[0] is short]
        wide = [f for f in flying if f[0] is mlp_sum]
        left = len(mix_sum.steps)
        if near:
            now = near + chain + rest
        elif left == 2:
            now = chain + across[:1] + wide + rest
        elif left == 1:
            now = across + wide + rest or chain
        else:
            now = chain + rest or flying
        final = [f for f in now if f[0] is mix_sum]
        finished, wide_grads = land_in_turn([[f for f in now if f not in final], final], (finished, wide_grads))
        flying = [f for f in flying if f not in now]
        if not mlp_sum.more() and not wide_grads:
            swap, held, arrived = mlp_sum.last
            wide_grads = (
                jnp.where(swap, arrived, held).astype(F32),
                jnp.where(swap, held, arrived).astype(F32),
            )
    finished = finish_ready(finished)
    block_out, token_grad = finished
    block_out, token_grad = block_out.T, token_grad.T
    swap, held, arrived = mix_sum.last
    left = 3 * part - held.shape[0]
    qkv_rows = joined(swap, held, arrived)[: 3 * part].astype(F32)
    attn_grad = jnp.where(swap, held[left:], arrived[left:]).astype(F32)
    qkv_grad = jnp.transpose(qkv_rows.reshape(3, part, width), (2, 0, 1))

    gain_grad = short.norm / norm_gain.astype(F32)
    rest = short.rest
    split = 2 * part + up_weight.shape[1]
    return (
        block_out,
        token_grad,
        gain_grad,
        qkv_grad,
        rest[: 2 * part].reshape(2, part),
        attn_grad,
        wide_grads[1],
        rest[2 * part : split],
        wide_grads[0],
        rest[split:],
    )


def solution(mesh):
    in_specs = (
        P("dp", "mp"),
        P("dp", None),
        P("mp"),
        P(None, None, "mp"),
        P(None, "mp"),
        P("mp", None),
        P(None, "mp"),
        P("mp"),
        P("mp", None),
        P("mp"),
        P("dp", None),
    )
    out_specs = (
        P("dp", "mp"),
        P("dp", "mp"),
        P("mp"),
        P(None, None, "mp"),
        P(None, "mp"),
        P("mp", None),
        P(None, "mp"),
        P("mp"),
        P("mp", None),
        P("mp"),
    )
    run = functools.partial(body, mesh.shape["dp"])
    return jax.shard_map(run, mesh=mesh, in_specs=in_specs, out_specs=out_specs, check_vma=False)
```

```python
import functools

import jax
import jax.numpy as jnp
from jax import lax
from jax.experimental import pallas as pl
from jax.experimental.pallas import tpu as pltpu
from jax.sharding import PartitionSpec as P

DH = 64
LEN = 1024
EPSILON = 1e-06
IMAGE_SLOTS = 16
PENALTY = 1024.0
BI = 256
BJ = 256
SUM_ROWS = 16
F32 = jnp.float32
BF16 = jnp.bfloat16

NN = (((1,), (0,)), ((), ()))
NT = (((1,), (1,)), ((), ()))
TN = (((0,), (0,)), ((), ()))
ANY = pl.BlockSpec(memory_space=pl.ANY)


def dot(left, right, dims=NN):
    return lax.dot_general(left, right, dims, preferred_element_type=F32)


def fold_lanes(rows):
    total = rows[:, :128]
    for start in range(128, rows.shape[1], 128):
        total = total + rows[:, start : start + 128]
    return total


def cost(microseconds, nbytes):
    return pl.CostEstimate(flops=int(microseconds * 1e3), bytes_accessed=nbytes // 1000, transcendentals=0)


def early_kernel(cot, down, attn, pick, d_act, d_att, cot_own, bias_sum):
    rows = cot[...]
    d_act[...] = dot(down[...], rows, NT).astype(BF16)
    d_att[...] = dot(attn[...], rows, NT).astype(BF16)
    own = dot(pick[...], rows, NT)
    cot_own[...] = own.astype(BF16)

    @pl.when(pl.program_id(0) == 0)
    def _():
        bias_sum[...] = jnp.zeros_like(bias_sum)

    bias_sum[...] += fold_lanes(own)


def early_call(cot, down, attn, pick, block=512):
    tokens, width = cot.shape
    seqs = tokens // LEN
    hidden, part = down.shape[0], attn.shape[0]
    steps = LEN // block
    fixed = lambda i: (0, 0)
    by_seq = lambda i: (i // steps, 0, i % steps)
    return pl.pallas_call(
        early_kernel,
        grid=(tokens // block,),
        in_specs=[
            pl.BlockSpec((block, width), lambda i: (i, 0)),
            pl.BlockSpec((hidden, width), fixed),
            pl.BlockSpec((part, width), fixed),
            pl.BlockSpec((part, width), fixed),
        ],
        out_specs=[
            pl.BlockSpec((None, hidden, block), by_seq),
            pl.BlockSpec((None, part, block), by_seq),
            pl.BlockSpec((part, block), lambda i: (0, i)),
            pl.BlockSpec((part, 128), fixed),
        ],
        out_shape=[
            jax.ShapeDtypeStruct((seqs, hidden, LEN), BF16),
            jax.ShapeDtypeStruct((seqs, part, LEN), BF16),
            jax.ShapeDtypeStruct((part, tokens), BF16),
            jax.ShapeDtypeStruct((part, 128), F32),
        ],
        cost_estimate=cost(10, 12_000_000),
        name="early",
    )(cot, down, attn, pick)


def mlp_kernel(
    pieces_order, place, own, flip_y, flip_c, flip_cy, gain_own, gain_y, gain_c, gain_cy, up, up_bias, d_act, cot,
    normed, active, d_pre, stats, bias_sum, gain_all, up_row, grads, low, high
):
    pieces = (own, flip_y, flip_c, flip_cy)
    part = own.shape[0]
    width = part * 4
    first = pl.program_id(0) == 0
    last = pl.program_id(0) == pl.num_programs(0) - 1

    @pl.when(first)
    def _():
        bias_sum[...] = jnp.zeros_like(bias_sum)
        low[...] = jnp.zeros_like(low)
        high[...] = jnp.zeros_like(high)
        for slot, piece in enumerate((gain_own, gain_y, gain_c, gain_cy)):
            gain_all[pl.ds(pl.multiple_of(place[slot], part), part), :] = piece[...].astype(F32)

    total = 0.0
    squares = 0.0
    for piece in pieces:
        rows = piece[...].astype(F32)
        total = total + jnp.sum(rows, axis=0, keepdims=True)
        squares = squares + jnp.sum(rows * rows, axis=0, keepdims=True)
    mean = total * (1.0 / width)
    scale = lax.rsqrt(squares * (1.0 / width) - mean * mean + EPSILON)
    stats[0:1, :] = mean
    stats[1:2, :] = scale
    stats[2:8, :] = jnp.zeros((6, stats.shape[1]), F32)
    for slot, piece in enumerate(pieces):
        rows = piece[...].astype(F32)
        here = pl.ds(pl.multiple_of(place[slot], part), part)
        normed[here, :] = ((rows - mean) * scale * gain_all[here, :1]).astype(BF16)

    c0 = 0.7978845608028654
    c1 = 0.044715 * c0
    def lift(start):
        here = slice(start, start + 256)
        return dot(up[:, here], normed[...], TN) + up_bias[here, :1].astype(F32)

    ahead = lift(0)
    for start in range(0, up.shape[1], 256):
        here = slice(start, start + 256)
        pre = ahead
        if start + 256 < up.shape[1]:
            ahead = lift(start + 256)
        square = pre * pre
        half = 0.5 * jnp.tanh(pre * (c0 + c1 * square)) + 0.5
        act = (pre * half).astype(BF16)
        active[here, :] = act
        slope = half + pre * (half - half * half) * (2.0 * c0 + 6.0 * c1 * square)
        grad = (d_act[here, :].astype(F32) * slope).astype(BF16)
        d_pre[here, :] = grad
        bias_sum[here, :] += fold_lanes(grad.astype(F32))
        low[here, :] += dot(act, cot[...])
        high[:, here] += dot(normed[...], grad, NT)

    @pl.when(last)
    def _():
        up_row[...] = fold_lanes(high[...] * up[...].astype(F32))
        half = low.shape[0]
        size = grads.shape[0] // len(pieces_order)
        for slot, piece in enumerate(pieces_order):
            source, start = (low, piece * size) if piece * size < half else (high, piece * size - half)
            grads[slot * size : (slot + 1) * size, :] = source[start : start + size, :].astype(BF16)


def mlp_call(pieces_order, place, pieces, gains, up, up_bias, d_act, cot, block=512):
    part, tokens = pieces[0].shape
    width = 4 * part
    seqs, hidden, _ = d_act.shape
    steps = LEN // block
    lanes = lambda i, *_: (0, i)
    by_seq = lambda i, *_: (i // steps, 0, i % steps)
    fixed = lambda i, *_: (0, 0)
    grid_spec = pltpu.PrefetchScalarGridSpec(
        num_scalar_prefetch=1,
        grid=(tokens // block,),
        in_specs=[pl.BlockSpec((part, block), lanes)] * 4
        + [pl.BlockSpec((part, 128), fixed)] * 4
        + [
            pl.BlockSpec((width, hidden), fixed),
            pl.BlockSpec((hidden, 128), fixed),
            pl.BlockSpec((None, hidden, block), by_seq),
            pl.BlockSpec((block, width), lambda i, *_: (i, 0)),
        ],
        out_specs=[
            pl.BlockSpec((None, width, block), by_seq),
            pl.BlockSpec((None, hidden, block), by_seq),
            pl.BlockSpec((None, hidden, block), by_seq),
            pl.BlockSpec((8, block), lanes),
            pl.BlockSpec((hidden, 128), fixed),
            pl.BlockSpec((width, 128), fixed),
            pl.BlockSpec((width, 128), fixed),
            pl.BlockSpec((hidden + width, width), fixed),
        ],
        scratch_shapes=[pltpu.VMEM((hidden, width), F32), pltpu.VMEM((width, hidden), F32)],
    )
    assert hidden == width
    return pl.pallas_call(
        functools.partial(mlp_kernel, pieces_order),
        grid_spec=grid_spec,
        out_shape=[
            jax.ShapeDtypeStruct((seqs, width, LEN), BF16),
            jax.ShapeDtypeStruct((seqs, hidden, LEN), BF16),
            jax.ShapeDtypeStruct((seqs, hidden, LEN), BF16),
            jax.ShapeDtypeStruct((8, tokens), F32),
            jax.ShapeDtypeStruct((hidden, 128), F32),
            jax.ShapeDtypeStruct((width, 128), F32),
            jax.ShapeDtypeStruct((width, 128), F32),
            jax.ShapeDtypeStruct((hidden + width, width), BF16),
        ],
        cost_estimate=cost(20, 30_000_000),
        name="mlp",
    )(place, *pieces, *gains, up, up_bias, d_act, cot)


def attention_kernel(
    first, count, normed, mixed_t, d_att, mask_q, mask_k, gains, cot, attended, d_mixed, gain_sum, norm_row, grads,
    total, qkv, qx, kx, vn, kt, vt, es, ps, dqa, dka, dva
):
    seq = pl.program_id(0)
    last = seq == pl.num_programs(0) - 1
    part = attended.shape[0]
    heads = part // DH
    inv_dh = 1.0 / DH

    @pl.when(seq == 0)
    def _():
        total[...] = jnp.zeros_like(total)
        gain_sum[...] = jnp.zeros_like(gain_sum)

    qkv[...] = dot(mixed_t[...], normed[...])

    def unit(start):
        raw = qkv[start : start + DH, :]
        shifted = raw - jnp.sum(raw, axis=0, keepdims=True) * inv_dh
        scale = lax.rsqrt(jnp.sum(shifted * shifted, axis=0, keepdims=True) * inv_dh + EPSILON)
        return shifted * scale, scale

    zeros = jnp.zeros((128 - DH - IMAGE_SLOTS, LEN), BF16)
    for head in range(heads):
        rows = slice(head * DH, (head + 1) * DH)
        query, _ = unit(head * DH)
        query = (query * (gains[rows, :1] * 0.125)).astype(BF16)
        qx[head] = jnp.concatenate([query, mask_q[...], zeros], axis=0)
        key, _ = unit(part + head * DH)
        key = (key * gains[part + head * DH : part + (head + 1) * DH, :1]).astype(BF16)
        kt[rows, :] = key
        kx[head] = jnp.concatenate([key, mask_k[...], zeros], axis=0).T
        value = qkv[2 * part + head * DH : 2 * part + (head + 1) * DH, :].astype(BF16)
        vt[rows, :] = value
        vn[head] = value.T
    dka[...] = jnp.zeros_like(dka)
    dva[...] = jnp.zeros_like(dva)

    def straight(units, i0, base):
        icols = pl.ds(i0, BI)
        edges = [(at, min(BJ, units * 128 - at)) for at in range(0, units * 128, BJ)]
        trips = len(edges)
        spots = [slice(at, at + size) for at, size in edges]
        places = [pl.ds(pl.multiple_of(base + at, 128), size) for at, size in edges]

        def scores(head, j, sums):
            rows = slice(head * DH, (head + 1) * DH)
            e = jnp.exp(dot(kx[head, places[j], :], qx[head, :, icols]))
            p = dot(vn[head, places[j], :], d_att[rows, icols])
            es[head % 2, spots[j], :] = e
            ps[head % 2, spots[j], :] = p
            more = (jnp.sum(e, axis=0, keepdims=True), jnp.sum(e * p, axis=0, keepdims=True))
            return more if sums is None else (sums[0] + more[0], sums[1] + more[1])

        def row_grads(head, j, inverse, inner, held):
            rows = slice(head * DH, (head + 1) * DH)
            w = es[head % 2, spots[j], :] * inverse
            d = (w * (ps[head % 2, spots[j], :] - inner)).astype(BF16)
            w = w.astype(BF16)
            out = dot(vt[rows, places[j]], w)
            query = dot(kt[rows, places[j]], d)
            dva[rows, places[j]] += dot(d_att[rows, icols], w, NT)
            dka[rows, places[j]] += dot(qx[head, :DH, icols], d, NT)
            return (out, query) if held is None else (held[0] + out, held[1] + query)

        sums = None
        for j in range(trips):
            sums = scores(0, j, sums)
        for head in range(heads):
            rows = slice(head * DH, (head + 1) * DH)
            inverse = 1.0 / sums[0]
            inner = sums[1] * inverse
            held = following = None
            for j in range(trips):
                if head + 1 < heads:
                    following = scores(head + 1, j, following)
                held = row_grads(head, j, inverse, inner, held)
            attended[rows, icols] = held[0].astype(BF16)
            dqa[rows, icols] = held[1]
            sums = following

    def query_block(ib, _):
        i0 = pl.multiple_of(ib * BI, BI)
        base = first[seq * (LEN // BI) + ib] * 128
        trips = count[seq * (LEN // BI) + ib]
        for number in range(BI // 128, LEN // 128 + 1):
            pl.when(trips == number)(functools.partial(straight, number, i0, base))
        return 0

    lax.fori_loop(0, LEN // BI, query_block, 0)

    for source, offset, factor in ((dqa, 0, 0.125), (dka, part, 1.0)):
        for head in range(heads):
            start = offset + head * DH
            u, scale = unit(start)
            e = source[head * DH : (head + 1) * DH, :] * factor
            gain_sum[start : start + DH, :] += fold_lanes(e * u)
            f = e * gains[start : start + DH, :1]
            mean_f = jnp.sum(f, axis=0, keepdims=True) * inv_dh
            mean_fu = jnp.sum(f * u, axis=0, keepdims=True) * inv_dh
            d_mixed[start : start + DH, :] = ((f - mean_f - u * mean_fu) * scale).astype(BF16)
    d_mixed[2 * part :, :] = dva[...].astype(BF16)

    split = 3 * part
    total[:split, :] += dot(d_mixed[...], normed[...], NT)
    total[split:, :] += dot(attended[...], cot[...])

    @pl.when(last)
    def _():
        norm_row[...] = jnp.sum(total[:split, :] * mixed_t[...].astype(F32), axis=0, keepdims=True)
        grads[...] = total[...].astype(BF16)


def attention_call(first, count, normed, mixed_t, d_att, mask_q, mask_k, gains, cot):
    seqs, part, _ = d_att.shape
    width = normed.shape[1]
    heads = part // DH
    fixed = lambda i, *_: (0, 0)
    by_seq = lambda i, *_: (i, 0, 0)
    grid_spec = pltpu.PrefetchScalarGridSpec(
        num_scalar_prefetch=2,
        grid=(seqs,),
        in_specs=[
            pl.BlockSpec((None, width, LEN), by_seq),
            pl.BlockSpec((3 * part, width), fixed),
            pl.BlockSpec((None, part, LEN), by_seq),
            pl.BlockSpec((None, IMAGE_SLOTS, LEN), by_seq),
            pl.BlockSpec((None, IMAGE_SLOTS, LEN), by_seq),
            pl.BlockSpec((2 * part, 128), fixed),
            pl.BlockSpec((LEN, width), lambda i, *_: (i, 0)),
        ],
        out_specs=[
            pl.BlockSpec((None, part, LEN), by_seq),
            pl.BlockSpec((None, 3 * part, LEN), by_seq),
            pl.BlockSpec((2 * part, 128), fixed),
            pl.BlockSpec((1, width), fixed),
            pl.BlockSpec((4 * part, width), fixed),
        ],
        scratch_shapes=[
            pltpu.VMEM((4 * part, width), F32),
            pltpu.VMEM((3 * part, LEN), F32),
            pltpu.VMEM((heads, 128, LEN), BF16),
            pltpu.VMEM((heads, LEN, 128), BF16),
            pltpu.VMEM((heads, LEN, DH), BF16),
            pltpu.VMEM((part, LEN), BF16),
            pltpu.VMEM((part, LEN), BF16),
            pltpu.VMEM((2, LEN, BI), F32),
            pltpu.VMEM((2, LEN, BI), F32),
            pltpu.VMEM((part, LEN), F32),
            pltpu.VMEM((part, LEN), F32),
            pltpu.VMEM((part, LEN), F32),
        ],
    )
    return pl.pallas_call(
        attention_kernel,
        grid_spec=grid_spec,
        out_shape=[
            jax.ShapeDtypeStruct((seqs, part, LEN), BF16),
            jax.ShapeDtypeStruct((seqs, 3 * part, LEN), BF16),
            jax.ShapeDtypeStruct((2 * part, 128), F32),
            jax.ShapeDtypeStruct((1, width), F32),
            jax.ShapeDtypeStruct((4 * part, width), BF16),
        ],
        cost_estimate=cost(18, 5_000_000),
        name="attention",
    )(first, count, normed, mixed_t, d_att, mask_q, mask_k, gains, cot)


def project_kernel(
    shard, active, attended, d_pre, d_mixed, normed, down, attn, up, mixed_t, gain, keep, send
):
    me = shard[0]
    part = attended.shape[0]
    out = dot(down[...], active[...], TN) + dot(attn[...], attended[...], TN)
    grad = dot(up[...], d_pre[...]) + dot(mixed_t[...], d_mixed[...], TN)
    product = grad * normed[...].astype(F32)
    sums = []
    for row in (jnp.sum(grad * gain[:, :1], axis=0, keepdims=True), jnp.sum(product, axis=0, keepdims=True)):
        high = row.astype(BF16)
        sums += [high, (row - high.astype(F32)).astype(BF16)]
    sums = jnp.concatenate(sums + [jnp.zeros((SUM_ROWS - 4, sums[0].shape[1]), BF16)], axis=0)
    for target in (keep, send):
        for slot in range(2):
            target[slot, 2 * part :, :] = sums
    for index in range(4):
        rows = slice(index * part, (index + 1) * part)
        away = jnp.bitwise_xor(me, index)
        slot = away // 2

        @pl.when(away % 2 == 0)
        def _():
            keep[slot, :part, :] = out[rows].astype(BF16)
            keep[slot, part : 2 * part, :] = grad[rows].astype(BF16)

        @pl.when(away % 2 == 1)
        def _():
            send[slot, :part, :] = out[rows].astype(BF16)
            send[slot, part : 2 * part, :] = grad[rows].astype(BF16)


def project_call(shard, active, attended, d_pre, d_mixed, normed, down, attn, up, mixed_t, gain, begin, size, block=256):
    hidden, width = down.shape
    part = attended.shape[1]
    steps = LEN // block
    ours = lambda i, *_: (begin + i // steps, 0, i % steps)
    out = lambda i, *_: (i // steps, 0, 0, i % steps)
    fixed = lambda i, *_: (0, 0)
    rows = 2 * part + SUM_ROWS
    grid_spec = pltpu.PrefetchScalarGridSpec(
        num_scalar_prefetch=1,
        grid=(size * steps,),
        in_specs=[
            pl.BlockSpec((None, hidden, block), ours),
            pl.BlockSpec((None, part, block), ours),
            pl.BlockSpec((None, hidden, block), ours),
            pl.BlockSpec((None, 3 * part, block), ours),
            pl.BlockSpec((None, width, block), ours),
            pl.BlockSpec((hidden, width), fixed),
            pl.BlockSpec((part, width), fixed),
            pl.BlockSpec((width, hidden), fixed),
            pl.BlockSpec((3 * part, width), fixed),
            pl.BlockSpec((width, 128), fixed),
        ],
        out_specs=[
            pl.BlockSpec((None, 2, rows, block), out),
            pl.BlockSpec((None, 2, rows, block), out),
        ],
    )
    return pl.pallas_call(
        project_kernel,
        grid_spec=grid_spec,
        out_shape=[
            jax.ShapeDtypeStruct((size, 2, rows, LEN), BF16),
            jax.ShapeDtypeStruct((size, 2, rows, LEN), BF16),
        ],
        cost_estimate=cost(8, 16_000_000),
        name="project",
    )(shard, active, attended, d_pre, d_mixed, normed, down, attn, up, mixed_t, gain)


def finish_kernel(keep, from_core, from_y, own_t, cot, stats, gain, bias, *rest):
    block_out, token_grad = rest[-2:]
    part = own_t.shape[0]
    inv_width = 0.25 / part
    total = keep[...].astype(F32) + from_core[...].astype(F32) + from_y[...].astype(F32)
    own = own_t[...].astype(F32)
    block_out[...] = (own + total[:part] + bias[:, :1].astype(F32)).astype(BF16)
    grad = total[part : 2 * part]
    sums = total[2 * part :]
    mean = stats[0:1, :]
    scale = stats[1:2, :]
    hat = (own - mean) * scale
    inner = grad * gain[:, :1].astype(F32) - (sums[0:1] + sums[1:2]) * inv_width - hat * ((sums[2:3] + sums[3:4]) * inv_width)
    token_grad[...] = cot[...].astype(F32) + inner * scale


def finish_call(keep, from_core, from_y, own_t, cot, stats, gain, bias, before, begin, block=512):
    part, tokens = own_t.shape
    steps = LEN // block
    size = keep.shape[0]
    fixed = lambda i: (0, 0)
    packed = pl.BlockSpec((None, None, 2 * part + SUM_ROWS, block), lambda i: (i // steps, 0, 0, i % steps))
    ours = lambda i: (0, begin * steps + i)
    here = pl.BlockSpec((part, block), ours)
    return pl.pallas_call(
        finish_kernel,
        grid=(size * steps,),
        in_specs=[
            packed, packed, packed,
            here, here,
            pl.BlockSpec((8, block), ours),
            pl.BlockSpec((part, 128), fixed),
            pl.BlockSpec((part, 128), fixed),
        ]
        + [ANY] * len(before),
        out_specs=[here, here],
        out_shape=[
            jax.ShapeDtypeStruct((part, tokens), BF16),
            jax.ShapeDtypeStruct((part, tokens), F32),
        ],
        input_output_aliases={8 + i: i for i in range(len(before))},
        cost_estimate=cost(3, 5_000_000),
        name="finish",
    )(keep, from_core, from_y, own_t, cot, stats, gain, bias, *before)


def flip(value, axis, size, bit):
    return lax.ppermute(value, axis, [(i, i ^ bit) for i in range(size)])


def tie(*trees):
    return lax.optimization_barrier(trees)


def joined(swap, held, arrived):
    return jnp.where(
        swap, jnp.concatenate([arrived, held], axis=0), jnp.concatenate([held, arrived], axis=0)
    )


def piece_order(size):
    bits = size.bit_length() - 1
    return [sum(((i >> b) & 1) << (bits - 1 - b) for b in range(bits)) for i in range(size)]


class SumOverDp:
    def __init__(self, value, size, index):
        self.size, self.index = size, index
        self.send = value
        self.steps = ["sum"] + [1 << i for i in reversed(range(size.bit_length() - 1))]

    def more(self):
        return bool(self.steps)

    def move(self, send):
        if self.steps[0] == "sum":
            return lax.all_to_all(send, "dp", 0, 0, tiled=True)
        return flip(send, "dp", self.size, self.steps[0])

    def take(self, arrived):
        step = self.steps.pop(0)
        if step == "sum":
            shares = arrived.reshape(self.size, -1, arrived.shape[1]).astype(F32)
            self.keep = jnp.sum(shares, axis=0).astype(BF16)
        else:
            self.last = ((self.index & step) > 0, self.keep, arrived)
            self.keep = joined(*self.last)
        self.send = self.keep


class ChainOverDp:
    def __init__(self, value, size, index):
        self.size, self.index = size, index
        bits = [1 << i for i in range(size.bit_length() - 1)]
        self.steps = [("sum", bit) for bit in bits] + [("join", bit) for bit in reversed(bits)]
        self.prepare(value, None)

    def prepare(self, held, arrived):
        def part(which, half):
            rows = lax.dynamic_slice_in_dim(held, which * half, half, 0)
            if arrived is None:
                return rows
            came = lax.dynamic_slice_in_dim(arrived, which * half, half, 0)
            return (rows.astype(F32) + came.astype(F32)).astype(BF16)

        rows = held.shape[0]
        if self.steps and self.steps[0][0] == "sum":
            side = ((self.index & self.steps[0][1]) > 0).astype(jnp.int32)
            self.send, self.keep = part(1 - side, rows // 2), part(side, rows // 2)
        else:
            self.keep = part(0, rows)
            self.send = self.keep

    def more(self):
        return bool(self.steps)

    def move(self, send):
        return flip(send, "dp", self.size, self.steps[0][1])

    def take(self, arrived):
        kind, bit = self.steps.pop(0)
        if kind == "sum":
            self.prepare(self.keep, arrived)
            return
        self.last = ((self.index & bit) > 0, self.keep, arrived)
        self.keep = self.send = joined(*self.last)


class ScatterOverMp:
    def __init__(self, keep, send):
        self.keep, self.send = keep, send
        self.bits = [1, 2]

    def more(self):
        return bool(self.bits)

    def move(self, send):
        return flip(send, "mp", 4, self.bits[0])

    def take(self, arrived):
        bit = self.bits.pop(0)
        if bit == 1:
            self.from_core = arrived
            self.send = (self.keep[:, 1:].astype(F32) + arrived[:, 1:].astype(F32)).astype(BF16)
        else:
            self.from_y = arrived


def land_in_turn(phases, outputs):
    movers = []
    for flights in phases:
        outputs, sends, arrivals = tie(outputs, [m.send for m in movers], [f[1] for f in flights])
        for mover, send in zip(movers, sends):
            mover.send = send
        for (mover, _), arrived in zip(flights, arrivals):
            mover.take(arrived)
        movers += [f[0] for f in flights]
    return outputs


class ShortSums:
    def __init__(self, keep, send, rest, size):
        self.keep, self.send, self.rest, self.size = keep, send, rest, size
        self.steps = [("mp", 1), ("mp", 2)] + [("dp", 1 << i) for i in range(size.bit_length() - 1)]

    def more(self):
        return bool(self.steps)

    def move(self, send):
        axis, bit = self.steps[0]
        return flip(send, axis, 4 if axis == "mp" else self.size, bit)

    def take(self, arrived):
        axis, bit = self.steps.pop(0)
        if (axis, bit) == ("mp", 1):
            both = self.keep + arrived
            self.norm, self.send = both[0], both[1]
            return
        if axis == "mp":
            self.send = jnp.concatenate([self.norm + arrived, self.rest])
        else:
            self.send = self.send + arrived
        size = self.norm.shape[0]
        self.norm, self.rest = self.send[:size], self.send[size:]


def launch(movers, inputs):
    movers = [m for m in movers if m.more()]
    inputs, sends = tie(inputs, [m.send for m in movers])
    return inputs, [(m, m.move(s)) for m, s in zip(movers, sends)]


def land(flights, outputs):
    outputs, arrivals = tie(outputs, [f[1] for f in flights])
    for (mover, _), arrived in zip(flights, arrivals):
        mover.take(arrived)
    return outputs


def body(
    dp_size,
    tokens,
    image_ids,
    norm_gain,
    qkv_weight,
    qk_gain,
    attn_weight,
    up_weight,
    up_bias,
    down_weight,
    down_bias,
    cotangent,
):
    part = tokens.shape[1]
    width = cotangent.shape[1]
    seqs = image_ids.shape[0]
    me = lax.axis_index("mp")
    dp = lax.axis_index("dp")
    shard = me.astype(jnp.int32)[None]
    place = jnp.bitwise_xor(shard, jnp.array([0, 2, 1, 3], jnp.int32)) * part

    own_t = tokens.T
    from_y = flip(own_t, "mp", 4, 2)
    gain_own = jnp.broadcast_to(norm_gain[:, None], (part, 128))
    gain_y = flip(gain_own, "mp", 4, 2)
    gain_c = flip(gain_own, "mp", 4, 1)

    mixed_t = jnp.transpose(qkv_weight, (1, 2, 0)).reshape(3 * part, width)
    def column(vector):
        return jnp.broadcast_to(vector[:, None], (vector.shape[0], 128))

    columns = (column(up_bias), column(qk_gain.astype(F32).reshape(2 * part)), column(down_bias))

    slots = jnp.arange(IMAGE_SLOTS, dtype=jnp.int32)[None, :, None]
    same = image_ids[:, None, :] == slots
    mask_q = same.astype(BF16)
    mask_k = jnp.where(same | (slots >= 8), 0.0, -PENALTY).astype(BF16)
    block_first = image_ids[:, ::BI]
    block_last = image_ids[:, BI - 1 :: BI]
    starts = jnp.sum(image_ids[:, None, :] < block_first[:, :, None], axis=2, dtype=jnp.int32)
    ends = jnp.sum(image_ids[:, None, :] <= block_last[:, :, None], axis=2, dtype=jnp.int32)
    first = starts // 128
    count = ((ends + 127) // 128 - first).reshape(-1)
    first = first.reshape(-1)

    pick = (jnp.arange(part)[:, None] + me * part == jnp.arange(width)[None, :]).astype(BF16)
    pick, place, columns, (gain_y, gain_c) = tie(pick, place, columns, (gain_y, gain_c))
    up_bias_col, head_gains, bias_col = columns
    gain_cy = flip(gain_y, "mp", 4, 1)
    d_act, d_att, cot_own, cot_sum = early_call(cotangent, down_weight, attn_weight, pick)
    prepared = (
        d_act, d_att, mixed_t, up_bias_col, head_gains, mask_q, mask_k, first, count,
        bias_col,
    )
    prepared, (from_y, gain_cy) = tie(prepared, (from_y, gain_cy))
    gains = (gain_own, gain_y, gain_c, gain_cy)
    (
        d_act, d_att, mixed_t, up_bias_col, head_gains, mask_q, mask_k, first, count,
        bias_col,
    ) = prepared
    pieces = (own_t, from_y, flip(own_t, "mp", 4, 1), flip(from_y, "mp", 4, 1))
    normed, active, d_pre, stats, upbias_part, gain_all, up_row, mlp_part = mlp_call(
        tuple(piece_order(dp_size)), place, pieces, gains, up_weight, up_bias_col, d_act, cotangent
    )
    mlp_sum = SumOverDp(mlp_part, dp_size, dp)

    (states,), flying = launch([mlp_sum], (normed,))
    attended, d_mixed, qk_part, norm_row, mix_part = attention_call(
        first, count, states, mixed_t, d_att, mask_q, mask_k, head_gains, cotangent
    )
    mix_sum = ChainOverDp(mix_part, dp_size, dp)

    norm_vec = norm_row[0] + jnp.sum(up_row, axis=1)
    norm_parts = norm_vec.reshape(4, part)
    norm_parts = [lax.dynamic_index_in_dim(norm_parts, jnp.bitwise_xor(me, m), 0, False) for m in range(4)]
    short = ShortSums(
        jnp.stack([norm_parts[0], norm_parts[2]]),
        jnp.stack([norm_parts[1], norm_parts[3]]),
        jnp.concatenate([jnp.sum(qk_part, axis=1), jnp.sum(upbias_part, axis=1), jnp.sum(cot_sum, axis=1)]),
        dp_size,
    )

    runs = [(seq, 1) for seq in range(seqs)]
    scatters = []
    for begin, size in runs:
        busy = [f[0] for f in flying]
        along = [m for m in [mix_sum, mlp_sum, short] + scatters if m.more() and m not in busy]
        (att, dm), flights = launch(along, (attended, d_mixed))
        flying = flying + flights
        sent = project_call(
            shard, active, att, d_pre, dm, normed, down_weight, attn_weight, up_weight, mixed_t, gain_all, begin, size
        )
        final = seqs - 1
        late = [f for f in flights if begin == 0 and f[0] is mix_sum or begin == final and f[0] is scatters[0]]
        wide = [f for f in flying if f[0] is mlp_sum]
        chain = [f for f in flying if f[0] is mix_sum and f not in late]
        quick = [f for f in flying if f not in late + wide + chain]
        keep, send = land_in_turn([quick, wide, chain], sent)
        if begin == final and begin > 0:
            _, ahead = launch([mix_sum], ())
            (keep, send), *_ = (land(late, (keep, send)),)
            late = ahead
        flying = late
        scatters.append(ScatterOverMp(keep, send))

    finished = ()
    wide_grads = ()
    done = set()

    def finish_ready(finished):
        for (begin, _), scatter in zip(runs, scatters):
            if not scatter.more() and begin not in done:
                done.add(begin)
                finished = finish_call(
                    scatter.keep, scatter.from_core, scatter.from_y, own_t, cot_own, stats, gain_own, bias_col,
                    finished, begin,
                )
        return finished

    while True:
        busy = [f[0] for f in flying]
        ready = [m for m in [mix_sum] + scatters + [short, mlp_sum] if m.more() and m not in busy]
        finished, flights = launch(ready, finished)
        flying = flying + flights
        if not flying:
            break
        finished = finish_ready(finished)
        near = [f for f in flying if f[0] in scatters and len(f[0].bits) == 2]
        across = [f for f in flying if f[0] in scatters and len(f[0].bits) == 1]
        chain = [f for f in flying if f[0] is mix_sum]
        rest = [f for f in flying if f[0] is short]
        wide = [f for f in flying if f[0] is mlp_sum]
        left = len(mix_sum.steps)
        if near:
            now = near + chain + rest
        elif left == 2:
            now = chain + across[:1] + rest
        elif left == 1:
            now = wide + rest or across[:1] or chain
        else:
            now = chain + rest or flying
        final = [f for f in now if f[0] is mix_sum]
        finished, wide_grads = land_in_turn([[f for f in now if f not in final], final], (finished, wide_grads))
        flying = [f for f in flying if f not in now]
        if not mlp_sum.more() and not wide_grads:
            swap, held, arrived = mlp_sum.last
            wide_grads = (
                jnp.where(swap, arrived, held).astype(F32),
                jnp.where(swap, held, arrived).astype(F32),
            )
    finished = finish_ready(finished)
    block_out, token_grad = finished
    block_out, token_grad = block_out.T, token_grad.T
    swap, held, arrived = mix_sum.last
    left = 3 * part - held.shape[0]
    qkv_rows = joined(swap, held, arrived)[: 3 * part].astype(F32)
    attn_grad = jnp.where(swap, held[left:], arrived[left:]).astype(F32)
    qkv_grad = jnp.transpose(qkv_rows.reshape(3, part, width), (2, 0, 1))

    gain_grad = short.norm / norm_gain.astype(F32)
    rest = short.rest
    split = 2 * part + up_weight.shape[1]
    return (
        block_out,
        token_grad,
        gain_grad,
        qkv_grad,
        rest[: 2 * part].reshape(2, part),
        attn_grad,
        wide_grads[1],
        rest[2 * part : split],
        wide_grads[0],
        rest[split:],
    )


def solution(mesh):
    in_specs = (
        P("dp", "mp"),
        P("dp", None),
        P("mp"),
        P(None, None, "mp"),
        P(None, "mp"),
        P("mp", None),
        P(None, "mp"),
        P("mp"),
        P("mp", None),
        P("mp"),
        P("dp", None),
    )
    out_specs = (
        P("dp", "mp"),
        P("dp", "mp"),
        P("mp"),
        P(None, None, "mp"),
        P(None, "mp"),
        P("mp", None),
        P(None, "mp"),
        P("mp"),
        P("mp", None),
        P("mp"),
    )
    run = functools.partial(body, mesh.shape["dp"])
    return jax.shard_map(run, mesh=mesh, in_specs=in_specs, out_specs=out_specs, check_vma=False)
```

```python
import functools

import jax
import jax.numpy as jnp
from jax import lax
from jax.experimental import pallas as pl
from jax.experimental.pallas import tpu as pltpu
from jax.sharding import PartitionSpec as P

DH = 64
LEN = 1024
EPSILON = 1e-06
IMAGE_SLOTS = 16
PENALTY = 1024.0
BI = 256
BJ = 256
SUM_ROWS = 16
F32 = jnp.float32
BF16 = jnp.bfloat16

NN = (((1,), (0,)), ((), ()))
NT = (((1,), (1,)), ((), ()))
TN = (((0,), (0,)), ((), ()))
ANY = pl.BlockSpec(memory_space=pl.ANY)


def dot(left, right, dims=NN):
    return lax.dot_general(left, right, dims, preferred_element_type=F32)


def fold_lanes(rows):
    total = rows[:, :128]
    for start in range(128, rows.shape[1], 128):
        total = total + rows[:, start : start + 128]
    return total


def cost(microseconds, nbytes):
    return pl.CostEstimate(flops=int(microseconds * 1e3), bytes_accessed=nbytes // 1000, transcendentals=0)


def early_kernel(cot, down, attn, pick, d_act, d_att, cot_own, bias_sum):
    rows = cot[...]
    d_act[...] = dot(down[...], rows, NT).astype(BF16)
    d_att[...] = dot(attn[...], rows, NT).astype(BF16)
    own = dot(pick[...], rows, NT)
    cot_own[...] = own.astype(BF16)

    @pl.when(pl.program_id(0) == 0)
    def _():
        bias_sum[...] = jnp.zeros_like(bias_sum)

    bias_sum[...] += fold_lanes(own)


def early_call(cot, down, attn, pick, block=512):
    tokens, width = cot.shape
    seqs = tokens // LEN
    hidden, part = down.shape[0], attn.shape[0]
    steps = LEN // block
    fixed = lambda i: (0, 0)
    by_seq = lambda i: (i // steps, 0, i % steps)
    return pl.pallas_call(
        early_kernel,
        grid=(tokens // block,),
        in_specs=[
            pl.BlockSpec((block, width), lambda i: (i, 0)),
            pl.BlockSpec((hidden, width), fixed),
            pl.BlockSpec((part, width), fixed),
            pl.BlockSpec((part, width), fixed),
        ],
        out_specs=[
            pl.BlockSpec((None, hidden, block), by_seq),
            pl.BlockSpec((None, part, block), by_seq),
            pl.BlockSpec((part, block), lambda i: (0, i)),
            pl.BlockSpec((part, 128), fixed),
        ],
        out_shape=[
            jax.ShapeDtypeStruct((seqs, hidden, LEN), BF16),
            jax.ShapeDtypeStruct((seqs, part, LEN), BF16),
            jax.ShapeDtypeStruct((part, tokens), BF16),
            jax.ShapeDtypeStruct((part, 128), F32),
        ],
        cost_estimate=cost(10, 12_000_000),
        name="early",
    )(cot, down, attn, pick)


def mlp_kernel(
    pieces_order, place, own, flip_y, flip_c, flip_cy, gain_own, gain_y, gain_c, gain_cy, up, up_bias, d_act, cot,
    normed, active, d_pre, stats, bias_sum, gain_all, up_row, grads, low, high
):
    pieces = (own, flip_y, flip_c, flip_cy)
    part = own.shape[0]
    width = part * 4
    first = pl.program_id(0) == 0
    last = pl.program_id(0) == pl.num_programs(0) - 1

    @pl.when(first)
    def _():
        bias_sum[...] = jnp.zeros_like(bias_sum)
        low[...] = jnp.zeros_like(low)
        high[...] = jnp.zeros_like(high)
        for slot, piece in enumerate((gain_own, gain_y, gain_c, gain_cy)):
            gain_all[pl.ds(pl.multiple_of(place[slot], part), part), :] = piece[...].astype(F32)

    total = 0.0
    squares = 0.0
    for piece in pieces:
        rows = piece[...].astype(F32)
        total = total + jnp.sum(rows, axis=0, keepdims=True)
        squares = squares + jnp.sum(rows * rows, axis=0, keepdims=True)
    mean = total * (1.0 / width)
    scale = lax.rsqrt(squares * (1.0 / width) - mean * mean + EPSILON)
    stats[0:1, :] = mean
    stats[1:2, :] = scale
    stats[2:8, :] = jnp.zeros((6, stats.shape[1]), F32)
    for slot, piece in enumerate(pieces):
        rows = piece[...].astype(F32)
        here = pl.ds(pl.multiple_of(place[slot], part), part)
        normed[here, :] = ((rows - mean) * scale * gain_all[here, :1]).astype(BF16)

    c0 = 0.7978845608028654
    c1 = 0.044715 * c0
    def lift(start):
        here = slice(start, start + 256)
        return dot(up[:, here], normed[...], TN) + up_bias[here, :1].astype(F32)

    ahead = lift(0)
    for start in range(0, up.shape[1], 256):
        here = slice(start, start + 256)
        pre = ahead
        if start + 256 < up.shape[1]:
            ahead = lift(start + 256)
        square = pre * pre
        half = 0.5 * jnp.tanh(pre * (c0 + c1 * square)) + 0.5
        act = (pre * half).astype(BF16)
        active[here, :] = act
        slope = half + pre * (half - half * half) * (2.0 * c0 + 6.0 * c1 * square)
        grad = (d_act[here, :].astype(F32) * slope).astype(BF16)
        d_pre[here, :] = grad
        bias_sum[here, :] += fold_lanes(grad.astype(F32))
        low[here, :] += dot(act, cot[...])
        high[:, here] += dot(normed[...], grad, NT)

    @pl.when(last)
    def _():
        up_row[...] = fold_lanes(high[...] * up[...].astype(F32))
        half = low.shape[0]
        size = grads.shape[0] // len(pieces_order)
        for slot, piece in enumerate(pieces_order):
            source, start = (low, piece * size) if piece * size < half else (high, piece * size - half)
            grads[slot * size : (slot + 1) * size, :] = source[start : start + size, :].astype(BF16)


def mlp_call(pieces_order, place, pieces, gains, up, up_bias, d_act, cot, block=512):
    part, tokens = pieces[0].shape
    width = 4 * part
    seqs, hidden, _ = d_act.shape
    steps = LEN // block
    lanes = lambda i, *_: (0, i)
    by_seq = lambda i, *_: (i // steps, 0, i % steps)
    fixed = lambda i, *_: (0, 0)
    grid_spec = pltpu.PrefetchScalarGridSpec(
        num_scalar_prefetch=1,
        grid=(tokens // block,),
        in_specs=[pl.BlockSpec((part, block), lanes)] * 4
        + [pl.BlockSpec((part, 128), fixed)] * 4
        + [
            pl.BlockSpec((width, hidden), fixed),
            pl.BlockSpec((hidden, 128), fixed),
            pl.BlockSpec((None, hidden, block), by_seq),
            pl.BlockSpec((block, width), lambda i, *_: (i, 0)),
        ],
        out_specs=[
            pl.BlockSpec((None, width, block), by_seq),
            pl.BlockSpec((None, hidden, block), by_seq),
            pl.BlockSpec((None, hidden, block), by_seq),
            pl.BlockSpec((8, block), lanes),
            pl.BlockSpec((hidden, 128), fixed),
            pl.BlockSpec((width, 128), fixed),
            pl.BlockSpec((width, 128), fixed),
            pl.BlockSpec((hidden + width, width), fixed),
        ],
        scratch_shapes=[pltpu.VMEM((hidden, width), F32), pltpu.VMEM((width, hidden), F32)],
    )
    assert hidden == width
    return pl.pallas_call(
        functools.partial(mlp_kernel, pieces_order),
        grid_spec=grid_spec,
        out_shape=[
            jax.ShapeDtypeStruct((seqs, width, LEN), BF16),
            jax.ShapeDtypeStruct((seqs, hidden, LEN), BF16),
            jax.ShapeDtypeStruct((seqs, hidden, LEN), BF16),
            jax.ShapeDtypeStruct((8, tokens), F32),
            jax.ShapeDtypeStruct((hidden, 128), F32),
            jax.ShapeDtypeStruct((width, 128), F32),
            jax.ShapeDtypeStruct((width, 128), F32),
            jax.ShapeDtypeStruct((hidden + width, width), BF16),
        ],
        cost_estimate=cost(20, 30_000_000),
        name="mlp",
    )(place, *pieces, *gains, up, up_bias, d_act, cot)


def attention_kernel(
    first, count, normed, mixed_t, d_att, mask_q, mask_k, gains, cot, attended, d_mixed, gain_sum, norm_row, grads,
    total, qkv, qx, kx, vn, kt, vt, es, ps, dqa, dka, dva
):
    seq = pl.program_id(0)
    last = seq == pl.num_programs(0) - 1
    part = attended.shape[0]
    heads = part // DH
    inv_dh = 1.0 / DH

    @pl.when(seq == 0)
    def _():
        total[...] = jnp.zeros_like(total)
        gain_sum[...] = jnp.zeros_like(gain_sum)

    qkv[...] = dot(mixed_t[...], normed[...])

    def unit(start):
        raw = qkv[start : start + DH, :]
        shifted = raw - jnp.sum(raw, axis=0, keepdims=True) * inv_dh
        scale = lax.rsqrt(jnp.sum(shifted * shifted, axis=0, keepdims=True) * inv_dh + EPSILON)
        return shifted * scale, scale

    zeros = jnp.zeros((128 - DH - IMAGE_SLOTS, LEN), BF16)
    for head in range(heads):
        rows = slice(head * DH, (head + 1) * DH)
        query, _ = unit(head * DH)
        query = (query * (gains[rows, :1] * 0.125)).astype(BF16)
        qx[head] = jnp.concatenate([query, mask_q[...], zeros], axis=0)
        key, _ = unit(part + head * DH)
        key = (key * gains[part + head * DH : part + (head + 1) * DH, :1]).astype(BF16)
        kt[rows, :] = key
        kx[head] = jnp.concatenate([key, mask_k[...], zeros], axis=0).T
        value = qkv[2 * part + head * DH : 2 * part + (head + 1) * DH, :].astype(BF16)
        vt[rows, :] = value
        vn[head] = value.T
    dka[...] = jnp.zeros_like(dka)
    dva[...] = jnp.zeros_like(dva)

    def straight(units, i0, base):
        icols = pl.ds(i0, BI)
        edges = [(at, min(BJ, units * 128 - at)) for at in range(0, units * 128, BJ)]
        trips = len(edges)
        spots = [slice(at, at + size) for at, size in edges]
        places = [pl.ds(pl.multiple_of(base + at, 128), size) for at, size in edges]

        def scores(head, j, sums):
            rows = slice(head * DH, (head + 1) * DH)
            e = jnp.exp(dot(kx[head, places[j], :], qx[head, :, icols]))
            p = dot(vn[head, places[j], :], d_att[rows, icols])
            es[head % 2, spots[j], :] = e
            ps[head % 2, spots[j], :] = p
            more = (jnp.sum(e, axis=0, keepdims=True), jnp.sum(e * p, axis=0, keepdims=True))
            return more if sums is None else (sums[0] + more[0], sums[1] + more[1])

        def row_grads(head, j, inverse, inner, held):
            rows = slice(head * DH, (head + 1) * DH)
            w = es[head % 2, spots[j], :] * inverse
            d = (w * (ps[head % 2, spots[j], :] - inner)).astype(BF16)
            w = w.astype(BF16)
            out = dot(vt[rows, places[j]], w)
            query = dot(kt[rows, places[j]], d)
            dva[rows, places[j]] += dot(d_att[rows, icols], w, NT)
            dka[rows, places[j]] += dot(qx[head, :DH, icols], d, NT)
            return (out, query) if held is None else (held[0] + out, held[1] + query)

        sums = None
        for j in range(trips):
            sums = scores(0, j, sums)
        for head in range(heads):
            rows = slice(head * DH, (head + 1) * DH)
            inverse = 1.0 / sums[0]
            inner = sums[1] * inverse
            held = following = None
            for j in range(trips):
                if head + 1 < heads:
                    following = scores(head + 1, j, following)
                held = row_grads(head, j, inverse, inner, held)
            attended[rows, icols] = held[0].astype(BF16)
            dqa[rows, icols] = held[1]
            sums = following

    def query_block(ib, _):
        i0 = pl.multiple_of(ib * BI, BI)
        base = first[seq * (LEN // BI) + ib] * 128
        trips = count[seq * (LEN // BI) + ib]
        for number in range(BI // 128, LEN // 128 + 1):
            pl.when(trips == number)(functools.partial(straight, number, i0, base))
        return 0

    lax.fori_loop(0, LEN // BI, query_block, 0)

    for source, offset, factor in ((dqa, 0, 0.125), (dka, part, 1.0)):
        for head in range(heads):
            start = offset + head * DH
            u, scale = unit(start)
            e = source[head * DH : (head + 1) * DH, :] * factor
            gain_sum[start : start + DH, :] += fold_lanes(e * u)
            f = e * gains[start : start + DH, :1]
            mean_f = jnp.sum(f, axis=0, keepdims=True) * inv_dh
            mean_fu = jnp.sum(f * u, axis=0, keepdims=True) * inv_dh
            d_mixed[start : start + DH, :] = ((f - mean_f - u * mean_fu) * scale).astype(BF16)
    d_mixed[2 * part :, :] = dva[...].astype(BF16)

    split = 3 * part
    total[:split, :] += dot(d_mixed[...], normed[...], NT)
    total[split:, :] += dot(attended[...], cot[...])

    @pl.when(last)
    def _():
        norm_row[...] = jnp.sum(total[:split, :] * mixed_t[...].astype(F32), axis=0, keepdims=True)
        grads[...] = total[...].astype(BF16)


def attention_call(first, count, normed, mixed_t, d_att, mask_q, mask_k, gains, cot):
    seqs, part, _ = d_att.shape
    width = normed.shape[1]
    heads = part // DH
    fixed = lambda i, *_: (0, 0)
    by_seq = lambda i, *_: (i, 0, 0)
    grid_spec = pltpu.PrefetchScalarGridSpec(
        num_scalar_prefetch=2,
        grid=(seqs,),
        in_specs=[
            pl.BlockSpec((None, width, LEN), by_seq),
            pl.BlockSpec((3 * part, width), fixed),
            pl.BlockSpec((None, part, LEN), by_seq),
            pl.BlockSpec((None, IMAGE_SLOTS, LEN), by_seq),
            pl.BlockSpec((None, IMAGE_SLOTS, LEN), by_seq),
            pl.BlockSpec((2 * part, 128), fixed),
            pl.BlockSpec((LEN, width), lambda i, *_: (i, 0)),
        ],
        out_specs=[
            pl.BlockSpec((None, part, LEN), by_seq),
            pl.BlockSpec((None, 3 * part, LEN), by_seq),
            pl.BlockSpec((2 * part, 128), fixed),
            pl.BlockSpec((1, width), fixed),
            pl.BlockSpec((4 * part, width), fixed),
        ],
        scratch_shapes=[
            pltpu.VMEM((4 * part, width), F32),
            pltpu.VMEM((3 * part, LEN), F32),
            pltpu.VMEM((heads, 128, LEN), BF16),
            pltpu.VMEM((heads, LEN, 128), BF16),
            pltpu.VMEM((heads, LEN, DH), BF16),
            pltpu.VMEM((part, LEN), BF16),
            pltpu.VMEM((part, LEN), BF16),
            pltpu.VMEM((2, LEN, BI), F32),
            pltpu.VMEM((2, LEN, BI), F32),
            pltpu.VMEM((part, LEN), F32),
            pltpu.VMEM((part, LEN), F32),
            pltpu.VMEM((part, LEN), F32),
        ],
    )
    return pl.pallas_call(
        attention_kernel,
        grid_spec=grid_spec,
        out_shape=[
            jax.ShapeDtypeStruct((seqs, part, LEN), BF16),
            jax.ShapeDtypeStruct((seqs, 3 * part, LEN), BF16),
            jax.ShapeDtypeStruct((2 * part, 128), F32),
            jax.ShapeDtypeStruct((1, width), F32),
            jax.ShapeDtypeStruct((4 * part, width), BF16),
        ],
        cost_estimate=cost(18, 5_000_000),
        name="attention",
    )(first, count, normed, mixed_t, d_att, mask_q, mask_k, gains, cot)


def project_kernel(
    shard, active, attended, d_pre, d_mixed, normed, down, attn, up, mixed_t, gain, keep, send
):
    me = shard[0]
    part = attended.shape[0]
    out = dot(down[...], active[...], TN) + dot(attn[...], attended[...], TN)
    grad = dot(up[...], d_pre[...]) + dot(mixed_t[...], d_mixed[...], TN)
    product = grad * normed[...].astype(F32)
    sums = []
    for row in (jnp.sum(grad * gain[:, :1], axis=0, keepdims=True), jnp.sum(product, axis=0, keepdims=True)):
        high = row.astype(BF16)
        sums += [high, (row - high.astype(F32)).astype(BF16)]
    sums = jnp.concatenate(sums + [jnp.zeros((SUM_ROWS - 4, sums[0].shape[1]), BF16)], axis=0)
    for target in (keep, send):
        for slot in range(2):
            target[slot, 2 * part :, :] = sums
    for index in range(4):
        rows = slice(index * part, (index + 1) * part)
        away = jnp.bitwise_xor(me, index)
        slot = away // 2

        @pl.when(away % 2 == 0)
        def _():
            keep[slot, :part, :] = out[rows].astype(BF16)
            keep[slot, part : 2 * part, :] = grad[rows].astype(BF16)

        @pl.when(away % 2 == 1)
        def _():
            send[slot, :part, :] = out[rows].astype(BF16)
            send[slot, part : 2 * part, :] = grad[rows].astype(BF16)


def project_call(shard, active, attended, d_pre, d_mixed, normed, down, attn, up, mixed_t, gain, begin, size, block=256):
    hidden, width = down.shape
    part = attended.shape[1]
    steps = LEN // block
    ours = lambda i, *_: (begin + i // steps, 0, i % steps)
    out = lambda i, *_: (i // steps, 0, 0, i % steps)
    fixed = lambda i, *_: (0, 0)
    rows = 2 * part + SUM_ROWS
    grid_spec = pltpu.PrefetchScalarGridSpec(
        num_scalar_prefetch=1,
        grid=(size * steps,),
        in_specs=[
            pl.BlockSpec((None, hidden, block), ours),
            pl.BlockSpec((None, part, block), ours),
            pl.BlockSpec((None, hidden, block), ours),
            pl.BlockSpec((None, 3 * part, block), ours),
            pl.BlockSpec((None, width, block), ours),
            pl.BlockSpec((hidden, width), fixed),
            pl.BlockSpec((part, width), fixed),
            pl.BlockSpec((width, hidden), fixed),
            pl.BlockSpec((3 * part, width), fixed),
            pl.BlockSpec((width, 128), fixed),
        ],
        out_specs=[
            pl.BlockSpec((None, 2, rows, block), out),
            pl.BlockSpec((None, 2, rows, block), out),
        ],
    )
    return pl.pallas_call(
        project_kernel,
        grid_spec=grid_spec,
        out_shape=[
            jax.ShapeDtypeStruct((size, 2, rows, LEN), BF16),
            jax.ShapeDtypeStruct((size, 2, rows, LEN), BF16),
        ],
        cost_estimate=cost(8, 16_000_000),
        name="project",
    )(shard, active, attended, d_pre, d_mixed, normed, down, attn, up, mixed_t, gain)


def finish_kernel(keep, from_core, from_y, own_t, cot, stats, gain, bias, *rest):
    block_out, token_grad = rest[-2:]
    part = own_t.shape[0]
    inv_width = 0.25 / part
    total = keep[...].astype(F32) + from_core[...].astype(F32) + from_y[...].astype(F32)
    own = own_t[...].astype(F32)
    block_out[...] = (own + total[:part] + bias[:, :1].astype(F32)).astype(BF16)
    grad = total[part : 2 * part]
    sums = total[2 * part :]
    mean = stats[0:1, :]
    scale = stats[1:2, :]
    hat = (own - mean) * scale
    inner = grad * gain[:, :1].astype(F32) - (sums[0:1] + sums[1:2]) * inv_width - hat * ((sums[2:3] + sums[3:4]) * inv_width)
    token_grad[...] = cot[...].astype(F32) + inner * scale


def finish_call(keep, from_core, from_y, own_t, cot, stats, gain, bias, before, begin, block=512):
    part, tokens = own_t.shape
    steps = LEN // block
    size = keep.shape[0]
    fixed = lambda i: (0, 0)
    packed = pl.BlockSpec((None, None, 2 * part + SUM_ROWS, block), lambda i: (i // steps, 0, 0, i % steps))
    ours = lambda i: (0, begin * steps + i)
    here = pl.BlockSpec((part, block), ours)
    return pl.pallas_call(
        finish_kernel,
        grid=(size * steps,),
        in_specs=[
            packed, packed, packed,
            here, here,
            pl.BlockSpec((8, block), ours),
            pl.BlockSpec((part, 128), fixed),
            pl.BlockSpec((part, 128), fixed),
        ]
        + [ANY] * len(before),
        out_specs=[here, here],
        out_shape=[
            jax.ShapeDtypeStruct((part, tokens), BF16),
            jax.ShapeDtypeStruct((part, tokens), F32),
        ],
        input_output_aliases={8 + i: i for i in range(len(before))},
        cost_estimate=cost(3, 5_000_000),
        compiler_params=pltpu.CompilerParams(vmem_limit_bytes=40 << 20),
        name="finish",
    )(keep, from_core, from_y, own_t, cot, stats, gain, bias, *before)


def flip(value, axis, size, bit):
    return lax.ppermute(value, axis, [(i, i ^ bit) for i in range(size)])


def tie(*trees):
    return lax.optimization_barrier(trees)


def joined(swap, held, arrived):
    return jnp.where(
        swap, jnp.concatenate([arrived, held], axis=0), jnp.concatenate([held, arrived], axis=0)
    )


def piece_order(size):
    bits = size.bit_length() - 1
    return [sum(((i >> b) & 1) << (bits - 1 - b) for b in range(bits)) for i in range(size)]


class SumOverDp:
    def __init__(self, value, size, index):
        self.size, self.index = size, index
        self.send = value
        self.steps = ["sum"] + [1 << i for i in reversed(range(size.bit_length() - 1))]

    def more(self):
        return bool(self.steps)

    def move(self, send):
        if self.steps[0] == "sum":
            return lax.all_to_all(send, "dp", 0, 0, tiled=True)
        return flip(send, "dp", self.size, self.steps[0])

    def take(self, arrived):
        step = self.steps.pop(0)
        if step == "sum":
            shares = arrived.reshape(self.size, -1, arrived.shape[1]).astype(F32)
            self.keep = jnp.sum(shares, axis=0).astype(BF16)
        else:
            self.last = ((self.index & step) > 0, self.keep, arrived)
            self.keep = joined(*self.last)
        self.send = self.keep


class ChainOverDp:
    def __init__(self, value, size, index):
        self.size, self.index = size, index
        bits = [1 << i for i in range(size.bit_length() - 1)]
        self.steps = [("sum", bit) for bit in bits] + [("join", bit) for bit in reversed(bits)]
        self.prepare(value, None)

    def prepare(self, held, arrived):
        def part(which, half):
            rows = lax.dynamic_slice_in_dim(held, which * half, half, 0)
            if arrived is None:
                return rows
            came = lax.dynamic_slice_in_dim(arrived, which * half, half, 0)
            return (rows.astype(F32) + came.astype(F32)).astype(BF16)

        rows = held.shape[0]
        if self.steps and self.steps[0][0] == "sum":
            side = ((self.index & self.steps[0][1]) > 0).astype(jnp.int32)
            self.send, self.keep = part(1 - side, rows // 2), part(side, rows // 2)
        else:
            self.keep = part(0, rows)
            self.send = self.keep

    def more(self):
        return bool(self.steps)

    def move(self, send):
        return flip(send, "dp", self.size, self.steps[0][1])

    def take(self, arrived):
        kind, bit = self.steps.pop(0)
        if kind == "sum":
            self.prepare(self.keep, arrived)
            return
        self.last = ((self.index & bit) > 0, self.keep, arrived)
        self.keep = self.send = joined(*self.last)


class ScatterOverMp:
    def __init__(self, keep, send):
        self.keep, self.send = keep, send
        self.bits = [1, 2]

    def more(self):
        return bool(self.bits)

    def move(self, send):
        return flip(send, "mp", 4, self.bits[0])

    def take(self, arrived):
        bit = self.bits.pop(0)
        if bit == 1:
            self.from_core = arrived
            self.send = (self.keep[:, 1:].astype(F32) + arrived[:, 1:].astype(F32)).astype(BF16)
        else:
            self.from_y = arrived


def land_in_turn(phases, outputs):
    movers = []
    for flights in phases:
        outputs, sends, arrivals = tie(outputs, [m.send for m in movers], [f[1] for f in flights])
        for mover, send in zip(movers, sends):
            mover.send = send
        for (mover, _), arrived in zip(flights, arrivals):
            mover.take(arrived)
        movers += [f[0] for f in flights]
    return outputs


class ShortSums:
    def __init__(self, keep, send, rest, size):
        self.keep, self.send, self.rest, self.size = keep, send, rest, size
        self.steps = [("mp", 1), ("mp", 2)] + [("dp", 1 << i) for i in range(size.bit_length() - 1)]

    def more(self):
        return bool(self.steps)

    def move(self, send):
        axis, bit = self.steps[0]
        return flip(send, axis, 4 if axis == "mp" else self.size, bit)

    def take(self, arrived):
        axis, bit = self.steps.pop(0)
        if (axis, bit) == ("mp", 1):
            both = self.keep + arrived
            self.norm, self.send = both[0], both[1]
            return
        if axis == "mp":
            self.send = jnp.concatenate([self.norm + arrived, self.rest])
        else:
            self.send = self.send + arrived
        size = self.norm.shape[0]
        self.norm, self.rest = self.send[:size], self.send[size:]


def launch(movers, inputs):
    movers = [m for m in movers if m.more()]
    inputs, sends = tie(inputs, [m.send for m in movers])
    return inputs, [(m, m.move(s)) for m, s in zip(movers, sends)]


def land(flights, outputs):
    outputs, arrivals = tie(outputs, [f[1] for f in flights])
    for (mover, _), arrived in zip(flights, arrivals):
        mover.take(arrived)
    return outputs


def body(
    dp_size,
    tokens,
    image_ids,
    norm_gain,
    qkv_weight,
    qk_gain,
    attn_weight,
    up_weight,
    up_bias,
    down_weight,
    down_bias,
    cotangent,
):
    part = tokens.shape[1]
    width = cotangent.shape[1]
    seqs = image_ids.shape[0]
    me = lax.axis_index("mp")
    dp = lax.axis_index("dp")
    shard = me.astype(jnp.int32)[None]
    place = jnp.bitwise_xor(shard, jnp.array([0, 2, 1, 3], jnp.int32)) * part

    own_t = tokens.T
    from_y = flip(own_t, "mp", 4, 2)
    gain_own = jnp.broadcast_to(norm_gain[:, None], (part, 128))
    gain_y = flip(gain_own, "mp", 4, 2)
    gain_c = flip(gain_own, "mp", 4, 1)

    mixed_t = jnp.transpose(qkv_weight, (1, 2, 0)).reshape(3 * part, width)
    def column(vector):
        return jnp.broadcast_to(vector[:, None], (vector.shape[0], 128))

    columns = (column(up_bias), column(qk_gain.astype(F32).reshape(2 * part)), column(down_bias))

    slots = jnp.arange(IMAGE_SLOTS, dtype=jnp.int32)[None, :, None]
    same = image_ids[:, None, :] == slots
    mask_q = same.astype(BF16)
    mask_k = jnp.where(same | (slots >= 8), 0.0, -PENALTY).astype(BF16)
    block_first = image_ids[:, ::BI]
    block_last = image_ids[:, BI - 1 :: BI]
    starts = jnp.sum(image_ids[:, None, :] < block_first[:, :, None], axis=2, dtype=jnp.int32)
    ends = jnp.sum(image_ids[:, None, :] <= block_last[:, :, None], axis=2, dtype=jnp.int32)
    first = starts // 128
    count = ((ends + 127) // 128 - first).reshape(-1)
    first = first.reshape(-1)

    pick = (jnp.arange(part)[:, None] + me * part == jnp.arange(width)[None, :]).astype(BF16)
    pick, place, columns, (gain_y, gain_c) = tie(pick, place, columns, (gain_y, gain_c))
    up_bias_col, head_gains, bias_col = columns
    gain_cy = flip(gain_y, "mp", 4, 1)
    d_act, d_att, cot_own, cot_sum = early_call(cotangent, down_weight, attn_weight, pick)
    prepared = (
        d_act, d_att, mixed_t, up_bias_col, head_gains, mask_q, mask_k, first, count,
        bias_col,
    )
    prepared, (from_y, gain_cy) = tie(prepared, (from_y, gain_cy))
    gains = (gain_own, gain_y, gain_c, gain_cy)
    (
        d_act, d_att, mixed_t, up_bias_col, head_gains, mask_q, mask_k, first, count,
        bias_col,
    ) = prepared
    pieces = (own_t, from_y, flip(own_t, "mp", 4, 1), flip(from_y, "mp", 4, 1))
    normed, active, d_pre, stats, upbias_part, gain_all, up_row, mlp_part = mlp_call(
        tuple(piece_order(dp_size)), place, pieces, gains, up_weight, up_bias_col, d_act, cotangent
    )
    mlp_sum = SumOverDp(mlp_part, dp_size, dp)

    (states,), flying = launch([mlp_sum], (normed,))
    attended, d_mixed, qk_part, norm_row, mix_part = attention_call(
        first, count, states, mixed_t, d_att, mask_q, mask_k, head_gains, cotangent
    )
    mix_sum = ChainOverDp(mix_part, dp_size, dp)

    norm_vec = norm_row[0] + jnp.sum(up_row, axis=1)
    norm_parts = norm_vec.reshape(4, part)
    norm_parts = [lax.dynamic_index_in_dim(norm_parts, jnp.bitwise_xor(me, m), 0, False) for m in range(4)]
    short = ShortSums(
        jnp.stack([norm_parts[0], norm_parts[2]]),
        jnp.stack([norm_parts[1], norm_parts[3]]),
        jnp.concatenate([jnp.sum(qk_part, axis=1), jnp.sum(upbias_part, axis=1), jnp.sum(cot_sum, axis=1)]),
        dp_size,
    )

    runs = [(seq, 1) for seq in range(seqs)]
    scatters = []
    for begin, size in runs:
        busy = [f[0] for f in flying]
        along = [m for m in [mix_sum, mlp_sum, short] + scatters if m.more() and m not in busy]
        (att, dm), flights = launch(along, (attended, d_mixed))
        flying = flying + flights
        sent = project_call(
            shard, active, att, d_pre, dm, normed, down_weight, attn_weight, up_weight, mixed_t, gain_all, begin, size
        )
        final = seqs - 1
        late = [f for f in flights if begin == 0 and f[0] is mix_sum or begin == final and f[0] is scatters[0]]
        wide = [f for f in flying if f[0] is mlp_sum]
        chain = [f for f in flying if f[0] is mix_sum and f not in late]
        quick = [f for f in flying if f not in late + wide + chain]
        keep, send = land_in_turn([quick, wide, chain], sent)
        if begin == final and begin > 0:
            _, ahead = launch([mix_sum], ())
            (keep, send), *_ = (land(late, (keep, send)),)
            late = ahead
        flying = late
        scatters.append(ScatterOverMp(keep, send))

    finished = ()
    wide_grads = ()
    done = set()

    def finish_ready(finished):
        for (begin, _), scatter in zip(runs, scatters):
            if not scatter.more() and begin not in done:
                done.add(begin)
                finished = finish_call(
                    scatter.keep, scatter.from_core, scatter.from_y, own_t, cot_own, stats, gain_own, bias_col,
                    finished, begin,
                )
        return finished

    while True:
        busy = [f[0] for f in flying]
        ready = [m for m in [mix_sum] + scatters + [short, mlp_sum] if m.more() and m not in busy]
        finished, flights = launch(ready, finished)
        flying = flying + flights
        if not flying:
            break
        finished = finish_ready(finished)
        near = [f for f in flying if f[0] in scatters and len(f[0].bits) == 2]
        across = [f for f in flying if f[0] in scatters and len(f[0].bits) == 1]
        chain = [f for f in flying if f[0] is mix_sum]
        rest = [f for f in flying if f[0] is short]
        wide = [f for f in flying if f[0] is mlp_sum]
        left = len(mix_sum.steps)
        if near:
            now = near + chain + rest
        elif left == 2:
            now = chain + across[:1] + rest
        elif left == 1:
            now = wide + rest or across[:1] or chain
        else:
            now = chain + rest or flying
        final = [f for f in now if f[0] is mix_sum]
        finished, wide_grads = land_in_turn([[f for f in now if f not in final], final], (finished, wide_grads))
        flying = [f for f in flying if f not in now]
        if not mlp_sum.more() and not wide_grads:
            swap, held, arrived = mlp_sum.last
            wide_grads = (
                jnp.where(swap, arrived, held).astype(F32),
                jnp.where(swap, held, arrived).astype(F32),
            )
    finished = finish_ready(finished)
    block_out, token_grad = finished
    block_out, token_grad = block_out.T, token_grad.T
    swap, held, arrived = mix_sum.last
    left = 3 * part - held.shape[0]
    qkv_rows = joined(swap, held, arrived)[: 3 * part].astype(F32)
    attn_grad = jnp.where(swap, held[left:], arrived[left:]).astype(F32)
    qkv_grad = jnp.transpose(qkv_rows.reshape(3, part, width), (2, 0, 1))

    gain_grad = short.norm / norm_gain.astype(F32)
    rest = short.rest
    split = 2 * part + up_weight.shape[1]
    return (
        block_out,
        token_grad,
        gain_grad,
        qkv_grad,
        rest[: 2 * part].reshape(2, part),
        attn_grad,
        wide_grads[1],
        rest[2 * part : split],
        wide_grads[0],
        rest[split:],
    )


def solution(mesh):
    in_specs = (
        P("dp", "mp"),
        P("dp", None),
        P("mp"),
        P(None, None, "mp"),
        P(None, "mp"),
        P("mp", None),
        P(None, "mp"),
        P("mp"),
        P("mp", None),
        P("mp"),
        P("dp", None),
    )
    out_specs = (
        P("dp", "mp"),
        P("dp", "mp"),
        P("mp"),
        P(None, None, "mp"),
        P(None, "mp"),
        P("mp", None),
        P(None, "mp"),
        P("mp"),
        P("mp", None),
        P("mp"),
    )
    run = functools.partial(body, mesh.shape["dp"])
    return jax.shard_map(run, mesh=mesh, in_specs=in_specs, out_specs=out_specs, check_vma=False)
```

```python
import functools

import jax
import jax.numpy as jnp
from jax import lax
from jax.experimental import pallas as pl
from jax.experimental.pallas import tpu as pltpu
from jax.sharding import PartitionSpec as P

DH = 64
LEN = 1024
EPSILON = 1e-06
IMAGE_SLOTS = 16
PENALTY = 1024.0
BI = 256
BJ = 256
SUM_ROWS = 16
F32 = jnp.float32
BF16 = jnp.bfloat16

NN = (((1,), (0,)), ((), ()))
NT = (((1,), (1,)), ((), ()))
TN = (((0,), (0,)), ((), ()))
ANY = pl.BlockSpec(memory_space=pl.ANY)


def dot(left, right, dims=NN):
    return lax.dot_general(left, right, dims, preferred_element_type=F32)


def fold_lanes(rows):
    total = rows[:, :128]
    for start in range(128, rows.shape[1], 128):
        total = total + rows[:, start : start + 128]
    return total


def cost(microseconds, nbytes):
    return pl.CostEstimate(flops=int(microseconds * 1e3), bytes_accessed=nbytes // 1000, transcendentals=0)


def early_kernel(cot, down, attn, pick, d_act, d_att, cot_own, bias_sum):
    rows = cot[...]
    d_act[...] = dot(down[...], rows, NT).astype(BF16)
    d_att[...] = dot(attn[...], rows, NT).astype(BF16)
    own = dot(pick[...], rows, NT)
    cot_own[...] = own.astype(BF16)

    @pl.when(pl.program_id(0) == 0)
    def _():
        bias_sum[...] = jnp.zeros_like(bias_sum)

    bias_sum[...] += fold_lanes(own)


def early_call(cot, down, attn, pick, block=512):
    tokens, width = cot.shape
    seqs = tokens // LEN
    hidden, part = down.shape[0], attn.shape[0]
    steps = LEN // block
    fixed = lambda i: (0, 0)
    by_seq = lambda i: (i // steps, 0, i % steps)
    return pl.pallas_call(
        early_kernel,
        grid=(tokens // block,),
        in_specs=[
            pl.BlockSpec((block, width), lambda i: (i, 0)),
            pl.BlockSpec((hidden, width), fixed),
            pl.BlockSpec((part, width), fixed),
            pl.BlockSpec((part, width), fixed),
        ],
        out_specs=[
            pl.BlockSpec((None, hidden, block), by_seq),
            pl.BlockSpec((None, part, block), by_seq),
            pl.BlockSpec((part, block), lambda i: (0, i)),
            pl.BlockSpec((part, 128), fixed),
        ],
        out_shape=[
            jax.ShapeDtypeStruct((seqs, hidden, LEN), BF16),
            jax.ShapeDtypeStruct((seqs, part, LEN), BF16),
            jax.ShapeDtypeStruct((part, tokens), BF16),
            jax.ShapeDtypeStruct((part, 128), F32),
        ],
        cost_estimate=cost(10, 12_000_000),
        name="early",
    )(cot, down, attn, pick)


def mlp_kernel(
    pieces_order, place, own, flip_y, flip_c, flip_cy, gain_own, gain_y, gain_c, gain_cy, up, up_bias, d_act, cot,
    normed, active, d_pre, stats, bias_sum, gain_all, up_row, grads, low, high
):
    pieces = (own, flip_y, flip_c, flip_cy)
    part = own.shape[0]
    width = part * 4
    first = pl.program_id(0) == 0
    last = pl.program_id(0) == pl.num_programs(0) - 1

    @pl.when(first)
    def _():
        bias_sum[...] = jnp.zeros_like(bias_sum)
        low[...] = jnp.zeros_like(low)
        high[...] = jnp.zeros_like(high)
        for slot, piece in enumerate((gain_own, gain_y, gain_c, gain_cy)):
            gain_all[pl.ds(pl.multiple_of(place[slot], part), part), :] = piece[...].astype(F32)

    total = 0.0
    squares = 0.0
    for piece in pieces:
        rows = piece[...].astype(F32)
        total = total + jnp.sum(rows, axis=0, keepdims=True)
        squares = squares + jnp.sum(rows * rows, axis=0, keepdims=True)
    mean = total * (1.0 / width)
    scale = lax.rsqrt(squares * (1.0 / width) - mean * mean + EPSILON)
    stats[0:1, :] = mean
    stats[1:2, :] = scale
    stats[2:8, :] = jnp.zeros((6, stats.shape[1]), F32)
    for slot, piece in enumerate(pieces):
        rows = piece[...].astype(F32)
        here = pl.ds(pl.multiple_of(place[slot], part), part)
        normed[here, :] = ((rows - mean) * scale * gain_all[here, :1]).astype(BF16)

    c0 = 0.7978845608028654
    c1 = 0.044715 * c0
    def lift(start):
        here = slice(start, start + 256)
        return dot(up[:, here], normed[...], TN) + up_bias[here, :1].astype(F32)

    ahead = lift(0)
    for start in range(0, up.shape[1], 256):
        here = slice(start, start + 256)
        pre = ahead
        if start + 256 < up.shape[1]:
            ahead = lift(start + 256)
        square = pre * pre
        half = 0.5 * jnp.tanh(pre * (c0 + c1 * square)) + 0.5
        act = (pre * half).astype(BF16)
        active[here, :] = act
        slope = half + pre * (half - half * half) * (2.0 * c0 + 6.0 * c1 * square)
        grad = (d_act[here, :].astype(F32) * slope).astype(BF16)
        d_pre[here, :] = grad
        bias_sum[here, :] += fold_lanes(grad.astype(F32))
        low[here, :] += dot(act, cot[...])
        high[:, here] += dot(normed[...], grad, NT)

    @pl.when(last)
    def _():
        up_row[...] = fold_lanes(high[...] * up[...].astype(F32))
        half = low.shape[0]
        size = grads.shape[0] // len(pieces_order)
        for slot, piece in enumerate(pieces_order):
            source, start = (low, piece * size) if piece * size < half else (high, piece * size - half)
            grads[slot * size : (slot + 1) * size, :] = source[start : start + size, :].astype(BF16)


def mlp_call(pieces_order, place, pieces, gains, up, up_bias, d_act, cot, block=512):
    part, tokens = pieces[0].shape
    width = 4 * part
    seqs, hidden, _ = d_act.shape
    steps = LEN // block
    lanes = lambda i, *_: (0, i)
    by_seq = lambda i, *_: (i // steps, 0, i % steps)
    fixed = lambda i, *_: (0, 0)
    grid_spec = pltpu.PrefetchScalarGridSpec(
        num_scalar_prefetch=1,
        grid=(tokens // block,),
        in_specs=[pl.BlockSpec((part, block), lanes)] * 4
        + [pl.BlockSpec((part, 128), fixed)] * 4
        + [
            pl.BlockSpec((width, hidden), fixed),
            pl.BlockSpec((hidden, 128), fixed),
            pl.BlockSpec((None, hidden, block), by_seq),
            pl.BlockSpec((block, width), lambda i, *_: (i, 0)),
        ],
        out_specs=[
            pl.BlockSpec((None, width, block), by_seq),
            pl.BlockSpec((None, hidden, block), by_seq),
            pl.BlockSpec((None, hidden, block), by_seq),
            pl.BlockSpec((8, block), lanes),
            pl.BlockSpec((hidden, 128), fixed),
            pl.BlockSpec((width, 128), fixed),
            pl.BlockSpec((width, 128), fixed),
            pl.BlockSpec((hidden + width, width), fixed),
        ],
        scratch_shapes=[pltpu.VMEM((hidden, width), F32), pltpu.VMEM((width, hidden), F32)],
    )
    assert hidden == width
    return pl.pallas_call(
        functools.partial(mlp_kernel, pieces_order),
        grid_spec=grid_spec,
        out_shape=[
            jax.ShapeDtypeStruct((seqs, width, LEN), BF16),
            jax.ShapeDtypeStruct((seqs, hidden, LEN), BF16),
            jax.ShapeDtypeStruct((seqs, hidden, LEN), BF16),
            jax.ShapeDtypeStruct((8, tokens), F32),
            jax.ShapeDtypeStruct((hidden, 128), F32),
            jax.ShapeDtypeStruct((width, 128), F32),
            jax.ShapeDtypeStruct((width, 128), F32),
            jax.ShapeDtypeStruct((hidden + width, width), BF16),
        ],
        cost_estimate=cost(20, 30_000_000),
        name="mlp",
    )(place, *pieces, *gains, up, up_bias, d_act, cot)


def attention_kernel(
    first, count, normed, mixed_t, d_att, mask_q, mask_k, gains, cot, attended, d_mixed, gain_sum, norm_row, grads,
    total, qkv, qx, kx, vn, kt, vt, es, ps, dqa, dka, dva
):
    seq = pl.program_id(0)
    last = seq == pl.num_programs(0) - 1
    part = attended.shape[0]
    heads = part // DH
    inv_dh = 1.0 / DH

    @pl.when(seq == 0)
    def _():
        total[...] = jnp.zeros_like(total)
        gain_sum[...] = jnp.zeros_like(gain_sum)

    qkv[...] = dot(mixed_t[...], normed[...])

    def unit(start):
        raw = qkv[start : start + DH, :]
        shifted = raw - jnp.sum(raw, axis=0, keepdims=True) * inv_dh
        scale = lax.rsqrt(jnp.sum(shifted * shifted, axis=0, keepdims=True) * inv_dh + EPSILON)
        return shifted * scale, scale

    zeros = jnp.zeros((128 - DH - IMAGE_SLOTS, LEN), BF16)
    for head in range(heads):
        rows = slice(head * DH, (head + 1) * DH)
        query, _ = unit(head * DH)
        query = (query * (gains[rows, :1] * 0.125)).astype(BF16)
        qx[head] = jnp.concatenate([query, mask_q[...], zeros], axis=0)
        key, _ = unit(part + head * DH)
        key = (key * gains[part + head * DH : part + (head + 1) * DH, :1]).astype(BF16)
        kt[rows, :] = key
        kx[head] = jnp.concatenate([key, mask_k[...], zeros], axis=0).T
        value = qkv[2 * part + head * DH : 2 * part + (head + 1) * DH, :].astype(BF16)
        vt[rows, :] = value
        vn[head] = value.T
    dka[...] = jnp.zeros_like(dka)
    dva[...] = jnp.zeros_like(dva)

    def straight(units, i0, base):
        icols = pl.ds(i0, BI)
        edges = [(at, min(BJ, units * 128 - at)) for at in range(0, units * 128, BJ)]
        trips = len(edges)
        spots = [slice(at, at + size) for at, size in edges]
        places = [pl.ds(pl.multiple_of(base + at, 128), size) for at, size in edges]

        def scores(head, j, sums):
            rows = slice(head * DH, (head + 1) * DH)
            e = jnp.exp(dot(kx[head, places[j], :], qx[head, :, icols]))
            p = dot(vn[head, places[j], :], d_att[rows, icols])
            es[head % 2, spots[j], :] = e
            ps[head % 2, spots[j], :] = p
            more = (jnp.sum(e, axis=0, keepdims=True), jnp.sum(e * p, axis=0, keepdims=True))
            return more if sums is None else (sums[0] + more[0], sums[1] + more[1])

        def row_grads(head, j, inverse, inner, held):
            rows = slice(head * DH, (head + 1) * DH)
            w = es[head % 2, spots[j], :] * inverse
            d = (w * (ps[head % 2, spots[j], :] - inner)).astype(BF16)
            w = w.astype(BF16)
            out = dot(vt[rows, places[j]], w)
            query = dot(kt[rows, places[j]], d)
            dva[rows, places[j]] += dot(d_att[rows, icols], w, NT)
            dka[rows, places[j]] += dot(qx[head, :DH, icols], d, NT)
            return (out, query) if held is None else (held[0] + out, held[1] + query)

        sums = None
        for j in range(trips):
            sums = scores(0, j, sums)
        for head in range(heads):
            rows = slice(head * DH, (head + 1) * DH)
            inverse = 1.0 / sums[0]
            inner = sums[1] * inverse
            held = following = None
            for j in range(trips):
                if head + 1 < heads:
                    following = scores(head + 1, j, following)
                held = row_grads(head, j, inverse, inner, held)
            attended[rows, icols] = held[0].astype(BF16)
            dqa[rows, icols] = held[1]
            sums = following

    def query_block(ib, _):
        i0 = pl.multiple_of(ib * BI, BI)
        base = first[seq * (LEN // BI) + ib] * 128
        trips = count[seq * (LEN // BI) + ib]
        for number in range(BI // 128, LEN // 128 + 1):
            pl.when(trips == number)(functools.partial(straight, number, i0, base))
        return 0

    lax.fori_loop(0, LEN // BI, query_block, 0)

    for source, offset, factor in ((dqa, 0, 0.125), (dka, part, 1.0)):
        for head in range(heads):
            start = offset + head * DH
            u, scale = unit(start)
            e = source[head * DH : (head + 1) * DH, :] * factor
            gain_sum[start : start + DH, :] += fold_lanes(e * u)
            f = e * gains[start : start + DH, :1]
            mean_f = jnp.sum(f, axis=0, keepdims=True) * inv_dh
            mean_fu = jnp.sum(f * u, axis=0, keepdims=True) * inv_dh
            d_mixed[start : start + DH, :] = ((f - mean_f - u * mean_fu) * scale).astype(BF16)
    d_mixed[2 * part :, :] = dva[...].astype(BF16)

    split = 3 * part
    total[:split, :] += dot(d_mixed[...], normed[...], NT)
    total[split:, :] += dot(attended[...], cot[...])

    @pl.when(last)
    def _():
        norm_row[...] = jnp.sum(total[:split, :] * mixed_t[...].astype(F32), axis=0, keepdims=True)
        grads[...] = total[...].astype(BF16)


def attention_call(first, count, normed, mixed_t, d_att, mask_q, mask_k, gains, cot):
    seqs, part, _ = d_att.shape
    width = normed.shape[1]
    heads = part // DH
    fixed = lambda i, *_: (0, 0)
    by_seq = lambda i, *_: (i, 0, 0)
    grid_spec = pltpu.PrefetchScalarGridSpec(
        num_scalar_prefetch=2,
        grid=(seqs,),
        in_specs=[
            pl.BlockSpec((None, width, LEN), by_seq),
            pl.BlockSpec((3 * part, width), fixed),
            pl.BlockSpec((None, part, LEN), by_seq),
            pl.BlockSpec((None, IMAGE_SLOTS, LEN), by_seq),
            pl.BlockSpec((None, IMAGE_SLOTS, LEN), by_seq),
            pl.BlockSpec((2 * part, 128), fixed),
            pl.BlockSpec((LEN, width), lambda i, *_: (i, 0)),
        ],
        out_specs=[
            pl.BlockSpec((None, part, LEN), by_seq),
            pl.BlockSpec((None, 3 * part, LEN), by_seq),
            pl.BlockSpec((2 * part, 128), fixed),
            pl.BlockSpec((1, width), fixed),
            pl.BlockSpec((4 * part, width), fixed),
        ],
        scratch_shapes=[
            pltpu.VMEM((4 * part, width), F32),
            pltpu.VMEM((3 * part, LEN), F32),
            pltpu.VMEM((heads, 128, LEN), BF16),
            pltpu.VMEM((heads, LEN, 128), BF16),
            pltpu.VMEM((heads, LEN, DH), BF16),
            pltpu.VMEM((part, LEN), BF16),
            pltpu.VMEM((part, LEN), BF16),
            pltpu.VMEM((2, LEN, BI), F32),
            pltpu.VMEM((2, LEN, BI), F32),
            pltpu.VMEM((part, LEN), F32),
            pltpu.VMEM((part, LEN), F32),
            pltpu.VMEM((part, LEN), F32),
        ],
    )
    return pl.pallas_call(
        attention_kernel,
        grid_spec=grid_spec,
        out_shape=[
            jax.ShapeDtypeStruct((seqs, part, LEN), BF16),
            jax.ShapeDtypeStruct((seqs, 3 * part, LEN), BF16),
            jax.ShapeDtypeStruct((2 * part, 128), F32),
            jax.ShapeDtypeStruct((1, width), F32),
            jax.ShapeDtypeStruct((4 * part, width), BF16),
        ],
        cost_estimate=cost(18, 5_000_000),
        name="attention",
    )(first, count, normed, mixed_t, d_att, mask_q, mask_k, gains, cot)


def project_kernel(
    shard, active, attended, d_pre, d_mixed, normed, down, attn, up, mixed_t, gain, keep, send
):
    me = shard[0]
    part = attended.shape[0]
    out = dot(down[...], active[...], TN) + dot(attn[...], attended[...], TN)
    grad = dot(up[...], d_pre[...]) + dot(mixed_t[...], d_mixed[...], TN)
    product = grad * normed[...].astype(F32)
    sums = []
    for row in (jnp.sum(grad * gain[:, :1], axis=0, keepdims=True), jnp.sum(product, axis=0, keepdims=True)):
        high = row.astype(BF16)
        sums += [high, (row - high.astype(F32)).astype(BF16)]
    sums = jnp.concatenate(sums + [jnp.zeros((SUM_ROWS - 4, sums[0].shape[1]), BF16)], axis=0)
    for target in (keep, send):
        for slot in range(2):
            target[slot, 2 * part :, :] = sums
    for index in range(4):
        rows = slice(index * part, (index + 1) * part)
        away = jnp.bitwise_xor(me, index)
        slot = away // 2

        @pl.when(away % 2 == 0)
        def _():
            keep[slot, :part, :] = out[rows].astype(BF16)
            keep[slot, part : 2 * part, :] = grad[rows].astype(BF16)

        @pl.when(away % 2 == 1)
        def _():
            send[slot, :part, :] = out[rows].astype(BF16)
            send[slot, part : 2 * part, :] = grad[rows].astype(BF16)


def project_call(shard, active, attended, d_pre, d_mixed, normed, down, attn, up, mixed_t, gain, begin, size, block=256):
    hidden, width = down.shape
    part = attended.shape[1]
    steps = LEN // block
    ours = lambda i, *_: (begin + i // steps, 0, i % steps)
    out = lambda i, *_: (i // steps, 0, 0, i % steps)
    fixed = lambda i, *_: (0, 0)
    rows = 2 * part + SUM_ROWS
    grid_spec = pltpu.PrefetchScalarGridSpec(
        num_scalar_prefetch=1,
        grid=(size * steps,),
        in_specs=[
            pl.BlockSpec((None, hidden, block), ours),
            pl.BlockSpec((None, part, block), ours),
            pl.BlockSpec((None, hidden, block), ours),
            pl.BlockSpec((None, 3 * part, block), ours),
            pl.BlockSpec((None, width, block), ours),
            pl.BlockSpec((hidden, width), fixed),
            pl.BlockSpec((part, width), fixed),
            pl.BlockSpec((width, hidden), fixed),
            pl.BlockSpec((3 * part, width), fixed),
            pl.BlockSpec((width, 128), fixed),
        ],
        out_specs=[
            pl.BlockSpec((None, 2, rows, block), out),
            pl.BlockSpec((None, 2, rows, block), out),
        ],
    )
    return pl.pallas_call(
        project_kernel,
        grid_spec=grid_spec,
        out_shape=[
            jax.ShapeDtypeStruct((size, 2, rows, LEN), BF16),
            jax.ShapeDtypeStruct((size, 2, rows, LEN), BF16),
        ],
        cost_estimate=cost(8, 16_000_000),
        name="project",
    )(shard, active, attended, d_pre, d_mixed, normed, down, attn, up, mixed_t, gain)


def finish_kernel(keep, from_core, from_y, own_t, cot, stats, gain, bias, *rest):
    block_out, token_grad = rest[-2:]
    part = own_t.shape[0]
    inv_width = 0.25 / part
    total = keep[...].astype(F32) + from_core[...].astype(F32) + from_y[...].astype(F32)
    own = own_t[...].astype(F32)
    block_out[...] = (own + total[:part] + bias[:, :1].astype(F32)).astype(BF16)
    grad = total[part : 2 * part]
    sums = total[2 * part :]
    mean = stats[0:1, :]
    scale = stats[1:2, :]
    hat = (own - mean) * scale
    inner = grad * gain[:, :1].astype(F32) - (sums[0:1] + sums[1:2]) * inv_width - hat * ((sums[2:3] + sums[3:4]) * inv_width)
    token_grad[...] = cot[...].astype(F32) + inner * scale


def finish_call(keep, from_core, from_y, own_t, cot, stats, gain, bias, before, begin, block=512):
    part, tokens = own_t.shape
    steps = LEN // block
    size = keep.shape[0]
    fixed = lambda i: (0, 0)
    packed = pl.BlockSpec((None, None, 2 * part + SUM_ROWS, block), lambda i: (i // steps, 0, 0, i % steps))
    ours = lambda i: (0, begin * steps + i)
    here = pl.BlockSpec((part, block), ours)
    return pl.pallas_call(
        finish_kernel,
        grid=(size * steps,),
        in_specs=[
            packed, packed, packed,
            here, here,
            pl.BlockSpec((8, block), ours),
            pl.BlockSpec((part, 128), fixed),
            pl.BlockSpec((part, 128), fixed),
        ]
        + [ANY] * len(before),
        out_specs=[here, here],
        out_shape=[
            jax.ShapeDtypeStruct((part, tokens), BF16),
            jax.ShapeDtypeStruct((part, tokens), F32),
        ],
        input_output_aliases={8 + i: i for i in range(len(before))},
        cost_estimate=cost(3, 5_000_000),
        name="finish",
    )(keep, from_core, from_y, own_t, cot, stats, gain, bias, *before)


def flip(value, axis, size, bit):
    return lax.ppermute(value, axis, [(i, i ^ bit) for i in range(size)])


def tie(*trees):
    return lax.optimization_barrier(trees)


def joined(swap, held, arrived):
    return jnp.where(
        swap, jnp.concatenate([arrived, held], axis=0), jnp.concatenate([held, arrived], axis=0)
    )


def piece_order(size):
    bits = size.bit_length() - 1
    return [sum(((i >> b) & 1) << (bits - 1 - b) for b in range(bits)) for i in range(size)]


class SumOverDp:
    def __init__(self, value, size, index):
        self.size, self.index = size, index
        self.send = value
        self.steps = ["sum"] + [1 << i for i in reversed(range(size.bit_length() - 1))]

    def more(self):
        return bool(self.steps)

    def move(self, send):
        if self.steps[0] == "sum":
            return lax.all_to_all(send, "dp", 0, 0, tiled=True)
        return flip(send, "dp", self.size, self.steps[0])

    def take(self, arrived):
        step = self.steps.pop(0)
        if step == "sum":
            shares = arrived.reshape(self.size, -1, arrived.shape[1]).astype(F32)
            self.keep = jnp.sum(shares, axis=0).astype(BF16)
        else:
            self.last = ((self.index & step) > 0, self.keep, arrived)
            self.keep = joined(*self.last)
        self.send = self.keep


class ChainOverDp:
    def __init__(self, value, size, index):
        self.size, self.index = size, index
        bits = [1 << i for i in range(size.bit_length() - 1)]
        self.steps = [("sum", bit) for bit in bits] + [("join", bit) for bit in reversed(bits)]
        self.prepare(value, None)

    def prepare(self, held, arrived):
        def part(which, half):
            rows = lax.dynamic_slice_in_dim(held, which * half, half, 0)
            if arrived is None:
                return rows
            came = lax.dynamic_slice_in_dim(arrived, which * half, half, 0)
            return (rows.astype(F32) + came.astype(F32)).astype(BF16)

        rows = held.shape[0]
        if self.steps and self.steps[0][0] == "sum":
            side = ((self.index & self.steps[0][1]) > 0).astype(jnp.int32)
            self.send, self.keep = part(1 - side, rows // 2), part(side, rows // 2)
        else:
            self.keep = part(0, rows)
            self.send = self.keep

    def more(self):
        return bool(self.steps)

    def move(self, send):
        return flip(send, "dp", self.size, self.steps[0][1])

    def take(self, arrived):
        kind, bit = self.steps.pop(0)
        if kind == "sum":
            self.prepare(self.keep, arrived)
            return
        self.last = ((self.index & bit) > 0, self.keep, arrived)
        self.keep = self.send = joined(*self.last)


class ScatterOverMp:
    def __init__(self, keep, send):
        self.keep, self.send = keep, send
        self.bits = [1, 2]

    def more(self):
        return bool(self.bits)

    def move(self, send):
        return flip(send, "mp", 4, self.bits[0])

    def take(self, arrived):
        bit = self.bits.pop(0)
        if bit == 1:
            self.from_core = arrived
            self.send = (self.keep[:, 1:].astype(F32) + arrived[:, 1:].astype(F32)).astype(BF16)
        else:
            self.from_y = arrived


def land_in_turn(phases, outputs):
    movers = []
    for flights in phases:
        outputs, sends, arrivals = tie(outputs, [m.send for m in movers], [f[1] for f in flights])
        for mover, send in zip(movers, sends):
            mover.send = send
        for (mover, _), arrived in zip(flights, arrivals):
            mover.take(arrived)
        movers += [f[0] for f in flights]
    return outputs


class ShortSums:
    def __init__(self, keep, send, rest, size):
        self.keep, self.send, self.rest, self.size = keep, send, rest, size
        self.steps = [("mp", 1), ("mp", 2)] + [("dp", 1 << i) for i in range(size.bit_length() - 1)]

    def more(self):
        return bool(self.steps)

    def move(self, send):
        axis, bit = self.steps[0]
        return flip(send, axis, 4 if axis == "mp" else self.size, bit)

    def take(self, arrived):
        axis, bit = self.steps.pop(0)
        if (axis, bit) == ("mp", 1):
            both = self.keep + arrived
            self.norm, self.send = both[0], both[1]
            return
        if axis == "mp":
            self.send = jnp.concatenate([self.norm + arrived, self.rest])
        else:
            self.send = self.send + arrived
        size = self.norm.shape[0]
        self.norm, self.rest = self.send[:size], self.send[size:]


def launch(movers, inputs):
    movers = [m for m in movers if m.more()]
    inputs, sends = tie(inputs, [m.send for m in movers])
    return inputs, [(m, m.move(s)) for m, s in zip(movers, sends)]


def land(flights, outputs):
    outputs, arrivals = tie(outputs, [f[1] for f in flights])
    for (mover, _), arrived in zip(flights, arrivals):
        mover.take(arrived)
    return outputs


def body(
    dp_size,
    tokens,
    image_ids,
    norm_gain,
    qkv_weight,
    qk_gain,
    attn_weight,
    up_weight,
    up_bias,
    down_weight,
    down_bias,
    cotangent,
):
    part = tokens.shape[1]
    width = cotangent.shape[1]
    seqs = image_ids.shape[0]
    me = lax.axis_index("mp")
    dp = lax.axis_index("dp")
    shard = me.astype(jnp.int32)[None]
    place = jnp.bitwise_xor(shard, jnp.array([0, 2, 1, 3], jnp.int32)) * part

    own_t = tokens.T
    from_y = flip(own_t, "mp", 4, 2)
    gain_own = jnp.broadcast_to(norm_gain[:, None], (part, 128))
    gain_y = flip(gain_own, "mp", 4, 2)
    gain_c = flip(gain_own, "mp", 4, 1)

    mixed_t = jnp.transpose(qkv_weight, (1, 2, 0)).reshape(3 * part, width)
    def column(vector):
        return jnp.broadcast_to(vector[:, None], (vector.shape[0], 128))

    columns = (column(up_bias), column(qk_gain.astype(F32).reshape(2 * part)), column(down_bias))

    slots = jnp.arange(IMAGE_SLOTS, dtype=jnp.int32)[None, :, None]
    same = image_ids[:, None, :] == slots
    mask_q = same.astype(BF16)
    mask_k = jnp.where(same | (slots >= 8), 0.0, -PENALTY).astype(BF16)
    block_first = image_ids[:, ::BI]
    block_last = image_ids[:, BI - 1 :: BI]
    starts = jnp.sum(image_ids[:, None, :] < block_first[:, :, None], axis=2, dtype=jnp.int32)
    ends = jnp.sum(image_ids[:, None, :] <= block_last[:, :, None], axis=2, dtype=jnp.int32)
    first = starts // 128
    count = ((ends + 127) // 128 - first).reshape(-1)
    first = first.reshape(-1)

    pick = (jnp.arange(part)[:, None] + me * part == jnp.arange(width)[None, :]).astype(BF16)
    pick, place, columns, (gain_y, gain_c) = tie(pick, place, columns, (gain_y, gain_c))
    up_bias_col, head_gains, bias_col = columns
    gain_cy = flip(gain_y, "mp", 4, 1)
    d_act, d_att, cot_own, cot_sum = early_call(cotangent, down_weight, attn_weight, pick)
    prepared = (
        d_act, d_att, mixed_t, up_bias_col, head_gains, mask_q, mask_k, first, count,
        bias_col,
    )
    prepared, (from_y, gain_cy) = tie(prepared, (from_y, gain_cy))
    gains = (gain_own, gain_y, gain_c, gain_cy)
    (
        d_act, d_att, mixed_t, up_bias_col, head_gains, mask_q, mask_k, first, count,
        bias_col,
    ) = prepared
    pieces = (own_t, from_y, flip(own_t, "mp", 4, 1), flip(from_y, "mp", 4, 1))
    normed, active, d_pre, stats, upbias_part, gain_all, up_row, mlp_part = mlp_call(
        tuple(piece_order(dp_size)), place, pieces, gains, up_weight, up_bias_col, d_act, cotangent
    )
    mlp_sum = SumOverDp(mlp_part, dp_size, dp)

    (states,), flying = launch([mlp_sum], (normed,))
    attended, d_mixed, qk_part, norm_row, mix_part = attention_call(
        first, count, states, mixed_t, d_att, mask_q, mask_k, head_gains, cotangent
    )
    mix_sum = ChainOverDp(mix_part, dp_size, dp)

    norm_vec = norm_row[0] + jnp.sum(up_row, axis=1)
    norm_parts = norm_vec.reshape(4, part)
    norm_parts = [lax.dynamic_index_in_dim(norm_parts, jnp.bitwise_xor(me, m), 0, False) for m in range(4)]
    short = ShortSums(
        jnp.stack([norm_parts[0], norm_parts[2]]),
        jnp.stack([norm_parts[1], norm_parts[3]]),
        jnp.concatenate([jnp.sum(qk_part, axis=1), jnp.sum(upbias_part, axis=1), jnp.sum(cot_sum, axis=1)]),
        dp_size,
    )

    runs = [(seq, 1) for seq in range(seqs)]
    scatters = []
    for begin, size in runs:
        busy = [f[0] for f in flying]
        along = [m for m in [mix_sum, mlp_sum, short] + scatters if m.more() and m not in busy]
        (att, dm), flights = launch(along, (attended, d_mixed))
        flying = flying + flights
        sent = project_call(
            shard, active, att, d_pre, dm, normed, down_weight, attn_weight, up_weight, mixed_t, gain_all, begin, size
        )
        final = seqs - 1
        late = [f for f in flights if begin == 0 and f[0] is mix_sum or begin == final and f[0] is scatters[0]]
        wide = [f for f in flying if f[0] is mlp_sum]
        chain = [f for f in flying if f[0] is mix_sum and f not in late]
        quick = [f for f in flying if f not in late + wide + chain]
        keep, send = land_in_turn([quick, wide, chain], sent)
        if begin == final and begin > 0:
            _, ahead = launch([mix_sum], ())
            (keep, send), *_ = (land(late, (keep, send)),)
            late = ahead
        flying = late
        scatters.append(ScatterOverMp(keep, send))

    finished = ()
    wide_grads = ()
    done = set()

    def finish_ready(finished):
        for (begin, _), scatter in zip(runs, scatters):
            if not scatter.more() and begin not in done:
                done.add(begin)
                finished = finish_call(
                    scatter.keep, scatter.from_core, scatter.from_y, own_t, cot_own, stats, gain_own, bias_col,
                    finished, begin,
                )
        return finished

    while True:
        busy = [f[0] for f in flying]
        ready = [m for m in [mix_sum] + scatters + [short, mlp_sum] if m.more() and m not in busy]
        finished, flights = launch(ready, finished)
        flying = flying + flights
        if not flying:
            break
        finished = finish_ready(finished)
        near = [f for f in flying if f[0] in scatters and len(f[0].bits) == 2]
        across = [f for f in flying if f[0] in scatters and len(f[0].bits) == 1]
        chain = [f for f in flying if f[0] is mix_sum]
        rest = [f for f in flying if f[0] is short]
        wide = [f for f in flying if f[0] is mlp_sum]
        left = len(mix_sum.steps)
        if near:
            now = near + chain + rest
        elif left == 2:
            now = chain + across[:1] + rest
        elif left == 1:
            now = wide + rest or across[:1] or chain
        else:
            now = chain + rest or flying
        final = [f for f in now if f[0] is mix_sum]
        phases = [[f for f in now if f not in final], final]
        finished, wide_grads = land_in_turn(phases[::-1] if near else phases, (finished, wide_grads))
        flying = [f for f in flying if f not in now]
        if not mlp_sum.more() and not wide_grads:
            swap, held, arrived = mlp_sum.last
            wide_grads = (
                jnp.where(swap, arrived, held).astype(F32),
                jnp.where(swap, held, arrived).astype(F32),
            )
    finished = finish_ready(finished)
    block_out, token_grad = finished
    block_out, token_grad = block_out.T, token_grad.T
    swap, held, arrived = mix_sum.last
    left = 3 * part - held.shape[0]
    qkv_rows = joined(swap, held, arrived)[: 3 * part].astype(F32)
    attn_grad = jnp.where(swap, held[left:], arrived[left:]).astype(F32)
    qkv_grad = jnp.transpose(qkv_rows.reshape(3, part, width), (2, 0, 1))

    gain_grad = short.norm / norm_gain.astype(F32)
    rest = short.rest
    split = 2 * part + up_weight.shape[1]
    return (
        block_out,
        token_grad,
        gain_grad,
        qkv_grad,
        rest[: 2 * part].reshape(2, part),
        attn_grad,
        wide_grads[1],
        rest[2 * part : split],
        wide_grads[0],
        rest[split:],
    )


def solution(mesh):
    in_specs = (
        P("dp", "mp"),
        P("dp", None),
        P("mp"),
        P(None, None, "mp"),
        P(None, "mp"),
        P("mp", None),
        P(None, "mp"),
        P("mp"),
        P("mp", None),
        P("mp"),
        P("dp", None),
    )
    out_specs = (
        P("dp", "mp"),
        P("dp", "mp"),
        P("mp"),
        P(None, None, "mp"),
        P(None, "mp"),
        P("mp", None),
        P(None, "mp"),
        P("mp"),
        P("mp", None),
        P("mp"),
    )
    run = functools.partial(body, mesh.shape["dp"])
    return jax.shard_map(run, mesh=mesh, in_specs=in_specs, out_specs=out_specs, check_vma=False)
```

```python
import functools

import jax
import jax.numpy as jnp
from jax import lax
from jax.experimental import pallas as pl
from jax.experimental.pallas import tpu as pltpu
from jax.sharding import PartitionSpec as P

DH = 64
LEN = 1024
EPSILON = 1e-06
IMAGE_SLOTS = 16
PENALTY = 1024.0
BI = 256
BJ = 256
SUM_ROWS = 16
F32 = jnp.float32
BF16 = jnp.bfloat16

NN = (((1,), (0,)), ((), ()))
NT = (((1,), (1,)), ((), ()))
TN = (((0,), (0,)), ((), ()))
ANY = pl.BlockSpec(memory_space=pl.ANY)


def dot(left, right, dims=NN):
    return lax.dot_general(left, right, dims, preferred_element_type=F32)


def fold_lanes(rows):
    total = rows[:, :128]
    for start in range(128, rows.shape[1], 128):
        total = total + rows[:, start : start + 128]
    return total


def cost(microseconds, nbytes):
    return pl.CostEstimate(flops=int(microseconds * 1e3), bytes_accessed=nbytes // 1000, transcendentals=0)


def early_kernel(cot, down, attn, pick, d_act, d_att, cot_own, bias_sum):
    rows = cot[...]
    d_act[...] = dot(down[...], rows, NT).astype(BF16)
    d_att[...] = dot(attn[...], rows, NT).astype(BF16)
    own = dot(pick[...], rows, NT)
    cot_own[...] = own.astype(BF16)

    @pl.when(pl.program_id(0) == 0)
    def _():
        bias_sum[...] = jnp.zeros_like(bias_sum)

    bias_sum[...] += fold_lanes(own)


def early_call(cot, down, attn, pick, block=512):
    tokens, width = cot.shape
    seqs = tokens // LEN
    hidden, part = down.shape[0], attn.shape[0]
    steps = LEN // block
    fixed = lambda i: (0, 0)
    by_seq = lambda i: (i // steps, 0, i % steps)
    return pl.pallas_call(
        early_kernel,
        grid=(tokens // block,),
        in_specs=[
            pl.BlockSpec((block, width), lambda i: (i, 0)),
            pl.BlockSpec((hidden, width), fixed),
            pl.BlockSpec((part, width), fixed),
            pl.BlockSpec((part, width), fixed),
        ],
        out_specs=[
            pl.BlockSpec((None, hidden, block), by_seq),
            pl.BlockSpec((None, part, block), by_seq),
            pl.BlockSpec((part, block), lambda i: (0, i)),
            pl.BlockSpec((part, 128), fixed),
        ],
        out_shape=[
            jax.ShapeDtypeStruct((seqs, hidden, LEN), BF16),
            jax.ShapeDtypeStruct((seqs, part, LEN), BF16),
            jax.ShapeDtypeStruct((part, tokens), BF16),
            jax.ShapeDtypeStruct((part, 128), F32),
        ],
        cost_estimate=cost(10, 12_000_000),
        name="early",
    )(cot, down, attn, pick)


def mlp_kernel(
    pieces_order, place, own, flip_y, flip_c, flip_cy, gain_own, gain_y, gain_c, gain_cy, up, up_bias, d_act, cot,
    normed, active, d_pre, stats, bias_sum, gain_all, up_row, grads, low, high
):
    pieces = (own, flip_y, flip_c, flip_cy)
    part = own.shape[0]
    width = part * 4
    first = pl.program_id(0) == 0
    last = pl.program_id(0) == pl.num_programs(0) - 1

    @pl.when(first)
    def _():
        bias_sum[...] = jnp.zeros_like(bias_sum)
        low[...] = jnp.zeros_like(low)
        high[...] = jnp.zeros_like(high)
        for slot, piece in enumerate((gain_own, gain_y, gain_c, gain_cy)):
            gain_all[pl.ds(pl.multiple_of(place[slot], part), part), :] = piece[...].astype(F32)

    total = 0.0
    squares = 0.0
    for piece in pieces:
        rows = piece[...].astype(F32)
        total = total + jnp.sum(rows, axis=0, keepdims=True)
        squares = squares + jnp.sum(rows * rows, axis=0, keepdims=True)
    mean = total * (1.0 / width)
    scale = lax.rsqrt(squares * (1.0 / width) - mean * mean + EPSILON)
    stats[0:1, :] = mean
    stats[1:2, :] = scale
    stats[2:8, :] = jnp.zeros((6, stats.shape[1]), F32)
    for slot, piece in enumerate(pieces):
        rows = piece[...].astype(F32)
        here = pl.ds(pl.multiple_of(place[slot], part), part)
        normed[here, :] = ((rows - mean) * scale * gain_all[here, :1]).astype(BF16)

    c0 = 0.7978845608028654
    c1 = 0.044715 * c0
    def lift(start):
        here = slice(start, start + 256)
        return dot(up[:, here], normed[...], TN) + up_bias[here, :1].astype(F32)

    ahead = lift(0)
    for start in range(0, up.shape[1], 256):
        here = slice(start, start + 256)
        pre = ahead
        if start + 256 < up.shape[1]:
            ahead = lift(start + 256)
        square = pre * pre
        half = 0.5 * jnp.tanh(pre * (c0 + c1 * square)) + 0.5
        act = (pre * half).astype(BF16)
        active[here, :] = act
        slope = half + pre * (half - half * half) * (2.0 * c0 + 6.0 * c1 * square)
        grad = (d_act[here, :].astype(F32) * slope).astype(BF16)
        d_pre[here, :] = grad
        bias_sum[here, :] += fold_lanes(grad.astype(F32))
        low[here, :] += dot(act, cot[...])
        high[:, here] += dot(normed[...], grad, NT)

    @pl.when(last)
    def _():
        up_row[...] = fold_lanes(high[...] * up[...].astype(F32))
        half = low.shape[0]
        size = grads.shape[0] // len(pieces_order)
        for slot, piece in enumerate(pieces_order):
            source, start = (low, piece * size) if piece * size < half else (high, piece * size - half)
            grads[slot * size : (slot + 1) * size, :] = source[start : start + size, :].astype(BF16)


def mlp_call(pieces_order, place, pieces, gains, up, up_bias, d_act, cot, block=512):
    part, tokens = pieces[0].shape
    width = 4 * part
    seqs, hidden, _ = d_act.shape
    steps = LEN // block
    lanes = lambda i, *_: (0, i)
    by_seq = lambda i, *_: (i // steps, 0, i % steps)
    fixed = lambda i, *_: (0, 0)
    grid_spec = pltpu.PrefetchScalarGridSpec(
        num_scalar_prefetch=1,
        grid=(tokens // block,),
        in_specs=[pl.BlockSpec((part, block), lanes)] * 4
        + [pl.BlockSpec((part, 128), fixed)] * 4
        + [
            pl.BlockSpec((width, hidden), fixed),
            pl.BlockSpec((hidden, 128), fixed),
            pl.BlockSpec((None, hidden, block), by_seq),
            pl.BlockSpec((block, width), lambda i, *_: (i, 0)),
        ],
        out_specs=[
            pl.BlockSpec((None, width, block), by_seq),
            pl.BlockSpec((None, hidden, block), by_seq),
            pl.BlockSpec((None, hidden, block), by_seq),
            pl.BlockSpec((8, block), lanes),
            pl.BlockSpec((hidden, 128), fixed),
            pl.BlockSpec((width, 128), fixed),
            pl.BlockSpec((width, 128), fixed),
            pl.BlockSpec((hidden + width, width), fixed),
        ],
        scratch_shapes=[pltpu.VMEM((hidden, width), F32), pltpu.VMEM((width, hidden), F32)],
    )
    assert hidden == width
    return pl.pallas_call(
        functools.partial(mlp_kernel, pieces_order),
        grid_spec=grid_spec,
        out_shape=[
            jax.ShapeDtypeStruct((seqs, width, LEN), BF16),
            jax.ShapeDtypeStruct((seqs, hidden, LEN), BF16),
            jax.ShapeDtypeStruct((seqs, hidden, LEN), BF16),
            jax.ShapeDtypeStruct((8, tokens), F32),
            jax.ShapeDtypeStruct((hidden, 128), F32),
            jax.ShapeDtypeStruct((width, 128), F32),
            jax.ShapeDtypeStruct((width, 128), F32),
            jax.ShapeDtypeStruct((hidden + width, width), BF16),
        ],
        cost_estimate=cost(20, 30_000_000),
        name="mlp",
    )(place, *pieces, *gains, up, up_bias, d_act, cot)


def attention_kernel(
    first, count, normed, mixed_t, d_att, mask_q, mask_k, gains, cot, attended, d_mixed, gain_sum, norm_row, grads,
    total, qkv, qx, kx, vn, kt, vt, es, ps, dqa, dka, dva
):
    seq = pl.program_id(0)
    last = seq == pl.num_programs(0) - 1
    part = attended.shape[0]
    heads = part // DH
    inv_dh = 1.0 / DH

    @pl.when(seq == 0)
    def _():
        total[...] = jnp.zeros_like(total)
        gain_sum[...] = jnp.zeros_like(gain_sum)

    qkv[...] = dot(mixed_t[...], normed[...])

    def unit(start):
        raw = qkv[start : start + DH, :]
        shifted = raw - jnp.sum(raw, axis=0, keepdims=True) * inv_dh
        scale = lax.rsqrt(jnp.sum(shifted * shifted, axis=0, keepdims=True) * inv_dh + EPSILON)
        return shifted * scale, scale

    zeros = jnp.zeros((128 - DH - IMAGE_SLOTS, LEN), BF16)
    for head in range(heads):
        rows = slice(head * DH, (head + 1) * DH)
        query, _ = unit(head * DH)
        query = (query * (gains[rows, :1] * 0.125)).astype(BF16)
        qx[head] = jnp.concatenate([query, mask_q[...], zeros], axis=0)
        key, _ = unit(part + head * DH)
        key = (key * gains[part + head * DH : part + (head + 1) * DH, :1]).astype(BF16)
        kt[rows, :] = key
        kx[head] = jnp.concatenate([key, mask_k[...], zeros], axis=0).T
        value = qkv[2 * part + head * DH : 2 * part + (head + 1) * DH, :].astype(BF16)
        vt[rows, :] = value
        vn[head] = value.T
    dka[...] = jnp.zeros_like(dka)
    dva[...] = jnp.zeros_like(dva)

    def straight(units, i0, base):
        icols = pl.ds(i0, BI)
        edges = [(at, min(BJ, units * 128 - at)) for at in range(0, units * 128, BJ)]
        trips = len(edges)
        spots = [slice(at, at + size) for at, size in edges]
        places = [pl.ds(pl.multiple_of(base + at, 128), size) for at, size in edges]

        def scores(head, j, sums):
            rows = slice(head * DH, (head + 1) * DH)
            e = jnp.exp(dot(kx[head, places[j], :], qx[head, :, icols]))
            p = dot(vn[head, places[j], :], d_att[rows, icols])
            es[head % 2, spots[j], :] = e
            ps[head % 2, spots[j], :] = p
            more = (jnp.sum(e, axis=0, keepdims=True), jnp.sum(e * p, axis=0, keepdims=True))
            return more if sums is None else (sums[0] + more[0], sums[1] + more[1])

        def row_grads(head, j, inverse, inner, held):
            rows = slice(head * DH, (head + 1) * DH)
            w = es[head % 2, spots[j], :] * inverse
            d = (w * (ps[head % 2, spots[j], :] - inner)).astype(BF16)
            w = w.astype(BF16)
            out = dot(vt[rows, places[j]], w)
            query = dot(kt[rows, places[j]], d)
            dva[rows, places[j]] += dot(d_att[rows, icols], w, NT)
            dka[rows, places[j]] += dot(qx[head, :DH, icols], d, NT)
            return (out, query) if held is None else (held[0] + out, held[1] + query)

        sums = None
        for j in range(trips):
            sums = scores(0, j, sums)
        for head in range(heads):
            rows = slice(head * DH, (head + 1) * DH)
            inverse = 1.0 / sums[0]
            inner = sums[1] * inverse
            held = following = None
            for j in range(trips):
                if head + 1 < heads:
                    following = scores(head + 1, j, following)
                held = row_grads(head, j, inverse, inner, held)
            attended[rows, icols] = held[0].astype(BF16)
            dqa[rows, icols] = held[1]
            sums = following

    def query_block(ib, _):
        i0 = pl.multiple_of(ib * BI, BI)
        base = first[seq * (LEN // BI) + ib] * 128
        trips = count[seq * (LEN // BI) + ib]
        for number in range(BI // 128, LEN // 128 + 1):
            pl.when(trips == number)(functools.partial(straight, number, i0, base))
        return 0

    lax.fori_loop(0, LEN // BI, query_block, 0)

    for source, offset, factor in ((dqa, 0, 0.125), (dka, part, 1.0)):
        for head in range(heads):
            start = offset + head * DH
            u, scale = unit(start)
            e = source[head * DH : (head + 1) * DH, :] * factor
            gain_sum[start : start + DH, :] += fold_lanes(e * u)
            f = e * gains[start : start + DH, :1]
            mean_f = jnp.sum(f, axis=0, keepdims=True) * inv_dh
            mean_fu = jnp.sum(f * u, axis=0, keepdims=True) * inv_dh
            d_mixed[start : start + DH, :] = ((f - mean_f - u * mean_fu) * scale).astype(BF16)
    d_mixed[2 * part :, :] = dva[...].astype(BF16)

    split = 3 * part
    total[:split, :] += dot(d_mixed[...], normed[...], NT)
    total[split:, :] += dot(attended[...], cot[...])

    @pl.when(last)
    def _():
        norm_row[...] = jnp.sum(total[:split, :] * mixed_t[...].astype(F32), axis=0, keepdims=True)
        grads[...] = total[...].astype(BF16)


def attention_call(first, count, normed, mixed_t, d_att, mask_q, mask_k, gains, cot):
    seqs, part, _ = d_att.shape
    width = normed.shape[1]
    heads = part // DH
    fixed = lambda i, *_: (0, 0)
    by_seq = lambda i, *_: (i, 0, 0)
    grid_spec = pltpu.PrefetchScalarGridSpec(
        num_scalar_prefetch=2,
        grid=(seqs,),
        in_specs=[
            pl.BlockSpec((None, width, LEN), by_seq),
            pl.BlockSpec((3 * part, width), fixed),
            pl.BlockSpec((None, part, LEN), by_seq),
            pl.BlockSpec((None, IMAGE_SLOTS, LEN), by_seq),
            pl.BlockSpec((None, IMAGE_SLOTS, LEN), by_seq),
            pl.BlockSpec((2 * part, 128), fixed),
            pl.BlockSpec((LEN, width), lambda i, *_: (i, 0)),
        ],
        out_specs=[
            pl.BlockSpec((None, part, LEN), by_seq),
            pl.BlockSpec((None, 3 * part, LEN), by_seq),
            pl.BlockSpec((2 * part, 128), fixed),
            pl.BlockSpec((1, width), fixed),
            pl.BlockSpec((4 * part, width), fixed),
        ],
        scratch_shapes=[
            pltpu.VMEM((4 * part, width), F32),
            pltpu.VMEM((3 * part, LEN), F32),
            pltpu.VMEM((heads, 128, LEN), BF16),
            pltpu.VMEM((heads, LEN, 128), BF16),
            pltpu.VMEM((heads, LEN, DH), BF16),
            pltpu.VMEM((part, LEN), BF16),
            pltpu.VMEM((part, LEN), BF16),
            pltpu.VMEM((2, LEN, BI), F32),
            pltpu.VMEM((2, LEN, BI), F32),
            pltpu.VMEM((part, LEN), F32),
            pltpu.VMEM((part, LEN), F32),
            pltpu.VMEM((part, LEN), F32),
        ],
    )
    return pl.pallas_call(
        attention_kernel,
        grid_spec=grid_spec,
        out_shape=[
            jax.ShapeDtypeStruct((seqs, part, LEN), BF16),
            jax.ShapeDtypeStruct((seqs, 3 * part, LEN), BF16),
            jax.ShapeDtypeStruct((2 * part, 128), F32),
            jax.ShapeDtypeStruct((1, width), F32),
            jax.ShapeDtypeStruct((4 * part, width), BF16),
        ],
        cost_estimate=cost(18, 5_000_000),
        name="attention",
    )(first, count, normed, mixed_t, d_att, mask_q, mask_k, gains, cot)


def project_kernel(
    shard, active, attended, d_pre, d_mixed, normed, down, attn, up, mixed_t, gain, keep, send
):
    me = shard[0]
    part = attended.shape[0]
    out = dot(down[...], active[...], TN) + dot(attn[...], attended[...], TN)
    grad = dot(up[...], d_pre[...]) + dot(mixed_t[...], d_mixed[...], TN)
    product = grad * normed[...].astype(F32)
    sums = []
    for row in (jnp.sum(grad * gain[:, :1], axis=0, keepdims=True), jnp.sum(product, axis=0, keepdims=True)):
        high = row.astype(BF16)
        sums += [high, (row - high.astype(F32)).astype(BF16)]
    sums = jnp.concatenate(sums + [jnp.zeros((SUM_ROWS - 4, sums[0].shape[1]), BF16)], axis=0)
    for target in (keep, send):
        for slot in range(2):
            target[slot, 2 * part :, :] = sums
    for index in range(4):
        rows = slice(index * part, (index + 1) * part)
        away = jnp.bitwise_xor(me, index)
        slot = away // 2

        @pl.when(away % 2 == 0)
        def _():
            keep[slot, :part, :] = out[rows].astype(BF16)
            keep[slot, part : 2 * part, :] = grad[rows].astype(BF16)

        @pl.when(away % 2 == 1)
        def _():
            send[slot, :part, :] = out[rows].astype(BF16)
            send[slot, part : 2 * part, :] = grad[rows].astype(BF16)


def project_call(shard, active, attended, d_pre, d_mixed, normed, down, attn, up, mixed_t, gain, begin, size, block=256):
    hidden, width = down.shape
    part = attended.shape[1]
    steps = LEN // block
    ours = lambda i, *_: (begin + i // steps, 0, i % steps)
    out = lambda i, *_: (i // steps, 0, 0, i % steps)
    fixed = lambda i, *_: (0, 0)
    rows = 2 * part + SUM_ROWS
    grid_spec = pltpu.PrefetchScalarGridSpec(
        num_scalar_prefetch=1,
        grid=(size * steps,),
        in_specs=[
            pl.BlockSpec((None, hidden, block), ours),
            pl.BlockSpec((None, part, block), ours),
            pl.BlockSpec((None, hidden, block), ours),
            pl.BlockSpec((None, 3 * part, block), ours),
            pl.BlockSpec((None, width, block), ours),
            pl.BlockSpec((hidden, width), fixed),
            pl.BlockSpec((part, width), fixed),
            pl.BlockSpec((width, hidden), fixed),
            pl.BlockSpec((3 * part, width), fixed),
            pl.BlockSpec((width, 128), fixed),
        ],
        out_specs=[
            pl.BlockSpec((None, 2, rows, block), out),
            pl.BlockSpec((None, 2, rows, block), out),
        ],
    )
    return pl.pallas_call(
        project_kernel,
        grid_spec=grid_spec,
        out_shape=[
            jax.ShapeDtypeStruct((size, 2, rows, LEN), BF16),
            jax.ShapeDtypeStruct((size, 2, rows, LEN), BF16),
        ],
        cost_estimate=cost(8, 16_000_000),
        name="project",
    )(shard, active, attended, d_pre, d_mixed, normed, down, attn, up, mixed_t, gain)


def finish_kernel(keep, from_core, from_y, own_t, cot, stats, gain, bias, *rest):
    block_out, token_grad = rest[-2:]
    part = own_t.shape[0]
    inv_width = 0.25 / part
    total = keep[...].astype(F32) + from_core[...].astype(F32) + from_y[...].astype(F32)
    own = own_t[...].astype(F32)
    block_out[...] = (own + total[:part] + bias[:, :1].astype(F32)).astype(BF16)
    grad = total[part : 2 * part]
    sums = total[2 * part :]
    mean = stats[0:1, :]
    scale = stats[1:2, :]
    hat = (own - mean) * scale
    inner = grad * gain[:, :1].astype(F32) - (sums[0:1] + sums[1:2]) * inv_width - hat * ((sums[2:3] + sums[3:4]) * inv_width)
    token_grad[...] = cot[...].astype(F32) + inner * scale


def finish_call(keep, from_core, from_y, own_t, cot, stats, gain, bias, before, begin, block=512):
    part, tokens = own_t.shape
    steps = LEN // block
    size = keep.shape[0]
    fixed = lambda i: (0, 0)
    packed = pl.BlockSpec((None, None, 2 * part + SUM_ROWS, block), lambda i: (i // steps, 0, 0, i % steps))
    ours = lambda i: (0, begin * steps + i)
    here = pl.BlockSpec((part, block), ours)
    return pl.pallas_call(
        finish_kernel,
        grid=(size * steps,),
        in_specs=[
            packed, packed, packed,
            here, here,
            pl.BlockSpec((8, block), ours),
            pl.BlockSpec((part, 128), fixed),
            pl.BlockSpec((part, 128), fixed),
        ]
        + [ANY] * len(before),
        out_specs=[here, here],
        out_shape=[
            jax.ShapeDtypeStruct((part, tokens), BF16),
            jax.ShapeDtypeStruct((part, tokens), F32),
        ],
        input_output_aliases={8 + i: i for i in range(len(before))},
        cost_estimate=cost(3, 5_000_000),
        name="finish",
    )(keep, from_core, from_y, own_t, cot, stats, gain, bias, *before)


def flip(value, axis, size, bit):
    return lax.ppermute(value, axis, [(i, i ^ bit) for i in range(size)])


def tie(*trees):
    return lax.optimization_barrier(trees)


def joined(swap, held, arrived):
    return jnp.where(
        swap, jnp.concatenate([arrived, held], axis=0), jnp.concatenate([held, arrived], axis=0)
    )


def piece_order(size):
    bits = size.bit_length() - 1
    return [sum(((i >> b) & 1) << (bits - 1 - b) for b in range(bits)) for i in range(size)]


class SumOverDp:
    def __init__(self, value, size, index):
        self.size, self.index = size, index
        self.send = value
        self.steps = ["sum"] + [1 << i for i in reversed(range(size.bit_length() - 1))]

    def more(self):
        return bool(self.steps)

    def move(self, send):
        if self.steps[0] == "sum":
            return lax.all_to_all(send, "dp", 0, 0, tiled=True)
        return flip(send, "dp", self.size, self.steps[0])

    def take(self, arrived):
        step = self.steps.pop(0)
        if step == "sum":
            shares = arrived.reshape(self.size, -1, arrived.shape[1]).astype(F32)
            self.keep = jnp.sum(shares, axis=0).astype(BF16)
        else:
            self.last = ((self.index & step) > 0, self.keep, arrived)
            self.keep = joined(*self.last)
        self.send = self.keep


class ChainOverDp:
    def __init__(self, value, size, index):
        self.size, self.index = size, index
        bits = [1 << i for i in range(size.bit_length() - 1)]
        self.steps = [("sum", bit) for bit in bits] + [("join", bit) for bit in reversed(bits)]
        self.prepare(value, None)

    def prepare(self, held, arrived):
        def part(which, half):
            rows = lax.dynamic_slice_in_dim(held, which * half, half, 0)
            if arrived is None:
                return rows
            came = lax.dynamic_slice_in_dim(arrived, which * half, half, 0)
            return (rows.astype(F32) + came.astype(F32)).astype(BF16)

        rows = held.shape[0]
        if self.steps and self.steps[0][0] == "sum":
            side = ((self.index & self.steps[0][1]) > 0).astype(jnp.int32)
            self.send, self.keep = part(1 - side, rows // 2), part(side, rows // 2)
        else:
            self.keep = part(0, rows)
            self.send = self.keep

    def more(self):
        return bool(self.steps)

    def move(self, send):
        return flip(send, "dp", self.size, self.steps[0][1])

    def take(self, arrived):
        kind, bit = self.steps.pop(0)
        if kind == "sum":
            self.prepare(self.keep, arrived)
            return
        self.last = ((self.index & bit) > 0, self.keep, arrived)
        self.keep = self.send = joined(*self.last)


class ScatterOverMp:
    def __init__(self, keep, send):
        self.keep, self.send = keep, send
        self.bits = [1, 2]

    def more(self):
        return bool(self.bits)

    def move(self, send):
        return flip(send, "mp", 4, self.bits[0])

    def take(self, arrived):
        bit = self.bits.pop(0)
        if bit == 1:
            self.from_core = arrived
            self.send = (self.keep[:, 1:].astype(F32) + arrived[:, 1:].astype(F32)).astype(BF16)
        else:
            self.from_y = arrived


def land_in_turn(phases, outputs):
    movers = []
    for flights in phases:
        outputs, sends, arrivals = tie(outputs, [m.send for m in movers], [f[1] for f in flights])
        for mover, send in zip(movers, sends):
            mover.send = send
        for (mover, _), arrived in zip(flights, arrivals):
            mover.take(arrived)
        movers += [f[0] for f in flights]
    return outputs


class ShortSums:
    def __init__(self, keep, send, rest, size):
        self.keep, self.send, self.rest, self.size = keep, send, rest, size
        self.steps = [("mp", 1), ("mp", 2)] + [("dp", 1 << i) for i in range(size.bit_length() - 1)]

    def more(self):
        return bool(self.steps)

    def move(self, send):
        axis, bit = self.steps[0]
        return flip(send, axis, 4 if axis == "mp" else self.size, bit)

    def take(self, arrived):
        axis, bit = self.steps.pop(0)
        if (axis, bit) == ("mp", 1):
            both = self.keep + arrived
            self.norm, self.send = both[0], both[1]
            return
        if axis == "mp":
            self.send = jnp.concatenate([self.norm + arrived, self.rest])
        else:
            self.send = self.send + arrived
        size = self.norm.shape[0]
        self.norm, self.rest = self.send[:size], self.send[size:]


def launch(movers, inputs):
    movers = [m for m in movers if m.more()]
    inputs, sends = tie(inputs, [m.send for m in movers])
    return inputs, [(m, m.move(s)) for m, s in zip(movers, sends)]


def land(flights, outputs):
    outputs, arrivals = tie(outputs, [f[1] for f in flights])
    for (mover, _), arrived in zip(flights, arrivals):
        mover.take(arrived)
    return outputs


def body(
    dp_size,
    tokens,
    image_ids,
    norm_gain,
    qkv_weight,
    qk_gain,
    attn_weight,
    up_weight,
    up_bias,
    down_weight,
    down_bias,
    cotangent,
):
    part = tokens.shape[1]
    width = cotangent.shape[1]
    seqs = image_ids.shape[0]
    me = lax.axis_index("mp")
    dp = lax.axis_index("dp")
    shard = me.astype(jnp.int32)[None]
    place = jnp.bitwise_xor(shard, jnp.array([0, 2, 1, 3], jnp.int32)) * part

    own_t = tokens.T
    from_y = flip(own_t, "mp", 4, 2)
    gain_own = jnp.broadcast_to(norm_gain[:, None], (part, 128))
    gain_y = flip(gain_own, "mp", 4, 2)
    gain_c = flip(gain_own, "mp", 4, 1)

    mixed_t = jnp.transpose(qkv_weight, (1, 2, 0)).reshape(3 * part, width)
    def column(vector):
        return jnp.broadcast_to(vector[:, None], (vector.shape[0], 128))

    columns = (column(up_bias), column(qk_gain.astype(F32).reshape(2 * part)), column(down_bias))

    slots = jnp.arange(IMAGE_SLOTS, dtype=jnp.int32)[None, :, None]
    same = image_ids[:, None, :] == slots
    mask_q = same.astype(BF16)
    mask_k = jnp.where(same | (slots >= 8), 0.0, -PENALTY).astype(BF16)
    block_first = image_ids[:, ::BI]
    block_last = image_ids[:, BI - 1 :: BI]
    starts = jnp.sum(image_ids[:, None, :] < block_first[:, :, None], axis=2, dtype=jnp.int32)
    ends = jnp.sum(image_ids[:, None, :] <= block_last[:, :, None], axis=2, dtype=jnp.int32)
    first = starts // 128
    count = ((ends + 127) // 128 - first).reshape(-1)
    first = first.reshape(-1)

    pick = (jnp.arange(part)[:, None] + me * part == jnp.arange(width)[None, :]).astype(BF16)
    pick, place, columns, (gain_y, gain_c) = tie(pick, place, columns, (gain_y, gain_c))
    up_bias_col, head_gains, bias_col = columns
    gain_cy = flip(gain_y, "mp", 4, 1)
    d_act, d_att, cot_own, cot_sum = early_call(cotangent, down_weight, attn_weight, pick)
    prepared = (
        d_act, d_att, mixed_t, up_bias_col, head_gains, mask_q, mask_k, first, count,
        bias_col,
    )
    prepared, (from_y, gain_cy) = tie(prepared, (from_y, gain_cy))
    gains = (gain_own, gain_y, gain_c, gain_cy)
    (
        d_act, d_att, mixed_t, up_bias_col, head_gains, mask_q, mask_k, first, count,
        bias_col,
    ) = prepared
    pieces = (own_t, from_y, flip(own_t, "mp", 4, 1), flip(from_y, "mp", 4, 1))
    normed, active, d_pre, stats, upbias_part, gain_all, up_row, mlp_part = mlp_call(
        tuple(piece_order(dp_size)), place, pieces, gains, up_weight, up_bias_col, d_act, cotangent
    )
    mlp_sum = SumOverDp(mlp_part, dp_size, dp)

    (states,), flying = launch([mlp_sum], (normed,))
    attended, d_mixed, qk_part, norm_row, mix_part = attention_call(
        first, count, states, mixed_t, d_att, mask_q, mask_k, head_gains, cotangent
    )
    mix_sum = ChainOverDp(mix_part, dp_size, dp)

    norm_vec = norm_row[0] + jnp.sum(up_row, axis=1)
    norm_parts = norm_vec.reshape(4, part)
    norm_parts = [lax.dynamic_index_in_dim(norm_parts, jnp.bitwise_xor(me, m), 0, False) for m in range(4)]
    short = ShortSums(
        jnp.stack([norm_parts[0], norm_parts[2]]),
        jnp.stack([norm_parts[1], norm_parts[3]]),
        jnp.concatenate([jnp.sum(qk_part, axis=1), jnp.sum(upbias_part, axis=1), jnp.sum(cot_sum, axis=1)]),
        dp_size,
    )

    runs = [(seq, 1) for seq in range(seqs)]
    scatters = []
    for begin, size in runs:
        busy = [f[0] for f in flying]
        along = [m for m in [mix_sum, mlp_sum, short] + scatters if m.more() and m not in busy]
        (att, dm), flights = launch(along, (attended, d_mixed))
        flying = flying + flights
        sent = project_call(
            shard, active, att, d_pre, dm, normed, down_weight, attn_weight, up_weight, mixed_t, gain_all, begin, size
        )
        final = seqs - 1
        late = [f for f in flights if begin == 0 and f[0] is mix_sum or begin == final and f[0] is scatters[0]]
        wide = [f for f in flying if f[0] is mlp_sum]
        chain = [f for f in flying if f[0] is mix_sum and f not in late]
        quick = [f for f in flying if f not in late + wide + chain]
        keep, send = land_in_turn([quick, wide, chain], sent)
        if begin == final and begin > 0:
            _, ahead = launch([mix_sum], ())
            (keep, send), *_ = (land(late, (keep, send)),)
            late = ahead
        flying = late
        scatters.append(ScatterOverMp(keep, send))

    finished = ()
    wide_grads = ()
    done = set()

    def finish_ready(finished):
        for (begin, _), scatter in zip(runs, scatters):
            if not scatter.more() and begin not in done:
                done.add(begin)
                finished = finish_call(
                    scatter.keep, scatter.from_core, scatter.from_y, own_t, cot_own, stats, gain_own, bias_col,
                    finished, begin,
                )
        return finished

    while True:
        busy = [f[0] for f in flying]
        ready = [m for m in [mix_sum] + scatters + [short, mlp_sum] if m.more() and m not in busy]
        finished, flights = launch(ready, finished)
        flying = flying + flights
        if not flying:
            break
        finished = finish_ready(finished)
        near = [f for f in flying if f[0] in scatters and len(f[0].bits) == 2]
        across = [f for f in flying if f[0] in scatters and len(f[0].bits) == 1]
        chain = [f for f in flying if f[0] is mix_sum]
        rest = [f for f in flying if f[0] is short]
        wide = [f for f in flying if f[0] is mlp_sum]
        left = len(mix_sum.steps)
        if near:
            now = near + chain + rest
        elif left == 2:
            now = chain + across[:1] + rest
        elif left == 1:
            now = wide + rest or across[:1] or chain
        else:
            now = chain or rest or flying
        final = [f for f in now if f[0] is mix_sum]
        finished, wide_grads = land_in_turn([[f for f in now if f not in final], final], (finished, wide_grads))
        flying = [f for f in flying if f not in now]
        if not mlp_sum.more() and not wide_grads:
            swap, held, arrived = mlp_sum.last
            wide_grads = (
                jnp.where(swap, arrived, held).astype(F32),
                jnp.where(swap, held, arrived).astype(F32),
            )
    finished = finish_ready(finished)
    block_out, token_grad = finished
    block_out, token_grad = block_out.T, token_grad.T
    swap, held, arrived = mix_sum.last
    left = 3 * part - held.shape[0]
    qkv_rows = joined(swap, held, arrived)[: 3 * part].astype(F32)
    attn_grad = jnp.where(swap, held[left:], arrived[left:]).astype(F32)
    qkv_grad = jnp.transpose(qkv_rows.reshape(3, part, width), (2, 0, 1))

    gain_grad = short.norm / norm_gain.astype(F32)
    rest = short.rest
    split = 2 * part + up_weight.shape[1]
    return (
        block_out,
        token_grad,
        gain_grad,
        qkv_grad,
        rest[: 2 * part].reshape(2, part),
        attn_grad,
        wide_grads[1],
        rest[2 * part : split],
        wide_grads[0],
        rest[split:],
    )


def solution(mesh):
    in_specs = (
        P("dp", "mp"),
        P("dp", None),
        P("mp"),
        P(None, None, "mp"),
        P(None, "mp"),
        P("mp", None),
        P(None, "mp"),
        P("mp"),
        P("mp", None),
        P("mp"),
        P("dp", None),
    )
    out_specs = (
        P("dp", "mp"),
        P("dp", "mp"),
        P("mp"),
        P(None, None, "mp"),
        P(None, "mp"),
        P("mp", None),
        P(None, "mp"),
        P("mp"),
        P("mp", None),
        P("mp"),
    )
    run = functools.partial(body, mesh.shape["dp"])
    return jax.shard_map(run, mesh=mesh, in_specs=in_specs, out_specs=out_specs, check_vma=False)
```

```python
import functools

import jax
import jax.numpy as jnp
from jax import lax
from jax.experimental import pallas as pl
from jax.experimental.pallas import tpu as pltpu
from jax.sharding import PartitionSpec as P

DH = 64
LEN = 1024
EPSILON = 1e-06
IMAGE_SLOTS = 16
PENALTY = 1024.0
BI = 256
BJ = 256
SUM_ROWS = 16
F32 = jnp.float32
BF16 = jnp.bfloat16

NN = (((1,), (0,)), ((), ()))
NT = (((1,), (1,)), ((), ()))
TN = (((0,), (0,)), ((), ()))
ANY = pl.BlockSpec(memory_space=pl.ANY)


def dot(left, right, dims=NN):
    return lax.dot_general(left, right, dims, preferred_element_type=F32)


def fold_lanes(rows):
    total = rows[:, :128]
    for start in range(128, rows.shape[1], 128):
        total = total + rows[:, start : start + 128]
    return total


def cost(microseconds, nbytes):
    return pl.CostEstimate(flops=int(microseconds * 1e3), bytes_accessed=nbytes // 1000, transcendentals=0)


def early_kernel(cot, down, attn, pick, d_act, d_att, cot_own, bias_sum):
    rows = cot[...]
    d_act[...] = dot(down[...], rows, NT).astype(BF16)
    d_att[...] = dot(attn[...], rows, NT).astype(BF16)
    own = dot(pick[...], rows, NT)
    cot_own[...] = own.astype(BF16)

    @pl.when(pl.program_id(0) == 0)
    def _():
        bias_sum[...] = jnp.zeros_like(bias_sum)

    bias_sum[...] += fold_lanes(own)


def early_call(cot, down, attn, pick, block=512):
    tokens, width = cot.shape
    seqs = tokens // LEN
    hidden, part = down.shape[0], attn.shape[0]
    steps = LEN // block
    fixed = lambda i: (0, 0)
    by_seq = lambda i: (i // steps, 0, i % steps)
    return pl.pallas_call(
        early_kernel,
        grid=(tokens // block,),
        in_specs=[
            pl.BlockSpec((block, width), lambda i: (i, 0)),
            pl.BlockSpec((hidden, width), fixed),
            pl.BlockSpec((part, width), fixed),
            pl.BlockSpec((part, width), fixed),
        ],
        out_specs=[
            pl.BlockSpec((None, hidden, block), by_seq),
            pl.BlockSpec((None, part, block), by_seq),
            pl.BlockSpec((part, block), lambda i: (0, i)),
            pl.BlockSpec((part, 128), fixed),
        ],
        out_shape=[
            jax.ShapeDtypeStruct((seqs, hidden, LEN), BF16),
            jax.ShapeDtypeStruct((seqs, part, LEN), BF16),
            jax.ShapeDtypeStruct((part, tokens), BF16),
            jax.ShapeDtypeStruct((part, 128), F32),
        ],
        cost_estimate=cost(10, 12_000_000),
        name="early",
    )(cot, down, attn, pick)


def mlp_kernel(
    pieces_order, place, own, flip_y, flip_c, flip_cy, gain_own, gain_y, gain_c, gain_cy, up, up_bias, d_act, cot,
    normed, active, d_pre, stats, bias_sum, gain_all, up_row, grads, low, high
):
    pieces = (own, flip_y, flip_c, flip_cy)
    part = own.shape[0]
    width = part * 4
    first = pl.program_id(0) == 0
    last = pl.program_id(0) == pl.num_programs(0) - 1

    @pl.when(first)
    def _():
        bias_sum[...] = jnp.zeros_like(bias_sum)
        low[...] = jnp.zeros_like(low)
        high[...] = jnp.zeros_like(high)
        for slot, piece in enumerate((gain_own, gain_y, gain_c, gain_cy)):
            gain_all[pl.ds(pl.multiple_of(place[slot], part), part), :] = piece[...].astype(F32)

    total = 0.0
    squares = 0.0
    for piece in pieces:
        rows = piece[...].astype(F32)
        total = total + jnp.sum(rows, axis=0, keepdims=True)
        squares = squares + jnp.sum(rows * rows, axis=0, keepdims=True)
    mean = total * (1.0 / width)
    scale = lax.rsqrt(squares * (1.0 / width) - mean * mean + EPSILON)
    stats[0:1, :] = mean
    stats[1:2, :] = scale
    stats[2:8, :] = jnp.zeros((6, stats.shape[1]), F32)
    for slot, piece in enumerate(pieces):
        rows = piece[...].astype(F32)
        here = pl.ds(pl.multiple_of(place[slot], part), part)
        normed[here, :] = ((rows - mean) * scale * gain_all[here, :1]).astype(BF16)

    c0 = 0.7978845608028654
    c1 = 0.044715 * c0
    def lift(start):
        here = slice(start, start + 256)
        return dot(up[:, here], normed[...], TN) + up_bias[here, :1].astype(F32)

    ahead = lift(0)
    for start in range(0, up.shape[1], 256):
        here = slice(start, start + 256)
        pre = ahead
        if start + 256 < up.shape[1]:
            ahead = lift(start + 256)
        square = pre * pre
        half = 0.5 * jnp.tanh(pre * (c0 + c1 * square)) + 0.5
        act = (pre * half).astype(BF16)
        active[here, :] = act
        slope = half + pre * (half - half * half) * (2.0 * c0 + 6.0 * c1 * square)
        grad = (d_act[here, :].astype(F32) * slope).astype(BF16)
        d_pre[here, :] = grad
        bias_sum[here, :] += fold_lanes(grad.astype(F32))
        low[here, :] += dot(act, cot[...])
        high[:, here] += dot(normed[...], grad, NT)

    @pl.when(last)
    def _():
        up_row[...] = fold_lanes(high[...] * up[...].astype(F32))
        half = low.shape[0]
        size = grads.shape[0] // len(pieces_order)
        for slot, piece in enumerate(pieces_order):
            source, start = (low, piece * size) if piece * size < half else (high, piece * size - half)
            grads[slot * size : (slot + 1) * size, :] = source[start : start + size, :].astype(BF16)


def mlp_call(pieces_order, place, pieces, gains, up, up_bias, d_act, cot, block=512):
    part, tokens = pieces[0].shape
    width = 4 * part
    seqs, hidden, _ = d_act.shape
    steps = LEN // block
    lanes = lambda i, *_: (0, i)
    by_seq = lambda i, *_: (i // steps, 0, i % steps)
    fixed = lambda i, *_: (0, 0)
    grid_spec = pltpu.PrefetchScalarGridSpec(
        num_scalar_prefetch=1,
        grid=(tokens // block,),
        in_specs=[pl.BlockSpec((part, block), lanes)] * 4
        + [pl.BlockSpec((part, 128), fixed)] * 4
        + [
            pl.BlockSpec((width, hidden), fixed),
            pl.BlockSpec((hidden, 128), fixed),
            pl.BlockSpec((None, hidden, block), by_seq),
            pl.BlockSpec((block, width), lambda i, *_: (i, 0)),
        ],
        out_specs=[
            pl.BlockSpec((None, width, block), by_seq),
            pl.BlockSpec((None, hidden, block), by_seq),
            pl.BlockSpec((None, hidden, block), by_seq),
            pl.BlockSpec((8, block), lanes),
            pl.BlockSpec((hidden, 128), fixed),
            pl.BlockSpec((width, 128), fixed),
            pl.BlockSpec((width, 128), fixed),
            pl.BlockSpec((hidden + width, width), fixed),
        ],
        scratch_shapes=[pltpu.VMEM((hidden, width), F32), pltpu.VMEM((width, hidden), F32)],
    )
    assert hidden == width
    return pl.pallas_call(
        functools.partial(mlp_kernel, pieces_order),
        grid_spec=grid_spec,
        out_shape=[
            jax.ShapeDtypeStruct((seqs, width, LEN), BF16),
            jax.ShapeDtypeStruct((seqs, hidden, LEN), BF16),
            jax.ShapeDtypeStruct((seqs, hidden, LEN), BF16),
            jax.ShapeDtypeStruct((8, tokens), F32),
            jax.ShapeDtypeStruct((hidden, 128), F32),
            jax.ShapeDtypeStruct((width, 128), F32),
            jax.ShapeDtypeStruct((width, 128), F32),
            jax.ShapeDtypeStruct((hidden + width, width), BF16),
        ],
        cost_estimate=cost(20, 30_000_000),
        name="mlp",
    )(place, *pieces, *gains, up, up_bias, d_act, cot)


def attention_kernel(
    first, count, normed, mixed_t, d_att, mask_q, mask_k, gains, cot, attended, d_mixed, gain_sum, norm_row, grads,
    total, qkv, qx, kx, vn, kt, vt, es, ps, dqa, dka, dva
):
    seq = pl.program_id(0)
    last = seq == pl.num_programs(0) - 1
    part = attended.shape[0]
    heads = part // DH
    inv_dh = 1.0 / DH

    @pl.when(seq == 0)
    def _():
        total[...] = jnp.zeros_like(total)
        gain_sum[...] = jnp.zeros_like(gain_sum)

    qkv[...] = dot(mixed_t[...], normed[...])

    def unit(start):
        raw = qkv[start : start + DH, :]
        shifted = raw - jnp.sum(raw, axis=0, keepdims=True) * inv_dh
        scale = lax.rsqrt(jnp.sum(shifted * shifted, axis=0, keepdims=True) * inv_dh + EPSILON)
        return shifted * scale, scale

    zeros = jnp.zeros((128 - DH - IMAGE_SLOTS, LEN), BF16)
    for head in range(heads):
        rows = slice(head * DH, (head + 1) * DH)
        query, _ = unit(head * DH)
        query = (query * (gains[rows, :1] * 0.125)).astype(BF16)
        qx[head] = jnp.concatenate([query, mask_q[...], zeros], axis=0)
        key, _ = unit(part + head * DH)
        key = (key * gains[part + head * DH : part + (head + 1) * DH, :1]).astype(BF16)
        kt[rows, :] = key
        kx[head] = jnp.concatenate([key, mask_k[...], zeros], axis=0).T
        value = qkv[2 * part + head * DH : 2 * part + (head + 1) * DH, :].astype(BF16)
        vt[rows, :] = value
        vn[head] = value.T
    dka[...] = jnp.zeros_like(dka)
    dva[...] = jnp.zeros_like(dva)

    def straight(units, i0, base):
        icols = pl.ds(i0, BI)
        edges = [(at, min(BJ, units * 128 - at)) for at in range(0, units * 128, BJ)]
        trips = len(edges)
        spots = [slice(at, at + size) for at, size in edges]
        places = [pl.ds(pl.multiple_of(base + at, 128), size) for at, size in edges]

        def scores(head, j, sums):
            rows = slice(head * DH, (head + 1) * DH)
            e = jnp.exp(dot(kx[head, places[j], :], qx[head, :, icols]))
            p = dot(vn[head, places[j], :], d_att[rows, icols])
            es[head % 2, spots[j], :] = e
            ps[head % 2, spots[j], :] = p
            more = (jnp.sum(e, axis=0, keepdims=True), jnp.sum(e * p, axis=0, keepdims=True))
            return more if sums is None else (sums[0] + more[0], sums[1] + more[1])

        def row_grads(head, j, inverse, inner, held):
            rows = slice(head * DH, (head + 1) * DH)
            w = es[head % 2, spots[j], :] * inverse
            d = (w * (ps[head % 2, spots[j], :] - inner)).astype(BF16)
            w = w.astype(BF16)
            out = dot(vt[rows, places[j]], w)
            query = dot(kt[rows, places[j]], d)
            dva[rows, places[j]] += dot(d_att[rows, icols], w, NT)
            dka[rows, places[j]] += dot(qx[head, :DH, icols], d, NT)
            return (out, query) if held is None else (held[0] + out, held[1] + query)

        sums = None
        for j in range(trips):
            sums = scores(0, j, sums)
        for head in range(heads):
            rows = slice(head * DH, (head + 1) * DH)
            inverse = 1.0 / sums[0]
            inner = sums[1] * inverse
            held = following = None
            for j in range(trips):
                if head + 1 < heads:
                    following = scores(head + 1, j, following)
                held = row_grads(head, j, inverse, inner, held)
            attended[rows, icols] = held[0].astype(BF16)
            dqa[rows, icols] = held[1]
            sums = following

    def query_block(ib, _):
        i0 = pl.multiple_of(ib * BI, BI)
        base = first[seq * (LEN // BI) + ib] * 128
        trips = count[seq * (LEN // BI) + ib]
        for number in range(BI // 128, LEN // 128 + 1):
            pl.when(trips == number)(functools.partial(straight, number, i0, base))
        return 0

    lax.fori_loop(0, LEN // BI, query_block, 0)

    for source, offset, factor in ((dqa, 0, 0.125), (dka, part, 1.0)):
        for head in range(heads):
            start = offset + head * DH
            u, scale = unit(start)
            e = source[head * DH : (head + 1) * DH, :] * factor
            gain_sum[start : start + DH, :] += fold_lanes(e * u)
            f = e * gains[start : start + DH, :1]
            mean_f = jnp.sum(f, axis=0, keepdims=True) * inv_dh
            mean_fu = jnp.sum(f * u, axis=0, keepdims=True) * inv_dh
            d_mixed[start : start + DH, :] = ((f - mean_f - u * mean_fu) * scale).astype(BF16)
    d_mixed[2 * part :, :] = dva[...].astype(BF16)

    split = 3 * part
    total[:split, :] += dot(d_mixed[...], normed[...], NT)
    total[split:, :] += dot(attended[...], cot[...])

    @pl.when(last)
    def _():
        norm_row[...] = jnp.sum(total[:split, :] * mixed_t[...].astype(F32), axis=0, keepdims=True)
        grads[...] = total[...].astype(BF16)


def attention_call(first, count, normed, mixed_t, d_att, mask_q, mask_k, gains, cot):
    seqs, part, _ = d_att.shape
    width = normed.shape[1]
    heads = part // DH
    fixed = lambda i, *_: (0, 0)
    by_seq = lambda i, *_: (i, 0, 0)
    grid_spec = pltpu.PrefetchScalarGridSpec(
        num_scalar_prefetch=2,
        grid=(seqs,),
        in_specs=[
            pl.BlockSpec((None, width, LEN), by_seq),
            pl.BlockSpec((3 * part, width), fixed),
            pl.BlockSpec((None, part, LEN), by_seq),
            pl.BlockSpec((None, IMAGE_SLOTS, LEN), by_seq),
            pl.BlockSpec((None, IMAGE_SLOTS, LEN), by_seq),
            pl.BlockSpec((2 * part, 128), fixed),
            pl.BlockSpec((LEN, width), lambda i, *_: (i, 0)),
        ],
        out_specs=[
            pl.BlockSpec((None, part, LEN), by_seq),
            pl.BlockSpec((None, 3 * part, LEN), by_seq),
            pl.BlockSpec((2 * part, 128), fixed),
            pl.BlockSpec((1, width), fixed),
            pl.BlockSpec((4 * part, width), fixed),
        ],
        scratch_shapes=[
            pltpu.VMEM((4 * part, width), F32),
            pltpu.VMEM((3 * part, LEN), F32),
            pltpu.VMEM((heads, 128, LEN), BF16),
            pltpu.VMEM((heads, LEN, 128), BF16),
            pltpu.VMEM((heads, LEN, DH), BF16),
            pltpu.VMEM((part, LEN), BF16),
            pltpu.VMEM((part, LEN), BF16),
            pltpu.VMEM((2, LEN, BI), F32),
            pltpu.VMEM((2, LEN, BI), F32),
            pltpu.VMEM((part, LEN), F32),
            pltpu.VMEM((part, LEN), F32),
            pltpu.VMEM((part, LEN), F32),
        ],
    )
    return pl.pallas_call(
        attention_kernel,
        grid_spec=grid_spec,
        out_shape=[
            jax.ShapeDtypeStruct((seqs, part, LEN), BF16),
            jax.ShapeDtypeStruct((seqs, 3 * part, LEN), BF16),
            jax.ShapeDtypeStruct((2 * part, 128), F32),
            jax.ShapeDtypeStruct((1, width), F32),
            jax.ShapeDtypeStruct((4 * part, width), BF16),
        ],
        cost_estimate=cost(18, 5_000_000),
        name="attention",
    )(first, count, normed, mixed_t, d_att, mask_q, mask_k, gains, cot)


def project_kernel(
    shard, active, attended, d_pre, d_mixed, normed, down, attn, up, mixed_t, gain, keep, send
):
    me = shard[0]
    part = attended.shape[0]
    out = dot(down[...], active[...], TN) + dot(attn[...], attended[...], TN)
    grad = dot(up[...], d_pre[...]) + dot(mixed_t[...], d_mixed[...], TN)
    product = grad * normed[...].astype(F32)
    sums = []
    for row in (jnp.sum(grad * gain[:, :1], axis=0, keepdims=True), jnp.sum(product, axis=0, keepdims=True)):
        high = row.astype(BF16)
        sums += [high, (row - high.astype(F32)).astype(BF16)]
    sums = jnp.concatenate(sums + [jnp.zeros((SUM_ROWS - 4, sums[0].shape[1]), BF16)], axis=0)
    for target in (keep, send):
        for slot in range(2):
            target[slot, 2 * part :, :] = sums
    for index in range(4):
        rows = slice(index * part, (index + 1) * part)
        away = jnp.bitwise_xor(me, index)
        slot = away // 2

        @pl.when(away % 2 == 0)
        def _():
            keep[slot, :part, :] = out[rows].astype(BF16)
            keep[slot, part : 2 * part, :] = grad[rows].astype(BF16)

        @pl.when(away % 2 == 1)
        def _():
            send[slot, :part, :] = out[rows].astype(BF16)
            send[slot, part : 2 * part, :] = grad[rows].astype(BF16)


def project_call(shard, active, attended, d_pre, d_mixed, normed, down, attn, up, mixed_t, gain, begin, size, block=256):
    hidden, width = down.shape
    part = attended.shape[1]
    steps = LEN // block
    ours = lambda i, *_: (begin + i // steps, 0, i % steps)
    out = lambda i, *_: (i // steps, 0, 0, i % steps)
    fixed = lambda i, *_: (0, 0)
    rows = 2 * part + SUM_ROWS
    grid_spec = pltpu.PrefetchScalarGridSpec(
        num_scalar_prefetch=1,
        grid=(size * steps,),
        in_specs=[
            pl.BlockSpec((None, hidden, block), ours),
            pl.BlockSpec((None, part, block), ours),
            pl.BlockSpec((None, hidden, block), ours),
            pl.BlockSpec((None, 3 * part, block), ours),
            pl.BlockSpec((None, width, block), ours),
            pl.BlockSpec((hidden, width), fixed),
            pl.BlockSpec((part, width), fixed),
            pl.BlockSpec((width, hidden), fixed),
            pl.BlockSpec((3 * part, width), fixed),
            pl.BlockSpec((width, 128), fixed),
        ],
        out_specs=[
            pl.BlockSpec((None, 2, rows, block), out),
            pl.BlockSpec((None, 2, rows, block), out),
        ],
    )
    return pl.pallas_call(
        project_kernel,
        grid_spec=grid_spec,
        out_shape=[
            jax.ShapeDtypeStruct((size, 2, rows, LEN), BF16),
            jax.ShapeDtypeStruct((size, 2, rows, LEN), BF16),
        ],
        cost_estimate=cost(8, 16_000_000),
        name="project",
    )(shard, active, attended, d_pre, d_mixed, normed, down, attn, up, mixed_t, gain)


def finish_kernel(keep, from_core, from_y, own_t, cot, stats, gain, bias, *rest):
    block_out, token_grad = rest[-2:]
    part = own_t.shape[0]
    inv_width = 0.25 / part
    total = keep[...].astype(F32) + from_core[...].astype(F32) + from_y[...].astype(F32)
    own = own_t[...].astype(F32)
    block_out[...] = (own + total[:part] + bias[:, :1].astype(F32)).astype(BF16)
    grad = total[part : 2 * part]
    sums = total[2 * part :]
    mean = stats[0:1, :]
    scale = stats[1:2, :]
    hat = (own - mean) * scale
    inner = grad * gain[:, :1].astype(F32) - (sums[0:1] + sums[1:2]) * inv_width - hat * ((sums[2:3] + sums[3:4]) * inv_width)
    token_grad[...] = cot[...].astype(F32) + inner * scale


def finish_call(keep, from_core, from_y, own_t, cot, stats, gain, bias, before, begin, block=512):
    part, tokens = own_t.shape
    steps = LEN // block
    size = keep.shape[0]
    fixed = lambda i: (0, 0)
    packed = pl.BlockSpec((None, None, 2 * part + SUM_ROWS, block), lambda i: (i // steps, 0, 0, i % steps))
    ours = lambda i: (0, begin * steps + i)
    here = pl.BlockSpec((part, block), ours)
    return pl.pallas_call(
        finish_kernel,
        grid=(size * steps,),
        in_specs=[
            packed, packed, packed,
            here, here,
            pl.BlockSpec((8, block), ours),
            pl.BlockSpec((part, 128), fixed),
            pl.BlockSpec((part, 128), fixed),
        ]
        + [ANY] * len(before),
        out_specs=[here, here],
        out_shape=[
            jax.ShapeDtypeStruct((part, tokens), BF16),
            jax.ShapeDtypeStruct((part, tokens), F32),
        ],
        input_output_aliases={8 + i: i for i in range(len(before))},
        cost_estimate=cost(3, 5_000_000),
        name="finish",
    )(keep, from_core, from_y, own_t, cot, stats, gain, bias, *before)


def flip(value, axis, size, bit):
    return lax.ppermute(value, axis, [(i, i ^ bit) for i in range(size)])


def tie(*trees):
    return lax.optimization_barrier(trees)


def joined(swap, held, arrived):
    return jnp.where(
        swap, jnp.concatenate([arrived, held], axis=0), jnp.concatenate([held, arrived], axis=0)
    )


def piece_order(size):
    bits = size.bit_length() - 1
    return [sum(((i >> b) & 1) << (bits - 1 - b) for b in range(bits)) for i in range(size)]


class SumOverDp:
    def __init__(self, value, size, index):
        self.size, self.index = size, index
        self.send = value
        self.steps = ["sum"] + [1 << i for i in reversed(range(size.bit_length() - 1))]

    def more(self):
        return bool(self.steps)

    def move(self, send):
        if self.steps[0] == "sum":
            return lax.all_to_all(send, "dp", 0, 0, tiled=True)
        return flip(send, "dp", self.size, self.steps[0])

    def take(self, arrived):
        step = self.steps.pop(0)
        if step == "sum":
            shares = arrived.reshape(self.size, -1, arrived.shape[1]).astype(F32)
            self.keep = jnp.sum(shares, axis=0).astype(BF16)
        else:
            self.last = ((self.index & step) > 0, self.keep, arrived)
            self.keep = joined(*self.last)
        self.send = self.keep


class ChainOverDp:
    def __init__(self, value, size, index):
        self.size, self.index = size, index
        bits = [1 << i for i in range(size.bit_length() - 1)]
        self.steps = [("sum", bit) for bit in bits] + [("join", bit) for bit in reversed(bits)]
        self.prepare(value, None)

    def prepare(self, held, arrived):
        def part(which, half):
            rows = lax.dynamic_slice_in_dim(held, which * half, half, 0)
            if arrived is None:
                return rows
            came = lax.dynamic_slice_in_dim(arrived, which * half, half, 0)
            return (rows.astype(F32) + came.astype(F32)).astype(BF16)

        rows = held.shape[0]
        if self.steps and self.steps[0][0] == "sum":
            side = ((self.index & self.steps[0][1]) > 0).astype(jnp.int32)
            self.send, self.keep = part(1 - side, rows // 2), part(side, rows // 2)
        else:
            self.keep = part(0, rows)
            self.send = self.keep

    def more(self):
        return bool(self.steps)

    def move(self, send):
        return flip(send, "dp", self.size, self.steps[0][1])

    def take(self, arrived):
        kind, bit = self.steps.pop(0)
        if kind == "sum":
            self.prepare(self.keep, arrived)
            return
        self.last = ((self.index & bit) > 0, self.keep, arrived)
        self.keep = self.send = joined(*self.last)


class ScatterOverMp:
    def __init__(self, keep, send):
        self.keep, self.send = keep, send
        self.bits = [1, 2]

    def more(self):
        return bool(self.bits)

    def move(self, send):
        return flip(send, "mp", 4, self.bits[0])

    def take(self, arrived):
        bit = self.bits.pop(0)
        if bit == 1:
            self.from_core = arrived
            self.send = (self.keep[:, 1:].astype(F32) + arrived[:, 1:].astype(F32)).astype(BF16)
        else:
            self.from_y = arrived


def land_in_turn(phases, outputs):
    movers = []
    for flights in phases:
        outputs, sends, arrivals = tie(outputs, [m.send for m in movers], [f[1] for f in flights])
        for mover, send in zip(movers, sends):
            mover.send = send
        for (mover, _), arrived in zip(flights, arrivals):
            mover.take(arrived)
        movers += [f[0] for f in flights]
    return outputs


class ShortSums:
    def __init__(self, keep, send, rest, size):
        self.keep, self.send, self.rest, self.size = keep, send, rest, size
        self.steps = [("mp", 1), ("mp", 2)] + [("dp", 1 << i) for i in range(size.bit_length() - 1)]

    def more(self):
        return bool(self.steps)

    def move(self, send):
        axis, bit = self.steps[0]
        return flip(send, axis, 4 if axis == "mp" else self.size, bit)

    def take(self, arrived):
        axis, bit = self.steps.pop(0)
        if (axis, bit) == ("mp", 1):
            both = self.keep + arrived
            self.norm, self.send = both[0], both[1]
            return
        if axis == "mp":
            self.send = jnp.concatenate([self.norm + arrived, self.rest])
        else:
            self.send = self.send + arrived
        size = self.norm.shape[0]
        self.norm, self.rest = self.send[:size], self.send[size:]


def launch(movers, inputs):
    movers = [m for m in movers if m.more()]
    inputs, sends = tie(inputs, [m.send for m in movers])
    return inputs, [(m, m.move(s)) for m, s in zip(movers, sends)]


def land(flights, outputs):
    outputs, arrivals = tie(outputs, [f[1] for f in flights])
    for (mover, _), arrived in zip(flights, arrivals):
        mover.take(arrived)
    return outputs


def body(
    dp_size,
    tokens,
    image_ids,
    norm_gain,
    qkv_weight,
    qk_gain,
    attn_weight,
    up_weight,
    up_bias,
    down_weight,
    down_bias,
    cotangent,
):
    part = tokens.shape[1]
    width = cotangent.shape[1]
    seqs = image_ids.shape[0]
    me = lax.axis_index("mp")
    dp = lax.axis_index("dp")
    shard = me.astype(jnp.int32)[None]
    place = jnp.bitwise_xor(shard, jnp.array([0, 2, 1, 3], jnp.int32)) * part

    own_t = tokens.T
    from_y = flip(own_t, "mp", 4, 2)
    gain_own = jnp.broadcast_to(norm_gain[:, None], (part, 128))
    gain_y = flip(gain_own, "mp", 4, 2)
    gain_c = flip(gain_own, "mp", 4, 1)

    mixed_t = jnp.transpose(qkv_weight, (1, 2, 0)).reshape(3 * part, width)
    def column(vector):
        return jnp.broadcast_to(vector[:, None], (vector.shape[0], 128))

    columns = (column(up_bias), column(qk_gain.astype(F32).reshape(2 * part)), column(down_bias))

    slots = jnp.arange(IMAGE_SLOTS, dtype=jnp.int32)[None, :, None]
    same = image_ids[:, None, :] == slots
    mask_q = same.astype(BF16)
    mask_k = jnp.where(same | (slots >= 8), 0.0, -PENALTY).astype(BF16)
    block_first = image_ids[:, ::BI]
    block_last = image_ids[:, BI - 1 :: BI]
    starts = jnp.sum(image_ids[:, None, :] < block_first[:, :, None], axis=2, dtype=jnp.int32)
    ends = jnp.sum(image_ids[:, None, :] <= block_last[:, :, None], axis=2, dtype=jnp.int32)
    first = starts // 128
    count = ((ends + 127) // 128 - first).reshape(-1)
    first = first.reshape(-1)

    pick = (jnp.arange(part)[:, None] + me * part == jnp.arange(width)[None, :]).astype(BF16)
    pick, place, columns, (gain_y, gain_c) = tie(pick, place, columns, (gain_y, gain_c))
    up_bias_col, head_gains, bias_col = columns
    gain_cy = flip(gain_y, "mp", 4, 1)
    d_act, d_att, cot_own, cot_sum = early_call(cotangent, down_weight, attn_weight, pick)
    prepared = (
        d_act, d_att, mixed_t, up_bias_col, head_gains, mask_q, mask_k, first, count,
        bias_col,
    )
    prepared, (from_y, gain_cy) = tie(prepared, (from_y, gain_cy))
    gains = (gain_own, gain_y, gain_c, gain_cy)
    (
        d_act, d_att, mixed_t, up_bias_col, head_gains, mask_q, mask_k, first, count,
        bias_col,
    ) = prepared
    pieces = (own_t, from_y, flip(own_t, "mp", 4, 1), flip(from_y, "mp", 4, 1))
    normed, active, d_pre, stats, upbias_part, gain_all, up_row, mlp_part = mlp_call(
        tuple(piece_order(dp_size)), place, pieces, gains, up_weight, up_bias_col, d_act, cotangent
    )
    mlp_sum = SumOverDp(mlp_part, dp_size, dp)

    (states,), flying = launch([mlp_sum], (normed,))
    attended, d_mixed, qk_part, norm_row, mix_part = attention_call(
        first, count, states, mixed_t, d_att, mask_q, mask_k, head_gains, cotangent
    )
    mix_sum = ChainOverDp(mix_part, dp_size, dp)

    norm_vec = norm_row[0] + jnp.sum(up_row, axis=1)
    norm_parts = norm_vec.reshape(4, part)
    norm_parts = [lax.dynamic_index_in_dim(norm_parts, jnp.bitwise_xor(me, m), 0, False) for m in range(4)]
    short = ShortSums(
        jnp.stack([norm_parts[0], norm_parts[2]]),
        jnp.stack([norm_parts[1], norm_parts[3]]),
        jnp.concatenate([jnp.sum(qk_part, axis=1), jnp.sum(upbias_part, axis=1), jnp.sum(cot_sum, axis=1)]),
        dp_size,
    )

    runs = [(seq, 1) for seq in range(seqs)]
    scatters = []
    for begin, size in runs:
        busy = [f[0] for f in flying]
        along = [m for m in [mix_sum, mlp_sum, short] + scatters if m.more() and m not in busy]
        (att, dm), flights = launch(along, (attended, d_mixed))
        flying = flying + flights
        sent = project_call(
            shard, active, att, d_pre, dm, normed, down_weight, attn_weight, up_weight, mixed_t, gain_all, begin, size
        )
        final = seqs - 1
        late = [f for f in flights if begin == 0 and f[0] is mix_sum or begin == final and f[0] is scatters[0]]
        wide = [f for f in flying if f[0] is mlp_sum]
        chain = [f for f in flying if f[0] is mix_sum and f not in late]
        quick = [f for f in flying if f not in late + wide + chain]
        keep, send = land_in_turn([quick, chain, wide] if begin == 1 else [quick, wide, chain], sent)
        if begin == final and begin > 0:
            _, ahead = launch([mix_sum], ())
            (keep, send), *_ = (land(late, (keep, send)),)
            late = ahead
        flying = late
        scatters.append(ScatterOverMp(keep, send))

    finished = ()
    wide_grads = ()
    done = set()

    def finish_ready(finished):
        for (begin, _), scatter in zip(runs, scatters):
            if not scatter.more() and begin not in done:
                done.add(begin)
                finished = finish_call(
                    scatter.keep, scatter.from_core, scatter.from_y, own_t, cot_own, stats, gain_own, bias_col,
                    finished, begin,
                )
        return finished

    while True:
        busy = [f[0] for f in flying]
        ready = [m for m in [mix_sum] + scatters + [short, mlp_sum] if m.more() and m not in busy]
        finished, flights = launch(ready, finished)
        flying = flying + flights
        if not flying:
            break
        finished = finish_ready(finished)
        near = [f for f in flying if f[0] in scatters and len(f[0].bits) == 2]
        across = [f for f in flying if f[0] in scatters and len(f[0].bits) == 1]
        chain = [f for f in flying if f[0] is mix_sum]
        rest = [f for f in flying if f[0] is short]
        wide = [f for f in flying if f[0] is mlp_sum]
        left = len(mix_sum.steps)
        if near:
            now = near + chain + rest
        elif left == 2:
            now = chain + across[:1] + rest
        elif left == 1:
            now = wide + rest or across[:1] or chain
        else:
            now = chain + rest or flying
        final = [f for f in now if f[0] is mix_sum]
        finished, wide_grads = land_in_turn([[f for f in now if f not in final], final], (finished, wide_grads))
        flying = [f for f in flying if f not in now]
        if not mlp_sum.more() and not wide_grads:
            swap, held, arrived = mlp_sum.last
            wide_grads = (
                jnp.where(swap, arrived, held).astype(F32),
                jnp.where(swap, held, arrived).astype(F32),
            )
    finished = finish_ready(finished)
    block_out, token_grad = finished
    block_out, token_grad = block_out.T, token_grad.T
    swap, held, arrived = mix_sum.last
    left = 3 * part - held.shape[0]
    qkv_rows = joined(swap, held, arrived)[: 3 * part].astype(F32)
    attn_grad = jnp.where(swap, held[left:], arrived[left:]).astype(F32)
    qkv_grad = jnp.transpose(qkv_rows.reshape(3, part, width), (2, 0, 1))

    gain_grad = short.norm / norm_gain.astype(F32)
    rest = short.rest
    split = 2 * part + up_weight.shape[1]
    return (
        block_out,
        token_grad,
        gain_grad,
        qkv_grad,
        rest[: 2 * part].reshape(2, part),
        attn_grad,
        wide_grads[1],
        rest[2 * part : split],
        wide_grads[0],
        rest[split:],
    )


def solution(mesh):
    in_specs = (
        P("dp", "mp"),
        P("dp", None),
        P("mp"),
        P(None, None, "mp"),
        P(None, "mp"),
        P("mp", None),
        P(None, "mp"),
        P("mp"),
        P("mp", None),
        P("mp"),
        P("dp", None),
    )
    out_specs = (
        P("dp", "mp"),
        P("dp", "mp"),
        P("mp"),
        P(None, None, "mp"),
        P(None, "mp"),
        P("mp", None),
        P(None, "mp"),
        P("mp"),
        P("mp", None),
        P("mp"),
    )
    run = functools.partial(body, mesh.shape["dp"])
    return jax.shard_map(run, mesh=mesh, in_specs=in_specs, out_specs=out_specs, check_vma=False)
```
